32 devices in a mesh: leaf: 8 (over z, y), front: 4 (over x, core).
Axes of the slice: x: 2, y: 2, z: 4, core: 2. Of those that a mesh axis runs over, the one named last changes fastest.
Arguments:
- rhs_local: float32 [256, 256, 256], P(('leaf', 'front')), may hold values from -6 to 6
- dinv_local: float32 [256, 256, 256], P(('leaf', 'front')), may hold values from -1 to 2
- update_local: float32 [256, 256, 256], P(('leaf', 'front')), may hold values from -0.25 to 0.25
- parent: int32 [256], P(('leaf', 'front')), may hold values from 1 to 8, as said below
- row_blocks: int32 [256, 256], P(('leaf', 'front')), may hold values from 0 to 255, each once within a row
- sep_rhs: float32 [2048, 256], P(('leaf', 'front')), may hold values from -6 to 6
- sep_dinv: float32 [2048, 256], P(('leaf', 'front')), may hold values from -1 to 2
- sep_coupling: float32 [2048, 256], P(('leaf', 'front')), may hold values from -2 to 1
Outputs:
- sol_local: float32 [256, 256, 256], P(('leaf', 'front'))
- sep_solution: float32 [2048, 256], P(('leaf', 'front'))
The draws below stay inside these ranges and needn't reach their ends.
Inputs may be any that keep to these rules, and one draw needn't show every extreme that they name: parent_k is the position of supernode k's parent within the same block of 8, always greater than k; the value 8 names the block's separator. `row_blocks`: each row is a permutation of 0 .. 255.
All inputs are finite; a program needn't handle non-finite values.
Results may differ from the reference program's by a relative error of at most 0.00024.
Values sent between devices are 32-bit elements; how exact they have to be, the bound alone decides.
No kernel may reach another device: no remote copies, remote signals or barrier semaphores. Data moves between devices by JAX's collectives and lax.ppermute only.
A program may use at most 128 MiB of HBM per device.

```python
import math
import jax
import jax.numpy as jnp
from jax import lax

B = 256
R = 256
S_DEV = 8
SUPER = 256
SEPROWS = 2048
N_LEAF = 8
N_FRONT = 4


def draw_dinv_local(key, part):
    first_key, second_key = jax.random.split(key, 2)
    unit_map = jnp.eye(B, dtype=jnp.float32)[None]
    diagonal = jnp.exp(jax.random.uniform(first_key, (SUPER, B, 1), minval=math.log(0.6), maxval=math.log(1.6)))
    spread = jnp.clip(jax.random.normal(second_key, (SUPER, B, B)), -4.0, 4.0) * (0.25 / math.sqrt(B))
    return unit_map * diagonal + (1.0 - unit_map) * spread


def separator_parts(key):
    base_key = jax.random.fold_in(key, 31)
    random_keys = jax.random.split(base_key, 8)
    block_list = SEPROWS // B
    row_pos = jnp.arange(SEPROWS)
    channel = row_pos % B
    block_number = row_pos // B
    gain = jnp.exp(jax.random.uniform(random_keys[0], (SEPROWS,), minval=math.log(0.7), maxval=math.log(1.4)))
    slow_share = 5
    slow_flag = jax.random.randint(random_keys[1], (B,), 0, 10) < slow_share
    sluggish_fraction = jnp.exp(-jax.random.uniform(random_keys[2], (SEPROWS,), minval=0.0, maxval=1.5) / block_list)
    fast_rate = jax.random.uniform(random_keys[3], (SEPROWS,), minval=0.2, maxval=0.6)
    surge_length = jax.random.randint(random_keys[4], (block_list,), 0, 16) == 0
    surge_retained = jax.random.uniform(random_keys[5], (block_list,), minval=0.5, maxval=0.8)
    sluggish_fraction = jnp.where(surge_length[block_number], sluggish_fraction * surge_retained[block_number], sluggish_fraction)
    rate = jnp.where(slow_flag[channel], sluggish_fraction, fast_rate)
    unit_map = jnp.arange(B)[None, :] == channel[:, None]
    return (gain, rate, unit_map, random_keys[6], random_keys[7])


def draw_sep_dinv(key, part):
    gain, rate, unit_map, first_key, second_key = separator_parts(key)
    spread = jnp.clip(jax.random.normal(first_key, (SEPROWS, B)), -4.0, 4.0) * (0.2 / math.sqrt(B))
    return jnp.where(unit_map, gain[:, None], spread)


def draw_sep_coupling(key, part):
    gain, rate, unit_map, first_key, second_key = separator_parts(key)
    spread = jnp.clip(jax.random.normal(second_key, (SEPROWS, B)), -4.0, 4.0) * (0.1 / math.sqrt(B))
    return jnp.where(unit_map, (-rate / gain)[:, None], spread)


def draw_parent(key, part):
    local_pos = jnp.arange(SUPER, dtype=jnp.int32) % S_DEV
    return jax.random.randint(key, (SUPER,), local_pos + 1, S_DEV + 1, dtype=jnp.int32)


def block_scale(key, shape, cuts, smallest, high):
    def one(dim, parts):
        heights = jax.random.uniform(jax.random.fold_in(jax.random.fold_in(key, 6), dim), (parts,), jnp.float32, smallest / len(cuts), high / len(cuts))
        return jnp.repeat(jnp.exp(heights), shape[dim] // parts).reshape((-1,) + (1,) * (len(shape) - dim - 1))

    loudness = one(*cuts[0])
    for cut in cuts[1:]:
        loudness = loudness * one(*cut)
    return loudness


def noise(key, shape, scale, reach, shards=(), kind=jnp.bfloat16):
    values = jax.random.normal(key, shape, jnp.float32) * scale
    if len(shards) > 0:
        values = block_scale(key, shape, shards, -0.22, 0.18) * values
    return jnp.clip(values, min=-reach, max=reach).astype(kind)


def setup_inputs(seed: int = 0) -> dict:
    key_of = jax.random.split(jax.random.key(seed), 9)
    return {
        "rhs_local": noise(key_of[0], (SUPER, B, R), 1.0, 6.0, ((0, 32),), jnp.float32),
        "dinv_local": draw_dinv_local(jax.random.fold_in(key_of[8], 71), 0),
        "update_local": noise(key_of[2], (SUPER, B, B), (2 * B) ** -0.5, 0.25, ((0, 32),), jnp.float32),
        "parent": draw_parent(jax.random.fold_in(key_of[8], 71), 0),
        "row_blocks": jax.vmap(lambda own: jax.random.permutation(own, B))(jax.random.split(key_of[4], SUPER)).reshape((SUPER, B)).astype(jnp.int32),
        "sep_rhs": noise(key_of[5], (SEPROWS, R), 1.0, 6.0, ((0, 32),), jnp.float32),
        "sep_dinv": draw_sep_dinv(jax.random.fold_in(key_of[8], 71), 0),
        "sep_coupling": draw_sep_coupling(jax.random.fold_in(key_of[8], 71), 0),
    }


def matmul(left, right):
    return jnp.dot(left, right, preferred_element_type=jnp.float32, precision=lax.Precision.HIGHEST)


def matmul_t(left, right):
    return lax.dot_general(left, right, (((0,), (0,)), ((), ())), precision=lax.Precision.HIGHEST, preferred_element_type=jnp.float32)


def forward_block(rhs_block, inverse, update, parent_block, row_index):
    count_nodes = rhs_block.shape[0]
    pending = jnp.zeros((count_nodes + 1,) + rhs_block.shape[1:], jnp.float32)
    finished_solution = jnp.zeros(rhs_block.shape, jnp.float32)

    def advance(step_no, state_pair):
        pending_rows, finished_rows = state_pair
        solved_node = matmul(inverse[step_no], rhs_block[step_no] - pending_rows[step_no])
        update_rows = jnp.take(matmul(update[step_no], solved_node), row_index[step_no], axis=0)
        pending_rows = pending_rows.at[parent_block[step_no]].add(update_rows)
        return pending_rows, finished_rows.at[step_no].set(solved_node)

    pending, finished_solution = lax.fori_loop(0, count_nodes, advance, (pending, finished_solution))
    return finished_solution, pending[count_nodes]


def backward_block(finished_solution, inverse, update, parent_block, row_index, top_value):
    count_nodes = finished_solution.shape[0]
    known_rows = jnp.concatenate([jnp.zeros(finished_solution.shape, jnp.float32), top_value[None]], axis=0)

    def retreat(step_no, known_state):
        node_pos = count_nodes - 1 - step_no
        parent_value = known_state[parent_block[node_pos]]
        placed = jnp.zeros(parent_value.shape, jnp.float32).at[row_index[node_pos]].set(parent_value)
        result = matmul_t(inverse[node_pos], finished_solution[node_pos] - matmul_t(update[node_pos], placed))
        return known_state.at[node_pos].set(result)

    known_rows = lax.fori_loop(0, count_nodes, retreat, known_rows)
    return known_rows[:count_nodes]


def reference(rhs_local, dinv_local, update_local, parent, row_blocks, sep_rhs, sep_dinv, sep_coupling):
    blocks_all = N_LEAF * N_FRONT

    def shaped(array):
        return array.reshape((blocks_all, S_DEV) + array.shape[1:])

    def run_forward(packed):
        return forward_block(packed[0], packed[1], packed[2], packed[3], packed[4])

    finished_solution, top_terms = lax.map(run_forward, (shaped(rhs_local), shaped(dinv_local), shaped(update_local), shaped(parent), shaped(row_blocks)))
    contrib = top_terms.reshape(N_LEAF, N_FRONT, B, R).sum(axis=1)
    drive_full = sep_rhs.reshape(N_LEAF, B, R) - contrib
    inverse_top = sep_dinv.reshape(N_LEAF, B, B)
    coupling_top = sep_coupling.reshape(N_LEAF, B, B)

    def forward_step(previous, packed):
        current = matmul(packed[0], packed[2] - matmul(packed[1], previous))
        return current, current

    start_value = jnp.zeros((B, R), jnp.float32)
    _, forward_top = lax.scan(forward_step, start_value, (inverse_top, coupling_top, drive_full))

    def backward_step(following, packed):
        current = matmul_t(packed[0], packed[2] - following)
        return matmul_t(packed[1], current), current

    _, top_solution = lax.scan(backward_step, start_value, (inverse_top, coupling_top, forward_top), reverse=True)
    top_rows = jnp.repeat(top_solution, N_FRONT, axis=0)

    def run_backward(packed):
        return backward_block(packed[0], packed[1], packed[2], packed[3], packed[4], packed[5])

    sol_blocks = lax.map(run_backward, (finished_solution, shaped(dinv_local), shaped(update_local), shaped(parent), shaped(row_blocks), top_rows))
    return sol_blocks.reshape(SUPER, B, R), top_solution.reshape(SEPROWS, R)
```

```python
import jax
import jax.numpy as jnp
from jax import lax
from jax.experimental import pallas as pl
from jax.experimental.pallas import tpu as pltpu
from jax.sharding import PartitionSpec as P

F32 = jnp.float32
BF16 = jnp.bfloat16
NN = (((1,), (0,)), ((), ()))
NT = (((1,), (1,)), ((), ()))
TN = (((0,), (0,)), ((), ()))
VMEM_BYTES = 48 << 20
HALVES = 2


def split(x):
    high = x.astype(BF16)
    return high, (x - high.astype(F32)).astype(BF16)


def dot1(a, b, dims):
    return lax.dot_general(a, b, dims, preferred_element_type=F32)


def dot3(a, b, dims):
    return dot1(a[0], b[0], dims) + (dot1(a[0], b[1], dims) + dot1(a[1], b[0], dims))


def keep_split(ref, value):
    ref[0], ref[1] = split(value)


def pair(ref):
    return ref[0], ref[1]


def bit_of(axis, bit):
    return (lax.axis_index(axis) // (1 << bit)) % 2


def call(kernel, name, ins, outs, scratch=()):
    specs = [pl.BlockSpec(memory_space=space) for space, _ in ins]
    return pl.pallas_call(
        kernel,
        name=name,
        in_specs=specs,
        out_specs=tuple(pl.BlockSpec(memory_space=pltpu.VMEM) for _ in outs),
        out_shape=tuple(jax.ShapeDtypeStruct(*o) for o in outs),
        scratch_shapes=list(scratch),
        compiler_params=pltpu.CompilerParams(vmem_limit_bytes=VMEM_BYTES),
    )(*[a for _, a in ins])


V = pltpu.VMEM


def exchange(x, axis, bit):
    n = lax.axis_size(axis)
    return lax.ppermute(x, axis, [(i, i ^ (1 << bit)) for i in range(n)])


def forward_kernel(nodes, fronts, *refs):
    (parent, rows, sep, rhs_h, dinv_h, upd_h), refs = refs[:6], refs[6:]
    (solved, inv_hi, inv_lo, upd_hi, upd_lo, send, keep), refs = refs[:7], refs[7:]
    (rhs_v, dinv_v, upd_v, square), refs = refs[:4], refs[4:]
    accs, sems = refs[:HALVES], refs[HALVES]
    size, cols = rhs_v.shape[1:]
    width = cols // HALVES
    copies = []
    for k in range(nodes):
        group = [
            pltpu.make_async_copy(dinv_h.at[k], dinv_v.at[k], sems.at[0, k]),
            pltpu.make_async_copy(rhs_h.at[k], rhs_v.at[k], sems.at[1, k]),
            pltpu.make_async_copy(upd_h.at[k], upd_v.at[k], sems.at[2, k]),
        ]
        for c in group:
            c.start()
        copies.append(group)
    front = lax.axis_index("front")
    share = sep.shape[0]
    square[...] = jnp.zeros_like(square)
    square[pl.ds(pl.multiple_of(front * share, 8), share), :] = sep[...]
    turned = square[...].T
    for h in range(HALVES):
        accs[h][nodes] = turned[h * width : (h + 1) * width]
    row_columns = rows[...].astype(F32).T
    lane = lax.broadcasted_iota(jnp.int32, (size, size), 1).astype(F32)
    for k in range(nodes):
        for c in copies[k]:
            c.wait()
        inv_hi[k], inv_lo[k] = split(dinv_v[k])
        high, low = split(upd_v[k])
        chosen = (lane == row_columns[:, k : k + 1]).astype(BF16)
        upd_hi[k] = dot1(chosen, high, NN).astype(BF16)
        upd_lo[k] = dot1(chosen, low, NN).astype(BF16)
        turned = rhs_v[k].T
        for h in range(HALVES):
            accs[h][k] = turned[h * width : (h + 1) * width]
    for k in range(nodes):
        inverse = (inv_hi[k], inv_lo[k])
        update = (upd_hi[k], upd_lo[k])
        above = parent[k]
        for h in range(HALVES):
            value = dot3(split(accs[h][k]), inverse, NT)
            solved[k, h * width : (h + 1) * width] = value
            accs[h][above] = accs[h][above] - dot3(split(value), update, NT)
    chunk = cols // fronts
    for h in range(HALVES):
        square[h * width : (h + 1) * width] = accs[h][nodes]
    low_bit = front % 2
    for i in range(fronts // 2):
        for ref, own in ((keep, low_bit), (send, 1 - low_bit)):
            start = pl.multiple_of((2 * i + own) * chunk, 8)
            ref[i * chunk : (i + 1) * chunk] = square[pl.ds(start, chunk), :]


def local_forward(rhs, dinv, update, parent, rows, sep, fronts):
    nodes, size, cols = rhs.shape
    big = pltpu.VMEM((nodes, size, size), F32)
    half = (nodes, size, size)
    part = (cols // 2, size)
    return call(
        lambda *refs: forward_kernel(nodes, fronts, *refs),
        "local_forward",
        [(pltpu.SMEM, parent), (V, rows), (V, sep), (pl.ANY, rhs), (pl.ANY, dinv), (pl.ANY, update)],
        [(half, F32), (half, BF16), (half, BF16), (half, BF16), (half, BF16), (part, F32), (part, F32)],
        [pltpu.VMEM((nodes, size, cols), F32), big, big, pltpu.VMEM((size, cols), F32)]
        + [pltpu.VMEM((nodes + 1, cols // HALVES, size), F32)] * HALVES
        + [pltpu.SemaphoreType.DMA((3, nodes))],
    )


def backward_kernel(nodes, fronts, *refs):
    parent, solved, inv_hi, inv_lo, upd_hi, upd_lo = refs[:6]
    pieces = refs[6 : 6 + fronts]
    sol, sep_out = refs[6 + fronts : 8 + fronts]
    square = refs[8 + fronts]
    known = refs[9 + fronts :]
    front = lax.axis_index("front")
    chunk = pieces[0].shape[0]
    width = known[0].shape[1]
    for i in range(fronts):
        start = pl.multiple_of((front ^ i) * chunk, 8)
        square[pl.ds(start, chunk), :] = pieces[i][...]
    for h in range(HALVES):
        known[h][nodes] = square[h * width : (h + 1) * width]
    square[...] = square[...].T
    share = sep_out.shape[0]
    sep_out[...] = square[pl.ds(pl.multiple_of(front * share, 8), share), :]
    for k in reversed(range(nodes)):
        inverse = (inv_hi[k], inv_lo[k])
        update = (upd_hi[k], upd_lo[k])
        above = parent[k]
        for h in range(HALVES):
            rows = slice(h * width, (h + 1) * width)
            part = solved[k, rows] - dot3(split(known[h][above]), update, NN)
            value = dot3(split(part), inverse, NN)
            known[h][k] = value
            sol[k, :, rows] = value.T


def local_backward(parent, solved, inv_hi, inv_lo, upd_hi, upd_lo, pieces):
    nodes, cols, size = solved.shape
    fronts = len(pieces)
    return call(
        lambda *refs: backward_kernel(nodes, fronts, *refs),
        "local_backward",
        [(pltpu.SMEM, parent)]
        + [(V, a) for a in (solved, inv_hi, inv_lo, upd_hi, upd_lo)]
        + [(V, a) for a in pieces],
        [((nodes, size, cols), F32), ((size // fronts, cols), F32)],
        [pltpu.VMEM((size, cols), F32)]
        + [pltpu.VMEM((nodes + 1, cols // HALVES, size), F32)] * HALVES,
    )


def block_map_kernel(fronts, *refs):
    inverse_parts, coupling_parts = refs[:fronts], refs[fronts : 2 * fronts]
    total, inverse_halves, square = refs[2 * fronts :]
    front = lax.axis_index("front")
    share = inverse_parts[0].shape[0]
    for parts, slot in ((inverse_parts, 0), (coupling_parts, 1)):
        for i in range(fronts):
            start = pl.multiple_of((front ^ i) * share, 8)
            square[slot, pl.ds(start, share), :] = parts[i][...]
    inverse = split(square[0])
    inverse_halves[0], inverse_halves[1] = inverse
    total[...] = -dot3(inverse, split(square[1]), NN)


def block_map(inverse_parts, coupling_parts):
    fronts = len(inverse_parts)
    share, size = inverse_parts[0].shape
    return call(
        lambda *refs: block_map_kernel(fronts, *refs),
        "block_map",
        [(V, a) for a in (*inverse_parts, *coupling_parts)],
        [((size, size), F32), ((2, size, size), BF16)],
        [pltpu.VMEM((2, size, size), F32)],
    )


def first_merge_kernel(*refs):
    own, other, total, curve, mixed, halves, curve_u, total_u, total_l = refs
    upper = bit_of("leaf", 0) == 1
    low = jnp.where(upper, other[...], own[...])
    up = jnp.where(upper, own[...], other[...])
    low_s, up_s = split(low), split(up)
    for ref, value in ((total_u, up_s), (total_l, low_s)):
        ref[0], ref[1] = value
    k_up = dot3(up_s, up_s, TN)
    k_up_s = split(k_up)
    curve_u[0], curve_u[1] = k_up_s
    x = dot3(k_up_s, low_s, NN)
    t = dot3(up_s, low_s, NN)
    total[...] = t
    curve[...] = dot3(low_s, low_s, TN) + dot3(low_s, split(x), TN)
    size = low.shape[0]
    row = lax.broadcasted_iota(jnp.int32, (size, size), 0)
    col = lax.broadcasted_iota(jnp.int32, (size, size), 1)
    unit = (row == col).astype(F32)
    keep_split(halves, jnp.where(upper, up.T, unit))
    mixed[0] = jnp.where(upper, t, low + x)
    mixed[1] = jnp.where(upper, unit, up)


def merge_kernel(bit, last, *refs):
    own_t, own_k, other_t, other_k, mixed = refs[:5]
    upper = bit_of("leaf", bit) == 1
    total, curve, mixed_n, halves, curve_u, total_u, total_l = refs[5:]
    low_s = split(jnp.where(upper, other_t[...], own_t[...]))
    up_s = split(jnp.where(upper, own_t[...], other_t[...]))
    k_low = jnp.where(upper, other_k[...], own_k[...])
    k_up_s = split(jnp.where(upper, own_k[...], other_k[...]))
    for ref, value in ((total_u, up_s), (total_l, low_s), (curve_u, k_up_s)):
        ref[0], ref[1] = value
    x = dot3(k_up_s, low_s, NN)
    x_s = split(x)
    if not last:
        total[...] = dot3(up_s, low_s, NN)
    curve[...] = k_low + dot3(low_s, x_s, TN)
    a, e = mixed[0], mixed[1]
    keep_split(halves, jnp.where(upper, a.T, e))
    a_s, e_s = split(a), split(e)
    mixed_n[0] = jnp.where(upper, dot3(a_s, low_s, NN), a + dot3(e_s, x_s, TN))
    mixed_n[1] = jnp.where(upper, e, dot3(up_s, e_s, NN))


def maps(size):
    square, both = ((size, size), F32), ((2, size, size), BF16)
    return [square, square, ((2, size, size), F32), both, both, both, both]


def last_map_kernel(bit, mixed, other_k, halves, curve_u):
    upper = bit_of("leaf", bit) == 1
    keep_split(halves, jnp.where(upper, mixed[0].T, mixed[1]))
    keep_split(curve_u, other_k[...])


def fold_kernel(bit, own, other, send, keep):
    total = send.shape[0]
    chunk = total
    value = own[...] + other[...]
    first, second = value[:chunk], value[chunk:]
    high = bit_of("front", bit) == 1
    send[...] = jnp.where(high, first, second)
    keep[...] = jnp.where(high, second, first)


def enter_kernel(own, other, inverse, own_map, sol, message):
    drive = own[...] + other[...]
    value = dot3(split(drive), pair(inverse), NT)
    sol[...] = value
    rows = value.shape[0]
    message[:rows] = value
    message[rows:] = dot3(split(value), split(own_map[...]), NN)


def step_kernel(bit, last, *refs):
    sol, own, other, halves, curve_u, total_u, total_l, sol_n, message = refs
    upper = bit_of("leaf", bit) == 1
    rows = sol.shape[0]
    z_own, p_own, z_other, p_other = own[:rows], own[rows:], other[:rows], other[rows:]
    z_low = jnp.where(upper, z_other, z_own)
    z_up = jnp.where(upper, z_own, z_other)
    p_low = jnp.where(upper, p_other, p_own)
    p_up = jnp.where(upper, p_own, p_other)
    z_low_s = split(z_low)
    middle = p_up + dot3(z_low_s, pair(curve_u), NN)
    middle_s = split(middle)
    z_new = z_up + dot3(z_low_s, pair(total_u), NT)
    p_new = p_low + dot3(middle_s, pair(total_l), NN)
    given = split(jnp.where(upper, z_low, middle))
    sol_n[...] = sol[...] + dot3(given, pair(halves), NN)
    if last:
        upper_next = bit_of("leaf", bit + 1) == 1
        message[0] = jnp.where(upper_next, p_new, z_new)
        message[1] = z_new
    else:
        message[:rows] = z_new
        message[rows:] = p_new


def leave_kernel(bit, sol, own_z, other, halves, curve_u, inverse, top):
    upper = bit_of("leaf", bit) == 1
    came = other[...]
    middle = came + dot3(split(own_z[...]), pair(curve_u), NN)
    given = split(jnp.where(upper, came, middle))
    value = sol[...] + dot3(given, pair(halves), NN)
    top[...] = dot3(split(value), pair(inverse), NN)


def gather_front(x, bits):
    pieces = {0: x}
    for bit in reversed(range(bits)):
        for i in list(pieces):
            pieces[i | (1 << bit)] = exchange(pieces[i], "front", bit)
    return [pieces[i] for i in range(1 << bits)]


def local(rhs_local, dinv_local, update_local, parent, row_blocks, sep_rhs, sep_dinv, sep_coupling):
    fronts, leaves = lax.axis_size("front"), lax.axis_size("leaf")
    front_bits, rounds = fronts.bit_length() - 1, leaves.bit_length() - 1
    size = sep_dinv.shape[1]
    cols = sep_rhs.shape[1]
    chunk = cols // fronts

    inverse_parts = gather_front(sep_dinv, front_bits)
    coupling_parts = gather_front(sep_coupling, front_bits)
    own_map, inverse = block_map(inverse_parts, coupling_parts)

    solved, inv_hi, inv_lo, upd_hi, upd_lo, send, keep = local_forward(
        rhs_local, dinv_local, update_local, parent, row_blocks, sep_rhs, fronts
    )

    other_map = exchange(own_map, "leaf", 0)
    square = maps(size)
    total, curve, mixed, *tools = call(
        first_merge_kernel, "merge_0", [(V, own_map), (V, other_map)], square
    )
    steps = [tools]
    for bit in range(1, rounds - 1):
        other_t, other_k = exchange(total, "leaf", bit), exchange(curve, "leaf", bit)
        total, curve, mixed, *tools = call(
            lambda *refs, bit=bit: merge_kernel(bit, bit == rounds - 2, *refs),
            f"merge_{bit}",
            [(V, a) for a in (total, curve, other_t, other_k, mixed)],
            square,
        )
        steps.append(tools)
    other_k = exchange(curve, "leaf", rounds - 1)
    last_halves, last_curve = call(
        lambda *refs: last_map_kernel(rounds - 1, *refs),
        "merge_last",
        [(V, mixed), (V, other_k)],
        [((2, size, size), BF16)] * 2,
    )

    for bit in range(front_bits):
        received = exchange(send, "front", bit)
        if bit + 1 < front_bits:
            half = ((keep.shape[0] // 2, size), F32)
            send, keep = call(
                lambda *refs, bit=bit: fold_kernel(bit + 1, *refs),
                "fold",
                [(V, keep), (V, received)],
                [half, half],
            )
    sol, message = call(
        enter_kernel,
        "enter",
        [(V, keep), (V, received), (V, inverse), (V, own_map)],
        [((chunk, size), F32), ((2 * chunk, size), F32)],
    )
    for bit in range(rounds - 1):
        received = exchange(message, "leaf", bit)
        last = bit == rounds - 2
        shape = (2, chunk, size) if last else (2 * chunk, size)
        sol, message = call(
            lambda *refs, bit=bit, last=last: step_kernel(bit, last, *refs),
            f"step_{bit}",
            [(V, a) for a in (sol, message, received, *steps[bit])],
            [((chunk, size), F32), (shape, F32)],
        )
    received = exchange(message[0], "leaf", rounds - 1)
    (top,) = call(
        lambda *refs: leave_kernel(rounds - 1, *refs),
        "leave",
        [(V, a) for a in (sol, message[1], received, last_halves, last_curve, inverse)],
        [((chunk, size), F32)],
    )
    pieces = gather_front(top, front_bits)
    sol_local, sep_solution = local_backward(
        parent, solved, inv_hi, inv_lo, upd_hi, upd_lo, pieces
    )
    return (sol_local, sep_solution)


def solution(mesh):
    spread3 = P(("leaf", "front"), None, None)
    spread2 = P(("leaf", "front"), None)
    spread1 = P(("leaf", "front"))
    return jax.shard_map(
        local,
        mesh=mesh,
        in_specs=(spread3, spread3, spread3, spread1, spread2, spread2, spread2, spread2),
        out_specs=(spread3, spread2),
        check_vma=False,
    )
```

```python
import jax
import jax.numpy as jnp
from jax import lax
from jax.experimental import pallas as pl
from jax.experimental.pallas import tpu as pltpu
from jax.sharding import PartitionSpec as P

F32 = jnp.float32
BF16 = jnp.bfloat16
NN = (((1,), (0,)), ((), ()))
NT = (((1,), (1,)), ((), ()))
TN = (((0,), (0,)), ((), ()))
VMEM_BYTES = 24 << 20
HALVES = 2


def split(x):
    high = x.astype(BF16)
    return high, (x - high.astype(F32)).astype(BF16)


def dot1(a, b, dims):
    return lax.dot_general(a, b, dims, preferred_element_type=F32)


def dot3(a, b, dims):
    return dot1(a[0], b[0], dims) + (dot1(a[0], b[1], dims) + dot1(a[1], b[0], dims))


def keep_split(ref, value):
    ref[0], ref[1] = split(value)


def pair(ref):
    return ref[0], ref[1]


def bit_of(axis, bit):
    return (lax.axis_index(axis) // (1 << bit)) % 2


def call(kernel, name, ins, outs, scratch=()):
    specs = [pl.BlockSpec(memory_space=space) for space, _ in ins]
    ins = [
        (space, pltpu.with_memory_space_constraint(a, HBM) if space == HBM else a)
        for space, a in ins
    ]
    return pl.pallas_call(
        kernel,
        name=name,
        in_specs=specs,
        out_specs=tuple(pl.BlockSpec(memory_space=pltpu.VMEM) for _ in outs),
        out_shape=tuple(jax.ShapeDtypeStruct(*o) for o in outs),
        scratch_shapes=list(scratch),
        compiler_params=pltpu.CompilerParams(vmem_limit_bytes=VMEM_BYTES),
    )(*[a for _, a in ins])


V = pltpu.VMEM
HBM = pltpu.HBM


def swap(x, axis, mask):
    n = lax.axis_size(axis)
    return lax.ppermute(x, axis, [(i, i ^ mask) for i in range(n)])


def exchange(x, axis, bit):
    return swap(x, axis, 1 << bit)


def prepare_kernel(nodes, *refs):
    (rows_h, sep_h, own_inv_h, own_cpl_h, rhs_h, dinv_h, upd_h), refs = refs[:7], refs[7:]
    (acc, inv_hi, inv_lo, upd_hi, upd_lo, own_inv, own_cpl), refs = refs[:7], refs[7:]
    rhs_v, dinv_v, upd_v, square, rows, sep, sems, small = refs
    size, cols = rhs_v.shape[1:]
    width = cols // HALVES
    few = [
        pltpu.make_async_copy(src, dst, small.at[i])
        for i, (src, dst) in enumerate(
            ((rows_h, rows), (sep_h, sep), (own_inv_h, own_inv), (own_cpl_h, own_cpl))
        )
    ]
    for c in few:
        c.start()
    copies = []
    for k in range(nodes):
        group = [
            pltpu.make_async_copy(upd_h.at[k], upd_v.at[k], sems.at[2, k]),
            pltpu.make_async_copy(dinv_h.at[k], dinv_v.at[k], sems.at[0, k]),
            pltpu.make_async_copy(rhs_h.at[k], rhs_v.at[k], sems.at[1, k]),
        ]
        for c in group:
            c.start()
        copies.append(group)
    front = lax.axis_index("front")
    square[...] = jnp.zeros_like(square)
    for c in few:
        c.wait()
    share = sep.shape[0]
    square[pl.ds(pl.multiple_of(front * share, 8), share), :] = sep[...]
    turned = square[...].T
    for h in range(HALVES):
        acc[h, nodes] = turned[h * width : (h + 1) * width]
    row_columns = rows[...].astype(F32).T
    lane = lax.broadcasted_iota(jnp.int32, (size, size), 1).astype(F32)
    for k in range(nodes):
        for c in copies[k]:
            c.wait()
        inv_hi[k], inv_lo[k] = split(dinv_v[k])
        high, low = split(upd_v[k])
        chosen = (lane == row_columns[:, k : k + 1]).astype(BF16)
        upd_hi[k] = dot1(chosen, high, NN).astype(BF16)
        upd_lo[k] = dot1(chosen, low, NN).astype(BF16)
        turned = rhs_v[k].T
        for h in range(HALVES):
            acc[h, k] = turned[h * width : (h + 1) * width]


def prepare(rhs, dinv, update, rows, sep, sep_dinv, sep_coupling):
    nodes, size, cols = rhs.shape
    big = pltpu.VMEM((nodes, size, size), F32)
    half = ((nodes, size, size), BF16)
    acc = ((HALVES, nodes + 1, cols // HALVES, size), F32)
    return call(
        lambda *refs: prepare_kernel(nodes, *refs),
        "prepare",
        [(HBM, a) for a in (rows, sep, sep_dinv, sep_coupling, rhs, dinv, update)],
        [acc, half, half, half, half, (sep_dinv.shape, F32), (sep_coupling.shape, F32)],
        [pltpu.VMEM((nodes, size, cols), F32), big, big, pltpu.VMEM((size, cols), F32)]
        + [pltpu.VMEM(rows.shape, jnp.int32), pltpu.VMEM(sep.shape, F32)]
        + [pltpu.SemaphoreType.DMA((3, nodes)), pltpu.SemaphoreType.DMA((4,))],
    )


def forward_kernel(nodes, fronts, *refs):
    parent_h, acc, inv_hi, inv_lo, upd_hi, upd_lo, _ = refs[:7]
    solved, send, keep, square, parent, sem = refs[7:13]
    accs = refs[13:]
    copy = pltpu.make_async_copy(parent_h, parent, sem)
    copy.start()
    width, size = acc.shape[2:]
    cols = width * HALVES
    for h in range(HALVES):
        accs[h][...] = acc[h]
    copy.wait()
    for k in range(nodes):
        inverse = (inv_hi[k], inv_lo[k])
        update = (upd_hi[k], upd_lo[k])
        above = parent[k]
        for h in range(HALVES):
            value = dot3(split(accs[h][k]), inverse, NT)
            solved[k, h * width : (h + 1) * width] = value
            accs[h][above] = accs[h][above] - dot3(split(value), update, NT)
    front = lax.axis_index("front")
    chunk = cols // fronts
    for h in range(HALVES):
        square[h * width : (h + 1) * width] = accs[h][nodes]
    low_bit = front % 2
    for i in range(fronts // 2):
        for ref, own in ((keep, low_bit), (send, 1 - low_bit)):
            start = pl.multiple_of((2 * i + own) * chunk, 8)
            ref[i * chunk : (i + 1) * chunk] = square[pl.ds(start, chunk), :]


def local_forward(parent, acc, halves, after, fronts):
    nodes, (width, size) = acc.shape[1] - 1, acc.shape[2:]
    cols = width * HALVES
    part = ((cols // 2, size), F32)
    return call(
        lambda *refs: forward_kernel(nodes, fronts, *refs),
        "local_forward",
        [(HBM, parent), (V, acc)] + [(V, a) for a in halves] + [(pl.ANY, after)],
        [((nodes, cols, size), F32), part, part],
        [pltpu.VMEM((cols, size), F32), pltpu.SMEM((nodes,), jnp.int32), pltpu.SemaphoreType.DMA]
        + [pltpu.VMEM((nodes + 1, width, size), F32)] * HALVES,
    )


def backward_kernel(nodes, fronts, *refs):
    parent_h, solved, inv_hi, inv_lo, upd_hi, upd_lo = refs[:6]
    pieces = refs[6 : 6 + fronts]
    sol, sep_out = refs[6 + fronts : 8 + fronts]
    square, parent, staged, sem, sems = refs[8 + fronts : 13 + fronts]
    known = refs[13 + fronts :]
    copy = pltpu.make_async_copy(parent_h, parent, sem)
    copy.start()
    front = lax.axis_index("front")
    chunk = pieces[0].shape[0]
    width = known[0].shape[1]
    for i in range(fronts):
        start = pl.multiple_of((front ^ i) * chunk, 8)
        square[pl.ds(start, chunk), :] = pieces[i][...]
    for h in range(HALVES):
        known[h][nodes] = square[h * width : (h + 1) * width]
    square[...] = square[...].T
    share = sep_out.shape[0]
    sep_out[...] = square[pl.ds(pl.multiple_of(front * share, 8), share), :]
    copy.wait()
    outs = []
    for k in reversed(range(nodes)):
        inverse = (inv_hi[k], inv_lo[k])
        update = (upd_hi[k], upd_lo[k])
        above = parent[k]
        for h in range(HALVES):
            rows = slice(h * width, (h + 1) * width)
            part = solved[k, rows] - dot3(split(known[h][above]), update, NN)
            value = dot3(split(part), inverse, NN)
            known[h][k] = value
            staged[k, :, rows] = value.T
        out = pltpu.make_async_copy(staged.at[k], sol.at[k], sems.at[k])
        out.start()
        outs.append(out)
    for out in outs:
        out.wait()


def local_backward(parent, solved, halves, pieces):
    nodes, cols, size = solved.shape
    fronts = len(pieces)
    sol, sep = jax.ShapeDtypeStruct((nodes, size, cols), F32), ((size // fronts, cols), F32)
    ins = [(HBM, parent)] + [(V, a) for a in (solved, *halves, *pieces)]
    return pl.pallas_call(
        lambda *refs: backward_kernel(nodes, fronts, *refs),
        name="local_backward",
        in_specs=[pl.BlockSpec(memory_space=space) for space, _ in ins],
        out_specs=(pl.BlockSpec(memory_space=HBM), pl.BlockSpec(memory_space=V)),
        out_shape=(sol, jax.ShapeDtypeStruct(*sep)),
        scratch_shapes=[pltpu.VMEM((size, cols), F32), pltpu.SMEM((nodes,), jnp.int32)]
        + [pltpu.VMEM((nodes, size, cols), F32), pltpu.SemaphoreType.DMA]
        + [pltpu.SemaphoreType.DMA((nodes,))]
        + [pltpu.VMEM((nodes + 1, cols // HALVES, size), F32)] * HALVES,
        compiler_params=pltpu.CompilerParams(vmem_limit_bytes=VMEM_BYTES),
    )(pltpu.with_memory_space_constraint(parent, HBM), *[a for _, a in ins[1:]])


def block_map_kernel(fronts, *refs):
    inverse_parts, coupling_parts = refs[:fronts], refs[fronts : 2 * fronts]
    total, inverse_halves, square = refs[2 * fronts :]
    front = lax.axis_index("front")
    share = inverse_parts[0].shape[0]
    for parts, slot in ((inverse_parts, 0), (coupling_parts, 1)):
        for i in range(fronts):
            start = pl.multiple_of((front ^ i) * share, 8)
            square[slot, pl.ds(start, share), :] = parts[i][...]
    inverse = split(square[0])
    inverse_halves[0], inverse_halves[1] = inverse
    total[...] = -dot3(inverse, split(square[1]), NN)


def block_map(inverse_parts, coupling_parts):
    fronts = len(inverse_parts)
    share, size = inverse_parts[0].shape
    return call(
        lambda *refs: block_map_kernel(fronts, *refs),
        "block_map",
        [(V, a) for a in (*inverse_parts, *coupling_parts)],
        [((size, size), F32), ((2, size, size), BF16)],
        [pltpu.VMEM((2, size, size), F32)],
    )


def half_rows(part, values):
    rows = values[0].shape[0] // 2
    low = bit_of("front", 0) == 0
    for i, value in enumerate(values):
        part[i] = jnp.where(low, value[:rows], value[rows:])


def whole(mine, pairs):
    low = bit_of("front", 0) == 0
    first, second = jnp.where(low, mine, pairs), jnp.where(low, pairs, mine)
    return jnp.concatenate([first, second], axis=0)


def first_merge_kernel(last, *refs):
    own, other, _, total, curve, mixed, halves, curve_u, total_u, total_l, part = refs
    upper = bit_of("leaf", 0) == 1
    low = jnp.where(upper, other[...], own[...])
    up = jnp.where(upper, own[...], other[...])
    low_s, up_s = split(low), split(up)
    for ref, value in ((total_u, up_s), (total_l, low_s)):
        ref[0], ref[1] = value
    k_up = dot3(up_s, up_s, TN)
    k_up_s = split(k_up)
    curve_u[0], curve_u[1] = k_up_s
    x = dot3(k_up_s, low_s, NN)
    t = dot3(up_s, low_s, NN)
    total[...] = t
    k = dot3(low_s, low_s, TN) + dot3(low_s, split(x), TN)
    curve[...] = k
    half_rows(part, (k,) if last else (k, t))
    size = low.shape[0]
    row = lax.broadcasted_iota(jnp.int32, (size, size), 0)
    col = lax.broadcasted_iota(jnp.int32, (size, size), 1)
    unit = (row == col).astype(F32)
    keep_split(halves, jnp.where(upper, up.T, unit))
    mixed[0] = jnp.where(upper, t, low + x)
    mixed[1] = jnp.where(upper, unit, up)


def merge_kernel(bit, last, *refs):
    own_t, own_k, mine, pairs, mixed = refs[:5]
    upper = bit_of("leaf", bit) == 1
    total, curve, mixed_n, halves, curve_u, total_u, total_l, part = refs[5:]
    other_k, other_t = whole(mine[0], pairs[0]), whole(mine[1], pairs[1])
    low_s = split(jnp.where(upper, other_t, own_t[...]))
    up_s = split(jnp.where(upper, own_t[...], other_t))
    k_low = jnp.where(upper, other_k, own_k[...])
    k_up_s = split(jnp.where(upper, own_k[...], other_k))
    for ref, value in ((total_u, up_s), (total_l, low_s), (curve_u, k_up_s)):
        ref[0], ref[1] = value
    x = dot3(k_up_s, low_s, NN)
    x_s = split(x)
    k = k_low + dot3(low_s, x_s, TN)
    curve[...] = k
    if last:
        half_rows(part, (k,))
    else:
        t = dot3(up_s, low_s, NN)
        total[...] = t
        half_rows(part, (k, t))
    a, e = mixed[0], mixed[1]
    keep_split(halves, jnp.where(upper, a.T, e))
    a_s, e_s = split(a), split(e)
    mixed_n[0] = jnp.where(upper, dot3(a_s, low_s, NN), a + dot3(e_s, x_s, TN))
    mixed_n[1] = jnp.where(upper, e, dot3(up_s, e_s, NN))


def maps(size, last):
    square, both = ((size, size), F32), ((2, size, size), BF16)
    part = ((1 if last else 2, size // 2, size), F32)
    return [square, square, ((2, size, size), F32), both, both, both, both, part]


def last_map_kernel(bit, mixed, mine, pairs, halves, curve_u):
    upper = bit_of("leaf", bit) == 1
    keep_split(halves, jnp.where(upper, mixed[0].T, mixed[1]))
    keep_split(curve_u, whole(mine[0], pairs[0]))


def fold_kernel(bit, own, other, send, keep):
    total = send.shape[0]
    chunk = total
    value = own[...] + other[...]
    first, second = value[:chunk], value[chunk:]
    high = bit_of("front", bit) == 1
    send[...] = jnp.where(high, first, second)
    keep[...] = jnp.where(high, second, first)


def enter_kernel(own, other, inverse, own_map, sol, message):
    drive = own[...] + other[...]
    value = dot3(split(drive), pair(inverse), NT)
    sol[...] = value
    rows = value.shape[0]
    message[:rows] = value
    message[rows:] = dot3(split(value), split(own_map[...]), NN)


def step_kernel(bit, last, *refs):
    sol, own, other, halves, curve_u, total_u, total_l, sol_n, message = refs
    upper = bit_of("leaf", bit) == 1
    rows = sol.shape[0]
    z_own, p_own, z_other, p_other = own[:rows], own[rows:], other[:rows], other[rows:]
    z_low = jnp.where(upper, z_other, z_own)
    z_up = jnp.where(upper, z_own, z_other)
    p_low = jnp.where(upper, p_other, p_own)
    p_up = jnp.where(upper, p_own, p_other)
    z_low_s = split(z_low)
    middle = p_up + dot3(z_low_s, pair(curve_u), NN)
    middle_s = split(middle)
    z_new = z_up + dot3(z_low_s, pair(total_u), NT)
    p_new = p_low + dot3(middle_s, pair(total_l), NN)
    given = split(jnp.where(upper, z_low, middle))
    sol_n[...] = sol[...] + dot3(given, pair(halves), NN)
    if last:
        upper_next = bit_of("leaf", bit + 1) == 1
        message[0] = jnp.where(upper_next, p_new, z_new)
        message[1] = z_new
    else:
        message[:rows] = z_new
        message[rows:] = p_new


def leave_kernel(bit, sol, own_z, other, halves, curve_u, inverse, top):
    upper = bit_of("leaf", bit) == 1
    came = other[...]
    middle = came + dot3(split(own_z[...]), pair(curve_u), NN)
    given = split(jnp.where(upper, came, middle))
    value = sol[...] + dot3(given, pair(halves), NN)
    top[...] = dot3(split(value), pair(inverse), NN)


def gather_front(x, bits):
    pieces = {0: x}
    for bit in reversed(range(bits)):
        for i in list(pieces):
            pieces[i | (1 << bit)] = exchange(pieces[i], "front", bit)
    return [pieces[i] for i in range(1 << bits)]


def local(rhs_local, dinv_local, update_local, parent, row_blocks, sep_rhs, sep_dinv, sep_coupling):
    fronts, leaves = lax.axis_size("front"), lax.axis_size("leaf")
    front_bits, rounds = fronts.bit_length() - 1, leaves.bit_length() - 1
    size = sep_dinv.shape[1]
    cols = sep_rhs.shape[1]
    chunk = cols // fronts

    masks = range(1, fronts)
    came_inverse = [swap(sep_dinv, "front", m) for m in masks]
    came_coupling = [swap(sep_coupling, "front", m) for m in masks]
    acc, *rest = prepare(
        rhs_local, dinv_local, update_local, row_blocks, sep_rhs, sep_dinv, sep_coupling
    )
    local_halves, own_inverse, own_coupling = rest[:4], rest[4], rest[5]
    own_map, inverse = block_map([own_inverse, *came_inverse], [own_coupling, *came_coupling])
    other_map = exchange(own_map, "leaf", 0)

    solved, send, keep = local_forward(parent, acc, local_halves, own_map, fronts)

    for bit in range(front_bits):
        received = exchange(send, "front", bit)
        if bit + 1 < front_bits:
            half = ((keep.shape[0] // 2, size), F32)
            send, keep = call(
                lambda *refs, bit=bit: fold_kernel(bit + 1, *refs),
                "fold",
                [(V, keep), (V, received)],
                [half, half],
            )
    total, curve, mixed, *tools, part = call(
        lambda *refs: first_merge_kernel(rounds == 2, *refs),
        "merge_0",
        [(V, own_map), (V, other_map), (pl.ANY, send)],
        maps(size, rounds == 2),
    )
    sol, message = call(
        enter_kernel,
        "enter",
        [(V, keep), (V, received), (V, inverse), (V, own_map)],
        [((chunk, size), F32), ((2 * chunk, size), F32)],
    )
    for bit in range(rounds - 1):
        last = bit == rounds - 2
        mine = exchange(part, "leaf", bit + 1)
        received = exchange(message, "leaf", bit)
        shape = (2, chunk, size) if last else (2 * chunk, size)
        sol, message = call(
            lambda *refs, bit=bit, last=last: step_kernel(bit, last, *refs),
            f"step_{bit}",
            [(V, a) for a in (sol, message, received, *tools)],
            [((chunk, size), F32), (shape, F32)],
        )
        mine, _ = lax.optimization_barrier((mine, sol))
        pairs = exchange(mine, "front", 0)
        if not last:
            last = bit == rounds - 3
            total, curve, mixed, *tools, part = call(
                lambda *refs, bit=bit, last=last: merge_kernel(bit + 1, last, *refs),
                f"merge_{bit + 1}",
                [(V, a) for a in (total, curve, mine, pairs, mixed)],
                maps(size, last),
            )
    last_halves, last_curve = call(
        lambda *refs: last_map_kernel(rounds - 1, *refs),
        "merge_last",
        [(V, mixed), (V, mine), (V, pairs)],
        [((2, size, size), BF16)] * 2,
    )
    received = exchange(message[0], "leaf", rounds - 1)
    (top,) = call(
        lambda *refs: leave_kernel(rounds - 1, *refs),
        "leave",
        [(V, a) for a in (sol, message[1], received, last_halves, last_curve, inverse)],
        [((chunk, size), F32)],
    )
    pieces = gather_front(top, front_bits)
    sol_local, sep_solution = local_backward(
        parent, solved, local_halves, pieces
    )
    return (sol_local, sep_solution)


def solution(mesh):
    spread3 = P(("leaf", "front"), None, None)
    spread2 = P(("leaf", "front"), None)
    spread1 = P(("leaf", "front"))
    return jax.shard_map(
        local,
        mesh=mesh,
        in_specs=(spread3, spread3, spread3, spread1, spread2, spread2, spread2, spread2),
        out_specs=(spread3, spread2),
        check_vma=False,
    )
```

```python
import jax
import jax.numpy as jnp
from jax import lax
from jax.experimental import pallas as pl
from jax.experimental.pallas import tpu as pltpu
from jax.sharding import PartitionSpec as P

F32 = jnp.float32
BF16 = jnp.bfloat16
NN = (((1,), (0,)), ((), ()))
NT = (((1,), (1,)), ((), ()))
TN = (((0,), (0,)), ((), ()))
VMEM_BYTES = 24 << 20
HALVES = 2


def split(x):
    high = x.astype(BF16)
    return high, (x - high.astype(F32)).astype(BF16)


def dot1(a, b, dims):
    return lax.dot_general(a, b, dims, preferred_element_type=F32)


def dot3(a, b, dims):
    return dot1(a[0], b[0], dims) + (dot1(a[0], b[1], dims) + dot1(a[1], b[0], dims))


def keep_split(ref, value):
    ref[0], ref[1] = split(value)


def pair(ref):
    return ref[0], ref[1]


def bit_of(axis, bit):
    return (lax.axis_index(axis) // (1 << bit)) % 2


def call(kernel, name, ins, outs, scratch=()):
    specs = [pl.BlockSpec(memory_space=space) for space, _ in ins]
    ins = [
        (space, pltpu.with_memory_space_constraint(a, HBM) if space == HBM else a)
        for space, a in ins
    ]
    return pl.pallas_call(
        kernel,
        name=name,
        in_specs=specs,
        out_specs=tuple(pl.BlockSpec(memory_space=pltpu.VMEM) for _ in outs),
        out_shape=tuple(jax.ShapeDtypeStruct(*o) for o in outs),
        scratch_shapes=list(scratch),
        compiler_params=pltpu.CompilerParams(vmem_limit_bytes=VMEM_BYTES),
    )(*[a for _, a in ins])


V = pltpu.VMEM
HBM = pltpu.HBM


def swap(x, axis, mask):
    n = lax.axis_size(axis)
    return lax.ppermute(x, axis, [(i, i ^ mask) for i in range(n)])


def exchange(x, axis, bit):
    return swap(x, axis, 1 << bit)


def prepare_kernel(nodes, *refs):
    (rows_h, sep_h, rhs_h, dinv_h, upd_h, _), refs = refs[:6], refs[6:]
    (acc, inv_hi, inv_lo, upd_hi, upd_lo), refs = refs[:5], refs[5:]
    rhs_v, dinv_v, upd_v, square, rows, sep, sems, small = refs
    size, cols = rhs_v.shape[1:]
    width = cols // HALVES
    few = [
        pltpu.make_async_copy(src, dst, small.at[i])
        for i, (src, dst) in enumerate(((rows_h, rows), (sep_h, sep)))
    ]
    for c in few:
        c.start()
    copies = []
    for k in range(nodes):
        group = [
            pltpu.make_async_copy(upd_h.at[k], upd_v.at[k], sems.at[2, k]),
            pltpu.make_async_copy(dinv_h.at[k], dinv_v.at[k], sems.at[0, k]),
            pltpu.make_async_copy(rhs_h.at[k], rhs_v.at[k], sems.at[1, k]),
        ]
        for c in group:
            c.start()
        copies.append(group)
    front = lax.axis_index("front")
    square[...] = jnp.zeros_like(square)
    for c in few:
        c.wait()
    share = sep.shape[0]
    square[pl.ds(pl.multiple_of(front * share, 8), share), :] = sep[...]
    turned = square[...].T
    for h in range(HALVES):
        acc[h, nodes] = turned[h * width : (h + 1) * width]
    row_columns = rows[...].astype(F32).T
    lane = lax.broadcasted_iota(jnp.int32, (size, size), 1).astype(F32)
    for k in range(nodes):
        for c in copies[k]:
            c.wait()
        inv_hi[k], inv_lo[k] = split(dinv_v[k])
        high, low = split(upd_v[k])
        chosen = (lane == row_columns[:, k : k + 1]).astype(BF16)
        upd_hi[k] = dot1(chosen, high, NN).astype(BF16)
        upd_lo[k] = dot1(chosen, low, NN).astype(BF16)
        turned = rhs_v[k].T
        for h in range(HALVES):
            acc[h, k] = turned[h * width : (h + 1) * width]


def prepare(rhs, dinv, update, rows, sep, after):
    nodes, size, cols = rhs.shape
    big = pltpu.VMEM((nodes, size, size), F32)
    half = ((nodes, size, size), BF16)
    acc = ((HALVES, nodes + 1, cols // HALVES, size), F32)
    return call(
        lambda *refs: prepare_kernel(nodes, *refs),
        "prepare",
        [(HBM, a) for a in (rows, sep, rhs, dinv, update)] + [(pl.ANY, after)],
        [acc, half, half, half, half],
        [pltpu.VMEM((nodes, size, cols), F32), big, big, pltpu.VMEM((size, cols), F32)]
        + [pltpu.VMEM(rows.shape, jnp.int32), pltpu.VMEM(sep.shape, F32)]
        + [pltpu.SemaphoreType.DMA((3, nodes)), pltpu.SemaphoreType.DMA((2,))],
    )


def forward_kernel(nodes, fronts, *refs):
    parent_h, acc, inv_hi, inv_lo, upd_hi, upd_lo, _ = refs[:7]
    solved, send, keep, square, parent, sem = refs[7:13]
    accs = refs[13:]
    copy = pltpu.make_async_copy(parent_h, parent, sem)
    copy.start()
    width, size = acc.shape[2:]
    cols = width * HALVES
    for h in range(HALVES):
        accs[h][...] = acc[h]
    copy.wait()
    for k in range(nodes):
        inverse = (inv_hi[k], inv_lo[k])
        update = (upd_hi[k], upd_lo[k])
        above = parent[k]
        for h in range(HALVES):
            value = dot3(split(accs[h][k]), inverse, NT)
            solved[k, h * width : (h + 1) * width] = value
            accs[h][above] = accs[h][above] - dot3(split(value), update, NT)
    front = lax.axis_index("front")
    chunk = cols // fronts
    for h in range(HALVES):
        square[h * width : (h + 1) * width] = accs[h][nodes]
    low_bit = front % 2
    for i in range(fronts // 2):
        for ref, own in ((keep, low_bit), (send, 1 - low_bit)):
            start = pl.multiple_of((2 * i + own) * chunk, 8)
            ref[i * chunk : (i + 1) * chunk] = square[pl.ds(start, chunk), :]


def local_forward(parent, acc, halves, after, fronts):
    nodes, (width, size) = acc.shape[1] - 1, acc.shape[2:]
    cols = width * HALVES
    part = ((cols // 2, size), F32)
    return call(
        lambda *refs: forward_kernel(nodes, fronts, *refs),
        "local_forward",
        [(HBM, parent), (V, acc)] + [(V, a) for a in halves] + [(pl.ANY, after)],
        [((nodes, cols, size), F32), part, part],
        [pltpu.VMEM((cols, size), F32), pltpu.SMEM((nodes,), jnp.int32), pltpu.SemaphoreType.DMA]
        + [pltpu.VMEM((nodes + 1, width, size), F32)] * HALVES,
    )


def backward_kernel(nodes, fronts, *refs):
    parent_h, solved, inv_hi, inv_lo, upd_hi, upd_lo = refs[:6]
    pieces = refs[6 : 6 + fronts]
    sol, sep_out = refs[6 + fronts : 8 + fronts]
    square, parent, staged, sem, sems = refs[8 + fronts : 13 + fronts]
    known = refs[13 + fronts :]
    copy = pltpu.make_async_copy(parent_h, parent, sem)
    copy.start()
    front = lax.axis_index("front")
    chunk = pieces[0].shape[0]
    width = known[0].shape[1]
    for i in range(fronts):
        start = pl.multiple_of((front ^ i) * chunk, 8)
        square[pl.ds(start, chunk), :] = pieces[i][...]
    for h in range(HALVES):
        known[h][nodes] = square[h * width : (h + 1) * width]
    square[...] = square[...].T
    share = sep_out.shape[0]
    sep_out[...] = square[pl.ds(pl.multiple_of(front * share, 8), share), :]
    copy.wait()
    outs = []
    for k in reversed(range(nodes)):
        inverse = (inv_hi[k], inv_lo[k])
        update = (upd_hi[k], upd_lo[k])
        above = parent[k]
        for h in range(HALVES):
            rows = slice(h * width, (h + 1) * width)
            part = solved[k, rows] - dot3(split(known[h][above]), update, NN)
            value = dot3(split(part), inverse, NN)
            known[h][k] = value
            staged[k, :, rows] = value.T
        out = pltpu.make_async_copy(staged.at[k], sol.at[k], sems.at[k])
        out.start()
        outs.append(out)
    for out in outs:
        out.wait()


def local_backward(parent, solved, halves, pieces):
    nodes, cols, size = solved.shape
    fronts = len(pieces)
    sol, sep = jax.ShapeDtypeStruct((nodes, size, cols), F32), ((size // fronts, cols), F32)
    ins = [(HBM, parent)] + [(V, a) for a in (solved, *halves, *pieces)]
    return pl.pallas_call(
        lambda *refs: backward_kernel(nodes, fronts, *refs),
        name="local_backward",
        in_specs=[pl.BlockSpec(memory_space=space) for space, _ in ins],
        out_specs=(pl.BlockSpec(memory_space=HBM), pl.BlockSpec(memory_space=V)),
        out_shape=(sol, jax.ShapeDtypeStruct(*sep)),
        scratch_shapes=[pltpu.VMEM((size, cols), F32), pltpu.SMEM((nodes,), jnp.int32)]
        + [pltpu.VMEM((nodes, size, cols), F32), pltpu.SemaphoreType.DMA]
        + [pltpu.SemaphoreType.DMA((nodes,))]
        + [pltpu.VMEM((nodes + 1, cols // HALVES, size), F32)] * HALVES,
        compiler_params=pltpu.CompilerParams(vmem_limit_bytes=VMEM_BYTES),
    )(pltpu.with_memory_space_constraint(parent, HBM), *[a for _, a in ins[1:]])


def stack_kernel(first, second, out, sems):
    copies = [pltpu.make_async_copy(a, out.at[i], sems.at[i]) for i, a in enumerate((first, second))]
    for c in copies:
        c.start()
    for c in copies:
        c.wait()


def block_map_kernel(fronts, *refs):
    parts = refs[:fronts]
    _, total, inverse_halves, square = refs[fronts:]
    front = lax.axis_index("front")
    share = parts[0].shape[1]
    for i in range(fronts):
        start = pl.multiple_of((front ^ i) * share, 8)
        square[:, pl.ds(start, share), :] = parts[i][...]
    inverse = split(square[0])
    inverse_halves[0], inverse_halves[1] = inverse
    total[...] = -dot3(inverse, split(square[1]), NN)


def block_map(parts, after):
    fronts = len(parts)
    size = parts[0].shape[2]
    return call(
        lambda *refs: block_map_kernel(fronts, *refs),
        "block_map",
        [(V, a) for a in parts] + [(pl.ANY, after)],
        [((size, size), F32), ((2, size, size), BF16)],
        [pltpu.VMEM((2, size, size), F32)],
    )


def first_merge_kernel(*refs):
    own, other, _, pack, mixed, halves, curve_u, total_u, total_l = refs
    upper = bit_of("leaf", 0) == 1
    low = jnp.where(upper, other[...], own[...])
    up = jnp.where(upper, own[...], other[...])
    low_s, up_s = split(low), split(up)
    for ref, value in ((total_u, up_s), (total_l, low_s)):
        ref[0], ref[1] = value
    k_up = dot3(up_s, up_s, TN)
    k_up_s = split(k_up)
    curve_u[0], curve_u[1] = k_up_s
    x = dot3(k_up_s, low_s, NN)
    t = dot3(up_s, low_s, NN)
    pack[1] = t
    pack[0] = dot3(low_s, low_s, TN) + dot3(low_s, split(x), TN)
    size = low.shape[0]
    row = lax.broadcasted_iota(jnp.int32, (size, size), 0)
    col = lax.broadcasted_iota(jnp.int32, (size, size), 1)
    unit = (row == col).astype(F32)
    keep_split(halves, jnp.where(upper, up.T, unit))
    mixed[0] = jnp.where(upper, t, low + x)
    mixed[1] = jnp.where(upper, unit, up)


def merge_kernel(bit, last, *refs):
    own, other, mixed = refs[:3]
    upper = bit_of("leaf", bit) == 1
    pack, mixed_n, halves, curve_u, total_u, total_l = refs[3:]
    low_s = split(jnp.where(upper, other[1], own[1]))
    up_s = split(jnp.where(upper, own[1], other[1]))
    k_low = jnp.where(upper, other[0], own[0])
    k_up_s = split(jnp.where(upper, own[0], other[0]))
    for ref, value in ((total_u, up_s), (total_l, low_s), (curve_u, k_up_s)):
        ref[0], ref[1] = value
    x = dot3(k_up_s, low_s, NN)
    x_s = split(x)
    k = k_low + dot3(low_s, x_s, TN)
    a, e = mixed[0], mixed[1]
    keep_split(halves, jnp.where(upper, a.T, e))
    a_s, e_s = split(a), split(e)
    a_n = jnp.where(upper, dot3(a_s, low_s, NN), a + dot3(e_s, x_s, TN))
    e_n = jnp.where(upper, e, dot3(up_s, e_s, NN))
    if last:
        keep_split(pack, k)
        keep_split(mixed_n, jnp.where(bit_of("leaf", bit + 1) == 1, a_n.T, e_n))
    else:
        pack[0] = k
        pack[1] = dot3(up_s, low_s, NN)
        mixed_n[0], mixed_n[1] = a_n, e_n


def maps(size, last):
    both = ((2, size, size), BF16)
    kept = both if last else ((2, size, size), F32)
    return [kept, kept, both, both, both, both]


def fold_kernel(bit, own, other, send, keep):
    total = send.shape[0]
    chunk = total
    value = own[...] + other[...]
    first, second = value[:chunk], value[chunk:]
    high = bit_of("front", bit) == 1
    send[...] = jnp.where(high, first, second)
    keep[...] = jnp.where(high, second, first)


def enter_kernel(own, other, inverse, own_map, sol, message):
    drive = own[...] + other[...]
    value = dot3(split(drive), pair(inverse), NT)
    sol[...] = value
    rows = value.shape[0]
    message[:rows] = value
    message[rows:] = dot3(split(value), split(own_map[...]), NN)


def step_kernel(bit, last, *refs):
    sol, own, other, halves, curve_u, total_u, total_l, sol_n = refs[:8]
    message = refs[8:]
    upper = bit_of("leaf", bit) == 1
    rows = sol.shape[0]
    z_own, p_own, z_other, p_other = own[:rows], own[rows:], other[:rows], other[rows:]
    z_low = jnp.where(upper, z_other, z_own)
    z_up = jnp.where(upper, z_own, z_other)
    p_low = jnp.where(upper, p_other, p_own)
    p_up = jnp.where(upper, p_own, p_other)
    z_low_s = split(z_low)
    middle = p_up + dot3(z_low_s, pair(curve_u), NN)
    middle_s = split(middle)
    z_new = z_up + dot3(z_low_s, pair(total_u), NT)
    p_new = p_low + dot3(middle_s, pair(total_l), NN)
    given = split(jnp.where(upper, z_low, middle))
    sol_n[...] = sol[...] + dot3(given, pair(halves), NN)
    if last:
        message[0][...], message[1][...] = z_new, p_new
    else:
        message[0][:rows], message[0][rows:] = z_new, p_new


def turn_kernel(message, came, curve, back):
    back[...] = message[...] + dot3(split(came[...]), pair(curve), NN)


def leave_kernel(bit, sol, came, back, halves, inverse, top):
    upper = bit_of("leaf", bit) == 1
    given = split(jnp.where(upper, came[...], back[...]))
    value = sol[...] + dot3(given, pair(halves), NN)
    top[...] = dot3(split(value), pair(inverse), NN)


def gather_front(x, bits):
    pieces = {0: x}
    for bit in reversed(range(bits)):
        for i in list(pieces):
            pieces[i | (1 << bit)] = exchange(pieces[i], "front", bit)
    return [pieces[i] for i in range(1 << bits)]


def local(rhs_local, dinv_local, update_local, parent, row_blocks, sep_rhs, sep_dinv, sep_coupling):
    fronts, leaves = lax.axis_size("front"), lax.axis_size("leaf")
    front_bits, rounds = fronts.bit_length() - 1, leaves.bit_length() - 1
    size = sep_dinv.shape[1]
    cols = sep_rhs.shape[1]
    chunk = cols // fronts

    (stacked,) = call(
        stack_kernel,
        "stack",
        [(HBM, sep_dinv), (HBM, sep_coupling)],
        [((2, *sep_dinv.shape), F32)],
        [pltpu.SemaphoreType.DMA((2,))],
    )
    came = [swap(stacked, "front", m) for m in range(1, fronts)]
    acc, *local_halves = prepare(
        rhs_local, dinv_local, update_local, row_blocks, sep_rhs, stacked
    )
    own_map, inverse = block_map([stacked, *came], acc)
    other_map = exchange(own_map, "leaf", 0)

    solved, send, keep = local_forward(parent, acc, local_halves, own_map, fronts)

    pack, mixed, *tools = call(
        first_merge_kernel,
        "merge_0",
        [(V, own_map), (V, other_map), (pl.ANY, send)],
        maps(size, False),
    )
    for bit in range(front_bits):
        received = exchange(send, "front", bit)
        if bit + 1 < front_bits:
            half = ((keep.shape[0] // 2, size), F32)
            send, keep = call(
                lambda *refs, bit=bit: fold_kernel(bit + 1, *refs),
                "fold",
                [(V, keep), (V, received)],
                [half, half],
            )
    sol, message = call(
        enter_kernel,
        "enter",
        [(V, keep), (V, received), (V, inverse), (V, own_map)],
        [((chunk, size), F32), ((2 * chunk, size), F32)],
    )
    part = ((chunk, size), F32)
    for bit in range(rounds - 1):
        last = bit == rounds - 2
        received = exchange(message, "leaf", bit)
        if not last:
            other_pack = exchange(pack, "leaf", bit + 1)
        sol, *message = call(
            lambda *refs, bit=bit, last=last: step_kernel(bit, last, *refs),
            f"step_{bit}",
            [(V, a) for a in (sol, message, received, *tools)],
            [part] + ([part, part] if last else [((2 * chunk, size), F32)]),
        )
        if not last:
            (message,) = message
            last = bit == rounds - 3
            pack, mixed, *tools = call(
                lambda *refs, bit=bit, last=last: merge_kernel(bit + 1, last, *refs),
                f"merge_{bit + 1}",
                [(V, a) for a in (pack, other_pack, mixed)],
                maps(size, last),
            )
    came = exchange(message[0], "leaf", rounds - 1)
    (back,) = call(turn_kernel, "turn", [(V, a) for a in (message[1], came, pack)], [part])
    back = exchange(back, "leaf", rounds - 1)
    (top,) = call(
        lambda *refs: leave_kernel(rounds - 1, *refs),
        "leave",
        [(V, a) for a in (sol, came, back, mixed, inverse)],
        [part],
    )
    pieces = gather_front(top, front_bits)
    sol_local, sep_solution = local_backward(
        parent, solved, local_halves, pieces
    )
    return (sol_local, sep_solution)


def solution(mesh):
    spread3 = P(("leaf", "front"), None, None)
    spread2 = P(("leaf", "front"), None)
    spread1 = P(("leaf", "front"))
    return jax.shard_map(
        local,
        mesh=mesh,
        in_specs=(spread3, spread3, spread3, spread1, spread2, spread2, spread2, spread2),
        out_specs=(spread3, spread2),
        check_vma=False,
    )
```

```python
import jax
import jax.numpy as jnp
from jax import lax
from jax.experimental import pallas as pl
from jax.experimental.pallas import tpu as pltpu
from jax.sharding import PartitionSpec as P

F32 = jnp.float32
BF16 = jnp.bfloat16
NN = (((1,), (0,)), ((), ()))
NT = (((1,), (1,)), ((), ()))
TN = (((0,), (0,)), ((), ()))
VMEM_BYTES = 24 << 20
HALVES = 2


def split(x):
    high = x.astype(BF16)
    return high, (x - high.astype(F32)).astype(BF16)


def dot1(a, b, dims):
    return lax.dot_general(a, b, dims, preferred_element_type=F32)


def dot3(a, b, dims):
    return dot1(a[0], b[0], dims) + (dot1(a[0], b[1], dims) + dot1(a[1], b[0], dims))


def keep_split(ref, value):
    ref[0], ref[1] = split(value)


def pair(ref):
    return ref[0], ref[1]


def bit_of(axis, bit):
    return (lax.axis_index(axis) // (1 << bit)) % 2


def call(kernel, name, ins, outs, scratch=()):
    specs = [pl.BlockSpec(memory_space=space) for space, _ in ins]
    ins = [
        (space, pltpu.with_memory_space_constraint(a, HBM) if space == HBM else a)
        for space, a in ins
    ]
    return pl.pallas_call(
        kernel,
        name=name,
        in_specs=specs,
        out_specs=tuple(pl.BlockSpec(memory_space=pltpu.VMEM) for _ in outs),
        out_shape=tuple(jax.ShapeDtypeStruct(*o) for o in outs),
        scratch_shapes=list(scratch),
        compiler_params=pltpu.CompilerParams(vmem_limit_bytes=VMEM_BYTES),
    )(*[a for _, a in ins])


V = pltpu.VMEM
HBM = pltpu.HBM


def swap(x, axis, mask):
    n = lax.axis_size(axis)
    return lax.ppermute(x, axis, [(i, i ^ mask) for i in range(n)])


def exchange(x, axis, bit):
    return swap(x, axis, 1 << bit)


def prepare_nodes(count, rows_at, row_columns, dinv, upd, rhs, outs, waits):
    acc, inv_hi, inv_lo, upd_hi, upd_lo = outs
    size = dinv.shape[1]
    width = acc.shape[2]
    lane = lax.broadcasted_iota(jnp.int32, (size, size), 1).astype(F32)
    for k in range(count):
        for c in waits[k]:
            c.wait()
        inv_hi[k], inv_lo[k] = split(dinv[k])
        high, low = split(upd[k])
        chosen = (lane == row_columns[:, rows_at + k : rows_at + k + 1]).astype(BF16)
        upd_hi[k] = dot1(chosen, high, NN).astype(BF16)
        upd_lo[k] = dot1(chosen, low, NN).astype(BF16)
        turned = rhs[k].T
        for h in range(HALVES):
            acc[h, k] = turned[h * width : (h + 1) * width]


def prepare_first_kernel(nodes, *refs):
    (rows_h, sep_h, rhs_h, dinv_h, upd_h, _), refs = refs[:6], refs[6:]
    outs, (top, row_columns, rhs_n, dinv_n, upd_n), refs = refs[:5], refs[5:10], refs[10:]
    rhs_v, dinv_v, upd_v, square, rows, sep, sems, small = refs
    cols = rhs_v.shape[2]
    width = cols // HALVES
    first = nodes // 2
    few = [
        pltpu.make_async_copy(src, dst, small.at[i])
        for i, (src, dst) in enumerate(((rows_h, rows), (sep_h, sep)))
    ]
    for c in few:
        c.start()
    copies = []
    for k in range(nodes):
        ins = (upd_v, dinv_v, rhs_v) if k < first else (upd_n, dinv_n, rhs_n)
        group = [
            pltpu.make_async_copy(src.at[k], dst.at[k % first], sems.at[i, k])
            for i, (src, dst) in enumerate(zip((upd_h, dinv_h, rhs_h), ins))
        ]
        for c in group:
            c.start()
        copies.append(group)
    front = lax.axis_index("front")
    square[...] = jnp.zeros_like(square)
    for c in few:
        c.wait()
    share = sep.shape[0]
    square[pl.ds(pl.multiple_of(front * share, 8), share), :] = sep[...]
    turned = square[...].T
    for h in range(HALVES):
        top[h] = turned[h * width : (h + 1) * width]
    row_columns[...] = rows[...].astype(F32).T
    prepare_nodes(first, 0, row_columns, dinv_v, upd_v, rhs_v, outs, copies[:first])
    for group in copies[first:]:
        for c in group:
            c.wait()


def prepare_second_kernel(first, row_columns, rhs, dinv, upd, _, *outs):
    count = rhs.shape[0]
    waits = [()] * count
    prepare_nodes(count, first, row_columns, dinv, upd, rhs, outs, waits)


def prepared(count, size, cols):
    half = ((count, size, size), BF16)
    return [((HALVES, count, cols // HALVES, size), F32), half, half, half, half]


def prepare_first(rhs, dinv, update, rows, sep, after):
    nodes, size, cols = rhs.shape
    first = nodes // 2
    some = (first, size, cols)
    big = pltpu.VMEM(some, F32)
    return call(
        lambda *refs: prepare_first_kernel(nodes, *refs),
        "prepare_first",
        [(HBM, a) for a in (rows, sep, rhs, dinv, update)] + [(pl.ANY, after)],
        prepared(first, size, cols)
        + [((HALVES, cols // HALVES, size), F32), ((size, nodes), F32)]
        + [((nodes - first, *some[1:]), F32)] * 3,
        [big, big, big, pltpu.VMEM((size, cols), F32)]
        + [pltpu.VMEM(rows.shape, jnp.int32), pltpu.VMEM(sep.shape, F32)]
        + [pltpu.SemaphoreType.DMA((3, nodes)), pltpu.SemaphoreType.DMA((2,))],
    )


def prepare_second(row_columns, rhs, dinv, update, after):
    count, size, cols = rhs.shape
    first = row_columns.shape[1] - count
    return call(
        lambda *refs: prepare_second_kernel(first, *refs),
        "prepare_second",
        [(V, a) for a in (row_columns, rhs, dinv, update)] + [(pl.ANY, after)],
        prepared(count, size, cols),
    )


def chain_up(begin, end, nodes, copy, parent, accs, halves, solved, offset):
    inv_hi, inv_lo, upd_hi, upd_lo = halves
    width = accs[0].shape[1]
    for k in range(begin, end):
        i = k - begin
        inverse = (inv_hi[i], inv_lo[i])
        update = (upd_hi[i], upd_lo[i])
        for h in range(HALVES):
            value = dot3(split(accs[h][k - offset]), inverse, NT)
            solved[i, h * width : (h + 1) * width] = value
            moved = dot3(split(value), update, NT)
            if copy is not None:
                copy.wait()
                copy = None
            above = (nodes if k == nodes - 1 else parent[k]) - offset
            accs[h][above] = accs[h][above] - moved


def chain_first_kernel(nodes, *refs):
    parent_h, acc_a, acc_b, top = refs[:4]
    halves, solved, rest, parent, sem = refs[4:8], refs[8], refs[9], refs[10], refs[11]
    accs = refs[12:]
    copy = pltpu.make_async_copy(parent_h, parent, sem)
    copy.start()
    first = acc_a.shape[1]
    for h in range(HALVES):
        for k in range(nodes):
            accs[h][k] = acc_a[h, k] if k < first else acc_b[h, k - first]
        accs[h][nodes] = top[h]
    chain_up(0, first, nodes, copy, parent, accs, halves, solved, 0)
    for h in range(HALVES):
        for k in range(first, nodes + 1):
            rest[h, k - first] = accs[h][k]


def chain_first(parent, acc_a, acc_b, top, halves):
    first, (width, size) = acc_a.shape[1], acc_a.shape[2:]
    nodes = first + acc_b.shape[1]
    return call(
        lambda *refs: chain_first_kernel(nodes, *refs),
        "chain_first",
        [(HBM, parent)] + [(V, a) for a in (acc_a, acc_b, top, *halves)],
        [((first, width * HALVES, size), F32), ((HALVES, nodes - first + 1, width, size), F32)],
        [pltpu.SMEM((nodes,), jnp.int32), pltpu.SemaphoreType.DMA]
        + [pltpu.VMEM((nodes + 1, width, size), F32)] * HALVES,
    )


def chain_second_kernel(nodes, fronts, *refs):
    parent_h, rest = refs[:2]
    halves, solved, send, keep, square, parent, sem = refs[2:6], *refs[7:13]
    accs = refs[13:]
    copy = pltpu.make_async_copy(parent_h, parent, sem)
    copy.start()
    count = rest.shape[1]
    width = rest.shape[2]
    for h in range(HALVES):
        accs[h][...] = rest[h]
    first = nodes + 1 - count
    chain_up(first, nodes, nodes, copy, parent, accs, halves, solved, first)
    front = lax.axis_index("front")
    chunk = width * HALVES // fronts
    for h in range(HALVES):
        square[h * width : (h + 1) * width] = accs[h][nodes - first]
    low_bit = front % 2
    for i in range(fronts // 2):
        for ref, own in ((keep, low_bit), (send, 1 - low_bit)):
            start = pl.multiple_of((2 * i + own) * chunk, 8)
            ref[i * chunk : (i + 1) * chunk] = square[pl.ds(start, chunk), :]


def chain_second(parent, rest, halves, after, fronts):
    nodes = parent.shape[0]
    count, width, size = rest.shape[1:]
    cols = width * HALVES
    part = ((cols // 2, size), F32)
    return call(
        lambda *refs: chain_second_kernel(nodes, fronts, *refs),
        "chain_second",
        [(HBM, parent)] + [(V, a) for a in (rest, *halves)] + [(pl.ANY, after)],
        [((count - 1, cols, size), F32), part, part],
        [pltpu.VMEM((cols, size), F32), pltpu.SMEM((nodes,), jnp.int32), pltpu.SemaphoreType.DMA]
        + [pltpu.VMEM((count, width, size), F32)] * HALVES,
    )


def backward_kernel(nodes, fronts, *refs):
    parent_h, parts, refs = refs[0], (refs[1:6], refs[6:11]), refs[11:]
    pieces = refs[:fronts]
    sol, sep_out = refs[fronts : 2 + fronts]
    square, parent, staged, sem, sems = refs[2 + fronts : 7 + fronts]
    known = refs[7 + fronts :]
    first = parts[0][0].shape[0]
    copy = pltpu.make_async_copy(parent_h, parent, sem)
    copy.start()
    front = lax.axis_index("front")
    chunk = pieces[0].shape[0]
    width = known[0].shape[1]
    for i in range(fronts):
        start = pl.multiple_of((front ^ i) * chunk, 8)
        square[pl.ds(start, chunk), :] = pieces[i][...]
    for h in range(HALVES):
        known[h][nodes] = square[h * width : (h + 1) * width]
    square[...] = square[...].T
    share = sep_out.shape[0]
    sep_out[...] = square[pl.ds(pl.multiple_of(front * share, 8), share), :]
    outs = []
    for k in reversed(range(nodes)):
        i = k % first
        solved, inv_hi, inv_lo, upd_hi, upd_lo = parts[k // first]
        inverse = (inv_hi[i], inv_lo[i])
        update = (upd_hi[i], upd_lo[i])
        if k == nodes - 2:
            copy.wait()
        above = nodes if k == nodes - 1 else parent[k]
        for h in range(HALVES):
            rows = slice(h * width, (h + 1) * width)
            part = solved[i, rows] - dot3(split(known[h][above]), update, NN)
            value = dot3(split(part), inverse, NN)
            known[h][k] = value
            staged[k, :, rows] = value.T
        out = pltpu.make_async_copy(staged.at[k], sol.at[k], sems.at[k])
        out.start()
        outs.append(out)
    for out in outs:
        out.wait()


def local_backward(parent, parts, pieces):
    nodes = parent.shape[0]
    cols, size = parts[0][0].shape[1:]
    fronts = len(pieces)
    sol, sep = jax.ShapeDtypeStruct((nodes, size, cols), F32), ((size // fronts, cols), F32)
    ins = [(HBM, parent)] + [(V, a) for a in (*parts[0], *parts[1], *pieces)]
    return pl.pallas_call(
        lambda *refs: backward_kernel(nodes, fronts, *refs),
        name="local_backward",
        in_specs=[pl.BlockSpec(memory_space=space) for space, _ in ins],
        out_specs=(pl.BlockSpec(memory_space=HBM), pl.BlockSpec(memory_space=V)),
        out_shape=(sol, jax.ShapeDtypeStruct(*sep)),
        scratch_shapes=[pltpu.VMEM((size, cols), F32), pltpu.SMEM((nodes,), jnp.int32)]
        + [pltpu.VMEM((nodes, size, cols), F32), pltpu.SemaphoreType.DMA]
        + [pltpu.SemaphoreType.DMA((nodes,))]
        + [pltpu.VMEM((nodes + 1, cols // HALVES, size), F32)] * HALVES,
        compiler_params=pltpu.CompilerParams(vmem_limit_bytes=VMEM_BYTES),
    )(pltpu.with_memory_space_constraint(parent, HBM), *[a for _, a in ins[1:]])


def stack_kernel(first, second, out, sems):
    copies = [pltpu.make_async_copy(a, out.at[i], sems.at[i]) for i, a in enumerate((first, second))]
    for c in copies:
        c.start()
    for c in copies:
        c.wait()


def block_map_kernel(fronts, *refs):
    parts = refs[:fronts]
    _, total, inverse_halves, square = refs[fronts:]
    front = lax.axis_index("front")
    share = parts[0].shape[1]
    for i in range(fronts):
        start = pl.multiple_of((front ^ i) * share, 8)
        square[:, pl.ds(start, share), :] = parts[i][...]
    inverse = split(square[0])
    inverse_halves[0], inverse_halves[1] = inverse
    total[...] = -dot3(inverse, split(square[1]), NN)


def block_map(parts, after):
    fronts = len(parts)
    size = parts[0].shape[2]
    return call(
        lambda *refs: block_map_kernel(fronts, *refs),
        "block_map",
        [(V, a) for a in parts] + [(pl.ANY, after)],
        [((size, size), F32), ((2, size, size), BF16)],
        [pltpu.VMEM((2, size, size), F32)],
    )


def pack_maps(pack, k, t):
    half = k.shape[0] // 2
    pack[0], pack[1], pack[2] = k[:half, :half], k[:half, half:], k[half:, half:]
    if t is not None:
        for i in range(4):
            r, c = (i // 2) * half, (i % 2) * half
            pack[3 + i] = t[r : r + half, c : c + half]


def pack_k(pack):
    first = jnp.concatenate([pack[0], pack[1]], axis=1)
    second = jnp.concatenate([pack[1].T, pack[2]], axis=1)
    return jnp.concatenate([first, second], axis=0)


def pack_t(pack):
    rows = [jnp.concatenate([pack[3 + i], pack[4 + i]], axis=1) for i in (0, 2)]
    return jnp.concatenate(rows, axis=0)


def first_merge_kernel(*refs):
    own, other, _, pack, mixed, halves, curve_u, total_u, total_l = refs
    upper = bit_of("leaf", 0) == 1
    low = jnp.where(upper, other[...], own[...])
    up = jnp.where(upper, own[...], other[...])
    low_s, up_s = split(low), split(up)
    for ref, value in ((total_u, up_s), (total_l, low_s)):
        ref[0], ref[1] = value
    k_up = dot3(up_s, up_s, TN)
    k_up_s = split(k_up)
    curve_u[0], curve_u[1] = k_up_s
    x = dot3(k_up_s, low_s, NN)
    t = dot3(up_s, low_s, NN)
    pack_maps(pack, dot3(low_s, low_s, TN) + dot3(low_s, split(x), TN), t)
    size = low.shape[0]
    row = lax.broadcasted_iota(jnp.int32, (size, size), 0)
    col = lax.broadcasted_iota(jnp.int32, (size, size), 1)
    unit = (row == col).astype(F32)
    keep_split(halves, jnp.where(upper, up.T, unit))
    mixed[0] = jnp.where(upper, t, low + x)
    mixed[1] = jnp.where(upper, unit, up)


def merge_kernel(bit, last, *refs):
    own, other, mixed = refs[:3]
    upper = bit_of("leaf", bit) == 1
    pack, mixed_n, halves, curve_u, total_u, total_l = refs[3:]
    own_k, own_t, other_k, other_t = pack_k(own), pack_t(own), pack_k(other), pack_t(other)
    low_s = split(jnp.where(upper, other_t, own_t))
    up_s = split(jnp.where(upper, own_t, other_t))
    k_low = jnp.where(upper, other_k, own_k)
    k_up_s = split(jnp.where(upper, own_k, other_k))
    for ref, value in ((total_u, up_s), (total_l, low_s), (curve_u, k_up_s)):
        ref[0], ref[1] = value
    x = dot3(k_up_s, low_s, NN)
    x_s = split(x)
    k = k_low + dot3(low_s, x_s, TN)
    a, e = mixed[0], mixed[1]
    keep_split(halves, jnp.where(upper, a.T, e))
    a_s, e_s = split(a), split(e)
    a_n = jnp.where(upper, dot3(a_s, low_s, NN), a + dot3(e_s, x_s, TN))
    e_n = jnp.where(upper, e, dot3(up_s, e_s, NN))
    if last:
        pack_maps(pack, k, None)
        keep_split(mixed_n, jnp.where(bit_of("leaf", bit + 1) == 1, a_n.T, e_n))
    else:
        pack_maps(pack, k, dot3(up_s, low_s, NN))
        mixed_n[0], mixed_n[1] = a_n, e_n


def maps(size, last):
    both = ((2, size, size), BF16)
    half = size // 2
    pack = ((3 if last else 7, half, half), F32)
    return [pack, both if last else ((2, size, size), F32), both, both, both, both]


def fold_kernel(bit, own, other, send, keep):
    total = send.shape[0]
    chunk = total
    value = own[...] + other[...]
    first, second = value[:chunk], value[chunk:]
    high = bit_of("front", bit) == 1
    send[...] = jnp.where(high, first, second)
    keep[...] = jnp.where(high, second, first)


def enter_kernel(own, other, inverse, own_map, sol, message):
    drive = own[...] + other[...]
    value = dot3(split(drive), pair(inverse), NT)
    sol[...] = value
    rows = value.shape[0]
    message[:rows] = value
    message[rows:] = dot3(split(value), split(own_map[...]), NN)


def step_kernel(bit, last, *refs):
    sol, own, other, halves, curve_u, total_u, total_l, sol_n = refs[:8]
    message = refs[8:]
    upper = bit_of("leaf", bit) == 1
    rows = sol.shape[0]
    z_own, p_own, z_other, p_other = own[:rows], own[rows:], other[:rows], other[rows:]
    z_low = jnp.where(upper, z_other, z_own)
    z_up = jnp.where(upper, z_own, z_other)
    p_low = jnp.where(upper, p_other, p_own)
    p_up = jnp.where(upper, p_own, p_other)
    z_low_s = split(z_low)
    middle = p_up + dot3(z_low_s, pair(curve_u), NN)
    middle_s = split(middle)
    z_new = z_up + dot3(z_low_s, pair(total_u), NT)
    p_new = p_low + dot3(middle_s, pair(total_l), NN)
    given = split(jnp.where(upper, z_low, middle))
    sol_n[...] = sol[...] + dot3(given, pair(halves), NN)
    if last:
        message[0][...] = jnp.where(bit_of("leaf", bit + 1) == 1, p_new, z_new)
        message[1][...] = z_new
    else:
        message[0][:rows], message[0][rows:] = z_new, p_new


def leave_kernel(bit, sol, own_z, came, halves, pack, inverse, top):
    upper = bit_of("leaf", bit) == 1
    value = came[...]
    middle = value + dot3(split(own_z[...]), split(pack_k(pack)), NN)
    given = split(jnp.where(upper, value, middle))
    value = sol[...] + dot3(given, pair(halves), NN)
    top[...] = dot3(split(value), pair(inverse), NN)


def gather_front(x, bits):
    pieces = {0: x}
    for bit in reversed(range(bits)):
        for i in list(pieces):
            pieces[i | (1 << bit)] = exchange(pieces[i], "front", bit)
    return [pieces[i] for i in range(1 << bits)]


def local(rhs_local, dinv_local, update_local, parent, row_blocks, sep_rhs, sep_dinv, sep_coupling):
    fronts, leaves = lax.axis_size("front"), lax.axis_size("leaf")
    front_bits, rounds = fronts.bit_length() - 1, leaves.bit_length() - 1
    size = sep_dinv.shape[1]
    cols = sep_rhs.shape[1]
    chunk = cols // fronts

    (stacked,) = call(
        stack_kernel,
        "stack",
        [(HBM, sep_dinv), (HBM, sep_coupling)],
        [((2, *sep_dinv.shape), F32)],
        [pltpu.SemaphoreType.DMA((2,))],
    )
    came = [swap(stacked, "front", m) for m in range(1, fronts)]
    acc_a, *first_halves = prepare_first(
        rhs_local, dinv_local, update_local, row_blocks, sep_rhs, stacked
    )
    first_halves, (top, row_columns, *raw) = first_halves[:4], first_halves[4:]
    own_map, inverse = block_map([stacked, *came], acc_a)
    other_map = exchange(own_map, "leaf", 0)
    acc_b, *second_halves = prepare_second(row_columns, *raw, own_map)
    first_solved, rest = chain_first(parent, acc_a, acc_b, top, first_halves)
    pack, mixed, *tools = call(
        first_merge_kernel,
        "merge_0",
        [(V, own_map), (V, other_map), (pl.ANY, rest)],
        maps(size, False),
    )
    other_pack = exchange(pack, "leaf", 1)
    second_solved, send, keep = chain_second(parent, rest, second_halves, mixed, fronts)
    for bit in range(front_bits):
        received = exchange(send, "front", bit)
        if bit + 1 < front_bits:
            half = ((keep.shape[0] // 2, size), F32)
            send, keep = call(
                lambda *refs, bit=bit: fold_kernel(bit + 1, *refs),
                "fold",
                [(V, keep), (V, received)],
                [half, half],
            )
    sol, message = call(
        enter_kernel,
        "enter",
        [(V, keep), (V, received), (V, inverse), (V, own_map)],
        [((chunk, size), F32), ((2 * chunk, size), F32)],
    )
    part = ((chunk, size), F32)
    for bit in range(rounds - 1):
        last = bit == rounds - 2
        received = exchange(message, "leaf", bit)
        sol, *message = call(
            lambda *refs, bit=bit, last=last: step_kernel(bit, last, *refs),
            f"step_{bit}",
            [(V, a) for a in (sol, message, received, *tools)],
            [part] + ([part, part] if last else [((2 * chunk, size), F32)]),
        )
        if not last:
            (message,) = message
            last = bit == rounds - 3
            pack, mixed, *tools = call(
                lambda *refs, bit=bit, last=last: merge_kernel(bit + 1, last, *refs),
                f"merge_{bit + 1}",
                [(V, a) for a in (pack, other_pack, mixed)],
                maps(size, last),
            )
            other_pack = exchange(pack, "leaf", bit + 2)
    came = exchange(message[0], "leaf", rounds - 1)
    (top,) = call(
        lambda *refs: leave_kernel(rounds - 1, *refs),
        "leave",
        [(V, a) for a in (sol, message[1], came, mixed, other_pack, inverse)],
        [part],
    )
    pieces = gather_front(top, front_bits)
    sol_local, sep_solution = local_backward(
        parent, [(first_solved, *first_halves), (second_solved, *second_halves)], pieces
    )
    return (sol_local, sep_solution)


def solution(mesh):
    spread3 = P(("leaf", "front"), None, None)
    spread2 = P(("leaf", "front"), None)
    spread1 = P(("leaf", "front"))
    return jax.shard_map(
        local,
        mesh=mesh,
        in_specs=(spread3, spread3, spread3, spread1, spread2, spread2, spread2, spread2),
        out_specs=(spread3, spread2),
        check_vma=False,
    )
```

```python
import jax
import jax.numpy as jnp
from jax import lax
from jax.experimental import pallas as pl
from jax.experimental.pallas import tpu as pltpu
from jax.sharding import PartitionSpec as P

F32 = jnp.float32
BF16 = jnp.bfloat16
NN = (((1,), (0,)), ((), ()))
NT = (((1,), (1,)), ((), ()))
TN = (((0,), (0,)), ((), ()))
VMEM_BYTES = 24 << 20
HALVES = 2


def split(x):
    high = x.astype(BF16)
    return high, (x - high.astype(F32)).astype(BF16)


def dot1(a, b, dims):
    return lax.dot_general(a, b, dims, preferred_element_type=F32)


def dot3(a, b, dims):
    axis = 1 - dims[0][0][0]
    rows = a[0].shape[axis]
    both = dot1(jnp.concatenate(a, axis=axis), b[0], dims)
    return both[:rows] + (both[rows:] + dot1(a[0], b[1], dims))


def keep_split(ref, value):
    ref[0], ref[1] = split(value)


def pair(ref):
    return ref[0], ref[1]


def bit_of(axis, bit):
    return (lax.axis_index(axis) // (1 << bit)) % 2


def call(kernel, name, ins, outs, scratch=()):
    specs = [pl.BlockSpec(memory_space=space) for space, _ in ins]
    ins = [
        (space, pltpu.with_memory_space_constraint(a, HBM) if space == HBM else a)
        for space, a in ins
    ]
    return pl.pallas_call(
        kernel,
        name=name,
        in_specs=specs,
        out_specs=tuple(pl.BlockSpec(memory_space=pltpu.VMEM) for _ in outs),
        out_shape=tuple(jax.ShapeDtypeStruct(*o) for o in outs),
        scratch_shapes=list(scratch),
        compiler_params=pltpu.CompilerParams(vmem_limit_bytes=VMEM_BYTES),
    )(*[a for _, a in ins])


V = pltpu.VMEM
HBM = pltpu.HBM


def swap(x, axis, mask):
    n = lax.axis_size(axis)
    return lax.ppermute(x, axis, [(i, i ^ mask) for i in range(n)])


def exchange(x, axis, bit):
    return swap(x, axis, 1 << bit)


def prepare_nodes(count, rows_at, row_columns, dinv, upd, rhs, outs, waits):
    acc, inv_hi, inv_lo, upd_hi, upd_lo = outs
    size = dinv.shape[1]
    width = acc.shape[2]
    lane = lax.broadcasted_iota(jnp.int32, (size, size), 1).astype(F32)
    for k in range(count):
        for c in waits[k]:
            c.wait()
        inv_hi[k], inv_lo[k] = split(dinv[k])
        high, low = split(upd[k])
        chosen = (lane == row_columns[:, rows_at + k : rows_at + k + 1]).astype(BF16)
        upd_hi[k] = dot1(chosen, high, NN).astype(BF16)
        upd_lo[k] = dot1(chosen, low, NN).astype(BF16)
        turned = rhs[k].T
        for h in range(HALVES):
            acc[h, k] = turned[h * width : (h + 1) * width]


def prepare_first_kernel(nodes, *refs):
    (rows_h, sep_h, rhs_h, dinv_h, upd_h, _), refs = refs[:6], refs[6:]
    outs, (top, row_columns, rhs_n, dinv_n, upd_n), refs = refs[:5], refs[5:10], refs[10:]
    rhs_v, dinv_v, upd_v, square, rows, sep, sems, small = refs
    cols = rhs_v.shape[2]
    width = cols // HALVES
    first = nodes // 2
    few = [
        pltpu.make_async_copy(src, dst, small.at[i])
        for i, (src, dst) in enumerate(((rows_h, rows), (sep_h, sep)))
    ]
    for c in few:
        c.start()
    copies = []
    for k in range(nodes):
        ins = (upd_v, dinv_v, rhs_v) if k < first else (upd_n, dinv_n, rhs_n)
        group = [
            pltpu.make_async_copy(src.at[k], dst.at[k % first], sems.at[i, k])
            for i, (src, dst) in enumerate(zip((upd_h, dinv_h, rhs_h), ins))
        ]
        for c in group:
            c.start()
        copies.append(group)
    front = lax.axis_index("front")
    square[...] = jnp.zeros_like(square)
    for c in few:
        c.wait()
    share = sep.shape[0]
    square[pl.ds(pl.multiple_of(front * share, 8), share), :] = sep[...]
    turned = square[...].T
    for h in range(HALVES):
        top[h] = turned[h * width : (h + 1) * width]
    row_columns[...] = rows[...].astype(F32).T
    prepare_nodes(first, 0, row_columns, dinv_v, upd_v, rhs_v, outs, copies[:first])
    for group in copies[first:]:
        for c in group:
            c.wait()


def prepare_second_kernel(first, row_columns, rhs, dinv, upd, _, *outs):
    count = rhs.shape[0]
    waits = [()] * count
    prepare_nodes(count, first, row_columns, dinv, upd, rhs, outs, waits)


def prepared(count, size, cols):
    half = ((count, size, size), BF16)
    return [((HALVES, count, cols // HALVES, size), F32), half, half, half, half]


def prepare_first(rhs, dinv, update, rows, sep, after):
    nodes, size, cols = rhs.shape
    first = nodes // 2
    some = (first, size, cols)
    big = pltpu.VMEM(some, F32)
    return call(
        lambda *refs: prepare_first_kernel(nodes, *refs),
        "prepare_first",
        [(HBM, a) for a in (rows, sep, rhs, dinv, update)] + [(pl.ANY, after)],
        prepared(first, size, cols)
        + [((HALVES, cols // HALVES, size), F32), ((size, nodes), F32)]
        + [((nodes - first, *some[1:]), F32)] * 3,
        [big, big, big, pltpu.VMEM((size, cols), F32)]
        + [pltpu.VMEM(rows.shape, jnp.int32), pltpu.VMEM(sep.shape, F32)]
        + [pltpu.SemaphoreType.DMA((3, nodes)), pltpu.SemaphoreType.DMA((2,))],
    )


def prepare_second(row_columns, rhs, dinv, update, after):
    count, size, cols = rhs.shape
    first = row_columns.shape[1] - count
    return call(
        lambda *refs: prepare_second_kernel(first, *refs),
        "prepare_second",
        [(V, a) for a in (row_columns, rhs, dinv, update)] + [(pl.ANY, after)],
        prepared(count, size, cols),
    )


def forward_kernel(nodes, fronts, *refs):
    (parent_h, acc_a, acc_b, top), parts, refs = refs[:4], (refs[4:8], refs[8:12]), refs[13:]
    solved, send, keep, square, parent, sem = refs[:6]
    accs = refs[6:]
    copy = pltpu.make_async_copy(parent_h, parent, sem)
    copy.start()
    first, width = acc_a.shape[1:3]
    for h in range(HALVES):
        for k in range(nodes):
            accs[h][k] = acc_a[h, k] if k < first else acc_b[h, k - first]
        accs[h][nodes] = top[h]
    for k in range(nodes):
        inv_hi, inv_lo, upd_hi, upd_lo = parts[k // first]
        i = k % first
        inverse = (inv_hi[i], inv_lo[i])
        update = (upd_hi[i], upd_lo[i])
        for h in range(HALVES):
            value = dot3(split(accs[h][k]), inverse, NT)
            solved[k, h * width : (h + 1) * width] = value
            moved = dot3(split(value), update, NT)
            if k + h == 0:
                copy.wait()
            above = nodes if k == nodes - 1 else parent[k]
            accs[h][above] = accs[h][above] - moved
    front = lax.axis_index("front")
    chunk = width * HALVES // fronts
    for h in range(HALVES):
        square[h * width : (h + 1) * width] = accs[h][nodes]
    low_bit = front % 2
    for i in range(fronts // 2):
        for ref, own in ((keep, low_bit), (send, 1 - low_bit)):
            start = pl.multiple_of((2 * i + own) * chunk, 8)
            ref[i * chunk : (i + 1) * chunk] = square[pl.ds(start, chunk), :]


def local_forward(parent, acc_a, acc_b, top, first_halves, second_halves, after, fronts):
    first, (width, size) = acc_a.shape[1], acc_a.shape[2:]
    nodes = first + acc_b.shape[1]
    cols = width * HALVES
    part = ((cols // 2, size), F32)
    return call(
        lambda *refs: forward_kernel(nodes, fronts, *refs),
        "local_forward",
        [(HBM, parent)]
        + [(V, a) for a in (acc_a, acc_b, top, *first_halves, *second_halves)]
        + [(pl.ANY, after)],
        [((nodes, cols, size), F32), part, part],
        [pltpu.VMEM((cols, size), F32), pltpu.SMEM((nodes,), jnp.int32), pltpu.SemaphoreType.DMA]
        + [pltpu.VMEM((nodes + 1, width, size), F32)] * HALVES,
    )


def backward_kernel(nodes, fronts, *refs):
    (parent_h, solved), parts, refs = refs[:2], (refs[2:6], refs[6:10]), refs[10:]
    pieces = refs[:fronts]
    sol, sep_out = refs[fronts : 2 + fronts]
    square, parent, staged, sem, sems = refs[2 + fronts : 7 + fronts]
    known = refs[7 + fronts :]
    first = parts[0][0].shape[0]
    copy = pltpu.make_async_copy(parent_h, parent, sem)
    copy.start()
    chunk = pieces[0].shape[0]
    width = known[0].shape[1]
    order = [p[...] for p in pieces]
    for bit in range(fronts.bit_length() - 1):
        flip = bit_of("front", bit) == 1
        order = [jnp.where(flip, order[i ^ (1 << bit)], order[i]) for i in range(fronts)]
    for i, value in enumerate(order):
        at = i * chunk
        known[at // width][nodes, at % width : at % width + chunk] = value
    outs = []
    for k in reversed(range(nodes)):
        i = k % first
        inv_hi, inv_lo, upd_hi, upd_lo = parts[k // first]
        inverse = (inv_hi[i], inv_lo[i])
        update = (upd_hi[i], upd_lo[i])
        if k == nodes - 2:
            copy.wait()
        above = nodes if k == nodes - 1 else parent[k]
        for h in range(HALVES):
            rows = slice(h * width, (h + 1) * width)
            part = solved[k, rows] - dot3(split(known[h][above]), update, NN)
            value = dot3(split(part), inverse, NN)
            known[h][k] = value
            staged[k, :, rows] = value.T
        out = pltpu.make_async_copy(staged.at[k], sol.at[k], sems.at[k])
        out.start()
        outs.append(out)
    for h in range(HALVES):
        square[:, h * width : (h + 1) * width] = known[h][nodes].T
    share = sep_out.shape[0]
    start = pl.multiple_of(lax.axis_index("front") * share, 8)
    sep_out[...] = square[pl.ds(start, share), :]
    for out in outs:
        out.wait()


def local_backward(parent, solved, first_halves, second_halves, pieces):
    nodes, cols, size = solved.shape
    fronts = len(pieces)
    sol, sep = jax.ShapeDtypeStruct((nodes, size, cols), F32), ((size // fronts, cols), F32)
    ins = (solved, *first_halves, *second_halves, *pieces)
    return pl.pallas_call(
        lambda *refs: backward_kernel(nodes, fronts, *refs),
        name="local_backward",
        in_specs=[pl.BlockSpec(memory_space=HBM)] + [pl.BlockSpec(memory_space=V)] * len(ins),
        out_specs=(pl.BlockSpec(memory_space=HBM), pl.BlockSpec(memory_space=V)),
        out_shape=(sol, jax.ShapeDtypeStruct(*sep)),
        scratch_shapes=[pltpu.VMEM((size, cols), F32), pltpu.SMEM((nodes,), jnp.int32)]
        + [pltpu.VMEM((nodes, size, cols), F32), pltpu.SemaphoreType.DMA]
        + [pltpu.SemaphoreType.DMA((nodes,))]
        + [pltpu.VMEM((nodes + 1, cols // HALVES, size), F32)] * HALVES,
        compiler_params=pltpu.CompilerParams(vmem_limit_bytes=VMEM_BYTES),
    )(pltpu.with_memory_space_constraint(parent, HBM), *ins)


def stack_kernel(first, second, out, sems):
    copies = [pltpu.make_async_copy(a, out.at[i], sems.at[i]) for i, a in enumerate((first, second))]
    for c in copies:
        c.start()
    for c in copies:
        c.wait()


def block_map_kernel(fronts, *refs):
    parts = refs[:fronts]
    _, total, part, inverse_halves, square = refs[fronts:]
    front = lax.axis_index("front")
    share = parts[0].shape[1]
    for i in range(fronts):
        start = pl.multiple_of((front ^ i) * share, 8)
        square[:, pl.ds(start, share), :] = parts[i][...]
    inverse = split(square[0])
    inverse_halves[0], inverse_halves[1] = inverse
    value = -dot3(inverse, split(square[1]), NN)
    total[...] = value
    half = part.shape[1]
    send_blocks(part, [value[:half], value[half:]])


def block_map(parts, after):
    fronts = len(parts)
    size = parts[0].shape[2]
    return call(
        lambda *refs: block_map_kernel(fronts, *refs),
        "block_map",
        [(V, a) for a in parts] + [(pl.ANY, after)],
        [((size, size), F32), ((1, size // 2, size), F32), ((2, size, size), BF16)],
        [pltpu.VMEM((2, size, size), F32)],
    )


def quarters(x):
    half = x.shape[0] // 2
    return [x[i : i + half, j : j + half] for i in (0, half) for j in (0, half)]


def joined(a, b, c, d):
    first, second = jnp.concatenate([a, b], axis=1), jnp.concatenate([c, d], axis=1)
    return jnp.concatenate([first, second], axis=0)


def low_core():
    return bit_of("front", 0) == 0


def send_blocks(part, blocks):
    count = part.shape[0]
    low = low_core()
    for i in range(count):
        part[i] = jnp.where(low, blocks[i], blocks[len(blocks) - count + i])


def came_blocks(mine, pairs, total):
    low = low_core()
    count = mine.shape[0]
    blocks = [jnp.where(low, mine[i], pairs[i]) for i in range(count)]
    for i in range(count, total):
        j = i - total + count
        blocks.append(jnp.where(low, pairs[j], mine[j]))
    return blocks


def k_blocks(k):
    a, b, _, d = quarters(k)
    return [a, b, d]


def k_of(blocks):
    return joined(blocks[0], blocks[1], blocks[1].T, blocks[2])


def first_merge_kernel(*refs):
    own, mine, pairs, _, kept, part, mixed, halves, curve_u, total_u, total_l = refs
    upper = bit_of("leaf", 0) == 1
    came = jnp.concatenate(came_blocks(mine, pairs, 2), axis=0)
    mine = own[...]
    low = jnp.where(upper, came, mine)
    up = jnp.where(upper, mine, came)
    low_s, up_s = split(low), split(up)
    for ref, value in ((total_u, up_s), (total_l, low_s)):
        ref[0], ref[1] = value
    k_up = dot3(up_s, up_s, TN)
    k_up_s = split(k_up)
    curve_u[0], curve_u[1] = k_up_s
    x = dot3(k_up_s, low_s, NN)
    t = dot3(up_s, low_s, NN)
    k = dot3(low_s, low_s, TN) + dot3(low_s, split(x), TN)
    kept[0], kept[1] = k, t
    send_blocks(part, k_blocks(k) + quarters(t))
    size = low.shape[0]
    row = lax.broadcasted_iota(jnp.int32, (size, size), 0)
    col = lax.broadcasted_iota(jnp.int32, (size, size), 1)
    unit = (row == col).astype(F32)
    keep_split(halves, jnp.where(upper, up.T, unit))
    mixed[0] = jnp.where(upper, t, low + x)
    mixed[1] = jnp.where(upper, unit, up)


def merge_kernel(bit, last, *refs):
    own, mine, pairs, mixed = refs[:4]
    upper = bit_of("leaf", bit) == 1
    kept, part, mixed_n, halves, curve_u, total_u, total_l = refs[4:]
    own_k, own_t = own[0], own[1]
    blocks = came_blocks(mine, pairs, 7)
    other_k, other_t = k_of(blocks), joined(*blocks[3:])
    low_s = split(jnp.where(upper, other_t, own_t))
    up_s = split(jnp.where(upper, own_t, other_t))
    k_low = jnp.where(upper, other_k, own_k)
    k_up_s = split(jnp.where(upper, own_k, other_k))
    for ref, value in ((total_u, up_s), (total_l, low_s), (curve_u, k_up_s)):
        ref[0], ref[1] = value
    x = dot3(k_up_s, low_s, NN)
    x_s = split(x)
    k = k_low + dot3(low_s, x_s, TN)
    a, e = mixed[0], mixed[1]
    keep_split(halves, jnp.where(upper, a.T, e))
    a_s, e_s = split(a), split(e)
    a_n = jnp.where(upper, dot3(a_s, low_s, NN), a + dot3(e_s, x_s, TN))
    e_n = jnp.where(upper, e, dot3(up_s, e_s, NN))
    if last:
        send_blocks(part, k_blocks(k))
        keep_split(mixed_n, jnp.where(bit_of("leaf", bit + 1) == 1, a_n.T, e_n))
    else:
        t = dot3(up_s, low_s, NN)
        kept[0], kept[1] = k, t
        send_blocks(part, k_blocks(k) + quarters(t))
        mixed_n[0], mixed_n[1] = a_n, e_n


def maps(size, last):
    both, whole = ((2, size, size), BF16), ((2, size, size), F32)
    half = size // 2
    part = ((2 if last else 4, half, half), F32)
    kept = ((8, 128), F32) if last else whole
    return [kept, part, both if last else whole, both, both, both, both]


def fold_kernel(bit, own, other, send, keep):
    total = send.shape[0]
    chunk = total
    value = own[...] + other[...]
    first, second = value[:chunk], value[chunk:]
    high = bit_of("front", bit) == 1
    send[...] = jnp.where(high, first, second)
    keep[...] = jnp.where(high, second, first)


def enter_kernel(own, other, inverse, own_map, sol, message):
    drive = own[...] + other[...]
    value = dot3(split(drive), pair(inverse), NT)
    sol[...] = value
    rows = value.shape[0]
    message[:rows] = value
    message[rows:] = dot3(split(value), split(own_map[...]), NN)


def step_kernel(bit, last, *refs):
    sol, own, other, halves, curve_u, total_u, total_l, sol_n = refs[:8]
    message = refs[8:]
    upper = bit_of("leaf", bit) == 1
    rows = sol.shape[0]
    z_own, p_own, z_other, p_other = own[:rows], own[rows:], other[:rows], other[rows:]
    z_low = jnp.where(upper, z_other, z_own)
    z_up = jnp.where(upper, z_own, z_other)
    p_low = jnp.where(upper, p_other, p_own)
    p_up = jnp.where(upper, p_own, p_other)
    z_low_s = split(z_low)
    middle = p_up + dot3(z_low_s, pair(curve_u), NN)
    middle_s = split(middle)
    z_new = z_up + dot3(z_low_s, pair(total_u), NT)
    p_new = p_low + dot3(middle_s, pair(total_l), NN)
    given = split(jnp.where(upper, z_low, middle))
    sol_n[...] = sol[...] + dot3(given, pair(halves), NN)
    if last:
        message[0][...] = jnp.where(bit_of("leaf", bit + 1) == 1, p_new, z_new)
        message[1][...] = z_new
    else:
        message[0][:rows], message[0][rows:] = z_new, p_new


def leave_kernel(bit, sol, own_z, came, halves, mine, pairs, inverse, top):
    upper = bit_of("leaf", bit) == 1
    value = came[...]
    middle = value + dot3(split(own_z[...]), split(k_of(came_blocks(mine, pairs, 3))), NN)
    given = split(jnp.where(upper, value, middle))
    value = sol[...] + dot3(given, pair(halves), NN)
    top[...] = dot3(split(value), pair(inverse), NN)


def gather_front(x, bits):
    pieces = {0: x}
    for bit in reversed(range(bits)):
        for i in list(pieces):
            pieces[i | (1 << bit)] = exchange(pieces[i], "front", bit)
    return [pieces[i] for i in range(1 << bits)]


def local(rhs_local, dinv_local, update_local, parent, row_blocks, sep_rhs, sep_dinv, sep_coupling):
    fronts, leaves = lax.axis_size("front"), lax.axis_size("leaf")
    front_bits, rounds = fronts.bit_length() - 1, leaves.bit_length() - 1
    size = sep_dinv.shape[1]
    cols = sep_rhs.shape[1]
    chunk = cols // fronts

    (stacked,) = call(
        stack_kernel,
        "stack",
        [(HBM, sep_dinv), (HBM, sep_coupling)],
        [((2, *sep_dinv.shape), F32)],
        [pltpu.SemaphoreType.DMA((2,))],
    )
    came = {0: stacked}
    for bit in reversed(range(1, front_bits)):
        for i in list(came):
            came[i | (1 << bit)] = exchange(came[i], "front", bit)
    came[1] = exchange(stacked, "front", 0)
    acc_a, *first_halves = prepare_first(
        rhs_local, dinv_local, update_local, row_blocks, sep_rhs, stacked
    )
    first_halves, (top, row_columns, *raw) = first_halves[:4], first_halves[4:]
    for i in range(2, fronts, 2):
        held, _ = lax.optimization_barrier((came[i], acc_a))
        came[i + 1] = exchange(held, "front", 0)
    acc_b, *second_halves = prepare_second(row_columns, *raw, acc_a)
    own_map, part, inverse = block_map([came[i] for i in range(fronts)], acc_b)
    mine = exchange(part, "leaf", 0)
    solved, send, keep = local_forward(
        parent, acc_a, acc_b, top, first_halves, second_halves, own_map, fronts
    )
    mine, _ = lax.optimization_barrier((mine, send))
    pairs = exchange(mine, "front", 0)
    for bit in range(front_bits):
        received = exchange(send, "front", bit)
        if bit + 1 < front_bits:
            half = ((keep.shape[0] // 2, size), F32)
            send, keep = call(
                lambda *refs, bit=bit: fold_kernel(bit + 1, *refs),
                "fold",
                [(V, keep), (V, received)],
                [half, half],
            )
    sol, message = call(
        enter_kernel,
        "enter",
        [(V, keep), (V, received), (V, inverse), (V, own_map)],
        [((chunk, size), F32), ((2 * chunk, size), F32)],
    )
    kept, part, mixed, *tools = call(
        first_merge_kernel,
        "merge_0",
        [(V, own_map), (V, mine), (V, pairs), (pl.ANY, message)],
        maps(size, False),
    )
    share = ((chunk, size), F32)
    for bit in range(rounds - 1):
        last = bit == rounds - 2
        received = exchange(message, "leaf", bit)
        mine = exchange(part, "leaf", bit + 1)
        sol, *message = call(
            lambda *refs, bit=bit, last=last: step_kernel(bit, last, *refs),
            f"step_{bit}",
            [(V, a) for a in (sol, message, received, *tools)],
            [share] + ([share, share] if last else [((2 * chunk, size), F32)]),
        )
        if last:
            came = exchange(message[0], "leaf", bit + 1)
            mine, _ = lax.optimization_barrier((mine, came))
            pairs = exchange(mine, "front", 0)
        else:
            mine, _ = lax.optimization_barrier((mine, sol))
            pairs = exchange(mine, "front", 0)
            (message,) = message
            last = bit == rounds - 3
            kept, part, mixed, *tools = call(
                lambda *refs, bit=bit, last=last: merge_kernel(bit + 1, last, *refs),
                f"merge_{bit + 1}",
                [(V, a) for a in (kept, mine, pairs, mixed)],
                maps(size, last),
            )
    (top,) = call(
        lambda *refs: leave_kernel(rounds - 1, *refs),
        "leave",
        [(V, a) for a in (sol, message[1], came, mixed, mine, pairs, inverse)],
        [share],
    )
    pieces = gather_front(top, front_bits)
    sol_local, sep_solution = local_backward(
        parent, solved, first_halves, second_halves, pieces
    )
    return (sol_local, sep_solution)


def solution(mesh):
    spread3 = P(("leaf", "front"), None, None)
    spread2 = P(("leaf", "front"), None)
    spread1 = P(("leaf", "front"))
    return jax.shard_map(
        local,
        mesh=mesh,
        in_specs=(spread3, spread3, spread3, spread1, spread2, spread2, spread2, spread2),
        out_specs=(spread3, spread2),
        check_vma=False,
    )
```

```python
import jax
import jax.numpy as jnp
from jax import lax
from jax.experimental import pallas as pl
from jax.experimental.pallas import tpu as pltpu
from jax.sharding import PartitionSpec as P

F32 = jnp.float32
BF16 = jnp.bfloat16
NN = (((1,), (0,)), ((), ()))
NT = (((1,), (1,)), ((), ()))
TN = (((0,), (0,)), ((), ()))
VMEM_BYTES = 24 << 20
HALVES = 2


def split(x):
    high = x.astype(BF16)
    return high, (x - high.astype(F32)).astype(BF16)


def dot1(a, b, dims):
    return lax.dot_general(a, b, dims, preferred_element_type=F32)


def dot3(a, b, dims):
    axis = 1 - dims[0][0][0]
    rows = a[0].shape[axis]
    both = dot1(jnp.concatenate(a, axis=axis), b[0], dims)
    return both[:rows] + (both[rows:] + dot1(a[0], b[1], dims))


def keep_split(ref, value):
    ref[0], ref[1] = split(value)


def pair(ref):
    return ref[0], ref[1]


def bit_of(axis, bit):
    return (lax.axis_index(axis) // (1 << bit)) % 2


def call(kernel, name, ins, outs, scratch=()):
    specs = [pl.BlockSpec(memory_space=space) for space, _ in ins]
    ins = [
        (space, pltpu.with_memory_space_constraint(a, HBM) if space == HBM else a)
        for space, a in ins
    ]
    return pl.pallas_call(
        kernel,
        name=name,
        in_specs=specs,
        out_specs=tuple(pl.BlockSpec(memory_space=pltpu.VMEM) for _ in outs),
        out_shape=tuple(jax.ShapeDtypeStruct(*o) for o in outs),
        scratch_shapes=list(scratch),
        compiler_params=pltpu.CompilerParams(vmem_limit_bytes=VMEM_BYTES),
    )(*[a for _, a in ins])


V = pltpu.VMEM
HBM = pltpu.HBM


def swap(x, axis, mask):
    n = lax.axis_size(axis)
    return lax.ppermute(x, axis, [(i, i ^ mask) for i in range(n)])


def exchange(x, axis, bit):
    return swap(x, axis, 1 << bit)


def prepare_nodes(count, rows_at, row_columns, dinv, upd, rhs, outs, waits):
    acc, inv_hi, inv_lo, upd_hi, upd_lo = outs
    size = dinv.shape[1]
    width = acc.shape[2]
    lane = lax.broadcasted_iota(jnp.int32, (size, size), 1).astype(F32)
    for k in range(count):
        for c in waits[k]:
            c.wait()
        inv_hi[k], inv_lo[k] = split(dinv[k])
        high, low = split(upd[k])
        chosen = (lane == row_columns[:, rows_at + k : rows_at + k + 1]).astype(BF16)
        upd_hi[k] = dot1(chosen, high, NN).astype(BF16)
        upd_lo[k] = dot1(chosen, low, NN).astype(BF16)
        turned = rhs[k].T
        for h in range(HALVES):
            acc[h, k] = turned[h * width : (h + 1) * width]


def prepare_first_kernel(nodes, *refs):
    (rows_h, sep_h, rhs_h, dinv_h, upd_h, _), refs = refs[:6], refs[6:]
    outs, (top, row_columns, rhs_n, dinv_n, upd_n), refs = refs[:5], refs[5:10], refs[10:]
    rhs_v, dinv_v, upd_v, square, rows, sep, sems, small = refs
    cols = rhs_v.shape[2]
    width = cols // HALVES
    first = nodes // 2
    few = [
        pltpu.make_async_copy(src, dst, small.at[i])
        for i, (src, dst) in enumerate(((rows_h, rows), (sep_h, sep)))
    ]
    for c in few:
        c.start()
    copies = []
    for k in range(nodes):
        ins = (upd_v, dinv_v, rhs_v) if k < first else (upd_n, dinv_n, rhs_n)
        group = [
            pltpu.make_async_copy(src.at[k], dst.at[k % first], sems.at[i, k])
            for i, (src, dst) in enumerate(zip((upd_h, dinv_h, rhs_h), ins))
        ]
        for c in group:
            c.start()
        copies.append(group)
    front = lax.axis_index("front")
    square[...] = jnp.zeros_like(square)
    for c in few:
        c.wait()
    share = sep.shape[0]
    square[pl.ds(pl.multiple_of(front * share, 8), share), :] = sep[...]
    turned = square[...].T
    for h in range(HALVES):
        top[h] = turned[h * width : (h + 1) * width]
    row_columns[...] = rows[...].astype(F32).T
    prepare_nodes(first, 0, row_columns, dinv_v, upd_v, rhs_v, outs, copies[:first])
    for group in copies[first:]:
        for c in group:
            c.wait()


def prepare_second_kernel(first, row_columns, rhs, dinv, upd, _, *outs):
    count = rhs.shape[0]
    waits = [()] * count
    prepare_nodes(count, first, row_columns, dinv, upd, rhs, outs, waits)


def prepared(count, size, cols):
    half = ((count, size, size), BF16)
    return [((HALVES, count, cols // HALVES, size), F32), half, half, half, half]


def prepare_first(rhs, dinv, update, rows, sep, after):
    nodes, size, cols = rhs.shape
    first = nodes // 2
    some = (first, size, cols)
    big = pltpu.VMEM(some, F32)
    return call(
        lambda *refs: prepare_first_kernel(nodes, *refs),
        "prepare_first",
        [(HBM, a) for a in (rows, sep, rhs, dinv, update)] + [(pl.ANY, after)],
        prepared(first, size, cols)
        + [((HALVES, cols // HALVES, size), F32), ((size, nodes), F32)]
        + [((nodes - first, *some[1:]), F32)] * 3,
        [big, big, big, pltpu.VMEM((size, cols), F32)]
        + [pltpu.VMEM(rows.shape, jnp.int32), pltpu.VMEM(sep.shape, F32)]
        + [pltpu.SemaphoreType.DMA((3, nodes)), pltpu.SemaphoreType.DMA((2,))],
    )


def prepare_second(row_columns, rhs, dinv, update, after):
    count, size, cols = rhs.shape
    first = row_columns.shape[1] - count
    return call(
        lambda *refs: prepare_second_kernel(first, *refs),
        "prepare_second",
        [(V, a) for a in (row_columns, rhs, dinv, update)] + [(pl.ANY, after)],
        prepared(count, size, cols),
    )


def forward_kernel(nodes, fronts, *refs):
    (parent_h, acc_a, acc_b, top), parts, refs = refs[:4], (refs[4:8], refs[8:12]), refs[13:]
    solved, send, keep, square, parent, sem = refs[:6]
    accs = refs[6:]
    copy = pltpu.make_async_copy(parent_h, parent, sem)
    copy.start()
    first, width = acc_a.shape[1:3]
    for h in range(HALVES):
        for k in range(nodes):
            accs[h][k] = acc_a[h, k] if k < first else acc_b[h, k - first]
        accs[h][nodes] = top[h]
    for k in range(nodes):
        inv_hi, inv_lo, upd_hi, upd_lo = parts[k // first]
        i = k % first
        inverse = (inv_hi[i], inv_lo[i])
        update = (upd_hi[i], upd_lo[i])
        for h in range(HALVES):
            value = dot3(split(accs[h][k]), inverse, NT)
            solved[k, h * width : (h + 1) * width] = value
            moved = dot3(split(value), update, NT)
            if k + h == 0:
                copy.wait()
            above = nodes if k == nodes - 1 else parent[k]
            accs[h][above] = accs[h][above] - moved
    front = lax.axis_index("front")
    chunk = width * HALVES // fronts
    for h in range(HALVES):
        square[h * width : (h + 1) * width] = accs[h][nodes]
    low_bit = front % 2
    for i in range(fronts // 2):
        for ref, own in ((keep, low_bit), (send, 1 - low_bit)):
            start = pl.multiple_of((2 * i + own) * chunk, 8)
            ref[i * chunk : (i + 1) * chunk] = square[pl.ds(start, chunk), :]


def local_forward(parent, acc_a, acc_b, top, first_halves, second_halves, after, fronts):
    first, (width, size) = acc_a.shape[1], acc_a.shape[2:]
    nodes = first + acc_b.shape[1]
    cols = width * HALVES
    part = ((cols // 2, size), F32)
    return call(
        lambda *refs: forward_kernel(nodes, fronts, *refs),
        "local_forward",
        [(HBM, parent)]
        + [(V, a) for a in (acc_a, acc_b, top, *first_halves, *second_halves)]
        + [(pl.ANY, after)],
        [((nodes, cols, size), F32), part, part],
        [pltpu.VMEM((cols, size), F32), pltpu.SMEM((nodes,), jnp.int32), pltpu.SemaphoreType.DMA]
        + [pltpu.VMEM((nodes + 1, width, size), F32)] * HALVES,
    )


def backward_kernel(nodes, fronts, *refs):
    (parent_h, solved), parts, refs = refs[:2], (refs[2:6], refs[6:10]), refs[10:]
    pieces = refs[:fronts]
    sol, sep_out = refs[fronts : 2 + fronts]
    square, parent, staged, sem, sems = refs[2 + fronts : 7 + fronts]
    known = refs[7 + fronts :]
    first = parts[0][0].shape[0]
    copy = pltpu.make_async_copy(parent_h, parent, sem)
    copy.start()
    chunk = pieces[0].shape[0]
    width = known[0].shape[1]
    order = [p[...] for p in pieces]
    for bit in range(fronts.bit_length() - 1):
        flip = bit_of("front", bit) == 1
        order = [jnp.where(flip, order[i ^ (1 << bit)], order[i]) for i in range(fronts)]
    for i, value in enumerate(order):
        at = i * chunk
        known[at // width][nodes, at % width : at % width + chunk] = value
    outs = []
    for k in reversed(range(nodes)):
        i = k % first
        inv_hi, inv_lo, upd_hi, upd_lo = parts[k // first]
        inverse = (inv_hi[i], inv_lo[i])
        update = (upd_hi[i], upd_lo[i])
        if k == nodes - 2:
            copy.wait()
        above = nodes if k == nodes - 1 else parent[k]
        for h in range(HALVES):
            rows = slice(h * width, (h + 1) * width)
            part = solved[k, rows] - dot3(split(known[h][above]), update, NN)
            value = dot3(split(part), inverse, NN)
            known[h][k] = value
            staged[k, :, rows] = value.T
        out = pltpu.make_async_copy(staged.at[k], sol.at[k], sems.at[k])
        out.start()
        outs.append(out)
    for h in range(HALVES):
        square[:, h * width : (h + 1) * width] = known[h][nodes].T
    share = sep_out.shape[0]
    start = pl.multiple_of(lax.axis_index("front") * share, 8)
    sep_out[...] = square[pl.ds(start, share), :]
    for out in outs:
        out.wait()


def local_backward(parent, solved, first_halves, second_halves, pieces):
    nodes, cols, size = solved.shape
    fronts = len(pieces)
    sol, sep = jax.ShapeDtypeStruct((nodes, size, cols), F32), ((size // fronts, cols), F32)
    ins = (solved, *first_halves, *second_halves, *pieces)
    return pl.pallas_call(
        lambda *refs: backward_kernel(nodes, fronts, *refs),
        name="local_backward",
        in_specs=[pl.BlockSpec(memory_space=HBM)] + [pl.BlockSpec(memory_space=V)] * len(ins),
        out_specs=(pl.BlockSpec(memory_space=HBM), pl.BlockSpec(memory_space=V)),
        out_shape=(sol, jax.ShapeDtypeStruct(*sep)),
        scratch_shapes=[pltpu.VMEM((size, cols), F32), pltpu.SMEM((nodes,), jnp.int32)]
        + [pltpu.VMEM((nodes, size, cols), F32), pltpu.SemaphoreType.DMA]
        + [pltpu.SemaphoreType.DMA((nodes,))]
        + [pltpu.VMEM((nodes + 1, cols // HALVES, size), F32)] * HALVES,
        compiler_params=pltpu.CompilerParams(vmem_limit_bytes=VMEM_BYTES),
    )(pltpu.with_memory_space_constraint(parent, HBM), *ins)


def stack_kernel(first, second, out, sems):
    copies = [pltpu.make_async_copy(a, out.at[i], sems.at[i]) for i, a in enumerate((first, second))]
    for c in copies:
        c.start()
    for c in copies:
        c.wait()


def block_map_kernel(fronts, *refs):
    parts = refs[:fronts]
    _, total, part, inverse_halves, square = refs[fronts:]
    front = lax.axis_index("front")
    share = parts[0].shape[1]
    for i in range(fronts):
        start = pl.multiple_of((front ^ i) * share, 8)
        square[:, pl.ds(start, share), :] = parts[i][...]
    inverse = split(square[0])
    inverse_halves[0], inverse_halves[1] = inverse
    value = -dot3(inverse, split(square[1]), NN)
    total[...] = value
    half = part.shape[0]
    send_blocks([part], [value[:half], value[half:]])


def block_map(parts, after):
    fronts = len(parts)
    size = parts[0].shape[2]
    return call(
        lambda *refs: block_map_kernel(fronts, *refs),
        "block_map",
        [(V, a) for a in parts] + [(pl.ANY, after)],
        [((size, size), F32), ((size // 2, size), F32), ((2, size, size), BF16)],
        [pltpu.VMEM((2, size, size), F32)],
    )


def quarters(x):
    half = x.shape[0] // 2
    return [x[i : i + half, j : j + half] for i in (0, half) for j in (0, half)]


def joined(a, b, c, d):
    first, second = jnp.concatenate([a, b], axis=1), jnp.concatenate([c, d], axis=1)
    return jnp.concatenate([first, second], axis=0)


def low_core():
    return bit_of("front", 0) == 0


def send_blocks(parts, blocks):
    count = len(parts)
    low = low_core()
    for i, part in enumerate(parts):
        part[...] = jnp.where(low, blocks[i], blocks[len(blocks) - count + i])


def came_blocks(mine, pairs, total):
    low = low_core()
    count = len(mine)
    mine, pairs = [m[...] for m in mine], [p[...] for p in pairs]
    blocks = [jnp.where(low, mine[i], pairs[i]) for i in range(count)]
    for i in range(count, total):
        j = i - total + count
        blocks.append(jnp.where(low, pairs[j], mine[j]))
    return blocks


def k_blocks(k):
    a, b, _, d = quarters(k)
    return [a, b, d]


def k_of(blocks):
    return joined(blocks[0], blocks[1], blocks[1].T, blocks[2])


def first_merge_kernel(*refs):
    own, mine, pairs, _, kept, mixed, halves, curve_u, total_u, total_l, *parts = refs
    upper = bit_of("leaf", 0) == 1
    came = jnp.concatenate(came_blocks([mine], [pairs], 2), axis=0)
    mine = own[...]
    low = jnp.where(upper, came, mine)
    up = jnp.where(upper, mine, came)
    low_s, up_s = split(low), split(up)
    for ref, value in ((total_u, up_s), (total_l, low_s)):
        ref[0], ref[1] = value
    k_up = dot3(up_s, up_s, TN)
    k_up_s = split(k_up)
    curve_u[0], curve_u[1] = k_up_s
    x = dot3(k_up_s, low_s, NN)
    t = dot3(up_s, low_s, NN)
    k = dot3(low_s, low_s, TN) + dot3(low_s, split(x), TN)
    kept[0], kept[1] = k, t
    send_blocks(parts, k_blocks(k) + quarters(t))
    size = low.shape[0]
    row = lax.broadcasted_iota(jnp.int32, (size, size), 0)
    col = lax.broadcasted_iota(jnp.int32, (size, size), 1)
    unit = (row == col).astype(F32)
    keep_split(halves, jnp.where(upper, up.T, unit))
    mixed[0] = jnp.where(upper, t, low + x)
    mixed[1] = jnp.where(upper, unit, up)


def merge_kernel(bit, last, *refs):
    own, mine, pairs, mixed = refs[0], refs[1:5], refs[5:9], refs[9]
    upper = bit_of("leaf", bit) == 1
    kept, mixed_n, halves, curve_u, total_u, total_l, *parts = refs[10:]
    own_k, own_t = own[0], own[1]
    blocks = came_blocks(mine, pairs, 7)
    other_k, other_t = k_of(blocks), joined(*blocks[3:])
    low_s = split(jnp.where(upper, other_t, own_t))
    up_s = split(jnp.where(upper, own_t, other_t))
    k_low = jnp.where(upper, other_k, own_k)
    k_up_s = split(jnp.where(upper, own_k, other_k))
    for ref, value in ((total_u, up_s), (total_l, low_s), (curve_u, k_up_s)):
        ref[0], ref[1] = value
    x = dot3(k_up_s, low_s, NN)
    x_s = split(x)
    k = k_low + dot3(low_s, x_s, TN)
    a, e = mixed[0], mixed[1]
    keep_split(halves, jnp.where(upper, a.T, e))
    a_s, e_s = split(a), split(e)
    a_n = jnp.where(upper, dot3(a_s, low_s, NN), a + dot3(e_s, x_s, TN))
    e_n = jnp.where(upper, e, dot3(up_s, e_s, NN))
    if last:
        keep_split(kept, k)
        keep_split(mixed_n, jnp.where(bit_of("leaf", bit + 1) == 1, a_n.T, e_n))
    else:
        t = dot3(up_s, low_s, NN)
        kept[0], kept[1] = k, t
        send_blocks(parts, k_blocks(k) + quarters(t))
        mixed_n[0], mixed_n[1] = a_n, e_n


def maps(size, last):
    both, whole = ((2, size, size), BF16), ((2, size, size), F32)
    if last:
        return [both] * 6
    return [whole, whole, both, both, both, both] + [((size // 2, size // 2), F32)] * 4


def fold_kernel(bit, own, other, send, keep):
    total = send.shape[0]
    chunk = total
    value = own[...] + other[...]
    first, second = value[:chunk], value[chunk:]
    high = bit_of("front", bit) == 1
    send[...] = jnp.where(high, first, second)
    keep[...] = jnp.where(high, second, first)


def enter_kernel(own, other, inverse, own_map, sol, message):
    drive = own[...] + other[...]
    value = dot3(split(drive), pair(inverse), NT)
    sol[...] = value
    rows = value.shape[0]
    message[:rows] = value
    message[rows:] = dot3(split(value), split(own_map[...]), NN)


def step_kernel(bit, last, *refs):
    sol, own, other, halves, curve_u, total_u, total_l, sol_n = refs[:8]
    message = refs[8:]
    upper = bit_of("leaf", bit) == 1
    rows = sol.shape[0]
    z_own, p_own, z_other, p_other = own[:rows], own[rows:], other[:rows], other[rows:]
    z_low = jnp.where(upper, z_other, z_own)
    z_up = jnp.where(upper, z_own, z_other)
    p_low = jnp.where(upper, p_other, p_own)
    p_up = jnp.where(upper, p_own, p_other)
    z_low_s = split(z_low)
    middle = p_up + dot3(z_low_s, pair(curve_u), NN)
    middle_s = split(middle)
    z_new = z_up + dot3(z_low_s, pair(total_u), NT)
    p_new = p_low + dot3(middle_s, pair(total_l), NN)
    given = split(jnp.where(upper, z_low, middle))
    sol_n[...] = sol[...] + dot3(given, pair(halves), NN)
    if last:
        message[0][...], message[1][...] = z_new, p_new
    else:
        message[0][:rows], message[0][rows:] = z_new, p_new


def turn_kernel(message, came, curve, back):
    back[...] = message[...] + dot3(split(came[...]), pair(curve), NN)


def leave_kernel(bit, sol, came, back, halves, inverse, top):
    upper = bit_of("leaf", bit) == 1
    given = split(jnp.where(upper, came[...], back[...]))
    value = sol[...] + dot3(given, pair(halves), NN)
    top[...] = dot3(split(value), pair(inverse), NN)


def gather_front(x, bits):
    pieces = {0: x}
    for bit in reversed(range(bits)):
        for i in list(pieces):
            pieces[i | (1 << bit)] = exchange(pieces[i], "front", bit)
    return [pieces[i] for i in range(1 << bits)]


def local(rhs_local, dinv_local, update_local, parent, row_blocks, sep_rhs, sep_dinv, sep_coupling):
    fronts, leaves = lax.axis_size("front"), lax.axis_size("leaf")
    front_bits, rounds = fronts.bit_length() - 1, leaves.bit_length() - 1
    size = sep_dinv.shape[1]
    cols = sep_rhs.shape[1]
    chunk = cols // fronts

    (stacked,) = call(
        stack_kernel,
        "stack",
        [(HBM, sep_dinv), (HBM, sep_coupling)],
        [((2, *sep_dinv.shape), F32)],
        [pltpu.SemaphoreType.DMA((2,))],
    )
    came = {0: stacked}
    for bit in reversed(range(1, front_bits)):
        for i in list(came):
            came[i | (1 << bit)] = exchange(came[i], "front", bit)
    came[1] = exchange(stacked, "front", 0)
    acc_a, *first_halves = prepare_first(
        rhs_local, dinv_local, update_local, row_blocks, sep_rhs, stacked
    )
    first_halves, (top, row_columns, *raw) = first_halves[:4], first_halves[4:]
    for i in range(2, fronts, 2):
        held, _ = lax.optimization_barrier((came[i], acc_a))
        came[i + 1] = exchange(held, "front", 0)
    acc_b, *second_halves = prepare_second(row_columns, *raw, acc_a)
    own_map, part, inverse = block_map([came[i] for i in range(fronts)], acc_b)
    mine = exchange(part, "leaf", 0)
    solved, send, keep = local_forward(
        parent, acc_a, acc_b, top, first_halves, second_halves, own_map, fronts
    )
    mine, send = lax.optimization_barrier((mine, send))
    pairs = exchange(mine, "front", 0)
    for bit in range(front_bits):
        received = exchange(send, "front", bit)
        if bit + 1 < front_bits:
            half = ((keep.shape[0] // 2, size), F32)
            send, keep = call(
                lambda *refs, bit=bit: fold_kernel(bit + 1, *refs),
                "fold",
                [(V, keep), (V, received)],
                [half, half],
            )
    kept, mixed, *tools = call(
        first_merge_kernel,
        "merge_0",
        [(V, own_map), (V, mine), (V, pairs), (pl.ANY, send)],
        maps(size, False),
    )
    tools, parts = tools[:4], tools[4:]
    sol, message = call(
        enter_kernel,
        "enter",
        [(V, keep), (V, received), (V, inverse), (V, own_map)],
        [((chunk, size), F32), ((2 * chunk, size), F32)],
    )
    share = ((chunk, size), F32)
    for bit in range(rounds - 1):
        last = bit == rounds - 2
        received = exchange(message, "leaf", bit)
        if not last:
            mine = [exchange(part, "leaf", bit + 1) for part in parts]
        sol, *message = call(
            lambda *refs, bit=bit, last=last: step_kernel(bit, last, *refs),
            f"step_{bit}",
            [(V, a) for a in (sol, message, received, *tools)],
            [share] + ([share, share] if last else [((2 * chunk, size), F32)]),
        )
        if not last:
            (message,) = message
            mine, _ = lax.optimization_barrier((mine, sol))
            pairs = [exchange(m, "front", 0) for m in mine]
            last = bit == rounds - 3
            kept, mixed, *tools = call(
                lambda *refs, bit=bit, last=last: merge_kernel(bit + 1, last, *refs),
                f"merge_{bit + 1}",
                [(V, a) for a in (kept, *mine, *pairs, mixed)],
                maps(size, last),
            )
            tools, parts = tools[:4], tools[4:]
    came = exchange(message[0], "leaf", rounds - 1)
    (back,) = call(turn_kernel, "turn", [(V, a) for a in (message[1], came, kept)], [share])
    back = exchange(back, "leaf", rounds - 1)
    (top,) = call(
        lambda *refs: leave_kernel(rounds - 1, *refs),
        "leave",
        [(V, a) for a in (sol, came, back, mixed, inverse)],
        [share],
    )
    pieces = gather_front(top, front_bits)
    sol_local, sep_solution = local_backward(
        parent, solved, first_halves, second_halves, pieces
    )
    return (sol_local, sep_solution)


def solution(mesh):
    spread3 = P(("leaf", "front"), None, None)
    spread2 = P(("leaf", "front"), None)
    spread1 = P(("leaf", "front"))
    return jax.shard_map(
        local,
        mesh=mesh,
        in_specs=(spread3, spread3, spread3, spread1, spread2, spread2, spread2, spread2),
        out_specs=(spread3, spread2),
        check_vma=False,
    )
```

```python
import jax
import jax.numpy as jnp
from jax import lax
from jax.experimental import pallas as pl
from jax.experimental.pallas import tpu as pltpu
from jax.sharding import PartitionSpec as P

F32 = jnp.float32
BF16 = jnp.bfloat16
NN = (((1,), (0,)), ((), ()))
NT = (((1,), (1,)), ((), ()))
TN = (((0,), (0,)), ((), ()))
VMEM_BYTES = 24 << 20
HALVES = 2
SENDS = 2


def split(x):
    high = x.astype(BF16)
    return high, (x - high.astype(F32)).astype(BF16)


def dot1(a, b, dims):
    return lax.dot_general(a, b, dims, preferred_element_type=F32)


def dot3(a, b, dims):
    axis = 1 - dims[0][0][0]
    rows = a[0].shape[axis]
    both = dot1(jnp.concatenate(a, axis=axis), b[0], dims)
    return both[:rows] + (both[rows:] + dot1(a[0], b[1], dims))


def keep_split(ref, value):
    ref[0], ref[1] = split(value)


def pair(ref):
    return ref[0], ref[1]


def bit_of(axis, bit):
    return (lax.axis_index(axis) // (1 << bit)) % 2


def call(kernel, name, ins, outs, scratch=()):
    specs = [pl.BlockSpec(memory_space=space) for space, _ in ins]
    ins = [
        (space, pltpu.with_memory_space_constraint(a, HBM) if space == HBM else a)
        for space, a in ins
    ]
    return pl.pallas_call(
        kernel,
        name=name,
        in_specs=specs,
        out_specs=tuple(pl.BlockSpec(memory_space=pltpu.VMEM) for _ in outs),
        out_shape=tuple(jax.ShapeDtypeStruct(*o) for o in outs),
        scratch_shapes=list(scratch),
        compiler_params=pltpu.CompilerParams(vmem_limit_bytes=VMEM_BYTES),
    )(*[a for _, a in ins])


V = pltpu.VMEM
HBM = pltpu.HBM


def swap(x, axis, mask):
    n = lax.axis_size(axis)
    return lax.ppermute(x, axis, [(i, i ^ mask) for i in range(n)])


def exchange(x, axis, bit):
    return swap(x, axis, 1 << bit)


def prepare_nodes(count, rows_at, row_columns, dinv, upd, rhs, outs, waits):
    acc, inv_hi, inv_lo, upd_hi, upd_lo = outs
    size = dinv.shape[1]
    width = acc.shape[2]
    lane = lax.broadcasted_iota(jnp.int32, (size, size), 1).astype(F32)
    for k in range(count):
        for c in waits[k]:
            c.wait()
        inv_hi[k], inv_lo[k] = split(dinv[k])
        high, low = split(upd[k])
        chosen = (lane == row_columns[:, rows_at + k : rows_at + k + 1]).astype(BF16)
        upd_hi[k] = dot1(chosen, high, NN).astype(BF16)
        upd_lo[k] = dot1(chosen, low, NN).astype(BF16)
        turned = rhs[k].T
        for h in range(HALVES):
            acc[h, k] = turned[h * width : (h + 1) * width]


def prepare_first_kernel(nodes, *refs):
    (rows_h, sep_h, rhs_h, dinv_h, upd_h, _), refs = refs[:6], refs[6:]
    outs, (top, row_columns, rhs_n, dinv_n, upd_n), refs = refs[:5], refs[5:10], refs[10:]
    rhs_v, dinv_v, upd_v, square, rows, sep, sems, small = refs
    cols = rhs_v.shape[2]
    width = cols // HALVES
    first = nodes // 2
    few = [
        pltpu.make_async_copy(src, dst, small.at[i])
        for i, (src, dst) in enumerate(((rows_h, rows), (sep_h, sep)))
    ]
    for c in few:
        c.start()
    copies = []
    for k in range(nodes):
        ins = (upd_v, dinv_v, rhs_v) if k < first else (upd_n, dinv_n, rhs_n)
        group = [
            pltpu.make_async_copy(src.at[k], dst.at[k % first], sems.at[i, k])
            for i, (src, dst) in enumerate(zip((upd_h, dinv_h, rhs_h), ins))
        ]
        for c in group:
            c.start()
        copies.append(group)
    front = lax.axis_index("front")
    square[...] = jnp.zeros_like(square)
    for c in few:
        c.wait()
    share = sep.shape[0]
    square[pl.ds(pl.multiple_of(front * share, 8), share), :] = sep[...]
    turned = square[...].T
    for h in range(HALVES):
        top[h] = turned[h * width : (h + 1) * width]
    row_columns[...] = rows[...].astype(F32).T
    prepare_nodes(first, 0, row_columns, dinv_v, upd_v, rhs_v, outs, copies[:first])
    for group in copies[first:]:
        for c in group:
            c.wait()


def prepare_second_kernel(first, row_columns, rhs, dinv, upd, _, *outs):
    count = rhs.shape[0]
    waits = [()] * count
    prepare_nodes(count, first, row_columns, dinv, upd, rhs, outs, waits)


def prepared(count, size, cols):
    half = ((count, size, size), BF16)
    return [((HALVES, count, cols // HALVES, size), F32), half, half, half, half]


def prepare_first(rhs, dinv, update, rows, sep, after):
    nodes, size, cols = rhs.shape
    first = nodes // 2
    some = (first, size, cols)
    big = pltpu.VMEM(some, F32)
    return call(
        lambda *refs: prepare_first_kernel(nodes, *refs),
        "prepare_first",
        [(HBM, a) for a in (rows, sep, rhs, dinv, update)] + [(pl.ANY, after)],
        prepared(first, size, cols)
        + [((HALVES, cols // HALVES, size), F32), ((size, nodes), F32)]
        + [((nodes - first, *some[1:]), F32)] * 3,
        [big, big, big, pltpu.VMEM((size, cols), F32)]
        + [pltpu.VMEM(rows.shape, jnp.int32), pltpu.VMEM(sep.shape, F32)]
        + [pltpu.SemaphoreType.DMA((3, nodes)), pltpu.SemaphoreType.DMA((2,))],
    )


def prepare_second(row_columns, rhs, dinv, update, after):
    count, size, cols = rhs.shape
    first = row_columns.shape[1] - count
    return call(
        lambda *refs: prepare_second_kernel(first, *refs),
        "prepare_second",
        [(V, a) for a in (row_columns, rhs, dinv, update)] + [(pl.ANY, after)],
        prepared(count, size, cols),
    )


def forward_kernel(nodes, fronts, *refs):
    (parent_h, acc_a, acc_b, top), parts, refs = refs[:4], (refs[4:8], refs[8:12]), refs[13:]
    solved, send, keep, square, parent, sem = refs[:6]
    accs = refs[6:]
    copy = pltpu.make_async_copy(parent_h, parent, sem)
    copy.start()
    first, width = acc_a.shape[1:3]
    for h in range(HALVES):
        for k in range(nodes):
            accs[h][k] = acc_a[h, k] if k < first else acc_b[h, k - first]
        accs[h][nodes] = top[h]
    for k in range(nodes):
        inv_hi, inv_lo, upd_hi, upd_lo = parts[k // first]
        i = k % first
        inverse = (inv_hi[i], inv_lo[i])
        update = (upd_hi[i], upd_lo[i])
        for h in range(HALVES):
            value = dot3(split(accs[h][k]), inverse, NT)
            solved[k, h * width : (h + 1) * width] = value
            moved = dot3(split(value), update, NT)
            if k + h == 0:
                copy.wait()
            above = nodes if k == nodes - 1 else parent[k]
            accs[h][above] = accs[h][above] - moved
    front = lax.axis_index("front")
    chunk = width * HALVES // fronts
    for h in range(HALVES):
        square[h * width : (h + 1) * width] = accs[h][nodes]
    low_bit = front % 2
    for i in range(fronts // 2):
        for ref, own in ((keep, low_bit), (send, 1 - low_bit)):
            start = pl.multiple_of((2 * i + own) * chunk, 8)
            ref[i * chunk : (i + 1) * chunk] = square[pl.ds(start, chunk), :]


def local_forward(parent, acc_a, acc_b, top, first_halves, second_halves, after, fronts):
    first, (width, size) = acc_a.shape[1], acc_a.shape[2:]
    nodes = first + acc_b.shape[1]
    cols = width * HALVES
    part = ((cols // 2, size), F32)
    return call(
        lambda *refs: forward_kernel(nodes, fronts, *refs),
        "local_forward",
        [(HBM, parent)]
        + [(V, a) for a in (acc_a, acc_b, top, *first_halves, *second_halves)]
        + [(pl.ANY, after)],
        [((nodes, cols, size), F32), part, part],
        [pltpu.VMEM((cols, size), F32), pltpu.SMEM((nodes,), jnp.int32), pltpu.SemaphoreType.DMA]
        + [pltpu.VMEM((nodes + 1, width, size), F32)] * HALVES,
    )


def backward_kernel(nodes, fronts, *refs):
    (parent_h, solved), parts, refs = refs[:2], (refs[2:6], refs[6:10]), refs[10:]
    pieces = refs[:fronts]
    sol, sep_out = refs[fronts : 2 + fronts]
    square, parent, staged, sem, sems = refs[2 + fronts : 7 + fronts]
    known = refs[7 + fronts :]
    first = parts[0][0].shape[0]
    copy = pltpu.make_async_copy(parent_h, parent, sem)
    copy.start()
    chunk = pieces[0].shape[0]
    width = known[0].shape[1]
    order = [p[...] for p in pieces]
    for bit in range(fronts.bit_length() - 1):
        flip = bit_of("front", bit) == 1
        order = [jnp.where(flip, order[i ^ (1 << bit)], order[i]) for i in range(fronts)]
    for i, value in enumerate(order):
        at = i * chunk
        known[at // width][nodes, at % width : at % width + chunk] = value
    outs = []
    for k in reversed(range(nodes)):
        i = k % first
        inv_hi, inv_lo, upd_hi, upd_lo = parts[k // first]
        inverse = (inv_hi[i], inv_lo[i])
        update = (upd_hi[i], upd_lo[i])
        if k == nodes - 2:
            copy.wait()
        above = nodes if k == nodes - 1 else parent[k]
        for h in range(HALVES):
            rows = slice(h * width, (h + 1) * width)
            part = solved[k, rows] - dot3(split(known[h][above]), update, NN)
            value = dot3(split(part), inverse, NN)
            known[h][k] = value
            staged[k, :, rows] = value.T
        out = pltpu.make_async_copy(staged.at[k], sol.at[k], sems.at[k])
        out.start()
        outs.append(out)
    for h in range(HALVES):
        square[:, h * width : (h + 1) * width] = known[h][nodes].T
    share = sep_out.shape[0]
    start = pl.multiple_of(lax.axis_index("front") * share, 8)
    sep_out[...] = square[pl.ds(start, share), :]
    for out in outs:
        out.wait()


def local_backward(parent, solved, first_halves, second_halves, pieces):
    nodes, cols, size = solved.shape
    fronts = len(pieces)
    sol, sep = jax.ShapeDtypeStruct((nodes, size, cols), F32), ((size // fronts, cols), F32)
    ins = (solved, *first_halves, *second_halves, *pieces)
    return pl.pallas_call(
        lambda *refs: backward_kernel(nodes, fronts, *refs),
        name="local_backward",
        in_specs=[pl.BlockSpec(memory_space=HBM)] + [pl.BlockSpec(memory_space=V)] * len(ins),
        out_specs=(pl.BlockSpec(memory_space=HBM), pl.BlockSpec(memory_space=V)),
        out_shape=(sol, jax.ShapeDtypeStruct(*sep)),
        scratch_shapes=[pltpu.VMEM((size, cols), F32), pltpu.SMEM((nodes,), jnp.int32)]
        + [pltpu.VMEM((nodes, size, cols), F32), pltpu.SemaphoreType.DMA]
        + [pltpu.SemaphoreType.DMA((nodes,))]
        + [pltpu.VMEM((nodes + 1, cols // HALVES, size), F32)] * HALVES,
        compiler_params=pltpu.CompilerParams(vmem_limit_bytes=VMEM_BYTES),
    )(pltpu.with_memory_space_constraint(parent, HBM), *ins)


def stack_kernel(first, second, out, sems):
    copies = [pltpu.make_async_copy(a, out.at[i], sems.at[i]) for i, a in enumerate((first, second))]
    for c in copies:
        c.start()
    for c in copies:
        c.wait()


def block_map_kernel(fronts, *refs):
    parts = refs[:fronts]
    _, total, part, inverse_halves, square = refs[fronts:]
    front = lax.axis_index("front")
    share = parts[0].shape[1]
    for i in range(fronts):
        start = pl.multiple_of((front ^ i) * share, 8)
        square[:, pl.ds(start, share), :] = parts[i][...]
    inverse = split(square[0])
    inverse_halves[0], inverse_halves[1] = inverse
    value = -dot3(inverse, split(square[1]), NN)
    total[...] = value
    half = part.shape[1]
    send_blocks([part], [value[:half], value[half:]])


def block_map(parts, after):
    fronts = len(parts)
    size = parts[0].shape[2]
    return call(
        lambda *refs: block_map_kernel(fronts, *refs),
        "block_map",
        [(V, a) for a in parts] + [(pl.ANY, after)],
        [((size, size), F32), ((1, size // 2, size), F32), ((2, size, size), BF16)],
        [pltpu.VMEM((2, size, size), F32)],
    )


def quarters(x):
    half = x.shape[0] // 2
    return [x[i : i + half, j : j + half] for i in (0, half) for j in (0, half)]


def joined(a, b, c, d):
    first, second = jnp.concatenate([a, b], axis=1), jnp.concatenate([c, d], axis=1)
    return jnp.concatenate([first, second], axis=0)


def low_core():
    return bit_of("front", 0) == 0


def send_blocks(parts, blocks):
    count = sum(part.shape[0] for part in parts)
    low = low_core()
    i = 0
    for part in parts:
        for j in range(part.shape[0]):
            part[j] = jnp.where(low, blocks[i], blocks[len(blocks) - count + i])
            i += 1


def came_blocks(mine, pairs, total):
    low = low_core()
    mine = [m[j] for m in mine for j in range(m.shape[0])]
    pairs = [p[j] for p in pairs for j in range(p.shape[0])]
    count = len(mine)
    blocks = [jnp.where(low, mine[i], pairs[i]) for i in range(count)]
    for i in range(count, total):
        j = i - total + count
        blocks.append(jnp.where(low, pairs[j], mine[j]))
    return blocks


def k_blocks(k):
    a, b, _, d = quarters(k)
    return [a, b, d]


def k_of(blocks):
    return joined(blocks[0], blocks[1], blocks[1].T, blocks[2])


def first_merge_kernel(*refs):
    own, mine, pairs, _, kept, mixed, halves, curve_u, total_u, total_l, *parts = refs
    upper = bit_of("leaf", 0) == 1
    came = jnp.concatenate(came_blocks([mine], [pairs], 2), axis=0)
    mine = own[...]
    low = jnp.where(upper, came, mine)
    up = jnp.where(upper, mine, came)
    low_s, up_s = split(low), split(up)
    for ref, value in ((total_u, up_s), (total_l, low_s)):
        ref[0], ref[1] = value
    k_up = dot3(up_s, up_s, TN)
    k_up_s = split(k_up)
    curve_u[0], curve_u[1] = k_up_s
    x = dot3(k_up_s, low_s, NN)
    t = dot3(up_s, low_s, NN)
    k = dot3(low_s, low_s, TN) + dot3(low_s, split(x), TN)
    kept[0], kept[1] = k, t
    send_blocks(parts, k_blocks(k) + quarters(t))
    size = low.shape[0]
    row = lax.broadcasted_iota(jnp.int32, (size, size), 0)
    col = lax.broadcasted_iota(jnp.int32, (size, size), 1)
    unit = (row == col).astype(F32)
    keep_split(halves, jnp.where(upper, up.T, unit))
    mixed[0] = jnp.where(upper, t, low + x)
    mixed[1] = jnp.where(upper, unit, up)


def merge_kernel(bit, last, *refs):
    own, mine, pairs, mixed = refs[0], refs[1 : 1 + SENDS], refs[1 + SENDS : 1 + 2 * SENDS], refs[1 + 2 * SENDS]
    upper = bit_of("leaf", bit) == 1
    kept, mixed_n, halves, curve_u, total_u, total_l, *parts = refs[2 + 2 * SENDS :]
    own_k, own_t = own[0], own[1]
    blocks = came_blocks(mine, pairs, 7)
    other_k, other_t = k_of(blocks), joined(*blocks[3:])
    low_s = split(jnp.where(upper, other_t, own_t))
    up_s = split(jnp.where(upper, own_t, other_t))
    k_low = jnp.where(upper, other_k, own_k)
    k_up_s = split(jnp.where(upper, own_k, other_k))
    for ref, value in ((total_u, up_s), (total_l, low_s), (curve_u, k_up_s)):
        ref[0], ref[1] = value
    x = dot3(k_up_s, low_s, NN)
    x_s = split(x)
    k = k_low + dot3(low_s, x_s, TN)
    a, e = mixed[0], mixed[1]
    keep_split(halves, jnp.where(upper, a.T, e))
    a_s, e_s = split(a), split(e)
    a_n = jnp.where(upper, dot3(a_s, low_s, NN), a + dot3(e_s, x_s, TN))
    e_n = jnp.where(upper, e, dot3(up_s, e_s, NN))
    if last:
        kept[...] = jnp.zeros_like(kept)
        send_blocks(parts, k_blocks(k))
        keep_split(mixed_n, jnp.where(bit_of("leaf", bit + 1) == 1, a_n.T, e_n))
    else:
        t = dot3(up_s, low_s, NN)
        kept[0], kept[1] = k, t
        send_blocks(parts, k_blocks(k) + quarters(t))
        mixed_n[0], mixed_n[1] = a_n, e_n


def maps(size, last):
    both, whole = ((2, size, size), BF16), ((2, size, size), F32)
    half = size // 2
    if last:
        return [((8, 128), F32)] + [both] * 5 + [((2, half, half), F32)]
    sends = [((4 // SENDS, half, half), F32)] * SENDS
    return [whole, whole, both, both, both, both] + sends


def fold_kernel(bit, own, other, send, keep):
    total = send.shape[0]
    chunk = total
    value = own[...] + other[...]
    first, second = value[:chunk], value[chunk:]
    high = bit_of("front", bit) == 1
    send[...] = jnp.where(high, first, second)
    keep[...] = jnp.where(high, second, first)


def enter_kernel(own, other, inverse, own_map, sol, message):
    drive = own[...] + other[...]
    value = dot3(split(drive), pair(inverse), NT)
    sol[...] = value
    rows = value.shape[0]
    message[:rows] = value
    message[rows:] = dot3(split(value), split(own_map[...]), NN)


def step_kernel(bit, last, held, *refs):
    sol, own, other, halves, curve_u, total_u, total_l = refs[:7]
    sol_n, message = refs[7 + held], refs[8 + held :]
    upper = bit_of("leaf", bit) == 1
    rows = sol.shape[0]
    z_own, p_own, z_other, p_other = own[:rows], own[rows:], other[:rows], other[rows:]
    z_low = jnp.where(upper, z_other, z_own)
    z_up = jnp.where(upper, z_own, z_other)
    p_low = jnp.where(upper, p_other, p_own)
    p_up = jnp.where(upper, p_own, p_other)
    z_low_s = split(z_low)
    middle = p_up + dot3(z_low_s, pair(curve_u), NN)
    middle_s = split(middle)
    z_new = z_up + dot3(z_low_s, pair(total_u), NT)
    p_new = p_low + dot3(middle_s, pair(total_l), NN)
    given = split(jnp.where(upper, z_low, middle))
    sol_n[...] = sol[...] + dot3(given, pair(halves), NN)
    if last:
        message[0][...] = jnp.where(bit_of("leaf", bit + 1) == 1, p_new, z_new)
        message[1][...] = z_new
    else:
        message[0][:rows], message[0][rows:] = z_new, p_new


def leave_kernel(bit, sol, own_z, came, halves, mine, pairs, inverse, top):
    upper = bit_of("leaf", bit) == 1
    value = came[...]
    curve = k_of(came_blocks([mine], [pairs], 3))
    middle = value + dot3(split(own_z[...]), split(curve), NN)
    given = split(jnp.where(upper, value, middle))
    value = sol[...] + dot3(given, pair(halves), NN)
    top[...] = dot3(split(value), pair(inverse), NN)


def gather_front(x, bits):
    pieces = {0: x}
    for bit in reversed(range(bits)):
        for i in list(pieces):
            pieces[i | (1 << bit)] = exchange(pieces[i], "front", bit)
    return [pieces[i] for i in range(1 << bits)]


def local(rhs_local, dinv_local, update_local, parent, row_blocks, sep_rhs, sep_dinv, sep_coupling):
    fronts, leaves = lax.axis_size("front"), lax.axis_size("leaf")
    front_bits, rounds = fronts.bit_length() - 1, leaves.bit_length() - 1
    size = sep_dinv.shape[1]
    cols = sep_rhs.shape[1]
    chunk = cols // fronts

    (stacked,) = call(
        stack_kernel,
        "stack",
        [(HBM, sep_dinv), (HBM, sep_coupling)],
        [((2, *sep_dinv.shape), F32)],
        [pltpu.SemaphoreType.DMA((2,))],
    )
    came = {0: stacked}
    for bit in reversed(range(1, front_bits)):
        for i in list(came):
            came[i | (1 << bit)] = exchange(came[i], "front", bit)
    came[1] = exchange(stacked, "front", 0)
    acc_a, *first_halves = prepare_first(
        rhs_local, dinv_local, update_local, row_blocks, sep_rhs, stacked
    )
    first_halves, (top, row_columns, *raw) = first_halves[:4], first_halves[4:]
    for i in range(2, fronts, 2):
        held, _ = lax.optimization_barrier((came[i], acc_a))
        came[i + 1] = exchange(held, "front", 0)
    acc_b, *second_halves = prepare_second(row_columns, *raw, acc_a)
    own_map, part, inverse = block_map([came[i] for i in range(fronts)], acc_b)
    mine = exchange(part, "leaf", 0)
    solved, send, keep = local_forward(
        parent, acc_a, acc_b, top, first_halves, second_halves, own_map, fronts
    )
    mine, send = lax.optimization_barrier((mine, send))
    pairs = exchange(mine, "front", 0)
    for bit in range(front_bits):
        received = exchange(send, "front", bit)
        if bit + 1 < front_bits:
            half = ((keep.shape[0] // 2, size), F32)
            send, keep = call(
                lambda *refs, bit=bit: fold_kernel(bit + 1, *refs),
                "fold",
                [(V, keep), (V, received)],
                [half, half],
            )
    kept, mixed, *tools = call(
        first_merge_kernel,
        "merge_0",
        [(V, own_map), (V, mine), (V, pairs), (pl.ANY, send)],
        maps(size, False),
    )
    tools, parts = tools[:4], tools[4:]
    sol, message = call(
        enter_kernel,
        "enter",
        [(V, keep), (V, received), (V, inverse), (V, own_map)],
        [((chunk, size), F32), ((2 * chunk, size), F32)],
    )
    share = ((chunk, size), F32)
    for bit in range(rounds - 1):
        last = bit == rounds - 2
        received = exchange(message, "leaf", bit)
        mine = [exchange(part, "leaf", bit + 1) for part in parts]
        held = [] if last else mine
        sol, *message = call(
            lambda *refs, bit=bit, last=last: step_kernel(bit, last, len(held), *refs),
            f"step_{bit}",
            [(V, a) for a in (sol, message, received, *tools)] + [(pl.ANY, a) for a in held],
            [share] + ([share, share] if last else [((2 * chunk, size), F32)]),
        )
        if last:
            came = exchange(message[0], "leaf", bit + 1)
            mine, _ = lax.optimization_barrier((mine, came))
            pairs = [exchange(m, "front", 0) for m in mine]
        else:
            (message,) = message
            mine, _ = lax.optimization_barrier((mine, sol))
            pairs = [exchange(m, "front", 0) for m in mine]
            last = bit == rounds - 3
            kept, mixed, *tools = call(
                lambda *refs, bit=bit, last=last: merge_kernel(bit + 1, last, *refs),
                f"merge_{bit + 1}",
                [(V, a) for a in (kept, *mine, *pairs, mixed)],
                maps(size, last),
            )
            tools, parts = tools[:4], tools[4:]
    (top,) = call(
        lambda *refs: leave_kernel(rounds - 1, *refs),
        "leave",
        [(V, a) for a in (sol, message[1], came, mixed, mine[0], pairs[0], inverse)],
        [share],
    )
    pieces = gather_front(top, front_bits)
    sol_local, sep_solution = local_backward(
        parent, solved, first_halves, second_halves, pieces
    )
    return (sol_local, sep_solution)


def solution(mesh):
    spread3 = P(("leaf", "front"), None, None)
    spread2 = P(("leaf", "front"), None)
    spread1 = P(("leaf", "front"))
    return jax.shard_map(
        local,
        mesh=mesh,
        in_specs=(spread3, spread3, spread3, spread1, spread2, spread2, spread2, spread2),
        out_specs=(spread3, spread2),
        check_vma=False,
    )
```

```python
import jax
import jax.numpy as jnp
from jax import lax
from jax.experimental import pallas as pl
from jax.experimental.pallas import tpu as pltpu
from jax.sharding import PartitionSpec as P

F32 = jnp.float32
BF16 = jnp.bfloat16
NN = (((1,), (0,)), ((), ()))
NT = (((1,), (1,)), ((), ()))
TN = (((0,), (0,)), ((), ()))
VMEM_BYTES = 24 << 20
HALVES = 2
SENDS = 2


def split(x):
    high = x.astype(BF16)
    return high, (x - high.astype(F32)).astype(BF16)


def dot1(a, b, dims):
    return lax.dot_general(a, b, dims, preferred_element_type=F32)


def dot3(a, b, dims):
    axis = 1 - dims[0][0][0]
    rows = a[0].shape[axis]
    both = dot1(jnp.concatenate(a, axis=axis), b[0], dims)
    return both[:rows] + (both[rows:] + dot1(a[0], b[1], dims))


def keep_split(ref, value):
    ref[0], ref[1] = split(value)


def pair(ref):
    return ref[0], ref[1]


def bit_of(axis, bit):
    return (lax.axis_index(axis) // (1 << bit)) % 2


def call(kernel, name, ins, outs, scratch=()):
    specs = [pl.BlockSpec(memory_space=space) for space, _ in ins]
    ins = [
        (space, pltpu.with_memory_space_constraint(a, HBM) if space == HBM else a)
        for space, a in ins
    ]
    return pl.pallas_call(
        kernel,
        name=name,
        in_specs=specs,
        out_specs=tuple(pl.BlockSpec(memory_space=pltpu.VMEM) for _ in outs),
        out_shape=tuple(jax.ShapeDtypeStruct(*o) for o in outs),
        scratch_shapes=list(scratch),
        compiler_params=pltpu.CompilerParams(vmem_limit_bytes=VMEM_BYTES),
    )(*[a for _, a in ins])


V = pltpu.VMEM
HBM = pltpu.HBM


def swap(x, axis, mask):
    n = lax.axis_size(axis)
    return lax.ppermute(x, axis, [(i, i ^ mask) for i in range(n)])


def exchange(x, axis, bit):
    return swap(x, axis, 1 << bit)


def prepare_nodes(count, rows_at, row_columns, dinv, upd, rhs, outs, waits):
    acc, inv_hi, inv_lo, upd_hi, upd_lo = outs
    size = dinv.shape[1]
    width = acc.shape[2]
    lane = lax.broadcasted_iota(jnp.int32, (size, size), 1).astype(F32)
    for k in range(count):
        for c in waits[k]:
            c.wait()
        inv_hi[k], inv_lo[k] = split(dinv[k])
        high, low = split(upd[k])
        chosen = (lane == row_columns[:, rows_at + k : rows_at + k + 1]).astype(BF16)
        upd_hi[k] = dot1(chosen, high, NN).astype(BF16)
        upd_lo[k] = dot1(chosen, low, NN).astype(BF16)
        turned = rhs[k].T
        for h in range(HALVES):
            acc[h, k] = turned[h * width : (h + 1) * width]


def prepare_first_kernel(nodes, *refs):
    (rows_h, sep_h, rhs_h, dinv_h, upd_h, _), refs = refs[:6], refs[6:]
    outs, (top, row_columns, rhs_n, dinv_n, upd_n), refs = refs[:5], refs[5:10], refs[10:]
    rhs_v, dinv_v, upd_v, square, rows, sep, sems, small = refs
    cols = rhs_v.shape[2]
    width = cols // HALVES
    first = nodes // 2
    few = [
        pltpu.make_async_copy(src, dst, small.at[i])
        for i, (src, dst) in enumerate(((rows_h, rows), (sep_h, sep)))
    ]
    for c in few:
        c.start()
    copies = []
    for k in range(nodes):
        ins = (upd_v, dinv_v, rhs_v) if k < first else (upd_n, dinv_n, rhs_n)
        group = [
            pltpu.make_async_copy(src.at[k], dst.at[k % first], sems.at[i, k])
            for i, (src, dst) in enumerate(zip((upd_h, dinv_h, rhs_h), ins))
        ]
        for c in group:
            c.start()
        copies.append(group)
    front = lax.axis_index("front")
    square[...] = jnp.zeros_like(square)
    for c in few:
        c.wait()
    share = sep.shape[0]
    square[pl.ds(pl.multiple_of(front * share, 8), share), :] = sep[...]
    turned = square[...].T
    for h in range(HALVES):
        top[h] = turned[h * width : (h + 1) * width]
    row_columns[...] = rows[...].astype(F32).T
    prepare_nodes(first, 0, row_columns, dinv_v, upd_v, rhs_v, outs, copies[:first])
    for group in copies[first:]:
        for c in group:
            c.wait()


def prepare_second_kernel(first, row_columns, rhs, dinv, upd, _, *outs):
    count = rhs.shape[0]
    waits = [()] * count
    prepare_nodes(count, first, row_columns, dinv, upd, rhs, outs, waits)


def prepared(count, size, cols):
    half = ((count, size, size), BF16)
    return [((HALVES, count, cols // HALVES, size), F32), half, half, half, half]


def prepare_first(rhs, dinv, update, rows, sep, after):
    nodes, size, cols = rhs.shape
    first = nodes // 2
    some = (first, size, cols)
    big = pltpu.VMEM(some, F32)
    return call(
        lambda *refs: prepare_first_kernel(nodes, *refs),
        "prepare_first",
        [(HBM, a) for a in (rows, sep, rhs, dinv, update)] + [(pl.ANY, after)],
        prepared(first, size, cols)
        + [((HALVES, cols // HALVES, size), F32), ((size, nodes), F32)]
        + [((nodes - first, *some[1:]), F32)] * 3,
        [big, big, big, pltpu.VMEM((size, cols), F32)]
        + [pltpu.VMEM(rows.shape, jnp.int32), pltpu.VMEM(sep.shape, F32)]
        + [pltpu.SemaphoreType.DMA((3, nodes)), pltpu.SemaphoreType.DMA((2,))],
    )


def prepare_second(row_columns, rhs, dinv, update, after):
    count, size, cols = rhs.shape
    first = row_columns.shape[1] - count
    return call(
        lambda *refs: prepare_second_kernel(first, *refs),
        "prepare_second",
        [(V, a) for a in (row_columns, rhs, dinv, update)] + [(pl.ANY, after)],
        prepared(count, size, cols),
    )


def forward_kernel(nodes, fronts, *refs):
    (parent_h, acc_a, acc_b, top), parts, refs = refs[:4], (refs[4:8], refs[8:12]), refs[13:]
    solved, send, keep, square, parent, sem = refs[:6]
    accs = refs[6:]
    copy = pltpu.make_async_copy(parent_h, parent, sem)
    copy.start()
    first, width = acc_a.shape[1:3]
    for h in range(HALVES):
        for k in range(nodes):
            accs[h][k] = acc_a[h, k] if k < first else acc_b[h, k - first]
        accs[h][nodes] = top[h]
    for k in range(nodes):
        inv_hi, inv_lo, upd_hi, upd_lo = parts[k // first]
        i = k % first
        inverse = (inv_hi[i], inv_lo[i])
        update = (upd_hi[i], upd_lo[i])
        for h in range(HALVES):
            value = dot3(split(accs[h][k]), inverse, NT)
            solved[k, h * width : (h + 1) * width] = value
            moved = dot3(split(value), update, NT)
            if k + h == 0:
                copy.wait()
            above = nodes if k == nodes - 1 else parent[k]
            accs[h][above] = accs[h][above] - moved
    front = lax.axis_index("front")
    chunk = width * HALVES // fronts
    for h in range(HALVES):
        square[h * width : (h + 1) * width] = accs[h][nodes]
    low_bit = front % 2
    for i in range(fronts // 2):
        for ref, own in ((keep, low_bit), (send, 1 - low_bit)):
            start = pl.multiple_of((2 * i + own) * chunk, 8)
            ref[i * chunk : (i + 1) * chunk] = square[pl.ds(start, chunk), :]


def local_forward(parent, acc_a, acc_b, top, first_halves, second_halves, after, fronts):
    first, (width, size) = acc_a.shape[1], acc_a.shape[2:]
    nodes = first + acc_b.shape[1]
    cols = width * HALVES
    part = ((cols // 2, size), F32)
    return call(
        lambda *refs: forward_kernel(nodes, fronts, *refs),
        "local_forward",
        [(HBM, parent)]
        + [(V, a) for a in (acc_a, acc_b, top, *first_halves, *second_halves)]
        + [(pl.ANY, after)],
        [((nodes, cols, size), F32), part, part],
        [pltpu.VMEM((cols, size), F32), pltpu.SMEM((nodes,), jnp.int32), pltpu.SemaphoreType.DMA]
        + [pltpu.VMEM((nodes + 1, width, size), F32)] * HALVES,
    )


def backward_kernel(nodes, fronts, *refs):
    (parent_h, solved), parts, refs = refs[:2], (refs[2:6], refs[6:10]), refs[10:]
    pieces = refs[:fronts]
    sol, sep_out = refs[fronts : 2 + fronts]
    square, parent, staged, sep_v, sem, sems = refs[2 + fronts : 8 + fronts]
    known = refs[8 + fronts :]
    first = parts[0][0].shape[0]
    copy = pltpu.make_async_copy(parent_h, parent, sem)
    copy.start()
    chunk = pieces[0].shape[0]
    width = known[0].shape[1]
    order = [p[...] for p in pieces]
    for bit in range(fronts.bit_length() - 1):
        flip = bit_of("front", bit) == 1
        order = [jnp.where(flip, order[i ^ (1 << bit)], order[i]) for i in range(fronts)]
    for i, value in enumerate(order):
        at = i * chunk
        known[at // width][nodes, at % width : at % width + chunk] = value
    outs = []
    for k in reversed(range(nodes)):
        i = k % first
        inv_hi, inv_lo, upd_hi, upd_lo = parts[k // first]
        inverse = (inv_hi[i], inv_lo[i])
        update = (upd_hi[i], upd_lo[i])
        if k == nodes - 2:
            copy.wait()
        above = nodes if k == nodes - 1 else parent[k]
        for h in range(HALVES):
            rows = slice(h * width, (h + 1) * width)
            part = solved[k, rows] - dot3(split(known[h][above]), update, NN)
            value = dot3(split(part), inverse, NN)
            known[h][k] = value
            staged[k, :, rows] = value.T
        out = pltpu.make_async_copy(staged.at[k], sol.at[k], sems.at[k])
        out.start()
        outs.append(out)
        if k == nodes - 1:
            for h in range(HALVES):
                square[:, h * width : (h + 1) * width] = known[h][nodes].T
            share = sep_v.shape[0]
            start = pl.multiple_of(lax.axis_index("front") * share, 8)
            sep_v[...] = square[pl.ds(start, share), :]
            out = pltpu.make_async_copy(sep_v, sep_out, sems.at[nodes])
            out.start()
            outs.append(out)
    for out in outs:
        out.wait()


def local_backward(parent, solved, first_halves, second_halves, pieces):
    nodes, cols, size = solved.shape
    fronts = len(pieces)
    sol, sep = jax.ShapeDtypeStruct((nodes, size, cols), F32), ((size // fronts, cols), F32)
    ins = (solved, *first_halves, *second_halves, *pieces)
    return pl.pallas_call(
        lambda *refs: backward_kernel(nodes, fronts, *refs),
        name="local_backward",
        in_specs=[pl.BlockSpec(memory_space=HBM)] + [pl.BlockSpec(memory_space=V)] * len(ins),
        out_specs=(pl.BlockSpec(memory_space=HBM),) * 2,
        out_shape=(sol, jax.ShapeDtypeStruct(*sep)),
        scratch_shapes=[pltpu.VMEM((size, cols), F32), pltpu.SMEM((nodes,), jnp.int32)]
        + [pltpu.VMEM((nodes, size, cols), F32), pltpu.VMEM(*sep), pltpu.SemaphoreType.DMA]
        + [pltpu.SemaphoreType.DMA((nodes + 1,))]
        + [pltpu.VMEM((nodes + 1, cols // HALVES, size), F32)] * HALVES,
        compiler_params=pltpu.CompilerParams(vmem_limit_bytes=VMEM_BYTES),
    )(pltpu.with_memory_space_constraint(parent, HBM), *ins)


def stack_kernel(first, second, out, sems):
    copies = [pltpu.make_async_copy(a, out.at[i], sems.at[i]) for i, a in enumerate((first, second))]
    for c in copies:
        c.start()
    for c in copies:
        c.wait()


def block_map_kernel(fronts, *refs):
    parts = refs[:fronts]
    _, total, part, inverse_halves, square = refs[fronts:]
    front = lax.axis_index("front")
    share = parts[0].shape[1]
    for i in range(fronts):
        start = pl.multiple_of((front ^ i) * share, 8)
        square[:, pl.ds(start, share), :] = parts[i][...]
    inverse = split(square[0])
    inverse_halves[0], inverse_halves[1] = inverse
    value = -dot3(inverse, split(square[1]), NN)
    total[...] = value
    half = part.shape[1]
    send_blocks([part], [value[:half], value[half:]])


def block_map(parts, after):
    fronts = len(parts)
    size = parts[0].shape[2]
    return call(
        lambda *refs: block_map_kernel(fronts, *refs),
        "block_map",
        [(V, a) for a in parts] + [(pl.ANY, after)],
        [((size, size), F32), ((1, size // 2, size), F32), ((2, size, size), BF16)],
        [pltpu.VMEM((2, size, size), F32)],
    )


def quarters(x):
    half = x.shape[0] // 2
    return [x[i : i + half, j : j + half] for i in (0, half) for j in (0, half)]


def joined(a, b, c, d):
    first, second = jnp.concatenate([a, b], axis=1), jnp.concatenate([c, d], axis=1)
    return jnp.concatenate([first, second], axis=0)


def low_core():
    return bit_of("front", 0) == 0


def send_blocks(parts, blocks):
    count = sum(part.shape[0] for part in parts)
    low = low_core()
    i = 0
    for part in parts:
        for j in range(part.shape[0]):
            part[j] = jnp.where(low, blocks[i], blocks[len(blocks) - count + i])
            i += 1


def came_blocks(mine, pairs, total):
    low = low_core()
    mine = [m[j] for m in mine for j in range(m.shape[0])]
    pairs = [p[j] for p in pairs for j in range(p.shape[0])]
    count = len(mine)
    blocks = [jnp.where(low, mine[i], pairs[i]) for i in range(count)]
    for i in range(count, total):
        j = i - total + count
        blocks.append(jnp.where(low, pairs[j], mine[j]))
    return blocks


def k_blocks(k):
    a, b, _, d = quarters(k)
    return [a, b, d]


def k_of(blocks):
    return joined(blocks[0], blocks[1], blocks[1].T, blocks[2])


def first_merge_kernel(*refs):
    own, mine, pairs, _, kept, mixed, halves, curve_u, total_u, total_l, *parts = refs
    upper = bit_of("leaf", 0) == 1
    came = jnp.concatenate(came_blocks([mine], [pairs], 2), axis=0)
    mine = own[...]
    low = jnp.where(upper, came, mine)
    up = jnp.where(upper, mine, came)
    low_s, up_s = split(low), split(up)
    for ref, value in ((total_u, up_s), (total_l, low_s)):
        ref[0], ref[1] = value
    k_up = dot3(up_s, up_s, TN)
    k_up_s = split(k_up)
    curve_u[0], curve_u[1] = k_up_s
    x = dot3(k_up_s, low_s, NN)
    t = dot3(up_s, low_s, NN)
    k = dot3(low_s, low_s, TN) + dot3(low_s, split(x), TN)
    kept[0], kept[1] = k, t
    send_blocks(parts, k_blocks(k) + quarters(t))
    size = low.shape[0]
    row = lax.broadcasted_iota(jnp.int32, (size, size), 0)
    col = lax.broadcasted_iota(jnp.int32, (size, size), 1)
    unit = (row == col).astype(F32)
    keep_split(halves, jnp.where(upper, up.T, unit))
    mixed[0] = jnp.where(upper, t, low + x)
    mixed[1] = jnp.where(upper, unit, up)


def merge_kernel(bit, last, *refs):
    own, refs = refs[0], refs[1:]
    mine, pairs, mixed = refs[:SENDS], refs[SENDS : 2 * SENDS], refs[2 * SENDS]
    upper = bit_of("leaf", bit) == 1
    kept, mixed_n, halves, curve_u, total_u, total_l, *parts = refs[1 + 2 * SENDS :]
    own_k, own_t = own[0], own[1]
    blocks = came_blocks(mine, pairs, 7)
    other_k, other_t = k_of(blocks), joined(*blocks[3:])
    low_s = split(jnp.where(upper, other_t, own_t))
    up_s = split(jnp.where(upper, own_t, other_t))
    k_low = jnp.where(upper, other_k, own_k)
    k_up_s = split(jnp.where(upper, own_k, other_k))
    for ref, value in ((total_u, up_s), (total_l, low_s), (curve_u, k_up_s)):
        ref[0], ref[1] = value
    x = dot3(k_up_s, low_s, NN)
    x_s = split(x)
    k = k_low + dot3(low_s, x_s, TN)
    a, e = mixed[0], mixed[1]
    keep_split(halves, jnp.where(upper, a.T, e))
    a_s, e_s = split(a), split(e)
    a_n = jnp.where(upper, dot3(a_s, low_s, NN), a + dot3(e_s, x_s, TN))
    e_n = jnp.where(upper, e, dot3(up_s, e_s, NN))
    if last:
        kept[...] = jnp.zeros_like(kept)
        for i, block in enumerate(k_blocks(k)):
            parts[0][i] = block
        keep_split(mixed_n, jnp.where(bit_of("leaf", bit + 1) == 1, a_n.T, e_n))
    else:
        t = dot3(up_s, low_s, NN)
        kept[0], kept[1] = k, t
        send_blocks(parts, k_blocks(k) + quarters(t))
        mixed_n[0], mixed_n[1] = a_n, e_n


def maps(size, last):
    both, whole = ((2, size, size), BF16), ((2, size, size), F32)
    half = size // 2
    if last:
        return [((8, 128), F32)] + [both] * 5 + [((3, half, half), F32)]
    sends = [((4 // SENDS, half, half), F32)] * SENDS
    return [whole, whole, both, both, both, both] + sends


def fold_kernel(bit, own, other, send, keep):
    total = send.shape[0]
    chunk = total
    value = own[...] + other[...]
    first, second = value[:chunk], value[chunk:]
    high = bit_of("front", bit) == 1
    send[...] = jnp.where(high, first, second)
    keep[...] = jnp.where(high, second, first)


def enter_kernel(own, other, inverse, own_map, sol, message):
    drive = own[...] + other[...]
    value = dot3(split(drive), pair(inverse), NT)
    sol[...] = value
    rows = value.shape[0]
    message[:rows] = value
    message[rows:] = dot3(split(value), split(own_map[...]), NN)


def step_kernel(bit, last, held, *refs):
    sol, own, other, halves, curve_u, total_u, total_l = refs[:7]
    sol_n, message = refs[7 + held], refs[8 + held :]
    upper = bit_of("leaf", bit) == 1
    rows = sol.shape[0]
    z_own, p_own, z_other, p_other = own[:rows], own[rows:], other[:rows], other[rows:]
    z_low = jnp.where(upper, z_other, z_own)
    z_up = jnp.where(upper, z_own, z_other)
    p_low = jnp.where(upper, p_other, p_own)
    p_up = jnp.where(upper, p_own, p_other)
    z_low_s = split(z_low)
    middle = p_up + dot3(z_low_s, pair(curve_u), NN)
    middle_s = split(middle)
    z_new = z_up + dot3(z_low_s, pair(total_u), NT)
    p_new = p_low + dot3(middle_s, pair(total_l), NN)
    given = split(jnp.where(upper, z_low, middle))
    sol_n[...] = sol[...] + dot3(given, pair(halves), NN)
    if last:
        message[0][...] = jnp.where(bit_of("leaf", bit + 1) == 1, p_new, z_new)
        message[1][...] = z_new
    else:
        message[0][:rows], message[0][rows:] = z_new, p_new


def turn_kernel(bit, own_z, came, blocks, given):
    value = came[...]
    middle = value + dot3(split(own_z[...]), split(k_of(blocks)), NN)
    given[...] = jnp.where(bit_of("leaf", bit) == 1, value, middle)


def passed_on(bit, last, given, received):
    away = bit_of("leaf", bit) == bit_of("leaf", last)
    return jnp.where(away, received, given)


def leave_kernel(last, sol, given, received, halves, inverse, top):
    came = passed_on(1, last, given[...], received[...])
    value = sol[...] + dot3(split(came), pair(halves), NN)
    top[...] = dot3(split(value), pair(inverse), NN)


def gather_front(x, bits):
    pieces = {0: x}
    for bit in reversed(range(bits)):
        for i in list(pieces):
            pieces[i | (1 << bit)] = exchange(pieces[i], "front", bit)
    return [pieces[i] for i in range(1 << bits)]


def local(rhs_local, dinv_local, update_local, parent, row_blocks, sep_rhs, sep_dinv, sep_coupling):
    fronts, leaves = lax.axis_size("front"), lax.axis_size("leaf")
    front_bits, rounds = fronts.bit_length() - 1, leaves.bit_length() - 1
    size = sep_dinv.shape[1]
    cols = sep_rhs.shape[1]
    chunk = cols // fronts

    (stacked,) = call(
        stack_kernel,
        "stack",
        [(HBM, sep_dinv), (HBM, sep_coupling)],
        [((2, *sep_dinv.shape), F32)],
        [pltpu.SemaphoreType.DMA((2,))],
    )
    came = {0: stacked}
    for bit in reversed(range(1, front_bits)):
        for i in list(came):
            came[i | (1 << bit)] = exchange(came[i], "front", bit)
    came[1] = exchange(stacked, "front", 0)
    acc_a, *first_halves = prepare_first(
        rhs_local, dinv_local, update_local, row_blocks, sep_rhs, stacked
    )
    first_halves, (top, row_columns, *raw) = first_halves[:4], first_halves[4:]
    for i in range(2, fronts, 2):
        held, _ = lax.optimization_barrier((came[i], acc_a))
        came[i + 1] = exchange(held, "front", 0)
    acc_b, *second_halves = prepare_second(row_columns, *raw, acc_a)
    own_map, part, inverse = block_map([came[i] for i in range(fronts)], acc_b)
    mine = exchange(part, "leaf", 0)
    solved, send, keep = local_forward(
        parent, acc_a, acc_b, top, first_halves, second_halves, own_map, fronts
    )
    mine, send = lax.optimization_barrier((mine, send))
    pairs = exchange(mine, "front", 0)
    for bit in range(front_bits):
        received = exchange(send, "front", bit)
        if bit + 1 < front_bits:
            half = ((keep.shape[0] // 2, size), F32)
            send, keep = call(
                lambda *refs, bit=bit: fold_kernel(bit + 1, *refs),
                "fold",
                [(V, keep), (V, received)],
                [half, half],
            )
    kept, mixed, *tools = call(
        first_merge_kernel,
        "merge_0",
        [(V, own_map), (V, mine), (V, pairs), (pl.ANY, send)],
        maps(size, False),
    )
    tools, parts = tools[:4], tools[4:]
    sol, message = call(
        enter_kernel,
        "enter",
        [(V, keep), (V, received), (V, inverse), (V, own_map)],
        [((chunk, size), F32), ((2 * chunk, size), F32)],
    )
    share = ((chunk, size), F32)
    for bit in range(rounds - 1):
        last = bit == rounds - 2
        received = exchange(message, "leaf", bit)
        mine = [] if last else [exchange(part, "leaf", bit + 1) for part in parts]
        sol, *message = call(
            lambda *refs, bit=bit, last=last: step_kernel(bit, last, len(mine), *refs),
            f"step_{bit}",
            [(V, a) for a in (sol, message, received, *tools)] + [(pl.ANY, a) for a in mine],
            [share] + ([share, share] if last else [((2 * chunk, size), F32)]),
        )
        if not last:
            (message,) = message
            mine, _ = lax.optimization_barrier((mine, sol))
            pairs = [exchange(m, "front", 0) for m in mine]
            last = bit == rounds - 3
            kept, mixed, *tools = call(
                lambda *refs, bit=bit, last=last: merge_kernel(bit + 1, last, *refs),
                f"merge_{bit + 1}",
                [(V, a) for a in (kept, *mine, *pairs, mixed)],
                maps(size, last),
            )
            tools, parts = tools[:4], tools[4:]
    middle = leaves // 2
    boundary = [(middle - 2 + i, middle + i) for i in range(2)]
    boundary += [(j, i) for i, j in boundary]
    blocks = lax.ppermute(parts[0], "leaf", boundary)
    came = lax.ppermute(message[0], "leaf", boundary)
    (given,) = call(
        lambda *refs: turn_kernel(rounds - 1, *refs),
        "turn",
        [(V, a) for a in (message[1], came, blocks)],
        [share],
    )
    for bit in reversed(range(2, rounds - 1)):
        given = passed_on(bit, rounds - 1, given, exchange(given, "leaf", bit))
    received = exchange(given, "leaf", 1)
    (top,) = call(
        lambda *refs: leave_kernel(rounds - 1, *refs),
        "leave",
        [(V, a) for a in (sol, given, received, mixed, inverse)],
        [share],
    )
    pieces = gather_front(top, front_bits)
    sol_local, sep_solution = local_backward(
        parent, solved, first_halves, second_halves, pieces
    )
    return (sol_local, sep_solution)


def solution(mesh):
    spread3 = P(("leaf", "front"), None, None)
    spread2 = P(("leaf", "front"), None)
    spread1 = P(("leaf", "front"))
    return jax.shard_map(
        local,
        mesh=mesh,
        in_specs=(spread3, spread3, spread3, spread1, spread2, spread2, spread2, spread2),
        out_specs=(spread3, spread2),
        check_vma=False,
    )
```

```python
import jax
import jax.numpy as jnp
from jax import lax
from jax.experimental import pallas as pl
from jax.experimental.pallas import tpu as pltpu
from jax.sharding import PartitionSpec as P

F32 = jnp.float32
BF16 = jnp.bfloat16
NN = (((1,), (0,)), ((), ()))
NT = (((1,), (1,)), ((), ()))
TN = (((0,), (0,)), ((), ()))
VMEM_BYTES = 24 << 20
HALVES = 2


def split(x):
    high = x.astype(BF16)
    return high, (x - high.astype(F32)).astype(BF16)


def dot1(a, b, dims):
    return lax.dot_general(a, b, dims, preferred_element_type=F32)


def dot3(a, b, dims):
    axis = 1 - dims[0][0][0]
    rows = a[0].shape[axis]
    both = dot1(jnp.concatenate(a, axis=axis), b[0], dims)
    return both[:rows] + (both[rows:] + dot1(a[0], b[1], dims))


def keep_split(ref, value):
    ref[0], ref[1] = split(value)


def pair(ref):
    return ref[0], ref[1]


def bit_of(axis, bit):
    return (lax.axis_index(axis) // (1 << bit)) % 2


def call(kernel, name, ins, outs, scratch=()):
    specs = [pl.BlockSpec(memory_space=space) for space, _ in ins]
    ins = [
        (space, pltpu.with_memory_space_constraint(a, HBM) if space == HBM else a)
        for space, a in ins
    ]
    return pl.pallas_call(
        kernel,
        name=name,
        in_specs=specs,
        out_specs=tuple(pl.BlockSpec(memory_space=pltpu.VMEM) for _ in outs),
        out_shape=tuple(jax.ShapeDtypeStruct(*o) for o in outs),
        scratch_shapes=list(scratch),
        compiler_params=pltpu.CompilerParams(vmem_limit_bytes=VMEM_BYTES),
    )(*[a for _, a in ins])


V = pltpu.VMEM
HBM = pltpu.HBM


def swap(x, axis, mask):
    n = lax.axis_size(axis)
    return lax.ppermute(x, axis, [(i, i ^ mask) for i in range(n)])


def exchange(x, axis, bit):
    return swap(x, axis, 1 << bit)


def prepare_nodes(count, rows_at, row_columns, dinv, upd, rhs, outs, waits):
    acc, inv_hi, inv_lo, upd_hi, upd_lo = outs
    size = dinv.shape[1]
    width = acc.shape[2]
    lane = lax.broadcasted_iota(jnp.int32, (size, size), 1).astype(F32)
    for k in range(count):
        for c in waits[k]:
            c.wait()
        inv_hi[k], inv_lo[k] = split(dinv[k])
        high, low = split(upd[k])
        chosen = (lane == row_columns[:, rows_at + k : rows_at + k + 1]).astype(BF16)
        upd_hi[k] = dot1(chosen, high, NN).astype(BF16)
        upd_lo[k] = dot1(chosen, low, NN).astype(BF16)
        turned = rhs[k].T
        for h in range(HALVES):
            acc[h, k] = turned[h * width : (h + 1) * width]


def prepare_first_kernel(nodes, *refs):
    (rows_h, sep_h, rhs_h, dinv_h, upd_h, _), refs = refs[:6], refs[6:]
    outs, (top, row_columns, rhs_n, dinv_n, upd_n), refs = refs[:5], refs[5:10], refs[10:]
    rhs_v, dinv_v, upd_v, square, rows, sep, sems, small = refs
    cols = rhs_v.shape[2]
    width = cols // HALVES
    first = nodes // 2
    few = [
        pltpu.make_async_copy(src, dst, small.at[i])
        for i, (src, dst) in enumerate(((rows_h, rows), (sep_h, sep)))
    ]
    for c in few:
        c.start()
    copies = []
    for k in range(nodes):
        ins = (upd_v, dinv_v, rhs_v) if k < first else (upd_n, dinv_n, rhs_n)
        group = [
            pltpu.make_async_copy(src.at[k], dst.at[k % first], sems.at[i, k])
            for i, (src, dst) in enumerate(zip((upd_h, dinv_h, rhs_h), ins))
        ]
        for c in group:
            c.start()
        copies.append(group)
    front = lax.axis_index("front")
    square[...] = jnp.zeros_like(square)
    for c in few:
        c.wait()
    share = sep.shape[0]
    square[pl.ds(pl.multiple_of(front * share, 8), share), :] = sep[...]
    turned = square[...].T
    for h in range(HALVES):
        top[h] = turned[h * width : (h + 1) * width]
    row_columns[...] = rows[...].astype(F32).T
    prepare_nodes(first, 0, row_columns, dinv_v, upd_v, rhs_v, outs, copies[:first])
    for group in copies[first:]:
        for c in group:
            c.wait()


def prepare_second_kernel(first, row_columns, rhs, dinv, upd, _, *outs):
    count = rhs.shape[0]
    waits = [()] * count
    prepare_nodes(count, first, row_columns, dinv, upd, rhs, outs, waits)


def prepared(count, size, cols):
    half = ((count, size, size), BF16)
    return [((HALVES, count, cols // HALVES, size), F32), half, half, half, half]


def prepare_first(rhs, dinv, update, rows, sep, after):
    nodes, size, cols = rhs.shape
    first = nodes // 2
    some = (first, size, cols)
    big = pltpu.VMEM(some, F32)
    return call(
        lambda *refs: prepare_first_kernel(nodes, *refs),
        "prepare_first",
        [(HBM, a) for a in (rows, sep, rhs, dinv, update)] + [(pl.ANY, after)],
        prepared(first, size, cols)
        + [((HALVES, cols // HALVES, size), F32), ((size, nodes), F32)]
        + [((nodes - first, *some[1:]), F32)] * 3,
        [big, big, big, pltpu.VMEM((size, cols), F32)]
        + [pltpu.VMEM(rows.shape, jnp.int32), pltpu.VMEM(sep.shape, F32)]
        + [pltpu.SemaphoreType.DMA((3, nodes)), pltpu.SemaphoreType.DMA((2,))],
    )


def prepare_second(row_columns, rhs, dinv, update, after):
    count, size, cols = rhs.shape
    first = row_columns.shape[1] - count
    return call(
        lambda *refs: prepare_second_kernel(first, *refs),
        "prepare_second",
        [(V, a) for a in (row_columns, rhs, dinv, update)] + [(pl.ANY, after)],
        prepared(count, size, cols),
    )


def forward_kernel(nodes, fronts, *refs):
    (parent_h, acc_a, acc_b, top), parts, refs = refs[:4], (refs[4:8], refs[8:12]), refs[13:]
    solved, send, keep, square, parent, sem = refs[:6]
    accs = refs[6:]
    copy = pltpu.make_async_copy(parent_h, parent, sem)
    copy.start()
    first, width = acc_a.shape[1:3]
    for h in range(HALVES):
        for k in range(nodes):
            accs[h][k] = acc_a[h, k] if k < first else acc_b[h, k - first]
        accs[h][nodes] = top[h]
    for k in range(nodes):
        inv_hi, inv_lo, upd_hi, upd_lo = parts[k // first]
        i = k % first
        inverse = (inv_hi[i], inv_lo[i])
        update = (upd_hi[i], upd_lo[i])
        for h in range(HALVES):
            value = dot3(split(accs[h][k]), inverse, NT)
            solved[k, h * width : (h + 1) * width] = value
            moved = dot3(split(value), update, NT)
            if k + h == 0:
                copy.wait()
            above = nodes if k == nodes - 1 else parent[k]
            accs[h][above] = accs[h][above] - moved
    front = lax.axis_index("front")
    chunk = width * HALVES // fronts
    for h in range(HALVES):
        square[h * width : (h + 1) * width] = accs[h][nodes]
    low_bit = front % 2
    for i in range(fronts // 2):
        for ref, own in ((keep, low_bit), (send, 1 - low_bit)):
            start = pl.multiple_of((2 * i + own) * chunk, 8)
            ref[i * chunk : (i + 1) * chunk] = square[pl.ds(start, chunk), :]


def local_forward(parent, acc_a, acc_b, top, first_halves, second_halves, after, fronts):
    first, (width, size) = acc_a.shape[1], acc_a.shape[2:]
    nodes = first + acc_b.shape[1]
    cols = width * HALVES
    part = ((cols // 2, size), F32)
    return call(
        lambda *refs: forward_kernel(nodes, fronts, *refs),
        "local_forward",
        [(HBM, parent)]
        + [(V, a) for a in (acc_a, acc_b, top, *first_halves, *second_halves)]
        + [(pl.ANY, after)],
        [((nodes, cols, size), F32), part, part],
        [pltpu.VMEM((cols, size), F32), pltpu.SMEM((nodes,), jnp.int32), pltpu.SemaphoreType.DMA]
        + [pltpu.VMEM((nodes + 1, width, size), F32)] * HALVES,
    )


def backward_kernel(nodes, fronts, *refs):
    (parent_h, solved), parts, refs = refs[:2], (refs[2:6], refs[6:10]), refs[10:]
    pieces = refs[:fronts]
    sol, sep_out = refs[fronts : 2 + fronts]
    square, parent, staged, sep_v, sem, sems = refs[2 + fronts : 8 + fronts]
    known = refs[8 + fronts :]
    first = parts[0][0].shape[0]
    copy = pltpu.make_async_copy(parent_h, parent, sem)
    copy.start()
    chunk = pieces[0].shape[0]
    width = known[0].shape[1]
    order = [p[...] for p in pieces]
    for bit in range(fronts.bit_length() - 1):
        flip = bit_of("front", bit) == 1
        order = [jnp.where(flip, order[i ^ (1 << bit)], order[i]) for i in range(fronts)]
    for i, value in enumerate(order):
        at = i * chunk
        known[at // width][nodes, at % width : at % width + chunk] = value
    outs = []
    for k in reversed(range(nodes)):
        i = k % first
        inv_hi, inv_lo, upd_hi, upd_lo = parts[k // first]
        inverse = (inv_hi[i], inv_lo[i])
        update = (upd_hi[i], upd_lo[i])
        if k == nodes - 2:
            copy.wait()
        above = nodes if k == nodes - 1 else parent[k]
        for h in range(HALVES):
            rows = slice(h * width, (h + 1) * width)
            part = solved[k, rows] - dot3(split(known[h][above]), update, NN)
            value = dot3(split(part), inverse, NN)
            known[h][k] = value
            staged[k, :, rows] = value.T
        out = pltpu.make_async_copy(staged.at[k], sol.at[k], sems.at[k])
        out.start()
        outs.append(out)
        if k == nodes - 1:
            for h in range(HALVES):
                square[:, h * width : (h + 1) * width] = known[h][nodes].T
            share = sep_v.shape[0]
            start = pl.multiple_of(lax.axis_index("front") * share, 8)
            sep_v[...] = square[pl.ds(start, share), :]
            out = pltpu.make_async_copy(sep_v, sep_out, sems.at[nodes])
            out.start()
            outs.append(out)
    for out in outs:
        out.wait()


def local_backward(parent, solved, first_halves, second_halves, pieces):
    nodes, cols, size = solved.shape
    fronts = len(pieces)
    sol, sep = jax.ShapeDtypeStruct((nodes, size, cols), F32), ((size // fronts, cols), F32)
    ins = (solved, *first_halves, *second_halves, *pieces)
    return pl.pallas_call(
        lambda *refs: backward_kernel(nodes, fronts, *refs),
        name="local_backward",
        in_specs=[pl.BlockSpec(memory_space=HBM)] + [pl.BlockSpec(memory_space=V)] * len(ins),
        out_specs=(pl.BlockSpec(memory_space=HBM),) * 2,
        out_shape=(sol, jax.ShapeDtypeStruct(*sep)),
        scratch_shapes=[pltpu.VMEM((size, cols), F32), pltpu.SMEM((nodes,), jnp.int32)]
        + [pltpu.VMEM((nodes, size, cols), F32), pltpu.VMEM(*sep), pltpu.SemaphoreType.DMA]
        + [pltpu.SemaphoreType.DMA((nodes + 1,))]
        + [pltpu.VMEM((nodes + 1, cols // HALVES, size), F32)] * HALVES,
        compiler_params=pltpu.CompilerParams(vmem_limit_bytes=VMEM_BYTES),
    )(pltpu.with_memory_space_constraint(parent, HBM), *ins)


def stack_kernel(first, second, out, sems):
    copies = [pltpu.make_async_copy(a, out.at[i], sems.at[i]) for i, a in enumerate((first, second))]
    for c in copies:
        c.start()
    for c in copies:
        c.wait()


def block_map_kernel(fronts, *refs):
    parts = refs[:fronts]
    _, total, part, inverse_halves, square = refs[fronts:]
    front = lax.axis_index("front")
    share = parts[0].shape[1]
    for i in range(fronts):
        start = pl.multiple_of((front ^ i) * share, 8)
        square[:, pl.ds(start, share), :] = parts[i][...]
    inverse = split(square[0])
    inverse_halves[0], inverse_halves[1] = inverse
    value = -dot3(inverse, split(square[1]), NN)
    total[...] = value
    half = part.shape[1]
    send_blocks([part], [value[:half], value[half:]])


def block_map(parts, after):
    fronts = len(parts)
    size = parts[0].shape[2]
    return call(
        lambda *refs: block_map_kernel(fronts, *refs),
        "block_map",
        [(V, a) for a in parts] + [(pl.ANY, after)],
        [((size, size), F32), ((1, size // 2, size), F32), ((2, size, size), BF16)],
        [pltpu.VMEM((2, size, size), F32)],
    )


def quarters(x):
    half = x.shape[0] // 2
    return [x[i : i + half, j : j + half] for i in (0, half) for j in (0, half)]


def joined(a, b, c, d):
    first, second = jnp.concatenate([a, b], axis=1), jnp.concatenate([c, d], axis=1)
    return jnp.concatenate([first, second], axis=0)


def low_core():
    return bit_of("front", 0) == 0


def send_blocks(parts, blocks):
    count = sum(part.shape[0] for part in parts)
    low = low_core()
    i = 0
    for part in parts:
        for j in range(part.shape[0]):
            part[j] = jnp.where(low, blocks[i], blocks[len(blocks) - count + i])
            i += 1


def came_blocks(mine, pairs, total):
    low = low_core()
    mine = [m[j] for m in mine for j in range(m.shape[0])]
    pairs = [p[j] for p in pairs for j in range(p.shape[0])]
    count = len(mine)
    blocks = [jnp.where(low, mine[i], pairs[i]) for i in range(count)]
    for i in range(count, total):
        j = i - total + count
        blocks.append(jnp.where(low, pairs[j], mine[j]))
    return blocks


def k_blocks(k):
    a, b, _, d = quarters(k)
    return [a, b, d]


def k_of(blocks):
    return joined(blocks[0], blocks[1], blocks[1].T, blocks[2])


def send_maps(parts, k, t):
    for i, block in enumerate(k_blocks(k)):
        parts[0][i] = block
    send_blocks(parts[1:], quarters(t))


def first_merge_kernel(*refs):
    own, mine, pairs, _, kept, mixed, halves, curve_u, total_u, total_l, *parts = refs
    upper = bit_of("leaf", 0) == 1
    came = jnp.concatenate(came_blocks([mine], [pairs], 2), axis=0)
    mine = own[...]
    low = jnp.where(upper, came, mine)
    up = jnp.where(upper, mine, came)
    low_s, up_s = split(low), split(up)
    for ref, value in ((total_u, up_s), (total_l, low_s)):
        ref[0], ref[1] = value
    k_up = dot3(up_s, up_s, TN)
    k_up_s = split(k_up)
    curve_u[0], curve_u[1] = k_up_s
    x = dot3(k_up_s, low_s, NN)
    t = dot3(up_s, low_s, NN)
    k = dot3(low_s, low_s, TN) + dot3(low_s, split(x), TN)
    kept[0], kept[1] = k, t
    send_maps(parts, k, t)
    size = low.shape[0]
    row = lax.broadcasted_iota(jnp.int32, (size, size), 0)
    col = lax.broadcasted_iota(jnp.int32, (size, size), 1)
    unit = (row == col).astype(F32)
    keep_split(halves, jnp.where(upper, up.T, unit))
    mixed[0] = jnp.where(upper, t, low + x)
    mixed[1] = jnp.where(upper, unit, up)


def merge_kernel(bit, last, *refs):
    own, other, mine, pairs, mixed = refs[:5]
    kept, mixed_n, halves, curve_u, total_u, total_l, *parts = refs[5:]
    upper = bit_of("leaf", bit) == 1
    own_k, own_t = own[0], own[1]
    other_k, other_t = k_of(other), joined(*came_blocks([mine], [pairs], 4))
    low_s = split(jnp.where(upper, other_t, own_t))
    up_s = split(jnp.where(upper, own_t, other_t))
    k_low = jnp.where(upper, other_k, own_k)
    k_up_s = split(jnp.where(upper, own_k, other_k))
    for ref, value in ((total_u, up_s), (total_l, low_s), (curve_u, k_up_s)):
        ref[0], ref[1] = value
    x = dot3(k_up_s, low_s, NN)
    x_s = split(x)
    a, e = mixed[0], mixed[1]
    keep_split(halves, jnp.where(upper, a.T, e))
    a_s, e_s = split(a), split(e)
    a_n = jnp.where(upper, dot3(a_s, low_s, NN), a + dot3(e_s, x_s, TN))
    e_n = jnp.where(upper, e, dot3(up_s, e_s, NN))
    if last:
        kept[...] = jnp.zeros_like(kept)
        keep_split(mixed_n, jnp.where(bit_of("leaf", bit + 1) == 1, a_n.T, e_n))
    else:
        k = k_low + dot3(low_s, x_s, TN)
        t = dot3(up_s, low_s, NN)
        kept[0], kept[1] = k, t
        send_maps(parts, k, t)
        mixed_n[0], mixed_n[1] = a_n, e_n


def boundary_kernel(own, other, blocks):
    k, t = own[0], split(own[1])
    x = dot3(split(k_of(other)), t, NN)
    for i, block in enumerate(k_blocks(k + dot3(t, split(x), TN))):
        blocks[i] = block


def maps(size, last):
    both, whole = ((2, size, size), BF16), ((2, size, size), F32)
    half = size // 2
    if last:
        return [((8, 128), F32)] + [both] * 5
    sends = [((i, half, half), F32) for i in (3, 2)]
    return [whole, whole, both, both, both, both] + sends


def fold_kernel(bit, own, other, send, keep):
    total = send.shape[0]
    chunk = total
    value = own[...] + other[...]
    first, second = value[:chunk], value[chunk:]
    high = bit_of("front", bit) == 1
    send[...] = jnp.where(high, first, second)
    keep[...] = jnp.where(high, second, first)


def enter_kernel(own, other, inverse, own_map, sol, message):
    drive = own[...] + other[...]
    value = dot3(split(drive), pair(inverse), NT)
    sol[...] = value
    rows = value.shape[0]
    message[:rows] = value
    message[rows:] = dot3(split(value), split(own_map[...]), NN)


def step_kernel(bit, last, held, *refs):
    sol, own, other, halves, curve_u, total_u, total_l = refs[:7]
    sol_n, message = refs[7 + held], refs[8 + held :]
    upper = bit_of("leaf", bit) == 1
    rows = sol.shape[0]
    z_own, p_own, z_other, p_other = own[:rows], own[rows:], other[:rows], other[rows:]
    z_low = jnp.where(upper, z_other, z_own)
    z_up = jnp.where(upper, z_own, z_other)
    p_low = jnp.where(upper, p_other, p_own)
    p_up = jnp.where(upper, p_own, p_other)
    z_low_s = split(z_low)
    middle = p_up + dot3(z_low_s, pair(curve_u), NN)
    middle_s = split(middle)
    z_new = z_up + dot3(z_low_s, pair(total_u), NT)
    p_new = p_low + dot3(middle_s, pair(total_l), NN)
    given = split(jnp.where(upper, z_low, middle))
    sol_n[...] = sol[...] + dot3(given, pair(halves), NN)
    if last:
        message[0][...] = jnp.where(bit_of("leaf", bit + 1) == 1, p_new, z_new)
        message[1][...] = z_new
    else:
        message[0][:rows], message[0][rows:] = z_new, p_new


def turn_kernel(bit, own_z, came, blocks, given):
    value = came[...]
    middle = value + dot3(split(own_z[...]), split(k_of(blocks)), NN)
    given[...] = jnp.where(bit_of("leaf", bit) == 1, value, middle)


def passed_on(bit, last, given, received):
    away = bit_of("leaf", bit) == bit_of("leaf", last)
    return jnp.where(away, received, given)


def leave_kernel(last, sol, given, received, halves, inverse, top):
    came = passed_on(1, last, given[...], received[...])
    value = sol[...] + dot3(split(came), pair(halves), NN)
    top[...] = dot3(split(value), pair(inverse), NN)


def gather_front(x, bits):
    pieces = {0: x}
    for bit in reversed(range(bits)):
        for i in list(pieces):
            pieces[i | (1 << bit)] = exchange(pieces[i], "front", bit)
    return [pieces[i] for i in range(1 << bits)]


def local(rhs_local, dinv_local, update_local, parent, row_blocks, sep_rhs, sep_dinv, sep_coupling):
    fronts, leaves = lax.axis_size("front"), lax.axis_size("leaf")
    front_bits, rounds = fronts.bit_length() - 1, leaves.bit_length() - 1
    size = sep_dinv.shape[1]
    cols = sep_rhs.shape[1]
    chunk = cols // fronts

    (stacked,) = call(
        stack_kernel,
        "stack",
        [(HBM, sep_dinv), (HBM, sep_coupling)],
        [((2, *sep_dinv.shape), F32)],
        [pltpu.SemaphoreType.DMA((2,))],
    )
    came = {0: stacked}
    for bit in reversed(range(1, front_bits)):
        for i in list(came):
            came[i | (1 << bit)] = exchange(came[i], "front", bit)
    came[1] = exchange(stacked, "front", 0)
    acc_a, *first_halves = prepare_first(
        rhs_local, dinv_local, update_local, row_blocks, sep_rhs, stacked
    )
    first_halves, (top, row_columns, *raw) = first_halves[:4], first_halves[4:]
    for i in range(2, fronts, 2):
        held, _ = lax.optimization_barrier((came[i], acc_a))
        came[i + 1] = exchange(held, "front", 0)
    acc_b, *second_halves = prepare_second(row_columns, *raw, acc_a)
    own_map, part, inverse = block_map([came[i] for i in range(fronts)], acc_b)
    mine = exchange(part, "leaf", 0)
    solved, send, keep = local_forward(
        parent, acc_a, acc_b, top, first_halves, second_halves, own_map, fronts
    )
    mine, send = lax.optimization_barrier((mine, send))
    pairs = exchange(mine, "front", 0)
    for bit in range(front_bits):
        received = exchange(send, "front", bit)
        if bit + 1 < front_bits:
            half = ((keep.shape[0] // 2, size), F32)
            send, keep = call(
                lambda *refs, bit=bit: fold_kernel(bit + 1, *refs),
                "fold",
                [(V, keep), (V, received)],
                [half, half],
            )
    kept, mixed, *tools = call(
        first_merge_kernel,
        "merge_0",
        [(V, own_map), (V, mine), (V, pairs), (pl.ANY, send)],
        maps(size, False),
    )
    tools, parts = tools[:4], tools[4:]
    sol, message = call(
        enter_kernel,
        "enter",
        [(V, keep), (V, received), (V, inverse), (V, own_map)],
        [((chunk, size), F32), ((2 * chunk, size), F32)],
    )
    share = ((chunk, size), F32)
    middle = leaves // 2
    boundary = [(middle - 2 + i, middle + i) for i in range(2)]
    boundary += [(j, i) for i, j in boundary]
    for bit in range(rounds - 1):
        last = bit == rounds - 2
        received = exchange(message, "leaf", bit)
        ahead = []
        if not last:
            other, mine = [exchange(part, "leaf", bit + 1) for part in parts]
            ahead = [other]
        if bit == rounds - 3:
            ahead = (blocks,) = call(
                boundary_kernel, "boundary", [(V, kept), (V, other)], [(other.shape, F32)]
            )
            blocks = lax.ppermute(blocks, "leaf", boundary)
        sol, *message = call(
            lambda *refs, bit=bit, last=last: step_kernel(bit, last, len(ahead), *refs),
            f"step_{bit}",
            [(V, a) for a in (sol, message, received, *tools)] + [(pl.ANY, a) for a in ahead],
            [share] + ([share, share] if last else [((2 * chunk, size), F32)]),
        )
        if not last:
            (message,) = message
            mine, _ = lax.optimization_barrier((mine, sol))
            pairs = exchange(mine, "front", 0)
            last = bit == rounds - 3
            kept, mixed, *tools = call(
                lambda *refs, bit=bit, last=last: merge_kernel(bit + 1, last, *refs),
                f"merge_{bit + 1}",
                [(V, a) for a in (kept, other, mine, pairs, mixed)],
                maps(size, last),
            )
            tools, parts = tools[:4], tools[4:]
    came = lax.ppermute(message[0], "leaf", boundary)
    (given,) = call(
        lambda *refs: turn_kernel(rounds - 1, *refs),
        "turn",
        [(V, a) for a in (message[1], came, blocks)],
        [share],
    )
    for bit in reversed(range(2, rounds - 1)):
        given = passed_on(bit, rounds - 1, given, exchange(given, "leaf", bit))
    received = exchange(given, "leaf", 1)
    (top,) = call(
        lambda *refs: leave_kernel(rounds - 1, *refs),
        "leave",
        [(V, a) for a in (sol, given, received, mixed, inverse)],
        [share],
    )
    pieces = gather_front(top, front_bits)
    sol_local, sep_solution = local_backward(
        parent, solved, first_halves, second_halves, pieces
    )
    return (sol_local, sep_solution)


def solution(mesh):
    spread3 = P(("leaf", "front"), None, None)
    spread2 = P(("leaf", "front"), None)
    spread1 = P(("leaf", "front"))
    return jax.shard_map(
        local,
        mesh=mesh,
        in_specs=(spread3, spread3, spread3, spread1, spread2, spread2, spread2, spread2),
        out_specs=(spread3, spread2),
        check_vma=False,
    )
```

```python
import jax
import jax.numpy as jnp
from jax import lax
from jax.experimental import pallas as pl
from jax.experimental.pallas import tpu as pltpu
from jax.sharding import PartitionSpec as P

F32 = jnp.float32
BF16 = jnp.bfloat16
NN = (((1,), (0,)), ((), ()))
NT = (((1,), (1,)), ((), ()))
TN = (((0,), (0,)), ((), ()))
VMEM_BYTES = 24 << 20
HALVES = 2


def split(x):
    high = x.astype(BF16)
    return high, (x - high.astype(F32)).astype(BF16)


def dot1(a, b, dims):
    return lax.dot_general(a, b, dims, preferred_element_type=F32)


def dot3(a, b, dims):
    axis = 1 - dims[0][0][0]
    rows = a[0].shape[axis]
    both = dot1(jnp.concatenate(a, axis=axis), b[0], dims)
    return both[:rows] + (both[rows:] + dot1(a[0], b[1], dims))


def keep_split(ref, value):
    ref[0], ref[1] = split(value)


def pair(ref):
    return ref[0], ref[1]


def bit_of(axis, bit):
    return (lax.axis_index(axis) // (1 << bit)) % 2


def call(kernel, name, ins, outs, scratch=()):
    specs = [pl.BlockSpec(memory_space=space) for space, _ in ins]
    ins = [
        (space, pltpu.with_memory_space_constraint(a, HBM) if space == HBM else a)
        for space, a in ins
    ]
    return pl.pallas_call(
        kernel,
        name=name,
        in_specs=specs,
        out_specs=tuple(pl.BlockSpec(memory_space=pltpu.VMEM) for _ in outs),
        out_shape=tuple(jax.ShapeDtypeStruct(*o) for o in outs),
        scratch_shapes=list(scratch),
        compiler_params=pltpu.CompilerParams(vmem_limit_bytes=VMEM_BYTES),
    )(*[a for _, a in ins])


V = pltpu.VMEM
HBM = pltpu.HBM


def swap(x, axis, mask):
    n = lax.axis_size(axis)
    return lax.ppermute(x, axis, [(i, i ^ mask) for i in range(n)])


def exchange(x, axis, bit):
    return swap(x, axis, 1 << bit)


def prepare_nodes(count, rows_at, row_columns, dinv, upd, rhs, outs, waits):
    acc, inv_hi, inv_lo, upd_hi, upd_lo = outs
    size = dinv.shape[1]
    width = acc.shape[2]
    lane = lax.broadcasted_iota(jnp.int32, (size, size), 1).astype(F32)
    for k in range(count):
        for c in waits[k]:
            c.wait()
        inv_hi[k], inv_lo[k] = split(dinv[k])
        high, low = split(upd[k])
        chosen = (lane == row_columns[:, rows_at + k : rows_at + k + 1]).astype(BF16)
        upd_hi[k] = dot1(chosen, high, NN).astype(BF16)
        upd_lo[k] = dot1(chosen, low, NN).astype(BF16)
        turned = rhs[k].T
        for h in range(HALVES):
            acc[h, k] = turned[h * width : (h + 1) * width]


def prepare_first_kernel(nodes, *refs):
    (rows_h, sep_h, rhs_h, dinv_h, upd_h, _), refs = refs[:6], refs[6:]
    outs, (top, row_columns, rhs_n, dinv_n, upd_n), refs = refs[:5], refs[5:10], refs[10:]
    rhs_v, dinv_v, upd_v, square, rows, sep, sems, small = refs
    cols = rhs_v.shape[2]
    width = cols // HALVES
    first = nodes // 2
    few = [
        pltpu.make_async_copy(src, dst, small.at[i])
        for i, (src, dst) in enumerate(((rows_h, rows), (sep_h, sep)))
    ]
    for c in few:
        c.start()
    copies = []
    for k in range(nodes):
        ins = (upd_v, dinv_v, rhs_v) if k < first else (upd_n, dinv_n, rhs_n)
        group = [
            pltpu.make_async_copy(src.at[k], dst.at[k % first], sems.at[i, k])
            for i, (src, dst) in enumerate(zip((upd_h, dinv_h, rhs_h), ins))
        ]
        for c in group:
            c.start()
        copies.append(group)
    front = lax.axis_index("front")
    square[...] = jnp.zeros_like(square)
    for c in few:
        c.wait()
    share = sep.shape[0]
    square[pl.ds(pl.multiple_of(front * share, 8), share), :] = sep[...]
    turned = square[...].T
    for h in range(HALVES):
        top[h] = turned[h * width : (h + 1) * width]
    row_columns[...] = rows[...].astype(F32).T
    prepare_nodes(first, 0, row_columns, dinv_v, upd_v, rhs_v, outs, copies[:first])
    for group in copies[first:]:
        for c in group:
            c.wait()


def prepare_second_kernel(first, row_columns, rhs, dinv, upd, _, *outs):
    count = rhs.shape[0]
    waits = [()] * count
    prepare_nodes(count, first, row_columns, dinv, upd, rhs, outs, waits)


def prepared(count, size, cols):
    half = ((count, size, size), BF16)
    return [((HALVES, count, cols // HALVES, size), F32), half, half, half, half]


def prepare_first(rhs, dinv, update, rows, sep, after):
    nodes, size, cols = rhs.shape
    first = nodes // 2
    some = (first, size, cols)
    big = pltpu.VMEM(some, F32)
    return call(
        lambda *refs: prepare_first_kernel(nodes, *refs),
        "prepare_first",
        [(HBM, a) for a in (rows, sep, rhs, dinv, update)] + [(pl.ANY, after)],
        prepared(first, size, cols)
        + [((HALVES, cols // HALVES, size), F32), ((size, nodes), F32)]
        + [((nodes - first, *some[1:]), F32)] * 3,
        [big, big, big, pltpu.VMEM((size, cols), F32)]
        + [pltpu.VMEM(rows.shape, jnp.int32), pltpu.VMEM(sep.shape, F32)]
        + [pltpu.SemaphoreType.DMA((3, nodes)), pltpu.SemaphoreType.DMA((2,))],
    )


def prepare_second(row_columns, rhs, dinv, update, after):
    count, size, cols = rhs.shape
    first = row_columns.shape[1] - count
    return call(
        lambda *refs: prepare_second_kernel(first, *refs),
        "prepare_second",
        [(V, a) for a in (row_columns, rhs, dinv, update)] + [(pl.ANY, after)],
        prepared(count, size, cols),
    )


def forward_kernel(nodes, fronts, *refs):
    (parent_h, acc_a, acc_b, top), parts, refs = refs[:4], (refs[4:8], refs[8:12]), refs[13:]
    solved, send, keep, square, parent, sem = refs[:6]
    accs = refs[6:]
    copy = pltpu.make_async_copy(parent_h, parent, sem)
    copy.start()
    first, width = acc_a.shape[1:3]
    for h in range(HALVES):
        for k in range(nodes):
            accs[h][k] = acc_a[h, k] if k < first else acc_b[h, k - first]
        accs[h][nodes] = top[h]
    for k in range(nodes):
        inv_hi, inv_lo, upd_hi, upd_lo = parts[k // first]
        i = k % first
        inverse = (inv_hi[i], inv_lo[i])
        update = (upd_hi[i], upd_lo[i])
        for h in range(HALVES):
            value = dot3(split(accs[h][k]), inverse, NT)
            solved[k, h * width : (h + 1) * width] = value
            moved = dot3(split(value), update, NT)
            if k + h == 0:
                copy.wait()
            above = nodes if k == nodes - 1 else parent[k]
            accs[h][above] = accs[h][above] - moved
    front = lax.axis_index("front")
    chunk = width * HALVES // fronts
    for h in range(HALVES):
        square[h * width : (h + 1) * width] = accs[h][nodes]
    low_bit = front % 2
    for i in range(fronts // 2):
        for ref, own in ((keep, low_bit), (send, 1 - low_bit)):
            start = pl.multiple_of((2 * i + own) * chunk, 8)
            ref[i * chunk : (i + 1) * chunk] = square[pl.ds(start, chunk), :]


def local_forward(parent, acc_a, acc_b, top, first_halves, second_halves, after, fronts):
    first, (width, size) = acc_a.shape[1], acc_a.shape[2:]
    nodes = first + acc_b.shape[1]
    cols = width * HALVES
    part = ((cols // 2, size), F32)
    return call(
        lambda *refs: forward_kernel(nodes, fronts, *refs),
        "local_forward",
        [(HBM, parent)]
        + [(V, a) for a in (acc_a, acc_b, top, *first_halves, *second_halves)]
        + [(pl.ANY, after)],
        [((nodes, cols, size), F32), part, part],
        [pltpu.VMEM((cols, size), F32), pltpu.SMEM((nodes,), jnp.int32), pltpu.SemaphoreType.DMA]
        + [pltpu.VMEM((nodes + 1, width, size), F32)] * HALVES,
    )


def backward_kernel(nodes, fronts, *refs):
    (parent_h, solved), parts, refs = refs[:2], (refs[2:6], refs[6:10]), refs[10:]
    pieces = refs[:fronts]
    sol, sep_out = refs[fronts : 2 + fronts]
    square, parent, staged, sep_v, sem, sems = refs[2 + fronts : 8 + fronts]
    known = refs[8 + fronts :]
    first = parts[0][0].shape[0]
    copy = pltpu.make_async_copy(parent_h, parent, sem)
    copy.start()
    chunk = pieces[0].shape[0]
    width = known[0].shape[1]
    order = [p[...] for p in pieces]
    for bit in range(fronts.bit_length() - 1):
        flip = bit_of("front", bit) == 1
        order = [jnp.where(flip, order[i ^ (1 << bit)], order[i]) for i in range(fronts)]
    for i, value in enumerate(order):
        at = i * chunk
        known[at // width][nodes, at % width : at % width + chunk] = value
    outs = []
    for k in reversed(range(nodes)):
        i = k % first
        inv_hi, inv_lo, upd_hi, upd_lo = parts[k // first]
        inverse = (inv_hi[i], inv_lo[i])
        update = (upd_hi[i], upd_lo[i])
        if k == nodes - 2:
            copy.wait()
        above = nodes if k == nodes - 1 else parent[k]
        for h in range(HALVES):
            rows = slice(h * width, (h + 1) * width)
            part = solved[k, rows] - dot3(split(known[h][above]), update, NN)
            value = dot3(split(part), inverse, NN)
            known[h][k] = value
            staged[k, :, rows] = value.T
        out = pltpu.make_async_copy(staged.at[k], sol.at[k], sems.at[k])
        out.start()
        outs.append(out)
        if k == nodes - 1:
            for h in range(HALVES):
                square[:, h * width : (h + 1) * width] = known[h][nodes].T
            share = sep_v.shape[0]
            start = pl.multiple_of(lax.axis_index("front") * share, 8)
            sep_v[...] = square[pl.ds(start, share), :]
            out = pltpu.make_async_copy(sep_v, sep_out, sems.at[nodes])
            out.start()
            outs.append(out)
    for out in outs:
        out.wait()


def local_backward(parent, solved, first_halves, second_halves, pieces):
    nodes, cols, size = solved.shape
    fronts = len(pieces)
    sol, sep = jax.ShapeDtypeStruct((nodes, size, cols), F32), ((size // fronts, cols), F32)
    ins = (solved, *first_halves, *second_halves, *pieces)
    return pl.pallas_call(
        lambda *refs: backward_kernel(nodes, fronts, *refs),
        name="local_backward",
        in_specs=[pl.BlockSpec(memory_space=HBM)] + [pl.BlockSpec(memory_space=V)] * len(ins),
        out_specs=(pl.BlockSpec(memory_space=HBM),) * 2,
        out_shape=(sol, jax.ShapeDtypeStruct(*sep)),
        scratch_shapes=[pltpu.VMEM((size, cols), F32), pltpu.SMEM((nodes,), jnp.int32)]
        + [pltpu.VMEM((nodes, size, cols), F32), pltpu.VMEM(*sep), pltpu.SemaphoreType.DMA]
        + [pltpu.SemaphoreType.DMA((nodes + 1,))]
        + [pltpu.VMEM((nodes + 1, cols // HALVES, size), F32)] * HALVES,
        compiler_params=pltpu.CompilerParams(vmem_limit_bytes=VMEM_BYTES),
    )(pltpu.with_memory_space_constraint(parent, HBM), *ins)


def stack_kernel(first, second, out, sems):
    copies = [pltpu.make_async_copy(a, out.at[i], sems.at[i]) for i, a in enumerate((first, second))]
    for c in copies:
        c.start()
    for c in copies:
        c.wait()


def block_map_kernel(fronts, *refs):
    parts = refs[:fronts]
    _, total, part, inverse_halves, square = refs[fronts:]
    front = lax.axis_index("front")
    share = parts[0].shape[1]
    for i in range(fronts):
        start = pl.multiple_of((front ^ i) * share, 8)
        square[:, pl.ds(start, share), :] = parts[i][...]
    inverse = split(square[0])
    inverse_halves[0], inverse_halves[1] = inverse
    value = -dot3(inverse, split(square[1]), NN)
    total[...] = value
    half = part.shape[1]
    send_blocks([part], [value[:half], value[half:]])


def block_map(parts, after):
    fronts = len(parts)
    size = parts[0].shape[2]
    return call(
        lambda *refs: block_map_kernel(fronts, *refs),
        "block_map",
        [(V, a) for a in parts] + [(pl.ANY, after)],
        [((size, size), F32), ((1, size // 2, size), F32), ((2, size, size), BF16)],
        [pltpu.VMEM((2, size, size), F32)],
    )


def quarters(x):
    half = x.shape[0] // 2
    return [x[i : i + half, j : j + half] for i in (0, half) for j in (0, half)]


def joined(a, b, c, d):
    first, second = jnp.concatenate([a, b], axis=1), jnp.concatenate([c, d], axis=1)
    return jnp.concatenate([first, second], axis=0)


def low_core():
    return bit_of("front", 0) == 0


def send_blocks(parts, blocks):
    count = sum(part.shape[0] for part in parts)
    low = low_core()
    i = 0
    for part in parts:
        for j in range(part.shape[0]):
            part[j] = jnp.where(low, blocks[i], blocks[len(blocks) - count + i])
            i += 1


def came_blocks(mine, pairs, total):
    low = low_core()
    mine = [m[j] for m in mine for j in range(m.shape[0])]
    pairs = [p[j] for p in pairs for j in range(p.shape[0])]
    count = len(mine)
    blocks = [jnp.where(low, mine[i], pairs[i]) for i in range(count)]
    for i in range(count, total):
        j = i - total + count
        blocks.append(jnp.where(low, pairs[j], mine[j]))
    return blocks


def k_blocks(k):
    a, b, _, d = quarters(k)
    return [a, b, d]


def k_of(blocks):
    return joined(blocks[0], blocks[1], blocks[1].T, blocks[2])


def send_maps(parts, k, t):
    for i, block in enumerate(k_blocks(k)):
        parts[0][i] = block
    send_blocks(parts[1:], quarters(t))


def first_merge_kernel(*refs):
    own, mine, pairs, _, kept, mixed, halves, curve_u, total_u, total_l, *parts = refs
    upper = bit_of("leaf", 0) == 1
    came = jnp.concatenate(came_blocks([mine], [pairs], 2), axis=0)
    mine = own[...]
    low = jnp.where(upper, came, mine)
    up = jnp.where(upper, mine, came)
    low_s, up_s = split(low), split(up)
    for ref, value in ((total_u, up_s), (total_l, low_s)):
        ref[0], ref[1] = value
    k_up = dot3(up_s, up_s, TN)
    k_up_s = split(k_up)
    curve_u[0], curve_u[1] = k_up_s
    x = dot3(k_up_s, low_s, NN)
    t = dot3(up_s, low_s, NN)
    k = dot3(low_s, low_s, TN) + dot3(low_s, split(x), TN)
    kept[0], kept[1] = k, t
    send_maps(parts, k, t)
    size = low.shape[0]
    row = lax.broadcasted_iota(jnp.int32, (size, size), 0)
    col = lax.broadcasted_iota(jnp.int32, (size, size), 1)
    unit = (row == col).astype(F32)
    keep_split(halves, jnp.where(upper, up.T, unit))
    mixed[0] = jnp.where(upper, t, low + x)
    mixed[1] = jnp.where(upper, unit, up)


def merge_kernel(bit, last, *refs):
    own, other, mine, pairs, mixed = refs[:5]
    kept, mixed_n, halves, curve_u, total_u, total_l, *parts = refs[5:]
    upper = bit_of("leaf", bit) == 1
    own_k, own_t = own[0], own[1]
    other_k, other_t = k_of(other), joined(*came_blocks([mine], [pairs], 4))
    low_s = split(jnp.where(upper, other_t, own_t))
    up_s = split(jnp.where(upper, own_t, other_t))
    k_low = jnp.where(upper, other_k, own_k)
    k_up_s = split(jnp.where(upper, own_k, other_k))
    for ref, value in ((total_u, up_s), (total_l, low_s), (curve_u, k_up_s)):
        ref[0], ref[1] = value
    x = dot3(k_up_s, low_s, NN)
    x_s = split(x)
    a, e = mixed[0], mixed[1]
    keep_split(halves, jnp.where(upper, a.T, e))
    a_s, e_s = split(a), split(e)
    a_n = jnp.where(upper, dot3(a_s, low_s, NN), a + dot3(e_s, x_s, TN))
    e_n = jnp.where(upper, e, dot3(up_s, e_s, NN))
    if last:
        kept[...] = jnp.zeros_like(kept)
        keep_split(mixed_n, jnp.where(bit_of("leaf", bit + 1) == 1, a_n.T, e_n))
    else:
        k = k_low + dot3(low_s, x_s, TN)
        t = dot3(up_s, low_s, NN)
        kept[0], kept[1] = k, t
        send_maps(parts, k, t)
        mixed_n[0], mixed_n[1] = a_n, e_n


def boundary_kernel(own, other, blocks):
    k, t = own[0], split(own[1])
    x = dot3(split(k_of(other)), t, NN)
    for i, block in enumerate(k_blocks(k + dot3(t, split(x), TN))):
        blocks[i] = block


def maps(size, last):
    both, whole = ((2, size, size), BF16), ((2, size, size), F32)
    half = size // 2
    if last:
        return [((8, 128), F32)] + [both] * 5
    sends = [((i, half, half), F32) for i in (3, 2)]
    return [whole, whole, both, both, both, both] + sends


def fold_kernel(bit, own, other, send, keep):
    total = send.shape[0]
    chunk = total
    value = own[...] + other[...]
    first, second = value[:chunk], value[chunk:]
    high = bit_of("front", bit) == 1
    send[...] = jnp.where(high, first, second)
    keep[...] = jnp.where(high, second, first)


def enter_kernel(own, other, inverse, own_map, sol, message):
    drive = own[...] + other[...]
    value = dot3(split(drive), pair(inverse), NT)
    sol[...] = value
    rows = value.shape[0]
    message[:rows] = value
    message[rows:] = dot3(split(value), split(own_map[...]), NN)


def step_kernel(bit, last, held, *refs):
    sol, own, other, halves, curve_u, total_u, total_l = refs[:7]
    sol_n, message = refs[7 + held], refs[8 + held :]
    upper = bit_of("leaf", bit) == 1
    rows = sol.shape[0]
    z_own, p_own, z_other, p_other = own[:rows], own[rows:], other[:rows], other[rows:]
    z_low = jnp.where(upper, z_other, z_own)
    z_up = jnp.where(upper, z_own, z_other)
    p_low = jnp.where(upper, p_other, p_own)
    p_up = jnp.where(upper, p_own, p_other)
    z_low_s = split(z_low)
    middle = p_up + dot3(z_low_s, pair(curve_u), NN)
    middle_s = split(middle)
    z_new = z_up + dot3(z_low_s, pair(total_u), NT)
    p_new = p_low + dot3(middle_s, pair(total_l), NN)
    given = split(jnp.where(upper, z_low, middle))
    sol_n[...] = sol[...] + dot3(given, pair(halves), NN)
    if last:
        message[0][...] = jnp.where(bit_of("leaf", bit + 1) == 1, p_new, z_new)
        message[1][...] = z_new
    else:
        message[0][:rows], message[0][rows:] = z_new, p_new


def turn_kernel(bit, own_z, came, blocks, given):
    value = came[...]
    middle = value + dot3(split(own_z[...]), split(k_of(blocks)), NN)
    given[...] = jnp.where(bit_of("leaf", bit) == 1, value, middle)


def passed_on(bit, last, given, received):
    away = bit_of("leaf", bit) == bit_of("leaf", last)
    return jnp.where(away, received, given)


def leave_kernel(last, sol, given, received, halves, inverse, top):
    came = passed_on(1, last, given[...], received[...])
    value = sol[...] + dot3(split(came), pair(halves), NN)
    top[...] = dot3(split(value), pair(inverse), NN)


def gather_front(x, bits):
    pieces = {0: x}
    for bit in reversed(range(bits)):
        for i in list(pieces):
            pieces[i | (1 << bit)] = exchange(pieces[i], "front", bit)
    return [pieces[i] for i in range(1 << bits)]


def local(rhs_local, dinv_local, update_local, parent, row_blocks, sep_rhs, sep_dinv, sep_coupling):
    fronts, leaves = lax.axis_size("front"), lax.axis_size("leaf")
    front_bits, rounds = fronts.bit_length() - 1, leaves.bit_length() - 1
    size = sep_dinv.shape[1]
    cols = sep_rhs.shape[1]
    chunk = cols // fronts

    (stacked,) = call(
        stack_kernel,
        "stack",
        [(HBM, sep_dinv), (HBM, sep_coupling)],
        [((2, *sep_dinv.shape), F32)],
        [pltpu.SemaphoreType.DMA((2,))],
    )
    came = {0: stacked}
    for bit in reversed(range(1, front_bits)):
        for i in list(came):
            came[i | (1 << bit)] = exchange(came[i], "front", bit)
    came[1] = exchange(stacked, "front", 0)
    acc_a, *first_halves = prepare_first(
        rhs_local, dinv_local, update_local, row_blocks, sep_rhs, stacked
    )
    first_halves, (top, row_columns, *raw) = first_halves[:4], first_halves[4:]
    for i in range(2, fronts, 2):
        held, _ = lax.optimization_barrier((came[i], acc_a))
        came[i + 1] = exchange(held, "front", 0)
    acc_b, *second_halves = prepare_second(row_columns, *raw, acc_a)
    own_map, part, inverse = block_map([came[i] for i in range(fronts)], acc_b)
    mine = exchange(part, "leaf", 0)
    solved, send, keep = local_forward(
        parent, acc_a, acc_b, top, first_halves, second_halves, own_map, fronts
    )
    mine, send = lax.optimization_barrier((mine, send))
    pairs = exchange(mine, "front", 0)
    for bit in range(front_bits):
        received = exchange(send, "front", bit)
        if bit + 1 < front_bits:
            half = ((keep.shape[0] // 2, size), F32)
            send, keep = call(
                lambda *refs, bit=bit: fold_kernel(bit + 1, *refs),
                "fold",
                [(V, keep), (V, received)],
                [half, half],
            )
    kept, mixed, *tools = call(
        first_merge_kernel,
        "merge_0",
        [(V, own_map), (V, mine), (V, pairs), (pl.ANY, send)],
        maps(size, False),
    )
    tools, parts = tools[:4], tools[4:]
    sol, message = call(
        enter_kernel,
        "enter",
        [(V, keep), (V, received), (V, inverse), (V, own_map)],
        [((chunk, size), F32), ((2 * chunk, size), F32)],
    )
    share = ((chunk, size), F32)
    middle = leaves // 2
    boundary = [(middle - 2 + i, middle + i) for i in range(2)]
    boundary += [(j, i) for i, j in boundary]
    paired = {i for i, _ in boundary}
    boundary += [(i, i ^ 1) for i in range(leaves) if i not in paired]
    for bit in range(rounds - 1):
        last = bit == rounds - 2
        received = exchange(message, "leaf", bit)
        ahead = []
        if not last:
            other, mine = [exchange(part, "leaf", bit + 1) for part in parts]
            ahead = [other]
        if bit == rounds - 3:
            ahead = (blocks,) = call(
                boundary_kernel, "boundary", [(V, kept), (V, other)], [(other.shape, F32)]
            )
            blocks = lax.ppermute(blocks, "leaf", boundary)
        sol, *message = call(
            lambda *refs, bit=bit, last=last: step_kernel(bit, last, len(ahead), *refs),
            f"step_{bit}",
            [(V, a) for a in (sol, message, received, *tools)] + [(pl.ANY, a) for a in ahead],
            [share] + ([share, share] if last else [((2 * chunk, size), F32)]),
        )
        if not last:
            (message,) = message
            mine, _ = lax.optimization_barrier((mine, sol))
            pairs = exchange(mine, "front", 0)
            last = bit == rounds - 3
            kept, mixed, *tools = call(
                lambda *refs, bit=bit, last=last: merge_kernel(bit + 1, last, *refs),
                f"merge_{bit + 1}",
                [(V, a) for a in (kept, other, mine, pairs, mixed)],
                maps(size, last),
            )
            tools, parts = tools[:4], tools[4:]
    came = lax.ppermute(message[0], "leaf", boundary)
    (given,) = call(
        lambda *refs: turn_kernel(rounds - 1, *refs),
        "turn",
        [(V, a) for a in (message[1], came, blocks)],
        [share],
    )
    for bit in reversed(range(2, rounds - 1)):
        given = passed_on(bit, rounds - 1, given, exchange(given, "leaf", bit))
    received = exchange(given, "leaf", 1)
    (top,) = call(
        lambda *refs: leave_kernel(rounds - 1, *refs),
        "leave",
        [(V, a) for a in (sol, given, received, mixed, inverse)],
        [share],
    )
    pieces = gather_front(top, front_bits)
    sol_local, sep_solution = local_backward(
        parent, solved, first_halves, second_halves, pieces
    )
    return (sol_local, sep_solution)


def solution(mesh):
    spread3 = P(("leaf", "front"), None, None)
    spread2 = P(("leaf", "front"), None)
    spread1 = P(("leaf", "front"))
    return jax.shard_map(
        local,
        mesh=mesh,
        in_specs=(spread3, spread3, spread3, spread1, spread2, spread2, spread2, spread2),
        out_specs=(spread3, spread2),
        check_vma=False,
    )
```

```python
import jax
import jax.numpy as jnp
from jax import lax
from jax.experimental import pallas as pl
from jax.experimental.pallas import tpu as pltpu
from jax.sharding import PartitionSpec as P

F32 = jnp.float32
BF16 = jnp.bfloat16
NN = (((1,), (0,)), ((), ()))
NT = (((1,), (1,)), ((), ()))
TN = (((0,), (0,)), ((), ()))
VMEM_BYTES = 24 << 20
HALVES = 2


def split(x):
    high = x.astype(BF16)
    return high, (x - high.astype(F32)).astype(BF16)


def dot1(a, b, dims):
    return lax.dot_general(a, b, dims, preferred_element_type=F32)


def dot3(a, b, dims):
    axis = 1 - dims[0][0][0]
    rows = a[0].shape[axis]
    both = dot1(jnp.concatenate(a, axis=axis), b[0], dims)
    return both[:rows] + (both[rows:] + dot1(a[0], b[1], dims))


def keep_split(ref, value):
    ref[0], ref[1] = split(value)


def pair(ref):
    return ref[0], ref[1]


def bit_of(axis, bit):
    return (lax.axis_index(axis) // (1 << bit)) % 2


def call(kernel, name, ins, outs, scratch=()):
    specs = [pl.BlockSpec(memory_space=space) for space, _ in ins]
    ins = [
        (space, pltpu.with_memory_space_constraint(a, HBM) if space == HBM else a)
        for space, a in ins
    ]
    return pl.pallas_call(
        kernel,
        name=name,
        in_specs=specs,
        out_specs=tuple(pl.BlockSpec(memory_space=pltpu.VMEM) for _ in outs),
        out_shape=tuple(jax.ShapeDtypeStruct(*o) for o in outs),
        scratch_shapes=list(scratch),
        compiler_params=pltpu.CompilerParams(vmem_limit_bytes=VMEM_BYTES),
    )(*[a for _, a in ins])


V = pltpu.VMEM
HBM = pltpu.HBM


def swap(x, axis, mask):
    n = lax.axis_size(axis)
    return lax.ppermute(x, axis, [(i, i ^ mask) for i in range(n)])


def exchange(x, axis, bit):
    return swap(x, axis, 1 << bit)


def prepare_nodes(count, rows_at, row_columns, dinv, upd, rhs, outs, waits):
    acc, inv_hi, inv_lo, upd_hi, upd_lo = outs
    size = dinv.shape[1]
    width = acc.shape[2]
    lane = lax.broadcasted_iota(jnp.int32, (size, size), 1).astype(F32)
    for k in range(count):
        for c in waits[k]:
            c.wait()
        inv_hi[k], inv_lo[k] = split(dinv[k])
        high, low = split(upd[k])
        chosen = (lane == row_columns[:, rows_at + k : rows_at + k + 1]).astype(BF16)
        upd_hi[k] = dot1(chosen, high, NN).astype(BF16)
        upd_lo[k] = dot1(chosen, low, NN).astype(BF16)
        turned = rhs[k].T
        for h in range(HALVES):
            acc[h, k] = turned[h * width : (h + 1) * width]


def prepare_first_kernel(nodes, *refs):
    (rows_h, sep_h, rhs_h, dinv_h, upd_h, _), refs = refs[:6], refs[6:]
    outs, (top, row_columns, rhs_n, dinv_n, upd_n), refs = refs[:5], refs[5:10], refs[10:]
    rhs_v, dinv_v, upd_v, square, rows, sep, sems, small = refs
    cols = rhs_v.shape[2]
    width = cols // HALVES
    first = nodes // 2
    few = [
        pltpu.make_async_copy(src, dst, small.at[i])
        for i, (src, dst) in enumerate(((rows_h, rows), (sep_h, sep)))
    ]
    for c in few:
        c.start()
    copies = []
    for k in range(nodes):
        ins = (upd_v, dinv_v, rhs_v) if k < first else (upd_n, dinv_n, rhs_n)
        group = [
            pltpu.make_async_copy(src.at[k], dst.at[k % first], sems.at[i, k])
            for i, (src, dst) in enumerate(zip((upd_h, dinv_h, rhs_h), ins))
        ]
        for c in group:
            c.start()
        copies.append(group)
    front = lax.axis_index("front")
    square[...] = jnp.zeros_like(square)
    for c in few:
        c.wait()
    share = sep.shape[0]
    square[pl.ds(pl.multiple_of(front * share, 8), share), :] = sep[...]
    turned = square[...].T
    for h in range(HALVES):
        top[h] = turned[h * width : (h + 1) * width]
    row_columns[...] = rows[...].astype(F32).T
    prepare_nodes(first, 0, row_columns, dinv_v, upd_v, rhs_v, outs, copies[:first])
    for group in copies[first:]:
        for c in group:
            c.wait()


def prepare_second_kernel(first, row_columns, rhs, dinv, upd, _, *outs):
    count = rhs.shape[0]
    waits = [()] * count
    prepare_nodes(count, first, row_columns, dinv, upd, rhs, outs, waits)


def prepared(count, size, cols):
    half = ((count, size, size), BF16)
    return [((HALVES, count, cols // HALVES, size), F32), half, half, half, half]


def prepare_first(rhs, dinv, update, rows, sep, after):
    nodes, size, cols = rhs.shape
    first = nodes // 2
    some = (first, size, cols)
    big = pltpu.VMEM(some, F32)
    return call(
        lambda *refs: prepare_first_kernel(nodes, *refs),
        "prepare_first",
        [(HBM, a) for a in (rows, sep, rhs, dinv, update)] + [(pl.ANY, after)],
        prepared(first, size, cols)
        + [((HALVES, cols // HALVES, size), F32), ((size, nodes), F32)]
        + [((nodes - first, *some[1:]), F32)] * 3,
        [big, big, big, pltpu.VMEM((size, cols), F32)]
        + [pltpu.VMEM(rows.shape, jnp.int32), pltpu.VMEM(sep.shape, F32)]
        + [pltpu.SemaphoreType.DMA((3, nodes)), pltpu.SemaphoreType.DMA((2,))],
    )


def prepare_second(row_columns, rhs, dinv, update, after):
    count, size, cols = rhs.shape
    first = row_columns.shape[1] - count
    return call(
        lambda *refs: prepare_second_kernel(first, *refs),
        "prepare_second",
        [(V, a) for a in (row_columns, rhs, dinv, update)] + [(pl.ANY, after)],
        prepared(count, size, cols),
    )


def forward_kernel(nodes, fronts, *refs):
    (parent_h, acc_a, acc_b, top), parts, refs = refs[:4], (refs[4:8], refs[8:12]), refs[13:]
    solved, send, keep, square, parent, sem = refs[:6]
    accs = refs[6:]
    copy = pltpu.make_async_copy(parent_h, parent, sem)
    copy.start()
    first, width = acc_a.shape[1:3]
    for h in range(HALVES):
        for k in range(nodes):
            accs[h][k] = acc_a[h, k] if k < first else acc_b[h, k - first]
        accs[h][nodes] = top[h]
    for k in range(nodes):
        inv_hi, inv_lo, upd_hi, upd_lo = parts[k // first]
        i = k % first
        inverse = (inv_hi[i], inv_lo[i])
        update = (upd_hi[i], upd_lo[i])
        for h in range(HALVES):
            value = dot3(split(accs[h][k]), inverse, NT)
            solved[k, h * width : (h + 1) * width] = value
            moved = dot3(split(value), update, NT)
            if k + h == 0:
                copy.wait()
            above = nodes if k == nodes - 1 else parent[k]
            accs[h][above] = accs[h][above] - moved
    front = lax.axis_index("front")
    chunk = width * HALVES // fronts
    for h in range(HALVES):
        square[h * width : (h + 1) * width] = accs[h][nodes]
    low_bit = front % 2
    for i in range(fronts // 2):
        for ref, own in ((keep, low_bit), (send, 1 - low_bit)):
            start = pl.multiple_of((2 * i + own) * chunk, 8)
            ref[i * chunk : (i + 1) * chunk] = square[pl.ds(start, chunk), :]


def local_forward(parent, acc_a, acc_b, top, first_halves, second_halves, after, fronts):
    first, (width, size) = acc_a.shape[1], acc_a.shape[2:]
    nodes = first + acc_b.shape[1]
    cols = width * HALVES
    part = ((cols // 2, size), F32)
    return call(
        lambda *refs: forward_kernel(nodes, fronts, *refs),
        "local_forward",
        [(HBM, parent)]
        + [(V, a) for a in (acc_a, acc_b, top, *first_halves, *second_halves)]
        + [(pl.ANY, after)],
        [((nodes, cols, size), F32), part, part],
        [pltpu.VMEM((cols, size), F32), pltpu.SMEM((nodes,), jnp.int32), pltpu.SemaphoreType.DMA]
        + [pltpu.VMEM((nodes + 1, width, size), F32)] * HALVES,
    )


def backward_kernel(nodes, fronts, *refs):
    (parent_h, solved), parts, refs = refs[:2], (refs[2:6], refs[6:10]), refs[10:]
    pieces = refs[:fronts]
    sol, sep_out = refs[fronts : 2 + fronts]
    square, parent, staged, sep_v, sem, sems = refs[2 + fronts : 8 + fronts]
    known = refs[8 + fronts :]
    first = parts[0][0].shape[0]
    copy = pltpu.make_async_copy(parent_h, parent, sem)
    copy.start()
    chunk = pieces[0].shape[0]
    width = known[0].shape[1]
    order = [p[...] for p in pieces]
    for bit in range(fronts.bit_length() - 1):
        flip = bit_of("front", bit) == 1
        order = [jnp.where(flip, order[i ^ (1 << bit)], order[i]) for i in range(fronts)]
    for i, value in enumerate(order):
        at = i * chunk
        known[at // width][nodes, at % width : at % width + chunk] = value
    outs = []
    for k in reversed(range(nodes)):
        i = k % first
        inv_hi, inv_lo, upd_hi, upd_lo = parts[k // first]
        inverse = (inv_hi[i], inv_lo[i])
        update = (upd_hi[i], upd_lo[i])
        if k == nodes - 2:
            copy.wait()
        above = nodes if k == nodes - 1 else parent[k]
        for h in range(HALVES):
            rows = slice(h * width, (h + 1) * width)
            part = solved[k, rows] - dot3(split(known[h][above]), update, NN)
            value = dot3(split(part), inverse, NN)
            known[h][k] = value
            staged[k, :, rows] = value.T
        out = pltpu.make_async_copy(staged.at[k], sol.at[k], sems.at[k])
        out.start()
        outs.append(out)
        if k == nodes - 1:
            for h in range(HALVES):
                square[:, h * width : (h + 1) * width] = known[h][nodes].T
            share = sep_v.shape[0]
            start = pl.multiple_of(lax.axis_index("front") * share, 8)
            sep_v[...] = square[pl.ds(start, share), :]
            out = pltpu.make_async_copy(sep_v, sep_out, sems.at[nodes])
            out.start()
            outs.append(out)
    for out in outs:
        out.wait()


def local_backward(parent, solved, first_halves, second_halves, pieces):
    nodes, cols, size = solved.shape
    fronts = len(pieces)
    sol, sep = jax.ShapeDtypeStruct((nodes, size, cols), F32), ((size // fronts, cols), F32)
    ins = (solved, *first_halves, *second_halves, *pieces)
    return pl.pallas_call(
        lambda *refs: backward_kernel(nodes, fronts, *refs),
        name="local_backward",
        in_specs=[pl.BlockSpec(memory_space=HBM)] + [pl.BlockSpec(memory_space=V)] * len(ins),
        out_specs=(pl.BlockSpec(memory_space=HBM),) * 2,
        out_shape=(sol, jax.ShapeDtypeStruct(*sep)),
        scratch_shapes=[pltpu.VMEM((size, cols), F32), pltpu.SMEM((nodes,), jnp.int32)]
        + [pltpu.VMEM((nodes, size, cols), F32), pltpu.VMEM(*sep), pltpu.SemaphoreType.DMA]
        + [pltpu.SemaphoreType.DMA((nodes + 1,))]
        + [pltpu.VMEM((nodes + 1, cols // HALVES, size), F32)] * HALVES,
        compiler_params=pltpu.CompilerParams(vmem_limit_bytes=VMEM_BYTES),
    )(pltpu.with_memory_space_constraint(parent, HBM), *ins)


def stack_kernel(first, second, out, sems):
    copies = [pltpu.make_async_copy(a, out.at[i], sems.at[i]) for i, a in enumerate((first, second))]
    for c in copies:
        c.start()
    for c in copies:
        c.wait()


def block_map_kernel(fronts, *refs):
    parts = refs[:fronts]
    _, total, part, inverse_halves, square = refs[fronts:]
    front = lax.axis_index("front")
    share = parts[0].shape[1]
    for i in range(fronts):
        start = pl.multiple_of((front ^ i) * share, 8)
        square[:, pl.ds(start, share), :] = parts[i][...]
    inverse = split(square[0])
    inverse_halves[0], inverse_halves[1] = inverse
    value = -dot3(inverse, split(square[1]), NN)
    total[...] = value
    half = part.shape[1]
    send_blocks([part], [value[:half], value[half:]])


def block_map(parts, after):
    fronts = len(parts)
    size = parts[0].shape[2]
    return call(
        lambda *refs: block_map_kernel(fronts, *refs),
        "block_map",
        [(V, a) for a in parts] + [(pl.ANY, after)],
        [((size, size), F32), ((1, size // 2, size), F32), ((2, size, size), BF16)],
        [pltpu.VMEM((2, size, size), F32)],
    )


def quarters(x):
    half = x.shape[0] // 2
    return [x[i : i + half, j : j + half] for i in (0, half) for j in (0, half)]


def joined(a, b, c, d):
    first, second = jnp.concatenate([a, b], axis=1), jnp.concatenate([c, d], axis=1)
    return jnp.concatenate([first, second], axis=0)


def low_core():
    return bit_of("front", 0) == 0


def send_blocks(parts, blocks):
    count = sum(part.shape[0] for part in parts)
    low = low_core()
    i = 0
    for part in parts:
        for j in range(part.shape[0]):
            part[j] = jnp.where(low, blocks[i], blocks[len(blocks) - count + i])
            i += 1


def came_blocks(mine, pairs, total):
    low = low_core()
    mine = [m[j] for m in mine for j in range(m.shape[0])]
    pairs = [p[j] for p in pairs for j in range(p.shape[0])]
    count = len(mine)
    blocks = [jnp.where(low, mine[i], pairs[i]) for i in range(count)]
    for i in range(count, total):
        j = i - total + count
        blocks.append(jnp.where(low, pairs[j], mine[j]))
    return blocks


def k_blocks(k):
    a, b, _, d = quarters(k)
    return [a, b, d]


def k_of(blocks):
    return joined(blocks[0], blocks[1], blocks[1].T, blocks[2])


def send_maps(parts, k, t):
    parts[0][0], parts[0][1], parts[-1][0] = k_blocks(k)
    half = t.shape[0] // 2
    parts[1][...], parts[2][...] = t[:half], t[half:]


def first_merge_kernel(*refs):
    own, mine, pairs, _, kept, mixed, halves, curve_u, total_u, total_l, *parts = refs
    upper = bit_of("leaf", 0) == 1
    came = jnp.concatenate(came_blocks([mine], [pairs], 2), axis=0)
    mine = own[...]
    low = jnp.where(upper, came, mine)
    up = jnp.where(upper, mine, came)
    low_s, up_s = split(low), split(up)
    for ref, value in ((total_u, up_s), (total_l, low_s)):
        ref[0], ref[1] = value
    k_up = dot3(up_s, up_s, TN)
    k_up_s = split(k_up)
    curve_u[0], curve_u[1] = k_up_s
    x = dot3(k_up_s, low_s, NN)
    t = dot3(up_s, low_s, NN)
    k = dot3(low_s, low_s, TN) + dot3(low_s, split(x), TN)
    kept[0], kept[1] = k, t
    send_maps(parts, k, t)
    size = low.shape[0]
    row = lax.broadcasted_iota(jnp.int32, (size, size), 0)
    col = lax.broadcasted_iota(jnp.int32, (size, size), 1)
    unit = (row == col).astype(F32)
    keep_split(halves, jnp.where(upper, up.T, unit))
    mixed[0] = jnp.where(upper, t, low + x)
    mixed[1] = jnp.where(upper, unit, up)


def merge_kernel(bit, last, *refs):
    own, other, rest, first_t, second_t, mixed = refs[:6]
    kept, mixed_n, halves, curve_u, total_u, total_l, *parts = refs[6:]
    upper = bit_of("leaf", bit) == 1
    own_k, own_t = own[0], own[1]
    other_k, other_t = k_of([other[0], other[1], rest[0]]), jnp.concatenate([first_t[...], second_t[...]], axis=0)
    low_s = split(jnp.where(upper, other_t, own_t))
    up_s = split(jnp.where(upper, own_t, other_t))
    k_low = jnp.where(upper, other_k, own_k)
    k_up_s = split(jnp.where(upper, own_k, other_k))
    for ref, value in ((total_u, up_s), (total_l, low_s), (curve_u, k_up_s)):
        ref[0], ref[1] = value
    x = dot3(k_up_s, low_s, NN)
    x_s = split(x)
    a, e = mixed[0], mixed[1]
    keep_split(halves, jnp.where(upper, a.T, e))
    a_s, e_s = split(a), split(e)
    a_n = jnp.where(upper, dot3(a_s, low_s, NN), a + dot3(e_s, x_s, TN))
    e_n = jnp.where(upper, e, dot3(up_s, e_s, NN))
    if last:
        kept[...] = jnp.zeros_like(kept)
        keep_split(mixed_n, jnp.where(bit_of("leaf", bit + 1) == 1, a_n.T, e_n))
    else:
        k = k_low + dot3(low_s, x_s, TN)
        t = dot3(up_s, low_s, NN)
        kept[0], kept[1] = k, t
        send_maps(parts, k, t)
        mixed_n[0], mixed_n[1] = a_n, e_n


def boundary_kernel(own, other, rest, blocks):
    k, t = own[0], split(own[1])
    x = dot3(split(k_of([other[0], other[1], rest[0]])), t, NN)
    for i, block in enumerate(k_blocks(k + dot3(t, split(x), TN))):
        blocks[i] = block


def maps(size, last):
    both, whole = ((2, size, size), BF16), ((2, size, size), F32)
    half = size // 2
    if last:
        return [((8, 128), F32)] + [both] * 5
    sends = [((2, half, half), F32)] + [((half, size), F32)] * 2 + [((1, half, half), F32)]
    return [whole, whole, both, both, both, both] + sends


def fold_kernel(bit, own, other, send, keep):
    total = send.shape[0]
    chunk = total
    value = own[...] + other[...]
    first, second = value[:chunk], value[chunk:]
    high = bit_of("front", bit) == 1
    send[...] = jnp.where(high, first, second)
    keep[...] = jnp.where(high, second, first)


def enter_kernel(own, other, inverse, own_map, sol, message):
    drive = own[...] + other[...]
    value = dot3(split(drive), pair(inverse), NT)
    sol[...] = value
    rows = value.shape[0]
    message[:rows] = value
    message[rows:] = dot3(split(value), split(own_map[...]), NN)


def step_kernel(bit, rounds, held, *refs):
    sol, own, other, halves, curve_u, total_u, total_l = refs[:7]
    sol_n, message = refs[7 + held], refs[8 + held :]
    last = bit == rounds - 2
    upper = bit_of("leaf", bit) == 1
    rows = sol.shape[0]
    z_own, p_own = own[:rows], own[rows:]
    if last:
        z_other = p_other = other[...]
    else:
        z_other, p_other = other[:rows], other[rows:]
    z_low = jnp.where(upper, z_other, z_own)
    p_up = jnp.where(upper, p_own, p_other)
    z_low_s = split(z_low)
    middle = p_up + dot3(z_low_s, pair(curve_u), NN)
    middle_s = split(middle)
    given = split(jnp.where(upper, z_low, middle))
    sol_n[...] = sol[...] + dot3(given, pair(halves), NN)
    z_up = z_own if last else jnp.where(upper, z_own, z_other)
    p_low = p_own if last else jnp.where(upper, p_other, p_own)
    z_new = z_up + dot3(z_low_s, pair(total_u), NT)
    p_new = p_low + dot3(middle_s, pair(total_l), NN)
    if last:
        message[0][...] = jnp.where(bit_of("leaf", bit + 1) == 1, p_new, z_new)
        message[1][...] = z_new
        return
    message[0][:rows], message[0][rows:] = z_new, p_new
    if bit == rounds - 3:
        message[1][...] = jnp.where(bit_of("leaf", bit + 1) == 1, p_new, z_new)


def turn_kernel(bit, own_z, came, blocks, given):
    value = came[...]
    middle = value + dot3(split(own_z[...]), split(k_of(blocks)), NN)
    given[...] = jnp.where(bit_of("leaf", bit) == 1, value, middle)


def passed_on(bit, last, given, received):
    away = bit_of("leaf", bit) == bit_of("leaf", last)
    return jnp.where(away, received, given)


def leave_kernel(last, sol, given, received, halves, inverse, top):
    came = passed_on(1, last, given[...], received[...])
    value = sol[...] + dot3(split(came), pair(halves), NN)
    top[...] = dot3(split(value), pair(inverse), NN)


def gather_front(x, bits):
    pieces = {0: x}
    for bit in reversed(range(bits)):
        for i in list(pieces):
            pieces[i | (1 << bit)] = exchange(pieces[i], "front", bit)
    return [pieces[i] for i in range(1 << bits)]


def local(rhs_local, dinv_local, update_local, parent, row_blocks, sep_rhs, sep_dinv, sep_coupling):
    fronts, leaves = lax.axis_size("front"), lax.axis_size("leaf")
    front_bits, rounds = fronts.bit_length() - 1, leaves.bit_length() - 1
    size = sep_dinv.shape[1]
    cols = sep_rhs.shape[1]
    chunk = cols // fronts

    (stacked,) = call(
        stack_kernel,
        "stack",
        [(HBM, sep_dinv), (HBM, sep_coupling)],
        [((2, *sep_dinv.shape), F32)],
        [pltpu.SemaphoreType.DMA((2,))],
    )
    came = {0: stacked}
    for bit in reversed(range(1, front_bits)):
        for i in list(came):
            came[i | (1 << bit)] = exchange(came[i], "front", bit)
    came[1] = exchange(stacked, "front", 0)
    acc_a, *first_halves = prepare_first(
        rhs_local, dinv_local, update_local, row_blocks, sep_rhs, stacked
    )
    first_halves, (top, row_columns, *raw) = first_halves[:4], first_halves[4:]
    for i in range(2, fronts, 2):
        held, _ = lax.optimization_barrier((came[i], acc_a))
        came[i + 1] = exchange(held, "front", 0)
    acc_b, *second_halves = prepare_second(row_columns, *raw, acc_a)
    own_map, part, inverse = block_map([came[i] for i in range(fronts)], acc_b)
    mine = exchange(part, "leaf", 0)
    solved, send, keep = local_forward(
        parent, acc_a, acc_b, top, first_halves, second_halves, own_map, fronts
    )
    mine, send = lax.optimization_barrier((mine, send))
    pairs = exchange(mine, "front", 0)
    for bit in range(front_bits):
        received = exchange(send, "front", bit)
        if bit + 1 < front_bits:
            half = ((keep.shape[0] // 2, size), F32)
            send, keep = call(
                lambda *refs, bit=bit: fold_kernel(bit + 1, *refs),
                "fold",
                [(V, keep), (V, received)],
                [half, half],
            )
    kept, mixed, *tools = call(
        first_merge_kernel,
        "merge_0",
        [(V, own_map), (V, mine), (V, pairs), (pl.ANY, send)],
        maps(size, False),
    )
    tools, parts = tools[:4], tools[4:]
    sol, message = call(
        enter_kernel,
        "enter",
        [(V, keep), (V, received), (V, inverse), (V, own_map)],
        [((chunk, size), F32), ((2 * chunk, size), F32)],
    )
    share = ((chunk, size), F32)
    middle = leaves // 2
    boundary = [(middle - 2 + i, middle + i) for i in range(2)]
    boundary += [(j, i) for i, j in boundary]
    paired = {i for i, _ in boundary}
    boundary += [(i, i ^ 1) for i in range(leaves) if i not in paired]
    for bit in range(rounds - 1):
        last = bit == rounds - 2
        received = exchange(short[0] if last else message, "leaf", bit)
        ahead = []
        if not last:
            other, *came_t, rest = [exchange(part, "leaf", bit + 1) for part in parts]
            ahead = [other]
        if bit == rounds - 3:
            ahead = (blocks,) = call(
                boundary_kernel,
                "boundary",
                [(V, kept), (V, other), (V, rest)],
                [((3, size // 2, size // 2), F32)],
            )
            blocks = lax.ppermute(blocks, "leaf", boundary)
        sol, *message = call(
            lambda *refs, bit=bit: step_kernel(bit, rounds, len(ahead), *refs),
            f"step_{bit}",
            [(V, a) for a in (sol, message, received, *tools)] + [(pl.ANY, a) for a in ahead],
            [share] + ([share] if last else [((2 * chunk, size), F32)]) + [share] * (bit >= rounds - 3),
        )
        if not last:
            message, *short = message
            last = bit == rounds - 3
            kept, mixed, *tools = call(
                lambda *refs, bit=bit, last=last: merge_kernel(bit + 1, last, *refs),
                f"merge_{bit + 1}",
                [(V, a) for a in (kept, other, rest, *came_t, mixed)],
                maps(size, last),
            )
            tools, parts = tools[:4], tools[4:]
    came = lax.ppermute(message[0], "leaf", boundary)
    (given,) = call(
        lambda *refs: turn_kernel(rounds - 1, *refs),
        "turn",
        [(V, a) for a in (message[1], came, blocks)],
        [share],
    )
    for bit in reversed(range(2, rounds - 1)):
        given = passed_on(bit, rounds - 1, given, exchange(given, "leaf", bit))
    received = exchange(given, "leaf", 1)
    (top,) = call(
        lambda *refs: leave_kernel(rounds - 1, *refs),
        "leave",
        [(V, a) for a in (sol, given, received, mixed, inverse)],
        [share],
    )
    pieces = gather_front(top, front_bits)
    sol_local, sep_solution = local_backward(
        parent, solved, first_halves, second_halves, pieces
    )
    return (sol_local, sep_solution)


def solution(mesh):
    spread3 = P(("leaf", "front"), None, None)
    spread2 = P(("leaf", "front"), None)
    spread1 = P(("leaf", "front"))
    return jax.shard_map(
        local,
        mesh=mesh,
        in_specs=(spread3, spread3, spread3, spread1, spread2, spread2, spread2, spread2),
        out_specs=(spread3, spread2),
        check_vma=False,
    )
```

```python
import jax
import jax.numpy as jnp
from jax import lax
from jax.experimental import pallas as pl
from jax.experimental.pallas import tpu as pltpu
from jax.sharding import PartitionSpec as P

F32 = jnp.float32
BF16 = jnp.bfloat16
NN = (((1,), (0,)), ((), ()))
NT = (((1,), (1,)), ((), ()))
TN = (((0,), (0,)), ((), ()))
VMEM_BYTES = 24 << 20
HALVES = 2


def split(x):
    high = x.astype(BF16)
    return high, (x - high.astype(F32)).astype(BF16)


def dot1(a, b, dims):
    return lax.dot_general(a, b, dims, preferred_element_type=F32)


def dot3(a, b, dims):
    axis = 1 - dims[0][0][0]
    rows = a[0].shape[axis]
    both = dot1(jnp.concatenate(a, axis=axis), b[0], dims)
    return both[:rows] + (both[rows:] + dot1(a[0], b[1], dims))


def keep_split(ref, value):
    ref[0], ref[1] = split(value)


def pair(ref):
    return ref[0], ref[1]


def bit_of(axis, bit):
    return (lax.axis_index(axis) // (1 << bit)) % 2


def call(kernel, name, ins, outs, scratch=()):
    specs = [pl.BlockSpec(memory_space=space) for space, _ in ins]
    ins = [
        (space, pltpu.with_memory_space_constraint(a, HBM) if space == HBM else a)
        for space, a in ins
    ]
    return pl.pallas_call(
        kernel,
        name=name,
        in_specs=specs,
        out_specs=tuple(pl.BlockSpec(memory_space=pltpu.VMEM) for _ in outs),
        out_shape=tuple(jax.ShapeDtypeStruct(*o) for o in outs),
        scratch_shapes=list(scratch),
        compiler_params=pltpu.CompilerParams(vmem_limit_bytes=VMEM_BYTES),
    )(*[a for _, a in ins])


V = pltpu.VMEM
HBM = pltpu.HBM


def swap(x, axis, mask):
    n = lax.axis_size(axis)
    return lax.ppermute(x, axis, [(i, i ^ mask) for i in range(n)])


def exchange(x, axis, bit):
    return swap(x, axis, 1 << bit)


def prepare_nodes(count, rows_at, row_columns, dinv, upd, rhs, outs, waits):
    acc, inv_hi, inv_lo, upd_hi, upd_lo = outs
    size = dinv.shape[1]
    width = acc.shape[2]
    lane = lax.broadcasted_iota(jnp.int32, (size, size), 1).astype(F32)
    for k in range(count):
        for c in waits[k]:
            c.wait()
        inv_hi[k], inv_lo[k] = split(dinv[k])
        high, low = split(upd[k])
        chosen = (lane == row_columns[:, rows_at + k : rows_at + k + 1]).astype(BF16)
        upd_hi[k] = dot1(chosen, high, NN).astype(BF16)
        upd_lo[k] = dot1(chosen, low, NN).astype(BF16)
        turned = rhs[k].T
        for h in range(HALVES):
            acc[h, k] = turned[h * width : (h + 1) * width]


def prepare_first_kernel(nodes, *refs):
    (rows_h, sep_h, rhs_h, dinv_h, upd_h, _), refs = refs[:6], refs[6:]
    outs, (top, row_columns, rhs_n, dinv_n, upd_n), refs = refs[:5], refs[5:10], refs[10:]
    rhs_v, dinv_v, upd_v, square, rows, sep, sems, small = refs
    cols = rhs_v.shape[2]
    width = cols // HALVES
    first = nodes // 2
    few = [
        pltpu.make_async_copy(src, dst, small.at[i])
        for i, (src, dst) in enumerate(((rows_h, rows), (sep_h, sep)))
    ]
    for c in few:
        c.start()
    copies = []
    for k in range(nodes):
        ins = (upd_v, dinv_v, rhs_v) if k < first else (upd_n, dinv_n, rhs_n)
        group = [
            pltpu.make_async_copy(src.at[k], dst.at[k % first], sems.at[i, k])
            for i, (src, dst) in enumerate(zip((upd_h, dinv_h, rhs_h), ins))
        ]
        for c in group:
            c.start()
        copies.append(group)
    front = lax.axis_index("front")
    square[...] = jnp.zeros_like(square)
    for c in few:
        c.wait()
    share = sep.shape[0]
    square[pl.ds(pl.multiple_of(front * share, 8), share), :] = sep[...]
    turned = square[...].T
    for h in range(HALVES):
        top[h] = turned[h * width : (h + 1) * width]
    row_columns[...] = rows[...].astype(F32).T
    prepare_nodes(first, 0, row_columns, dinv_v, upd_v, rhs_v, outs, copies[:first])
    for group in copies[first:]:
        for c in group:
            c.wait()


def prepare_second_kernel(first, row_columns, rhs, dinv, upd, _, *outs):
    count = rhs.shape[0]
    waits = [()] * count
    prepare_nodes(count, first, row_columns, dinv, upd, rhs, outs, waits)


def prepared(count, size, cols):
    half = ((count, size, size), BF16)
    return [((HALVES, count, cols // HALVES, size), F32), half, half, half, half]


def prepare_first(rhs, dinv, update, rows, sep, after):
    nodes, size, cols = rhs.shape
    first = nodes // 2
    some = (first, size, cols)
    big = pltpu.VMEM(some, F32)
    return call(
        lambda *refs: prepare_first_kernel(nodes, *refs),
        "prepare_first",
        [(HBM, a) for a in (rows, sep, rhs, dinv, update)] + [(pl.ANY, after)],
        prepared(first, size, cols)
        + [((HALVES, cols // HALVES, size), F32), ((size, nodes), F32)]
        + [((nodes - first, *some[1:]), F32)] * 3,
        [big, big, big, pltpu.VMEM((size, cols), F32)]
        + [pltpu.VMEM(rows.shape, jnp.int32), pltpu.VMEM(sep.shape, F32)]
        + [pltpu.SemaphoreType.DMA((3, nodes)), pltpu.SemaphoreType.DMA((2,))],
    )


def prepare_second(row_columns, rhs, dinv, update, after):
    count, size, cols = rhs.shape
    first = row_columns.shape[1] - count
    return call(
        lambda *refs: prepare_second_kernel(first, *refs),
        "prepare_second",
        [(V, a) for a in (row_columns, rhs, dinv, update)] + [(pl.ANY, after)],
        prepared(count, size, cols),
    )


def forward_kernel(nodes, fronts, *refs):
    (parent_h, acc_a, acc_b, top), parts, refs = refs[:4], (refs[4:8], refs[8:12]), refs[13:]
    solved, send, keep, square, parent, sem = refs[:6]
    accs = refs[6:]
    copy = pltpu.make_async_copy(parent_h, parent, sem)
    copy.start()
    first, width = acc_a.shape[1:3]
    for h in range(HALVES):
        for k in range(nodes):
            accs[h][k] = acc_a[h, k] if k < first else acc_b[h, k - first]
        accs[h][nodes] = top[h]
    for k in range(nodes):
        inv_hi, inv_lo, upd_hi, upd_lo = parts[k // first]
        i = k % first
        inverse = (inv_hi[i], inv_lo[i])
        update = (upd_hi[i], upd_lo[i])
        for h in range(HALVES):
            value = dot3(split(accs[h][k]), inverse, NT)
            solved[k, h * width : (h + 1) * width] = value
            moved = dot3(split(value), update, NT)
            if k + h == 0:
                copy.wait()
            above = nodes if k == nodes - 1 else parent[k]
            accs[h][above] = accs[h][above] - moved
    front = lax.axis_index("front")
    chunk = width * HALVES // fronts
    for h in range(HALVES):
        square[h * width : (h + 1) * width] = accs[h][nodes]
    low_bit = front % 2
    for i in range(fronts // 2):
        for ref, own in ((keep, low_bit), (send, 1 - low_bit)):
            start = pl.multiple_of((2 * i + own) * chunk, 8)
            ref[i * chunk : (i + 1) * chunk] = square[pl.ds(start, chunk), :]


def local_forward(parent, acc_a, acc_b, top, first_halves, second_halves, after, fronts):
    first, (width, size) = acc_a.shape[1], acc_a.shape[2:]
    nodes = first + acc_b.shape[1]
    cols = width * HALVES
    part = ((cols // 2, size), F32)
    return call(
        lambda *refs: forward_kernel(nodes, fronts, *refs),
        "local_forward",
        [(HBM, parent)]
        + [(V, a) for a in (acc_a, acc_b, top, *first_halves, *second_halves)]
        + [(pl.ANY, after)],
        [((nodes, cols, size), F32), part, part],
        [pltpu.VMEM((cols, size), F32), pltpu.SMEM((nodes,), jnp.int32), pltpu.SemaphoreType.DMA]
        + [pltpu.VMEM((nodes + 1, width, size), F32)] * HALVES,
    )


def backward_kernel(nodes, fronts, *refs):
    (parent_h, solved), parts, refs = refs[:2], (refs[2:6], refs[6:10]), refs[10:]
    pieces = refs[:fronts]
    sol, sep_out = refs[fronts : 2 + fronts]
    square, parent, staged, sep_v, sem, sems = refs[2 + fronts : 8 + fronts]
    known = refs[8 + fronts :]
    first = parts[0][0].shape[0]
    copy = pltpu.make_async_copy(parent_h, parent, sem)
    copy.start()
    chunk = pieces[0].shape[0]
    width = known[0].shape[1]
    order = [p[...] for p in pieces]
    for bit in range(fronts.bit_length() - 1):
        flip = bit_of("front", bit) == 1
        order = [jnp.where(flip, order[i ^ (1 << bit)], order[i]) for i in range(fronts)]
    for i, value in enumerate(order):
        at = i * chunk
        known[at // width][nodes, at % width : at % width + chunk] = value
    outs = []
    for k in reversed(range(nodes)):
        i = k % first
        inv_hi, inv_lo, upd_hi, upd_lo = parts[k // first]
        inverse = (inv_hi[i], inv_lo[i])
        update = (upd_hi[i], upd_lo[i])
        if k == nodes - 2:
            copy.wait()
        above = nodes if k == nodes - 1 else parent[k]
        for h in range(HALVES):
            rows = slice(h * width, (h + 1) * width)
            part = solved[k, rows] - dot3(split(known[h][above]), update, NN)
            value = dot3(split(part), inverse, NN)
            known[h][k] = value
            staged[k, :, rows] = value.T
        out = pltpu.make_async_copy(staged.at[k], sol.at[k], sems.at[k])
        out.start()
        outs.append(out)
        if k == nodes - 1:
            for h in range(HALVES):
                square[:, h * width : (h + 1) * width] = known[h][nodes].T
            share = sep_v.shape[0]
            start = pl.multiple_of(lax.axis_index("front") * share, 8)
            sep_v[...] = square[pl.ds(start, share), :]
            out = pltpu.make_async_copy(sep_v, sep_out, sems.at[nodes])
            out.start()
            outs.append(out)
    for out in outs:
        out.wait()


def local_backward(parent, solved, first_halves, second_halves, pieces):
    nodes, cols, size = solved.shape
    fronts = len(pieces)
    sol, sep = jax.ShapeDtypeStruct((nodes, size, cols), F32), ((size // fronts, cols), F32)
    ins = (solved, *first_halves, *second_halves, *pieces)
    return pl.pallas_call(
        lambda *refs: backward_kernel(nodes, fronts, *refs),
        name="local_backward",
        in_specs=[pl.BlockSpec(memory_space=HBM)] + [pl.BlockSpec(memory_space=V)] * len(ins),
        out_specs=(pl.BlockSpec(memory_space=HBM),) * 2,
        out_shape=(sol, jax.ShapeDtypeStruct(*sep)),
        scratch_shapes=[pltpu.VMEM((size, cols), F32), pltpu.SMEM((nodes,), jnp.int32)]
        + [pltpu.VMEM((nodes, size, cols), F32), pltpu.VMEM(*sep), pltpu.SemaphoreType.DMA]
        + [pltpu.SemaphoreType.DMA((nodes + 1,))]
        + [pltpu.VMEM((nodes + 1, cols // HALVES, size), F32)] * HALVES,
        compiler_params=pltpu.CompilerParams(vmem_limit_bytes=VMEM_BYTES),
    )(pltpu.with_memory_space_constraint(parent, HBM), *ins)


def stack_kernel(first, second, out, sems):
    copies = [pltpu.make_async_copy(a, out.at[i], sems.at[i]) for i, a in enumerate((first, second))]
    for c in copies:
        c.start()
    for c in copies:
        c.wait()


def block_map_kernel(fronts, *refs):
    parts = refs[:fronts]
    _, total, part, inverse_halves, square = refs[fronts:]
    front = lax.axis_index("front")
    share = parts[0].shape[1]
    for i in range(fronts):
        start = pl.multiple_of((front ^ i) * share, 8)
        square[:, pl.ds(start, share), :] = parts[i][...]
    inverse = split(square[0])
    inverse_halves[0], inverse_halves[1] = inverse
    value = -dot3(inverse, split(square[1]), NN)
    total[...] = value
    half = part.shape[1]
    send_blocks([part], [value[:half], value[half:]])


def block_map(parts, after):
    fronts = len(parts)
    size = parts[0].shape[2]
    return call(
        lambda *refs: block_map_kernel(fronts, *refs),
        "block_map",
        [(V, a) for a in parts] + [(pl.ANY, after)],
        [((size, size), F32), ((1, size // 2, size), F32), ((2, size, size), BF16)],
        [pltpu.VMEM((2, size, size), F32)],
    )


def quarters(x):
    half = x.shape[0] // 2
    return [x[i : i + half, j : j + half] for i in (0, half) for j in (0, half)]


def joined(a, b, c, d):
    first, second = jnp.concatenate([a, b], axis=1), jnp.concatenate([c, d], axis=1)
    return jnp.concatenate([first, second], axis=0)


def low_core():
    return bit_of("front", 0) == 0


def send_blocks(parts, blocks):
    count = sum(part.shape[0] for part in parts)
    low = low_core()
    i = 0
    for part in parts:
        for j in range(part.shape[0]):
            part[j] = jnp.where(low, blocks[i], blocks[len(blocks) - count + i])
            i += 1


def came_blocks(mine, pairs, total):
    low = low_core()
    mine = [m[j] for m in mine for j in range(m.shape[0])]
    pairs = [p[j] for p in pairs for j in range(p.shape[0])]
    count = len(mine)
    blocks = [jnp.where(low, mine[i], pairs[i]) for i in range(count)]
    for i in range(count, total):
        j = i - total + count
        blocks.append(jnp.where(low, pairs[j], mine[j]))
    return blocks


def k_blocks(k):
    a, b, _, d = quarters(k)
    return [a, b, d]


def k_of(blocks):
    return joined(blocks[0], blocks[1], blocks[1].T, blocks[2])


def send_maps(parts, k, t):
    for i, block in enumerate(k_blocks(k)):
        parts[0][i] = block
    send_blocks(parts[1:], quarters(t))


def first_merge_kernel(*refs):
    own, mine, pairs, _, kept, mixed, halves, curve_u, total_u, total_l, *parts = refs
    upper = bit_of("leaf", 0) == 1
    came = jnp.concatenate(came_blocks([mine], [pairs], 2), axis=0)
    mine = own[...]
    low = jnp.where(upper, came, mine)
    up = jnp.where(upper, mine, came)
    low_s, up_s = split(low), split(up)
    for ref, value in ((total_u, up_s), (total_l, low_s)):
        ref[0], ref[1] = value
    k_up = dot3(up_s, up_s, TN)
    k_up_s = split(k_up)
    curve_u[0], curve_u[1] = k_up_s
    x = dot3(k_up_s, low_s, NN)
    t = dot3(up_s, low_s, NN)
    k = dot3(low_s, low_s, TN) + dot3(low_s, split(x), TN)
    kept[0], kept[1] = k, t
    send_maps(parts, k, t)
    size = low.shape[0]
    row = lax.broadcasted_iota(jnp.int32, (size, size), 0)
    col = lax.broadcasted_iota(jnp.int32, (size, size), 1)
    unit = (row == col).astype(F32)
    keep_split(halves, jnp.where(upper, up.T, unit))
    mixed[0] = jnp.where(upper, t, low + x)
    mixed[1] = jnp.where(upper, unit, up)


def merge_kernel(bit, last, *refs):
    own, other, mine, pairs, mixed = refs[:5]
    kept, mixed_n, halves, curve_u, total_u, total_l, *parts = refs[5:]
    upper = bit_of("leaf", bit) == 1
    own_k, own_t = own[0], own[1]
    other_k, other_t = k_of(other), joined(*came_blocks([mine], [pairs], 4))
    low_s = split(jnp.where(upper, other_t, own_t))
    up_s = split(jnp.where(upper, own_t, other_t))
    k_low = jnp.where(upper, other_k, own_k)
    k_up_s = split(jnp.where(upper, own_k, other_k))
    for ref, value in ((total_u, up_s), (total_l, low_s), (curve_u, k_up_s)):
        ref[0], ref[1] = value
    x = dot3(k_up_s, low_s, NN)
    x_s = split(x)
    a, e = mixed[0], mixed[1]
    keep_split(halves, jnp.where(upper, a.T, e))
    a_s, e_s = split(a), split(e)
    a_n = jnp.where(upper, dot3(a_s, low_s, NN), a + dot3(e_s, x_s, TN))
    e_n = jnp.where(upper, e, dot3(up_s, e_s, NN))
    if last:
        kept[...] = jnp.zeros_like(kept)
        keep_split(mixed_n, jnp.where(bit_of("leaf", bit + 1) == 1, a_n.T, e_n))
    else:
        k = k_low + dot3(low_s, x_s, TN)
        t = dot3(up_s, low_s, NN)
        kept[0], kept[1] = k, t
        send_maps(parts, k, t)
        mixed_n[0], mixed_n[1] = a_n, e_n


def boundary_kernel(own, other, blocks):
    k, t = own[0], split(own[1])
    x = dot3(split(k_of(other)), t, NN)
    for i, block in enumerate(k_blocks(k + dot3(t, split(x), TN))):
        blocks[i] = block


def maps(size, last):
    both, whole = ((2, size, size), BF16), ((2, size, size), F32)
    half = size // 2
    if last:
        return [((8, 128), F32)] + [both] * 5
    sends = [((i, half, half), F32) for i in (3, 2)]
    return [whole, whole, both, both, both, both] + sends


def fold_kernel(bit, own, other, send, keep):
    total = send.shape[0]
    chunk = total
    value = own[...] + other[...]
    first, second = value[:chunk], value[chunk:]
    high = bit_of("front", bit) == 1
    send[...] = jnp.where(high, first, second)
    keep[...] = jnp.where(high, second, first)


def enter_kernel(own, other, inverse, own_map, sol, message):
    drive = own[...] + other[...]
    value = dot3(split(drive), pair(inverse), NT)
    sol[...] = value
    rows = value.shape[0]
    message[:rows] = value
    message[rows:] = dot3(split(value), split(own_map[...]), NN)


def step_kernel(bit, rounds, held, *refs):
    sol, own, other, halves, curve_u, total_u, total_l = refs[:7]
    sol_n, message = refs[7 + held], refs[8 + held :]
    last = bit == rounds - 2
    upper = bit_of("leaf", bit) == 1
    rows = sol.shape[0]
    z_own, p_own = own[:rows], own[rows:]
    if last:
        z_other = p_other = other[...]
    else:
        z_other, p_other = other[:rows], other[rows:]
    z_low = jnp.where(upper, z_other, z_own)
    p_up = jnp.where(upper, p_own, p_other)
    z_low_s = split(z_low)
    middle = p_up + dot3(z_low_s, pair(curve_u), NN)
    middle_s = split(middle)
    given = split(jnp.where(upper, z_low, middle))
    sol_n[...] = sol[...] + dot3(given, pair(halves), NN)
    z_up = z_own if last else jnp.where(upper, z_own, z_other)
    p_low = p_own if last else jnp.where(upper, p_other, p_own)
    z_new = z_up + dot3(z_low_s, pair(total_u), NT)
    p_new = p_low + dot3(middle_s, pair(total_l), NN)
    if last:
        message[0][...] = jnp.where(bit_of("leaf", bit + 1) == 1, p_new, z_new)
        message[1][...] = z_new
        return
    message[0][:rows], message[0][rows:] = z_new, p_new
    if bit == rounds - 3:
        message[1][...] = jnp.where(bit_of("leaf", bit + 1) == 1, p_new, z_new)


def turn_kernel(bit, own_z, came, blocks, given):
    value = came[...]
    middle = value + dot3(split(own_z[...]), split(k_of(blocks)), NN)
    given[...] = jnp.where(bit_of("leaf", bit) == 1, value, middle)


def passed_on(bit, last, given, received):
    away = bit_of("leaf", bit) == bit_of("leaf", last)
    return jnp.where(away, received, given)


def leave_kernel(last, sol, given, received, halves, inverse, top):
    came = passed_on(1, last, given[...], received[...])
    value = sol[...] + dot3(split(came), pair(halves), NN)
    top[...] = dot3(split(value), pair(inverse), NN)


def gather_front(x, bits):
    pieces = {0: x}
    for bit in reversed(range(bits)):
        for i in list(pieces):
            pieces[i | (1 << bit)] = exchange(pieces[i], "front", bit)
    return [pieces[i] for i in range(1 << bits)]


def local(rhs_local, dinv_local, update_local, parent, row_blocks, sep_rhs, sep_dinv, sep_coupling):
    fronts, leaves = lax.axis_size("front"), lax.axis_size("leaf")
    front_bits, rounds = fronts.bit_length() - 1, leaves.bit_length() - 1
    size = sep_dinv.shape[1]
    cols = sep_rhs.shape[1]
    chunk = cols // fronts

    (stacked,) = call(
        stack_kernel,
        "stack",
        [(HBM, sep_dinv), (HBM, sep_coupling)],
        [((2, *sep_dinv.shape), F32)],
        [pltpu.SemaphoreType.DMA((2,))],
    )
    came = {0: stacked}
    for bit in reversed(range(1, front_bits)):
        for i in list(came):
            came[i | (1 << bit)] = exchange(came[i], "front", bit)
    came[1] = exchange(stacked, "front", 0)
    acc_a, *first_halves = prepare_first(
        rhs_local, dinv_local, update_local, row_blocks, sep_rhs, stacked
    )
    first_halves, (top, row_columns, *raw) = first_halves[:4], first_halves[4:]
    for i in range(2, fronts, 2):
        held, _ = lax.optimization_barrier((came[i], acc_a))
        came[i + 1] = exchange(held, "front", 0)
    acc_b, *second_halves = prepare_second(row_columns, *raw, acc_a)
    own_map, part, inverse = block_map([came[i] for i in range(fronts)], acc_b)
    mine = exchange(part, "leaf", 0)
    solved, send, keep = local_forward(
        parent, acc_a, acc_b, top, first_halves, second_halves, own_map, fronts
    )
    mine, send = lax.optimization_barrier((mine, send))
    pairs = exchange(mine, "front", 0)
    for bit in range(front_bits):
        received = exchange(send, "front", bit)
        if bit + 1 < front_bits:
            half = ((keep.shape[0] // 2, size), F32)
            send, keep = call(
                lambda *refs, bit=bit: fold_kernel(bit + 1, *refs),
                "fold",
                [(V, keep), (V, received)],
                [half, half],
            )
    kept, mixed, *tools = call(
        first_merge_kernel,
        "merge_0",
        [(V, own_map), (V, mine), (V, pairs), (pl.ANY, send)],
        maps(size, False),
    )
    tools, parts = tools[:4], tools[4:]
    sol, message = call(
        enter_kernel,
        "enter",
        [(V, keep), (V, received), (V, inverse), (V, own_map)],
        [((chunk, size), F32), ((2 * chunk, size), F32)],
    )
    share = ((chunk, size), F32)
    middle = leaves // 2
    boundary = [(middle - 2 + i, middle + i) for i in range(2)]
    boundary += [(j, i) for i, j in boundary]
    paired = {i for i, _ in boundary}
    boundary += [(i, i ^ 1) for i in range(leaves) if i not in paired]
    for bit in range(rounds - 1):
        last = bit == rounds - 2
        received = exchange(short[0] if last else message, "leaf", bit)
        ahead = []
        if not last:
            other, mine = [exchange(part, "leaf", bit + 1) for part in parts]
            ahead = [other]
        if bit == rounds - 3:
            ahead = (blocks,) = call(
                boundary_kernel, "boundary", [(V, kept), (V, other)], [(other.shape, F32)]
            )
            blocks = lax.ppermute(blocks, "leaf", boundary)
        sol, *message = call(
            lambda *refs, bit=bit: step_kernel(bit, rounds, len(ahead), *refs),
            f"step_{bit}",
            [(V, a) for a in (sol, message, received, *tools)] + [(pl.ANY, a) for a in ahead],
            [share] + ([share] if last else [((2 * chunk, size), F32)]) + [share] * (bit >= rounds - 3),
        )
        if not last:
            message, *short = message
            mine, _ = lax.optimization_barrier((mine, sol))
            pairs = exchange(mine, "front", 0)
            last = bit == rounds - 3
            kept, mixed, *tools = call(
                lambda *refs, bit=bit, last=last: merge_kernel(bit + 1, last, *refs),
                f"merge_{bit + 1}",
                [(V, a) for a in (kept, other, mine, pairs, mixed)],
                maps(size, last),
            )
            tools, parts = tools[:4], tools[4:]
    came = lax.ppermute(message[0], "leaf", boundary)
    (given,) = call(
        lambda *refs: turn_kernel(rounds - 1, *refs),
        "turn",
        [(V, a) for a in (message[1], came, blocks)],
        [share],
    )
    for bit in reversed(range(2, rounds - 1)):
        given = passed_on(bit, rounds - 1, given, exchange(given, "leaf", bit))
    received = exchange(given, "leaf", 1)
    (top,) = call(
        lambda *refs: leave_kernel(rounds - 1, *refs),
        "leave",
        [(V, a) for a in (sol, given, received, mixed, inverse)],
        [share],
    )
    pieces = gather_front(top, front_bits)
    sol_local, sep_solution = local_backward(
        parent, solved, first_halves, second_halves, pieces
    )
    return (sol_local, sep_solution)


def solution(mesh):
    spread3 = P(("leaf", "front"), None, None)
    spread2 = P(("leaf", "front"), None)
    spread1 = P(("leaf", "front"))
    return jax.shard_map(
        local,
        mesh=mesh,
        in_specs=(spread3, spread3, spread3, spread1, spread2, spread2, spread2, spread2),
        out_specs=(spread3, spread2),
        check_vma=False,
    )
```

```python
import jax
import jax.numpy as jnp
from jax import lax
from jax.experimental import pallas as pl
from jax.experimental.pallas import tpu as pltpu
from jax.sharding import PartitionSpec as P

F32 = jnp.float32
BF16 = jnp.bfloat16
NN = (((1,), (0,)), ((), ()))
NT = (((1,), (1,)), ((), ()))
TN = (((0,), (0,)), ((), ()))
VMEM_BYTES = 24 << 20
HALVES = 2


def split(x):
    high = x.astype(BF16)
    return high, (x - high.astype(F32)).astype(BF16)


def dot1(a, b, dims):
    return lax.dot_general(a, b, dims, preferred_element_type=F32)


def dot3(a, b, dims):
    axis = 1 - dims[0][0][0]
    rows = a[0].shape[axis]
    both = dot1(jnp.concatenate(a, axis=axis), b[0], dims)
    return both[:rows] + (both[rows:] + dot1(a[0], b[1], dims))


def keep_split(ref, value):
    ref[0], ref[1] = split(value)


def pair(ref):
    return ref[0], ref[1]


def bit_of(axis, bit):
    return (lax.axis_index(axis) // (1 << bit)) % 2


def call(kernel, name, ins, outs, scratch=()):
    specs = [pl.BlockSpec(memory_space=space) for space, _ in ins]
    ins = [
        (space, pltpu.with_memory_space_constraint(a, HBM) if space == HBM else a)
        for space, a in ins
    ]
    return pl.pallas_call(
        kernel,
        name=name,
        in_specs=specs,
        out_specs=tuple(pl.BlockSpec(memory_space=pltpu.VMEM) for _ in outs),
        out_shape=tuple(jax.ShapeDtypeStruct(*o) for o in outs),
        scratch_shapes=list(scratch),
        compiler_params=pltpu.CompilerParams(vmem_limit_bytes=VMEM_BYTES),
    )(*[a for _, a in ins])


V = pltpu.VMEM
HBM = pltpu.HBM


def swap(x, axis, mask):
    n = lax.axis_size(axis)
    return lax.ppermute(x, axis, [(i, i ^ mask) for i in range(n)])


def exchange(x, axis, bit):
    return swap(x, axis, 1 << bit)


def node_copies(nodes, sources, targets, sems):
    copies = []
    for i, k in enumerate(nodes):
        group = [
            pltpu.make_async_copy(src.at[k], dst.at[i], sems.at[j, i])
            for j, (src, dst) in enumerate(zip(sources, targets))
        ]
        for c in group:
            c.start()
        copies.append(group)
    return copies


def prepare_node(node, k, waits, row_columns, values, halves):
    upd, dinv, rhs = values
    inv_hi, inv_lo, upd_hi, upd_lo = halves
    size = dinv.shape[1]
    for c in waits:
        c.wait()
    lane = lax.broadcasted_iota(jnp.int32, (size, size), 1).astype(F32)
    inv_hi[k], inv_lo[k] = split(dinv[k])
    high, low = split(upd[k])
    chosen = (lane == row_columns[:, node : node + 1]).astype(BF16)
    upd_hi[k] = dot1(chosen, high, NN).astype(BF16)
    upd_lo[k] = dot1(chosen, low, NN).astype(BF16)
    return rhs[k].T


def prepare_first_kernel(nodes, *refs):
    (rows_h, sep_h, rhs_h, dinv_h, upd_h, _), refs = refs[:6], refs[6:]
    outs, (top, row_columns), refs = refs[:5], refs[5:7], refs[7:]
    rhs_v, dinv_v, upd_v, square, rows, sep, sems, small = refs
    cols = rhs_v.shape[2]
    width = cols // HALVES
    first = nodes // 2
    few = [
        pltpu.make_async_copy(src, dst, small.at[i])
        for i, (src, dst) in enumerate(((rows_h, rows), (sep_h, sep)))
    ]
    for c in few:
        c.start()
    copies = node_copies(range(first), (upd_h, dinv_h, rhs_h), (upd_v, dinv_v, rhs_v), sems)
    front = lax.axis_index("front")
    square[...] = jnp.zeros_like(square)
    for c in few:
        c.wait()
    share = sep.shape[0]
    square[pl.ds(pl.multiple_of(front * share, 8), share), :] = sep[...]
    turned = square[...].T
    for h in range(HALVES):
        top[h] = turned[h * width : (h + 1) * width]
    row_columns[...] = rows[...].astype(F32).T
    acc, *halves = outs
    for k in range(first):
        turned = prepare_node(k, k, copies[k], row_columns, (upd_v, dinv_v, rhs_v), halves)
        for h in range(HALVES):
            acc[h, k] = turned[h * width : (h + 1) * width]


def prepared(count, size, cols):
    half = ((count, size, size), BF16)
    return [((HALVES, count, cols // HALVES, size), F32), half, half, half, half]


def prepare_first(rhs, dinv, update, rows, sep, after):
    nodes, size, cols = rhs.shape
    first = nodes // 2
    some = (first, size, cols)
    big = pltpu.VMEM(some, F32)
    return call(
        lambda *refs: prepare_first_kernel(nodes, *refs),
        "prepare_first",
        [(HBM, a) for a in (rows, sep, rhs, dinv, update)] + [(pl.ANY, after)],
        prepared(first, size, cols)
        + [((HALVES, cols // HALVES, size), F32), ((size, nodes), F32)],
        [big, big, big, pltpu.VMEM((size, cols), F32)]
        + [pltpu.VMEM(rows.shape, jnp.int32), pltpu.VMEM(sep.shape, F32)]
        + [pltpu.SemaphoreType.DMA((3, first)), pltpu.SemaphoreType.DMA((2,))],
    )


def forward_kernel(nodes, fronts, *refs):
    (parent_h, rhs_h, dinv_h, upd_h, acc, top, row_columns), refs = refs[:7], refs[7:]
    first_halves, (solved, send, keep), halves, refs = refs[:4], refs[5:8], refs[8:12], refs[12:]
    square, parent, rhs_v, dinv_v, upd_v, sem, sems = refs[:7]
    accs = refs[7:]
    first, width = acc.shape[1:3]
    copy = pltpu.make_async_copy(parent_h, parent, sem)
    copy.start()
    values = (upd_v, dinv_v, rhs_v)
    copies = node_copies(range(first, nodes), (upd_h, dinv_h, rhs_h), values, sems)
    for h in range(HALVES):
        for k in range(first):
            accs[h][k] = acc[h, k]
        accs[h][first:nodes] = jnp.zeros_like(accs[h][first:nodes])
        accs[h][nodes] = top[h]
    ready = 0
    for k in range(nodes):
        while ready < nodes - first and ready < k:
            node = first + ready
            turned = prepare_node(node, ready, copies[ready], row_columns, values, halves)
            for h in range(HALVES):
                accs[h][node] = accs[h][node] + turned[h * width : (h + 1) * width]
            ready += 1
        inv_hi, inv_lo, upd_hi, upd_lo = first_halves if k < first else halves
        i = k % first
        inverse = (inv_hi[i], inv_lo[i])
        update = (upd_hi[i], upd_lo[i])
        for h in range(HALVES):
            value = dot3(split(accs[h][k]), inverse, NT)
            solved[k, h * width : (h + 1) * width] = value
            moved = dot3(split(value), update, NT)
            if k + h == 0:
                copy.wait()
            above = nodes if k == nodes - 1 else parent[k]
            accs[h][above] = accs[h][above] - moved
    front = lax.axis_index("front")
    chunk = width * HALVES // fronts
    for h in range(HALVES):
        square[h * width : (h + 1) * width] = accs[h][nodes]
    low_bit = front % 2
    for i in range(fronts // 2):
        for ref, own in ((keep, low_bit), (send, 1 - low_bit)):
            start = pl.multiple_of((2 * i + own) * chunk, 8)
            ref[i * chunk : (i + 1) * chunk] = square[pl.ds(start, chunk), :]


def local_forward(parent, rhs, dinv, update, acc, top, row_columns, first_halves, after, fronts):
    nodes, size, cols = rhs.shape
    first, width = acc.shape[1:3]
    count = nodes - first
    part = ((cols // 2, size), F32)
    half = ((count, size, size), BF16)
    big = pltpu.VMEM((count, size, cols), F32)
    return call(
        lambda *refs: forward_kernel(nodes, fronts, *refs),
        "local_forward",
        [(HBM, a) for a in (parent, rhs, dinv, update)]
        + [(V, a) for a in (acc, top, row_columns, *first_halves)]
        + [(pl.ANY, after)],
        [((nodes, cols, size), F32), part, part, half, half, half, half],
        [pltpu.VMEM((cols, size), F32), pltpu.SMEM((nodes,), jnp.int32), big, big, big]
        + [pltpu.SemaphoreType.DMA, pltpu.SemaphoreType.DMA((3, count))]
        + [pltpu.VMEM((nodes + 1, width, size), F32)] * HALVES,
    )


def backward_kernel(nodes, fronts, *refs):
    (parent_h, solved), parts, refs = refs[:2], (refs[2:6], refs[6:10]), refs[10:]
    pieces = refs[:fronts]
    sol, sep_out = refs[fronts : 2 + fronts]
    square, parent, staged, sep_v, sem, sems = refs[2 + fronts : 8 + fronts]
    known = refs[8 + fronts :]
    first = parts[0][0].shape[0]
    copy = pltpu.make_async_copy(parent_h, parent, sem)
    copy.start()
    chunk = pieces[0].shape[0]
    width = known[0].shape[1]
    order = [p[...] for p in pieces]
    for bit in range(fronts.bit_length() - 1):
        flip = bit_of("front", bit) == 1
        order = [jnp.where(flip, order[i ^ (1 << bit)], order[i]) for i in range(fronts)]
    for i, value in enumerate(order):
        at = i * chunk
        known[at // width][nodes, at % width : at % width + chunk] = value
    outs = []
    for k in reversed(range(nodes)):
        i = k % first
        inv_hi, inv_lo, upd_hi, upd_lo = parts[k // first]
        inverse = (inv_hi[i], inv_lo[i])
        update = (upd_hi[i], upd_lo[i])
        if k == nodes - 2:
            copy.wait()
        above = nodes if k == nodes - 1 else parent[k]
        for h in range(HALVES):
            rows = slice(h * width, (h + 1) * width)
            part = solved[k, rows] - dot3(split(known[h][above]), update, NN)
            value = dot3(split(part), inverse, NN)
            known[h][k] = value
            staged[k, :, rows] = value.T
        out = pltpu.make_async_copy(staged.at[k], sol.at[k], sems.at[k])
        out.start()
        outs.append(out)
        if k == nodes - 1:
            for h in range(HALVES):
                square[:, h * width : (h + 1) * width] = known[h][nodes].T
            share = sep_v.shape[0]
            start = pl.multiple_of(lax.axis_index("front") * share, 8)
            sep_v[...] = square[pl.ds(start, share), :]
            out = pltpu.make_async_copy(sep_v, sep_out, sems.at[nodes])
            out.start()
            outs.append(out)
    for out in outs:
        out.wait()


def local_backward(parent, solved, first_halves, second_halves, pieces):
    nodes, cols, size = solved.shape
    fronts = len(pieces)
    sol, sep = jax.ShapeDtypeStruct((nodes, size, cols), F32), ((size // fronts, cols), F32)
    ins = (solved, *first_halves, *second_halves, *pieces)
    return pl.pallas_call(
        lambda *refs: backward_kernel(nodes, fronts, *refs),
        name="local_backward",
        in_specs=[pl.BlockSpec(memory_space=HBM)] + [pl.BlockSpec(memory_space=V)] * len(ins),
        out_specs=(pl.BlockSpec(memory_space=HBM),) * 2,
        out_shape=(sol, jax.ShapeDtypeStruct(*sep)),
        scratch_shapes=[pltpu.VMEM((size, cols), F32), pltpu.SMEM((nodes,), jnp.int32)]
        + [pltpu.VMEM((nodes, size, cols), F32), pltpu.VMEM(*sep), pltpu.SemaphoreType.DMA]
        + [pltpu.SemaphoreType.DMA((nodes + 1,))]
        + [pltpu.VMEM((nodes + 1, cols // HALVES, size), F32)] * HALVES,
        compiler_params=pltpu.CompilerParams(vmem_limit_bytes=VMEM_BYTES),
    )(pltpu.with_memory_space_constraint(parent, HBM), *ins)


def stack_kernel(first, second, out, sems):
    copies = [pltpu.make_async_copy(a, out.at[i], sems.at[i]) for i, a in enumerate((first, second))]
    for c in copies:
        c.start()
    for c in copies:
        c.wait()


def block_map_kernel(fronts, *refs):
    parts = refs[:fronts]
    _, total, part, inverse_halves, square = refs[fronts:]
    front = lax.axis_index("front")
    share = parts[0].shape[1]
    for i in range(fronts):
        start = pl.multiple_of((front ^ i) * share, 8)
        square[:, pl.ds(start, share), :] = parts[i][...]
    inverse = split(square[0])
    inverse_halves[0], inverse_halves[1] = inverse
    value = -dot3(inverse, split(square[1]), NN)
    total[...] = value
    half = part.shape[1]
    send_blocks([part], [value[:half], value[half:]])


def block_map(parts, after):
    fronts = len(parts)
    size = parts[0].shape[2]
    return call(
        lambda *refs: block_map_kernel(fronts, *refs),
        "block_map",
        [(V, a) for a in parts] + [(pl.ANY, after)],
        [((size, size), F32), ((1, size // 2, size), F32), ((2, size, size), BF16)],
        [pltpu.VMEM((2, size, size), F32)],
    )


def quarters(x):
    half = x.shape[0] // 2
    return [x[i : i + half, j : j + half] for i in (0, half) for j in (0, half)]


def joined(a, b, c, d):
    first, second = jnp.concatenate([a, b], axis=1), jnp.concatenate([c, d], axis=1)
    return jnp.concatenate([first, second], axis=0)


def low_core():
    return bit_of("front", 0) == 0


def send_blocks(parts, blocks):
    count = sum(part.shape[0] for part in parts)
    low = low_core()
    i = 0
    for part in parts:
        for j in range(part.shape[0]):
            part[j] = jnp.where(low, blocks[i], blocks[len(blocks) - count + i])
            i += 1


def came_blocks(mine, pairs, total):
    low = low_core()
    mine = [m[j] for m in mine for j in range(m.shape[0])]
    pairs = [p[j] for p in pairs for j in range(p.shape[0])]
    count = len(mine)
    blocks = [jnp.where(low, mine[i], pairs[i]) for i in range(count)]
    for i in range(count, total):
        j = i - total + count
        blocks.append(jnp.where(low, pairs[j], mine[j]))
    return blocks


def k_blocks(k):
    a, b, _, d = quarters(k)
    return [a, b, d]


def k_of(blocks):
    return joined(blocks[0], blocks[1], blocks[1].T, blocks[2])


def send_maps(parts, k, t):
    for i, block in enumerate(k_blocks(k)):
        parts[0][i] = block
    send_blocks(parts[1:], quarters(t))


def first_merge_kernel(*refs):
    own, mine, pairs, _, kept, mixed, halves, curve_u, total_u, total_l, *parts = refs
    upper = bit_of("leaf", 0) == 1
    came = jnp.concatenate(came_blocks([mine], [pairs], 2), axis=0)
    mine = own[...]
    low = jnp.where(upper, came, mine)
    up = jnp.where(upper, mine, came)
    low_s, up_s = split(low), split(up)
    for ref, value in ((total_u, up_s), (total_l, low_s)):
        ref[0], ref[1] = value
    k_up = dot3(up_s, up_s, TN)
    k_up_s = split(k_up)
    curve_u[0], curve_u[1] = k_up_s
    x = dot3(k_up_s, low_s, NN)
    t = dot3(up_s, low_s, NN)
    k = dot3(low_s, low_s, TN) + dot3(low_s, split(x), TN)
    kept[0], kept[1] = k, t
    send_maps(parts, k, t)
    size = low.shape[0]
    row = lax.broadcasted_iota(jnp.int32, (size, size), 0)
    col = lax.broadcasted_iota(jnp.int32, (size, size), 1)
    unit = (row == col).astype(F32)
    keep_split(halves, jnp.where(upper, up.T, unit))
    mixed[0] = jnp.where(upper, t, low + x)
    mixed[1] = jnp.where(upper, unit, up)


def merge_kernel(bit, last, *refs):
    own, other, mine, pairs, mixed = refs[:5]
    kept, mixed_n, halves, curve_u, total_u, total_l, *parts = refs[5:]
    upper = bit_of("leaf", bit) == 1
    own_k, own_t = own[0], own[1]
    other_k, other_t = k_of(other), joined(*came_blocks([mine], [pairs], 4))
    low_s = split(jnp.where(upper, other_t, own_t))
    up_s = split(jnp.where(upper, own_t, other_t))
    k_low = jnp.where(upper, other_k, own_k)
    k_up_s = split(jnp.where(upper, own_k, other_k))
    for ref, value in ((total_u, up_s), (total_l, low_s), (curve_u, k_up_s)):
        ref[0], ref[1] = value
    x = dot3(k_up_s, low_s, NN)
    x_s = split(x)
    a, e = mixed[0], mixed[1]
    keep_split(halves, jnp.where(upper, a.T, e))
    a_s, e_s = split(a), split(e)
    a_n = jnp.where(upper, dot3(a_s, low_s, NN), a + dot3(e_s, x_s, TN))
    e_n = jnp.where(upper, e, dot3(up_s, e_s, NN))
    if last:
        kept[...] = jnp.zeros_like(kept)
        keep_split(mixed_n, jnp.where(bit_of("leaf", bit + 1) == 1, a_n.T, e_n))
    else:
        k = k_low + dot3(low_s, x_s, TN)
        t = dot3(up_s, low_s, NN)
        kept[0], kept[1] = k, t
        send_maps(parts, k, t)
        mixed_n[0], mixed_n[1] = a_n, e_n


def boundary_kernel(own, other, blocks):
    k, t = own[0], split(own[1])
    x = dot3(split(k_of(other)), t, NN)
    for i, block in enumerate(k_blocks(k + dot3(t, split(x), TN))):
        blocks[i] = block


def maps(size, last):
    both, whole = ((2, size, size), BF16), ((2, size, size), F32)
    half = size // 2
    if last:
        return [((8, 128), F32)] + [both] * 5
    sends = [((i, half, half), F32) for i in (3, 2)]
    return [whole, whole, both, both, both, both] + sends


def fold_kernel(bit, own, other, send, keep):
    total = send.shape[0]
    chunk = total
    value = own[...] + other[...]
    first, second = value[:chunk], value[chunk:]
    high = bit_of("front", bit) == 1
    send[...] = jnp.where(high, first, second)
    keep[...] = jnp.where(high, second, first)


def enter_kernel(own, other, inverse, own_map, sol, message):
    drive = own[...] + other[...]
    value = dot3(split(drive), pair(inverse), NT)
    sol[...] = value
    rows = value.shape[0]
    message[:rows] = value
    message[rows:] = dot3(split(value), split(own_map[...]), NN)


def step_kernel(bit, rounds, held, *refs):
    sol, own, other, halves, curve_u, total_u, total_l = refs[:7]
    sol_n, message = refs[7 + held], refs[8 + held :]
    last = bit == rounds - 2
    upper = bit_of("leaf", bit) == 1
    rows = sol.shape[0]
    z_own, p_own = own[:rows], own[rows:]
    if last:
        z_other = p_other = other[...]
    else:
        z_other, p_other = other[:rows], other[rows:]
    z_low = jnp.where(upper, z_other, z_own)
    p_up = jnp.where(upper, p_own, p_other)
    z_low_s = split(z_low)
    middle = p_up + dot3(z_low_s, pair(curve_u), NN)
    middle_s = split(middle)
    given = split(jnp.where(upper, z_low, middle))
    sol_n[...] = sol[...] + dot3(given, pair(halves), NN)
    z_up = z_own if last else jnp.where(upper, z_own, z_other)
    p_low = p_own if last else jnp.where(upper, p_other, p_own)
    z_new = z_up + dot3(z_low_s, pair(total_u), NT)
    p_new = p_low + dot3(middle_s, pair(total_l), NN)
    if last:
        message[0][...] = jnp.where(bit_of("leaf", bit + 1) == 1, p_new, z_new)
        message[1][...] = z_new
        return
    message[0][:rows], message[0][rows:] = z_new, p_new
    if bit == rounds - 3:
        message[1][...] = jnp.where(bit_of("leaf", bit + 1) == 1, p_new, z_new)


def turn_kernel(bit, own_z, came, blocks, given):
    value = came[...]
    middle = value + dot3(split(own_z[...]), split(k_of(blocks)), NN)
    given[...] = jnp.where(bit_of("leaf", bit) == 1, value, middle)


def passed_on(bit, last, given, received):
    away = bit_of("leaf", bit) == bit_of("leaf", last)
    return jnp.where(away, received, given)


def leave_kernel(last, sol, given, received, halves, inverse, top):
    came = passed_on(1, last, given[...], received[...])
    value = sol[...] + dot3(split(came), pair(halves), NN)
    top[...] = dot3(split(value), pair(inverse), NN)


def gather_front(x, bits):
    pieces = {0: x}
    for bit in reversed(range(bits)):
        for i in list(pieces):
            pieces[i | (1 << bit)] = exchange(pieces[i], "front", bit)
    return [pieces[i] for i in range(1 << bits)]


def local(rhs_local, dinv_local, update_local, parent, row_blocks, sep_rhs, sep_dinv, sep_coupling):
    fronts, leaves = lax.axis_size("front"), lax.axis_size("leaf")
    front_bits, rounds = fronts.bit_length() - 1, leaves.bit_length() - 1
    size = sep_dinv.shape[1]
    cols = sep_rhs.shape[1]
    chunk = cols // fronts

    (stacked,) = call(
        stack_kernel,
        "stack",
        [(HBM, sep_dinv), (HBM, sep_coupling)],
        [((2, *sep_dinv.shape), F32)],
        [pltpu.SemaphoreType.DMA((2,))],
    )
    came = {0: stacked}
    for bit in reversed(range(1, front_bits)):
        for i in list(came):
            came[i | (1 << bit)] = exchange(came[i], "front", bit)
    came[1] = exchange(stacked, "front", 0)
    acc_a, *first_halves = prepare_first(
        rhs_local, dinv_local, update_local, row_blocks, sep_rhs, stacked
    )
    first_halves, (top, row_columns) = first_halves[:4], first_halves[4:]
    for i in range(2, fronts, 2):
        held, _ = lax.optimization_barrier((came[i], acc_a))
        came[i + 1] = exchange(held, "front", 0)
    own_map, part, inverse = block_map([came[i] for i in range(fronts)], acc_a)
    mine = exchange(part, "leaf", 0)
    solved, send, keep, *second_halves = local_forward(
        parent,
        rhs_local,
        dinv_local,
        update_local,
        acc_a,
        top,
        row_columns,
        first_halves,
        own_map,
        fronts,
    )
    mine, send = lax.optimization_barrier((mine, send))
    pairs = exchange(mine, "front", 0)
    for bit in range(front_bits):
        received = exchange(send, "front", bit)
        if bit + 1 < front_bits:
            half = ((keep.shape[0] // 2, size), F32)
            send, keep = call(
                lambda *refs, bit=bit: fold_kernel(bit + 1, *refs),
                "fold",
                [(V, keep), (V, received)],
                [half, half],
            )
    kept, mixed, *tools = call(
        first_merge_kernel,
        "merge_0",
        [(V, own_map), (V, mine), (V, pairs), (pl.ANY, send)],
        maps(size, False),
    )
    tools, parts = tools[:4], tools[4:]
    sol, message = call(
        enter_kernel,
        "enter",
        [(V, keep), (V, received), (V, inverse), (V, own_map)],
        [((chunk, size), F32), ((2 * chunk, size), F32)],
    )
    share = ((chunk, size), F32)
    middle = leaves // 2
    boundary = [(middle - 2 + i, middle + i) for i in range(2)]
    boundary += [(j, i) for i, j in boundary]
    paired = {i for i, _ in boundary}
    boundary += [(i, i ^ 1) for i in range(leaves) if i not in paired]
    for bit in range(rounds - 1):
        last = bit == rounds - 2
        received = exchange(short[0] if last else message, "leaf", bit)
        ahead = []
        if not last:
            other, mine = [exchange(part, "leaf", bit + 1) for part in parts]
            ahead = [other]
        if bit == rounds - 3:
            ahead = (blocks,) = call(
                boundary_kernel, "boundary", [(V, kept), (V, other)], [(other.shape, F32)]
            )
            blocks = lax.ppermute(blocks, "leaf", boundary)
        sol, *message = call(
            lambda *refs, bit=bit: step_kernel(bit, rounds, len(ahead), *refs),
            f"step_{bit}",
            [(V, a) for a in (sol, message, received, *tools)] + [(pl.ANY, a) for a in ahead],
            [share] + ([share] if last else [((2 * chunk, size), F32)]) + [share] * (bit >= rounds - 3),
        )
        if not last:
            message, *short = message
            mine, _ = lax.optimization_barrier((mine, sol))
            pairs = exchange(mine, "front", 0)
            last = bit == rounds - 3
            kept, mixed, *tools = call(
                lambda *refs, bit=bit, last=last: merge_kernel(bit + 1, last, *refs),
                f"merge_{bit + 1}",
                [(V, a) for a in (kept, other, mine, pairs, mixed)],
                maps(size, last),
            )
            tools, parts = tools[:4], tools[4:]
    came = lax.ppermute(message[0], "leaf", boundary)
    (given,) = call(
        lambda *refs: turn_kernel(rounds - 1, *refs),
        "turn",
        [(V, a) for a in (message[1], came, blocks)],
        [share],
    )
    for bit in reversed(range(2, rounds - 1)):
        given = passed_on(bit, rounds - 1, given, exchange(given, "leaf", bit))
    received = exchange(given, "leaf", 1)
    (top,) = call(
        lambda *refs: leave_kernel(rounds - 1, *refs),
        "leave",
        [(V, a) for a in (sol, given, received, mixed, inverse)],
        [share],
    )
    pieces = gather_front(top, front_bits)
    sol_local, sep_solution = local_backward(
        parent, solved, first_halves, second_halves, pieces
    )
    return (sol_local, sep_solution)


def solution(mesh):
    spread3 = P(("leaf", "front"), None, None)
    spread2 = P(("leaf", "front"), None)
    spread1 = P(("leaf", "front"))
    return jax.shard_map(
        local,
        mesh=mesh,
        in_specs=(spread3, spread3, spread3, spread1, spread2, spread2, spread2, spread2),
        out_specs=(spread3, spread2),
        check_vma=False,
    )
```

```python
import jax
import jax.numpy as jnp
from jax import lax
from jax.experimental import pallas as pl
from jax.experimental.pallas import tpu as pltpu
from jax.sharding import PartitionSpec as P

F32 = jnp.float32
BF16 = jnp.bfloat16
NN = (((1,), (0,)), ((), ()))
NT = (((1,), (1,)), ((), ()))
TN = (((0,), (0,)), ((), ()))
VMEM_BYTES = 24 << 20
HALVES = 2


def split(x):
    high = x.astype(BF16)
    return high, (x - high.astype(F32)).astype(BF16)


def dot1(a, b, dims):
    return lax.dot_general(a, b, dims, preferred_element_type=F32)


def dot3(a, b, dims):
    axis = 1 - dims[0][0][0]
    rows = a[0].shape[axis]
    both = dot1(jnp.concatenate(a, axis=axis), b[0], dims)
    return both[:rows] + (both[rows:] + dot1(a[0], b[1], dims))


def keep_split(ref, value):
    ref[0], ref[1] = split(value)


def pair(ref):
    return ref[0], ref[1]


def bit_of(axis, bit):
    return (lax.axis_index(axis) // (1 << bit)) % 2


def call(kernel, name, ins, outs, scratch=()):
    specs = [pl.BlockSpec(memory_space=space) for space, _ in ins]
    ins = [
        (space, pltpu.with_memory_space_constraint(a, HBM) if space == HBM else a)
        for space, a in ins
    ]
    return pl.pallas_call(
        kernel,
        name=name,
        in_specs=specs,
        out_specs=tuple(pl.BlockSpec(memory_space=pltpu.VMEM) for _ in outs),
        out_shape=tuple(jax.ShapeDtypeStruct(*o) for o in outs),
        scratch_shapes=list(scratch),
        compiler_params=pltpu.CompilerParams(vmem_limit_bytes=VMEM_BYTES),
    )(*[a for _, a in ins])


V = pltpu.VMEM
HBM = pltpu.HBM


def swap(x, axis, mask):
    n = lax.axis_size(axis)
    return lax.ppermute(x, axis, [(i, i ^ mask) for i in range(n)])


def exchange(x, axis, bit):
    return swap(x, axis, 1 << bit)


def prepare_nodes(count, rows_at, row_columns, dinv, upd, rhs, outs, waits):
    acc, inv_hi, inv_lo, upd_hi, upd_lo = outs
    size = dinv.shape[1]
    width = acc.shape[2]
    lane = lax.broadcasted_iota(jnp.int32, (size, size), 1).astype(F32)
    for k in range(count):
        for c in waits[k]:
            c.wait()
        inv_hi[k], inv_lo[k] = split(dinv[k])
        high, low = split(upd[k])
        chosen = (lane == row_columns[:, rows_at + k : rows_at + k + 1]).astype(BF16)
        upd_hi[k] = dot1(chosen, high, NN).astype(BF16)
        upd_lo[k] = dot1(chosen, low, NN).astype(BF16)
        turned = rhs[k].T
        for h in range(HALVES):
            acc[h, k] = turned[h * width : (h + 1) * width]


def prepare_first_kernel(nodes, *refs):
    (rows_h, sep_h, rhs_h, dinv_h, upd_h, _), refs = refs[:6], refs[6:]
    outs, (top, row_columns, rhs_n, dinv_n, upd_n), refs = refs[:5], refs[5:10], refs[10:]
    rhs_v, dinv_v, upd_v, square, rows, sep, sems, small = refs
    cols = rhs_v.shape[2]
    width = cols // HALVES
    first = nodes // 2
    few = [
        pltpu.make_async_copy(src, dst, small.at[i])
        for i, (src, dst) in enumerate(((rows_h, rows), (sep_h, sep)))
    ]
    for c in few:
        c.start()
    copies = []
    for k in range(nodes):
        ins = (upd_v, dinv_v, rhs_v) if k < first else (upd_n, dinv_n, rhs_n)
        group = [
            pltpu.make_async_copy(src.at[k], dst.at[k % first], sems.at[i, k])
            for i, (src, dst) in enumerate(zip((upd_h, dinv_h, rhs_h), ins))
        ]
        for c in group:
            c.start()
        copies.append(group)
    front = lax.axis_index("front")
    square[...] = jnp.zeros_like(square)
    for c in few:
        c.wait()
    share = sep.shape[0]
    square[pl.ds(pl.multiple_of(front * share, 8), share), :] = sep[...]
    turned = square[...].T
    for h in range(HALVES):
        top[h] = turned[h * width : (h + 1) * width]
    row_columns[...] = rows[...].astype(F32).T
    prepare_nodes(first, 0, row_columns, dinv_v, upd_v, rhs_v, outs, copies[:first])
    for group in copies[first:]:
        for c in group:
            c.wait()


def prepare_second_kernel(first, row_columns, rhs, dinv, upd, _, *outs):
    count = rhs.shape[0]
    waits = [()] * count
    prepare_nodes(count, first, row_columns, dinv, upd, rhs, outs, waits)


def prepared(count, size, cols):
    half = ((count, size, size), BF16)
    return [((HALVES, count, cols // HALVES, size), F32), half, half, half, half]


def prepare_first(rhs, dinv, update, rows, sep, after):
    nodes, size, cols = rhs.shape
    first = nodes // 2
    some = (first, size, cols)
    big = pltpu.VMEM(some, F32)
    return call(
        lambda *refs: prepare_first_kernel(nodes, *refs),
        "prepare_first",
        [(HBM, a) for a in (rows, sep, rhs, dinv, update)] + [(pl.ANY, after)],
        prepared(first, size, cols)
        + [((HALVES, cols // HALVES, size), F32), ((size, nodes), F32)]
        + [((nodes - first, *some[1:]), F32)] * 3,
        [big, big, big, pltpu.VMEM((size, cols), F32)]
        + [pltpu.VMEM(rows.shape, jnp.int32), pltpu.VMEM(sep.shape, F32)]
        + [pltpu.SemaphoreType.DMA((3, nodes)), pltpu.SemaphoreType.DMA((2,))],
    )


def prepare_second(row_columns, rhs, dinv, update, after):
    count, size, cols = rhs.shape
    first = row_columns.shape[1] - count
    return call(
        lambda *refs: prepare_second_kernel(first, *refs),
        "prepare_second",
        [(V, a) for a in (row_columns, rhs, dinv, update)] + [(pl.ANY, after)],
        prepared(count, size, cols),
    )


def forward_kernel(nodes, fronts, *refs):
    (parent_h, acc_a, acc_b, top), parts, refs = refs[:4], (refs[4:8], refs[8:12]), refs[13:]
    solved, send, keep, square, parent, sem = refs[:6]
    accs = refs[6:]
    copy = pltpu.make_async_copy(parent_h, parent, sem)
    copy.start()
    first, width = acc_a.shape[1:3]
    for h in range(HALVES):
        for k in range(nodes):
            accs[h][k] = acc_a[h, k] if k < first else acc_b[h, k - first]
        accs[h][nodes] = top[h]
    for k in range(nodes):
        inv_hi, inv_lo, upd_hi, upd_lo = parts[k // first]
        i = k % first
        inverse = (inv_hi[i], inv_lo[i])
        update = (upd_hi[i], upd_lo[i])
        for h in range(HALVES):
            value = dot3(split(accs[h][k]), inverse, NT)
            solved[k, h * width : (h + 1) * width] = value
            moved = dot3(split(value), update, NT)
            if k + h == 0:
                copy.wait()
            above = nodes if k == nodes - 1 else parent[k]
            accs[h][above] = accs[h][above] - moved
    front = lax.axis_index("front")
    chunk = width * HALVES // fronts
    for h in range(HALVES):
        square[h * width : (h + 1) * width] = accs[h][nodes]
    low_bit = front % 2
    for i in range(fronts // 2):
        for ref, own in ((keep, low_bit), (send, 1 - low_bit)):
            start = pl.multiple_of((2 * i + own) * chunk, 8)
            ref[i * chunk : (i + 1) * chunk] = square[pl.ds(start, chunk), :]


def local_forward(parent, acc_a, acc_b, top, first_halves, second_halves, after, fronts):
    first, (width, size) = acc_a.shape[1], acc_a.shape[2:]
    nodes = first + acc_b.shape[1]
    cols = width * HALVES
    part = ((cols // 2, size), F32)
    return call(
        lambda *refs: forward_kernel(nodes, fronts, *refs),
        "local_forward",
        [(HBM, parent)]
        + [(V, a) for a in (acc_a, acc_b, top, *first_halves, *second_halves)]
        + [(pl.ANY, after)],
        [((nodes, cols, size), F32), part, part],
        [pltpu.VMEM((cols, size), F32), pltpu.SMEM((nodes,), jnp.int32), pltpu.SemaphoreType.DMA]
        + [pltpu.VMEM((nodes + 1, width, size), F32)] * HALVES,
    )


def backward_kernel(nodes, fronts, *refs):
    (parent_h, solved), parts, refs = refs[:2], (refs[2:6], refs[6:10]), refs[10:]
    pieces = refs[:fronts]
    sol, sep_out = refs[fronts : 2 + fronts]
    square, parent, staged, sep_v, sem, sems = refs[2 + fronts : 8 + fronts]
    known = refs[8 + fronts :]
    first = parts[0][0].shape[0]
    copy = pltpu.make_async_copy(parent_h, parent, sem)
    copy.start()
    chunk = pieces[0].shape[0]
    width = known[0].shape[1]
    order = [p[...] for p in pieces]
    for bit in range(fronts.bit_length() - 1):
        flip = bit_of("front", bit) == 1
        order = [jnp.where(flip, order[i ^ (1 << bit)], order[i]) for i in range(fronts)]
    for i, value in enumerate(order):
        at = i * chunk
        known[at // width][nodes, at % width : at % width + chunk] = value
    outs = []
    for k in reversed(range(nodes)):
        i = k % first
        inv_hi, inv_lo, upd_hi, upd_lo = parts[k // first]
        inverse = (inv_hi[i], inv_lo[i])
        update = (upd_hi[i], upd_lo[i])
        if k == nodes - 2:
            copy.wait()
        above = nodes if k == nodes - 1 else parent[k]
        for h in range(HALVES):
            rows = slice(h * width, (h + 1) * width)
            part = solved[k, rows] - dot3(split(known[h][above]), update, NN)
            value = dot3(split(part), inverse, NN)
            known[h][k] = value
            staged[k, :, rows] = value.T
        out = pltpu.make_async_copy(staged.at[k], sol.at[k], sems.at[k])
        out.start()
        outs.append(out)
        if k == nodes - 1:
            for h in range(HALVES):
                square[:, h * width : (h + 1) * width] = known[h][nodes].T
            share = sep_v.shape[0]
            start = pl.multiple_of(lax.axis_index("front") * share, 8)
            sep_v[...] = square[pl.ds(start, share), :]
            out = pltpu.make_async_copy(sep_v, sep_out, sems.at[nodes])
            out.start()
            outs.append(out)
    for out in outs:
        out.wait()


def local_backward(parent, solved, first_halves, second_halves, pieces):
    nodes, cols, size = solved.shape
    fronts = len(pieces)
    sol, sep = jax.ShapeDtypeStruct((nodes, size, cols), F32), ((size // fronts, cols), F32)
    ins = (solved, *first_halves, *second_halves, *pieces)
    return pl.pallas_call(
        lambda *refs: backward_kernel(nodes, fronts, *refs),
        name="local_backward",
        in_specs=[pl.BlockSpec(memory_space=HBM)] + [pl.BlockSpec(memory_space=V)] * len(ins),
        out_specs=(pl.BlockSpec(memory_space=HBM),) * 2,
        out_shape=(sol, jax.ShapeDtypeStruct(*sep)),
        scratch_shapes=[pltpu.VMEM((size, cols), F32), pltpu.SMEM((nodes,), jnp.int32)]
        + [pltpu.VMEM((nodes, size, cols), F32), pltpu.VMEM(*sep), pltpu.SemaphoreType.DMA]
        + [pltpu.SemaphoreType.DMA((nodes + 1,))]
        + [pltpu.VMEM((nodes + 1, cols // HALVES, size), F32)] * HALVES,
        compiler_params=pltpu.CompilerParams(vmem_limit_bytes=VMEM_BYTES),
    )(pltpu.with_memory_space_constraint(parent, HBM), *ins)


def stack_kernel(first, second, out, sems):
    copies = [pltpu.make_async_copy(a, out.at[i], sems.at[i]) for i, a in enumerate((first, second))]
    for c in copies:
        c.start()
    for c in copies:
        c.wait()


def block_map_kernel(fronts, *refs):
    parts = refs[:fronts]
    _, total, part, inverse_halves, square = refs[fronts:]
    front = lax.axis_index("front")
    share = parts[0].shape[1]
    for i in range(fronts):
        start = pl.multiple_of((front ^ i) * share, 8)
        square[:, pl.ds(start, share), :] = parts[i][...]
    inverse = split(square[0])
    inverse_halves[0], inverse_halves[1] = inverse
    value = -dot3(inverse, split(square[1]), NN)
    total[...] = value
    half = part.shape[1]
    send_blocks([part], [value[:half], value[half:]])


def block_map(parts, after):
    fronts = len(parts)
    size = parts[0].shape[2]
    return call(
        lambda *refs: block_map_kernel(fronts, *refs),
        "block_map",
        [(V, a) for a in parts] + [(pl.ANY, after)],
        [((size, size), F32), ((1, size // 2, size), F32), ((2, size, size), BF16)],
        [pltpu.VMEM((2, size, size), F32)],
    )


def quarters(x):
    half = x.shape[0] // 2
    return [x[i : i + half, j : j + half] for i in (0, half) for j in (0, half)]


def joined(a, b, c, d):
    first, second = jnp.concatenate([a, b], axis=1), jnp.concatenate([c, d], axis=1)
    return jnp.concatenate([first, second], axis=0)


def low_core():
    return bit_of("front", 0) == 0


def send_blocks(parts, blocks):
    count = sum(part.shape[0] for part in parts)
    low = low_core()
    i = 0
    for part in parts:
        for j in range(part.shape[0]):
            part[j] = jnp.where(low, blocks[i], blocks[len(blocks) - count + i])
            i += 1


def came_blocks(mine, pairs, total):
    low = low_core()
    mine = [m[j] for m in mine for j in range(m.shape[0])]
    pairs = [p[j] for p in pairs for j in range(p.shape[0])]
    count = len(mine)
    blocks = [jnp.where(low, mine[i], pairs[i]) for i in range(count)]
    for i in range(count, total):
        j = i - total + count
        blocks.append(jnp.where(low, pairs[j], mine[j]))
    return blocks


def k_blocks(k):
    a, b, _, d = quarters(k)
    return [a, b, d]


def k_of(blocks):
    return joined(blocks[0], blocks[1], blocks[1].T, blocks[2])


def send_maps(parts, k, t):
    for i, block in enumerate(k_blocks(k)):
        parts[0][i] = block
    send_blocks(parts[1:], quarters(t))


def first_merge_kernel(*refs):
    own, mine, pairs, _, kept, mixed, halves, curve_u, total_u, total_l, *parts = refs
    upper = bit_of("leaf", 0) == 1
    came = jnp.concatenate(came_blocks([mine], [pairs], 2), axis=0)
    mine = own[...]
    low = jnp.where(upper, came, mine)
    up = jnp.where(upper, mine, came)
    low_s, up_s = split(low), split(up)
    for ref, value in ((total_u, up_s), (total_l, low_s)):
        ref[0], ref[1] = value
    k_up = dot3(up_s, up_s, TN)
    k_up_s = split(k_up)
    curve_u[0], curve_u[1] = k_up_s
    x = dot3(k_up_s, low_s, NN)
    t = dot3(up_s, low_s, NN)
    k = dot3(low_s, low_s, TN) + dot3(low_s, split(x), TN)
    kept[0], kept[1] = k, t
    send_maps(parts, k, t)
    size = low.shape[0]
    row = lax.broadcasted_iota(jnp.int32, (size, size), 0)
    col = lax.broadcasted_iota(jnp.int32, (size, size), 1)
    unit = (row == col).astype(F32)
    keep_split(halves, jnp.where(upper, up.T, unit))
    mixed[0] = jnp.where(upper, t, low + x)
    mixed[1] = jnp.where(upper, unit, up)


def merge_kernel(bit, last, *refs):
    own, other, mine, pairs, mixed = refs[:5]
    kept, mixed_n, halves, curve_u, total_u, total_l, *parts = refs[5:]
    upper = bit_of("leaf", bit) == 1
    own_k, own_t = own[0], own[1]
    other_k, other_t = k_of(other), joined(*came_blocks([mine], [pairs], 4))
    low_s = split(jnp.where(upper, other_t, own_t))
    up_s = split(jnp.where(upper, own_t, other_t))
    k_low = jnp.where(upper, other_k, own_k)
    k_up_s = split(jnp.where(upper, own_k, other_k))
    for ref, value in ((total_u, up_s), (total_l, low_s), (curve_u, k_up_s)):
        ref[0], ref[1] = value
    x = dot3(k_up_s, low_s, NN)
    x_s = split(x)
    a, e = mixed[0], mixed[1]
    keep_split(halves, jnp.where(upper, a.T, e))
    a_s, e_s = split(a), split(e)
    a_n = jnp.where(upper, dot3(a_s, low_s, NN), a + dot3(e_s, x_s, TN))
    e_n = jnp.where(upper, e, dot3(up_s, e_s, NN))
    if last:
        kept[...] = jnp.zeros_like(kept)
        keep_split(mixed_n, jnp.where(bit_of("leaf", bit + 1) == 1, a_n.T, e_n))
    else:
        k = k_low + dot3(low_s, x_s, TN)
        t = dot3(up_s, low_s, NN)
        kept[0], kept[1] = k, t
        send_maps(parts, k, t)
        mixed_n[0], mixed_n[1] = a_n, e_n


def boundary_kernel(own, other, two, one):
    k, t = own[0], split(own[1])
    x = dot3(split(k_of(other)), t, NN)
    two[0], two[1], one[0] = k_blocks(k + dot3(t, split(x), TN))


def maps(size, last):
    both, whole = ((2, size, size), BF16), ((2, size, size), F32)
    half = size // 2
    if last:
        return [((8, 128), F32)] + [both] * 5
    sends = [((i, half, half), F32) for i in (3, 2)]
    return [whole, whole, both, both, both, both] + sends


def fold_kernel(bit, own, other, send, keep):
    total = send.shape[0]
    chunk = total
    value = own[...] + other[...]
    first, second = value[:chunk], value[chunk:]
    high = bit_of("front", bit) == 1
    send[...] = jnp.where(high, first, second)
    keep[...] = jnp.where(high, second, first)


def enter_kernel(own, other, inverse, own_map, sol, message):
    drive = own[...] + other[...]
    value = dot3(split(drive), pair(inverse), NT)
    sol[...] = value
    rows = value.shape[0]
    message[:rows] = value
    message[rows:] = dot3(split(value), split(own_map[...]), NN)


def step_kernel(bit, rounds, held, *refs):
    sol, own, other, halves, curve_u, total_u, total_l = refs[:7]
    sol_n, message = refs[7 + held], refs[8 + held :]
    last = bit == rounds - 2
    upper = bit_of("leaf", bit) == 1
    rows = sol.shape[0]
    z_own, p_own = own[:rows], own[rows:]
    if last:
        z_other = p_other = other[...]
    else:
        z_other, p_other = other[:rows], other[rows:]
    z_low = jnp.where(upper, z_other, z_own)
    p_up = jnp.where(upper, p_own, p_other)
    z_low_s = split(z_low)
    middle = p_up + dot3(z_low_s, pair(curve_u), NN)
    middle_s = split(middle)
    given = split(jnp.where(upper, z_low, middle))
    sol_n[...] = sol[...] + dot3(given, pair(halves), NN)
    z_up = z_own if last else jnp.where(upper, z_own, z_other)
    p_low = p_own if last else jnp.where(upper, p_other, p_own)
    z_new = z_up + dot3(z_low_s, pair(total_u), NT)
    p_new = p_low + dot3(middle_s, pair(total_l), NN)
    if last:
        message[0][...] = jnp.where(bit_of("leaf", bit + 1) == 1, p_new, z_new)
        message[1][...] = z_new
        return
    message[0][:rows], message[0][rows:] = z_new, p_new
    if bit == rounds - 3:
        message[1][...] = jnp.where(bit_of("leaf", bit + 1) == 1, p_new, z_new)


def turn_kernel(bit, own_z, came, two, one, given):
    value = came[...]
    middle = value + dot3(split(own_z[...]), split(k_of([two[0], two[1], one[0]])), NN)
    given[...] = jnp.where(bit_of("leaf", bit) == 1, value, middle)


def passed_on(bit, last, given, received):
    away = bit_of("leaf", bit) == bit_of("leaf", last)
    return jnp.where(away, received, given)


def leave_kernel(last, sol, given, received, halves, inverse, top):
    came = passed_on(1, last, given[...], received[...])
    value = sol[...] + dot3(split(came), pair(halves), NN)
    top[...] = dot3(split(value), pair(inverse), NN)


def gather_front(x, bits):
    pieces = {0: x}
    for bit in reversed(range(bits)):
        for i in list(pieces):
            pieces[i | (1 << bit)] = exchange(pieces[i], "front", bit)
    return [pieces[i] for i in range(1 << bits)]


def local(rhs_local, dinv_local, update_local, parent, row_blocks, sep_rhs, sep_dinv, sep_coupling):
    fronts, leaves = lax.axis_size("front"), lax.axis_size("leaf")
    front_bits, rounds = fronts.bit_length() - 1, leaves.bit_length() - 1
    size = sep_dinv.shape[1]
    cols = sep_rhs.shape[1]
    chunk = cols // fronts

    (stacked,) = call(
        stack_kernel,
        "stack",
        [(HBM, sep_dinv), (HBM, sep_coupling)],
        [((2, *sep_dinv.shape), F32)],
        [pltpu.SemaphoreType.DMA((2,))],
    )
    came = {0: stacked}
    for bit in reversed(range(1, front_bits)):
        for i in list(came):
            came[i | (1 << bit)] = exchange(came[i], "front", bit)
    came[1] = exchange(stacked, "front", 0)
    acc_a, *first_halves = prepare_first(
        rhs_local, dinv_local, update_local, row_blocks, sep_rhs, stacked
    )
    first_halves, (top, row_columns, *raw) = first_halves[:4], first_halves[4:]
    for i in range(2, fronts, 2):
        held, _ = lax.optimization_barrier((came[i], acc_a))
        came[i + 1] = exchange(held, "front", 0)
    acc_b, *second_halves = prepare_second(row_columns, *raw, acc_a)
    own_map, part, inverse = block_map([came[i] for i in range(fronts)], acc_b)
    mine = exchange(part, "leaf", 0)
    solved, send, keep = local_forward(
        parent, acc_a, acc_b, top, first_halves, second_halves, own_map, fronts
    )
    mine, send = lax.optimization_barrier((mine, send))
    pairs = exchange(mine, "front", 0)
    for bit in range(front_bits):
        received = exchange(send, "front", bit)
        if bit + 1 < front_bits:
            half = ((keep.shape[0] // 2, size), F32)
            send, keep = call(
                lambda *refs, bit=bit: fold_kernel(bit + 1, *refs),
                "fold",
                [(V, keep), (V, received)],
                [half, half],
            )
    kept, mixed, *tools = call(
        first_merge_kernel,
        "merge_0",
        [(V, own_map), (V, mine), (V, pairs), (pl.ANY, send)],
        maps(size, False),
    )
    tools, parts = tools[:4], tools[4:]
    sol, message = call(
        enter_kernel,
        "enter",
        [(V, keep), (V, received), (V, inverse), (V, own_map)],
        [((chunk, size), F32), ((2 * chunk, size), F32)],
    )
    share = ((chunk, size), F32)
    middle = leaves // 2
    boundary = [(middle - 2 + i, middle + i) for i in range(2)]
    boundary += [(j, i) for i, j in boundary]
    paired = {i for i, _ in boundary}
    boundary += [(i, i ^ 1) for i in range(leaves) if i not in paired]
    for bit in range(rounds - 1):
        last = bit == rounds - 2
        received = exchange(short[0] if last else message, "leaf", bit)
        ahead = []
        if not last:
            other, mine = [exchange(part, "leaf", bit + 1) for part in parts]
            ahead = [other]
        if bit == rounds - 3:
            half = size // 2
            ahead = call(
                boundary_kernel,
                "boundary",
                [(V, kept), (V, other)],
                [((2, half, half), F32), ((1, half, half), F32)],
            )
            blocks = [lax.ppermute(b, "leaf", boundary) for b in ahead]
        sol, *message = call(
            lambda *refs, bit=bit: step_kernel(bit, rounds, len(ahead), *refs),
            f"step_{bit}",
            [(V, a) for a in (sol, message, received, *tools)] + [(pl.ANY, a) for a in ahead],
            [share] + ([share] if last else [((2 * chunk, size), F32)]) + [share] * (bit >= rounds - 3),
        )
        if not last:
            message, *short = message
            mine, _ = lax.optimization_barrier((mine, sol))
            pairs = exchange(mine, "front", 0)
            last = bit == rounds - 3
            kept, mixed, *tools = call(
                lambda *refs, bit=bit, last=last: merge_kernel(bit + 1, last, *refs),
                f"merge_{bit + 1}",
                [(V, a) for a in (kept, other, mine, pairs, mixed)],
                maps(size, last),
            )
            tools, parts = tools[:4], tools[4:]
    came = lax.ppermute(message[0], "leaf", boundary)
    (given,) = call(
        lambda *refs: turn_kernel(rounds - 1, *refs),
        "turn",
        [(V, a) for a in (message[1], came, *blocks)],
        [share],
    )
    for bit in reversed(range(2, rounds - 1)):
        given = passed_on(bit, rounds - 1, given, exchange(given, "leaf", bit))
    received = exchange(given, "leaf", 1)
    (top,) = call(
        lambda *refs: leave_kernel(rounds - 1, *refs),
        "leave",
        [(V, a) for a in (sol, given, received, mixed, inverse)],
        [share],
    )
    pieces = gather_front(top, front_bits)
    sol_local, sep_solution = local_backward(
        parent, solved, first_halves, second_halves, pieces
    )
    return (sol_local, sep_solution)


def solution(mesh):
    spread3 = P(("leaf", "front"), None, None)
    spread2 = P(("leaf", "front"), None)
    spread1 = P(("leaf", "front"))
    return jax.shard_map(
        local,
        mesh=mesh,
        in_specs=(spread3, spread3, spread3, spread1, spread2, spread2, spread2, spread2),
        out_specs=(spread3, spread2),
        check_vma=False,
    )
```

```python
import jax
import jax.numpy as jnp
from jax import lax
from jax.experimental import pallas as pl
from jax.experimental.pallas import tpu as pltpu
from jax.sharding import PartitionSpec as P

F32 = jnp.float32
BF16 = jnp.bfloat16
NN = (((1,), (0,)), ((), ()))
NT = (((1,), (1,)), ((), ()))
TN = (((0,), (0,)), ((), ()))
VMEM_BYTES = 24 << 20
HALVES = 2


def split(x):
    high = x.astype(BF16)
    return high, (x - high.astype(F32)).astype(BF16)


def dot1(a, b, dims):
    return lax.dot_general(a, b, dims, preferred_element_type=F32)


def dot3(a, b, dims):
    axis = 1 - dims[0][0][0]
    rows = a[0].shape[axis]
    both = dot1(jnp.concatenate(a, axis=axis), b[0], dims)
    return both[:rows] + (both[rows:] + dot1(a[0], b[1], dims))


def keep_split(ref, value):
    ref[0], ref[1] = split(value)


def pair(ref):
    return ref[0], ref[1]


def bit_of(axis, bit):
    return (lax.axis_index(axis) // (1 << bit)) % 2


def call(kernel, name, ins, outs, scratch=()):
    specs = [pl.BlockSpec(memory_space=space) for space, _ in ins]
    ins = [
        (space, pltpu.with_memory_space_constraint(a, HBM) if space == HBM else a)
        for space, a in ins
    ]
    return pl.pallas_call(
        kernel,
        name=name,
        in_specs=specs,
        out_specs=tuple(pl.BlockSpec(memory_space=pltpu.VMEM) for _ in outs),
        out_shape=tuple(jax.ShapeDtypeStruct(*o) for o in outs),
        scratch_shapes=list(scratch),
        compiler_params=pltpu.CompilerParams(vmem_limit_bytes=VMEM_BYTES),
    )(*[a for _, a in ins])


V = pltpu.VMEM
HBM = pltpu.HBM


def swap(x, axis, mask):
    n = lax.axis_size(axis)
    return lax.ppermute(x, axis, [(i, i ^ mask) for i in range(n)])


def exchange(x, axis, bit):
    return swap(x, axis, 1 << bit)


def prepare_nodes(count, rows_at, row_columns, dinv, upd, rhs, outs, waits):
    acc, inv_hi, inv_lo, upd_hi, upd_lo = outs
    size = dinv.shape[1]
    width = acc.shape[2]
    lane = lax.broadcasted_iota(jnp.int32, (size, size), 1).astype(F32)
    for k in range(count):
        for c in waits[k]:
            c.wait()
        inv_hi[k], inv_lo[k] = split(dinv[k])
        high, low = split(upd[k])
        chosen = (lane == row_columns[:, rows_at + k : rows_at + k + 1]).astype(BF16)
        upd_hi[k] = dot1(chosen, high, NN).astype(BF16)
        upd_lo[k] = dot1(chosen, low, NN).astype(BF16)
        turned = rhs[k].T
        for h in range(HALVES):
            acc[h, k] = turned[h * width : (h + 1) * width]


def prepare_first_kernel(nodes, *refs):
    (rows_h, sep_h, rhs_h, dinv_h, upd_h, _), refs = refs[:6], refs[6:]
    outs, (top, row_columns, rhs_n, dinv_n, upd_n), refs = refs[:5], refs[5:10], refs[10:]
    rhs_v, dinv_v, upd_v, square, rows, sep, sems, small = refs
    cols = rhs_v.shape[2]
    width = cols // HALVES
    first = nodes // 2
    few = [
        pltpu.make_async_copy(src, dst, small.at[i])
        for i, (src, dst) in enumerate(((rows_h, rows), (sep_h, sep)))
    ]
    for c in few:
        c.start()
    copies = []
    for k in range(nodes):
        ins = (upd_v, dinv_v, rhs_v) if k < first else (upd_n, dinv_n, rhs_n)
        group = [
            pltpu.make_async_copy(src.at[k], dst.at[k % first], sems.at[i, k])
            for i, (src, dst) in enumerate(zip((upd_h, dinv_h, rhs_h), ins))
        ]
        for c in group:
            c.start()
        copies.append(group)
    front = lax.axis_index("front")
    square[...] = jnp.zeros_like(square)
    for c in few:
        c.wait()
    share = sep.shape[0]
    square[pl.ds(pl.multiple_of(front * share, 8), share), :] = sep[...]
    turned = square[...].T
    for h in range(HALVES):
        top[h] = turned[h * width : (h + 1) * width]
    row_columns[...] = rows[...].astype(F32).T
    prepare_nodes(first, 0, row_columns, dinv_v, upd_v, rhs_v, outs, copies[:first])
    for group in copies[first:]:
        for c in group:
            c.wait()


def prepare_second_kernel(first, row_columns, rhs, dinv, upd, _, *outs):
    count = rhs.shape[0]
    waits = [()] * count
    prepare_nodes(count, first, row_columns, dinv, upd, rhs, outs, waits)


def prepared(count, size, cols):
    half = ((count, size, size), BF16)
    return [((HALVES, count, cols // HALVES, size), F32), half, half, half, half]


def prepare_first(rhs, dinv, update, rows, sep, after):
    nodes, size, cols = rhs.shape
    first = nodes // 2
    some = (first, size, cols)
    big = pltpu.VMEM(some, F32)
    return call(
        lambda *refs: prepare_first_kernel(nodes, *refs),
        "prepare_first",
        [(HBM, a) for a in (rows, sep, rhs, dinv, update)] + [(pl.ANY, after)],
        prepared(first, size, cols)
        + [((HALVES, cols // HALVES, size), F32), ((size, nodes), F32)]
        + [((nodes - first, *some[1:]), F32)] * 3,
        [big, big, big, pltpu.VMEM((size, cols), F32)]
        + [pltpu.VMEM(rows.shape, jnp.int32), pltpu.VMEM(sep.shape, F32)]
        + [pltpu.SemaphoreType.DMA((3, nodes)), pltpu.SemaphoreType.DMA((2,))],
    )


def prepare_second(row_columns, rhs, dinv, update, after):
    count, size, cols = rhs.shape
    first = row_columns.shape[1] - count
    return call(
        lambda *refs: prepare_second_kernel(first, *refs),
        "prepare_second",
        [(V, a) for a in (row_columns, rhs, dinv, update)] + [(pl.ANY, after)],
        prepared(count, size, cols),
    )


def forward_kernel(nodes, fronts, *refs):
    (parent_h, acc_a, acc_b, top), parts, refs = refs[:4], (refs[4:8], refs[8:12]), refs[13:]
    solved, send, keep, square, parent, sem = refs[:6]
    accs = refs[6:]
    copy = pltpu.make_async_copy(parent_h, parent, sem)
    copy.start()
    first, width = acc_a.shape[1:3]
    for h in range(HALVES):
        for k in range(nodes):
            accs[h][k] = acc_a[h, k] if k < first else acc_b[h, k - first]
        accs[h][nodes] = top[h]
    for k in range(nodes):
        inv_hi, inv_lo, upd_hi, upd_lo = parts[k // first]
        i = k % first
        inverse = (inv_hi[i], inv_lo[i])
        update = (upd_hi[i], upd_lo[i])
        for h in range(HALVES):
            value = dot3(split(accs[h][k]), inverse, NT)
            solved[k, h * width : (h + 1) * width] = value
            moved = dot3(split(value), update, NT)
            if k + h == 0:
                copy.wait()
            above = nodes if k == nodes - 1 else parent[k]
            accs[h][above] = accs[h][above] - moved
    front = lax.axis_index("front")
    chunk = width * HALVES // fronts
    for h in range(HALVES):
        square[h * width : (h + 1) * width] = accs[h][nodes]
    low_bit = front % 2
    for i in range(fronts // 2):
        for ref, own in ((keep, low_bit), (send, 1 - low_bit)):
            start = pl.multiple_of((2 * i + own) * chunk, 8)
            ref[i * chunk : (i + 1) * chunk] = square[pl.ds(start, chunk), :]


def local_forward(parent, acc_a, acc_b, top, first_halves, second_halves, after, fronts):
    first, (width, size) = acc_a.shape[1], acc_a.shape[2:]
    nodes = first + acc_b.shape[1]
    cols = width * HALVES
    part = ((cols // 2, size), F32)
    return call(
        lambda *refs: forward_kernel(nodes, fronts, *refs),
        "local_forward",
        [(HBM, parent)]
        + [(V, a) for a in (acc_a, acc_b, top, *first_halves, *second_halves)]
        + [(pl.ANY, after)],
        [((nodes, cols, size), F32), part, part],
        [pltpu.VMEM((cols, size), F32), pltpu.SMEM((nodes,), jnp.int32), pltpu.SemaphoreType.DMA]
        + [pltpu.VMEM((nodes + 1, width, size), F32)] * HALVES,
    )


def backward_kernel(nodes, fronts, *refs):
    (parent_h, solved), parts, refs = refs[:2], (refs[2:6], refs[6:10]), refs[10:]
    pieces = refs[:fronts]
    sol, sep_out = refs[fronts : 2 + fronts]
    square, parent, staged, sep_v, sem, sems = refs[2 + fronts : 8 + fronts]
    known = refs[8 + fronts :]
    first = parts[0][0].shape[0]
    copy = pltpu.make_async_copy(parent_h, parent, sem)
    copy.start()
    chunk = pieces[0].shape[0]
    width = known[0].shape[1]
    order = [p[...] for p in pieces]
    for bit in range(fronts.bit_length() - 1):
        flip = bit_of("front", bit) == 1
        order = [jnp.where(flip, order[i ^ (1 << bit)], order[i]) for i in range(fronts)]
    for i, value in enumerate(order):
        at = i * chunk
        known[at // width][nodes, at % width : at % width + chunk] = value
    outs = []
    for k in reversed(range(nodes)):
        i = k % first
        inv_hi, inv_lo, upd_hi, upd_lo = parts[k // first]
        inverse = (inv_hi[i], inv_lo[i])
        update = (upd_hi[i], upd_lo[i])
        if k == nodes - 2:
            copy.wait()
        above = nodes if k == nodes - 1 else parent[k]
        for h in range(HALVES):
            rows = slice(h * width, (h + 1) * width)
            part = solved[k, rows] - dot3(split(known[h][above]), update, NN)
            value = dot3(split(part), inverse, NN)
            known[h][k] = value
            staged[k, :, rows] = value.T
        out = pltpu.make_async_copy(staged.at[k], sol.at[k], sems.at[k])
        out.start()
        outs.append(out)
        if k == nodes - 1:
            for h in range(HALVES):
                square[:, h * width : (h + 1) * width] = known[h][nodes].T
            share = sep_v.shape[0]
            start = pl.multiple_of(lax.axis_index("front") * share, 8)
            sep_v[...] = square[pl.ds(start, share), :]
            out = pltpu.make_async_copy(sep_v, sep_out, sems.at[nodes])
            out.start()
            outs.append(out)
    for out in outs:
        out.wait()


def local_backward(parent, solved, first_halves, second_halves, pieces):
    nodes, cols, size = solved.shape
    fronts = len(pieces)
    sol, sep = jax.ShapeDtypeStruct((nodes, size, cols), F32), ((size // fronts, cols), F32)
    ins = (solved, *first_halves, *second_halves, *pieces)
    return pl.pallas_call(
        lambda *refs: backward_kernel(nodes, fronts, *refs),
        name="local_backward",
        in_specs=[pl.BlockSpec(memory_space=HBM)] + [pl.BlockSpec(memory_space=V)] * len(ins),
        out_specs=(pl.BlockSpec(memory_space=HBM),) * 2,
        out_shape=(sol, jax.ShapeDtypeStruct(*sep)),
        scratch_shapes=[pltpu.VMEM((size, cols), F32), pltpu.SMEM((nodes,), jnp.int32)]
        + [pltpu.VMEM((nodes, size, cols), F32), pltpu.VMEM(*sep), pltpu.SemaphoreType.DMA]
        + [pltpu.SemaphoreType.DMA((nodes + 1,))]
        + [pltpu.VMEM((nodes + 1, cols // HALVES, size), F32)] * HALVES,
        compiler_params=pltpu.CompilerParams(vmem_limit_bytes=VMEM_BYTES),
    )(pltpu.with_memory_space_constraint(parent, HBM), *ins)


def stack_kernel(first, second, out, sems):
    copies = [pltpu.make_async_copy(a, out.at[i], sems.at[i]) for i, a in enumerate((first, second))]
    for c in copies:
        c.start()
    for c in copies:
        c.wait()


def block_map_kernel(fronts, *refs):
    parts = refs[:fronts]
    _, total, part, inverse_halves, square = refs[fronts:]
    front = lax.axis_index("front")
    share = parts[0].shape[1]
    for i in range(fronts):
        start = pl.multiple_of((front ^ i) * share, 8)
        square[:, pl.ds(start, share), :] = parts[i][...]
    inverse = split(square[0])
    inverse_halves[0], inverse_halves[1] = inverse
    value = -dot3(inverse, split(square[1]), NN)
    total[...] = value
    half = part.shape[1]
    send_blocks([part], [value[:half], value[half:]])


def block_map(parts, after):
    fronts = len(parts)
    size = parts[0].shape[2]
    return call(
        lambda *refs: block_map_kernel(fronts, *refs),
        "block_map",
        [(V, a) for a in parts] + [(pl.ANY, after)],
        [((size, size), F32), ((1, size // 2, size), F32), ((2, size, size), BF16)],
        [pltpu.VMEM((2, size, size), F32)],
    )


def quarters(x):
    half = x.shape[0] // 2
    return [x[i : i + half, j : j + half] for i in (0, half) for j in (0, half)]


def joined(a, b, c, d):
    first, second = jnp.concatenate([a, b], axis=1), jnp.concatenate([c, d], axis=1)
    return jnp.concatenate([first, second], axis=0)


def low_core():
    return bit_of("front", 0) == 0


def send_blocks(parts, blocks):
    count = sum(part.shape[0] for part in parts)
    low = low_core()
    i = 0
    for part in parts:
        for j in range(part.shape[0]):
            part[j] = jnp.where(low, blocks[i], blocks[len(blocks) - count + i])
            i += 1


def came_blocks(mine, pairs, total):
    low = low_core()
    mine = [m[j] for m in mine for j in range(m.shape[0])]
    pairs = [p[j] for p in pairs for j in range(p.shape[0])]
    count = len(mine)
    blocks = [jnp.where(low, mine[i], pairs[i]) for i in range(count)]
    for i in range(count, total):
        j = i - total + count
        blocks.append(jnp.where(low, pairs[j], mine[j]))
    return blocks


def k_blocks(k):
    a, b, _, d = quarters(k)
    return [a, b, d]


def k_of(blocks):
    return joined(blocks[0], blocks[1], blocks[1].T, blocks[2])


def send_maps(parts, k, t):
    for i, block in enumerate(k_blocks(k)):
        parts[0][i] = block
    send_blocks(parts[1:], quarters(t))


def first_merge_kernel(*refs):
    own, mine, pairs, _, kept, mixed, halves, curve_u, total_u, total_l, *parts = refs
    upper = bit_of("leaf", 0) == 1
    came = jnp.concatenate(came_blocks([mine], [pairs], 2), axis=0)
    mine = own[...]
    low = jnp.where(upper, came, mine)
    up = jnp.where(upper, mine, came)
    low_s, up_s = split(low), split(up)
    for ref, value in ((total_u, up_s), (total_l, low_s)):
        ref[0], ref[1] = value
    k_up = dot3(up_s, up_s, TN)
    k_up_s = split(k_up)
    curve_u[0], curve_u[1] = k_up_s
    x = dot3(k_up_s, low_s, NN)
    t = dot3(up_s, low_s, NN)
    k = dot3(low_s, low_s, TN) + dot3(low_s, split(x), TN)
    kept[0], kept[1] = k, t
    send_maps(parts, k, t)
    size = low.shape[0]
    row = lax.broadcasted_iota(jnp.int32, (size, size), 0)
    col = lax.broadcasted_iota(jnp.int32, (size, size), 1)
    unit = (row == col).astype(F32)
    keep_split(halves, jnp.where(upper, up.T, unit))
    mixed[0] = jnp.where(upper, t, low + x)
    mixed[1] = jnp.where(upper, unit, up)


def merge_kernel(bit, *refs):
    own, other, mine, pairs, mixed = refs[:5]
    kept, mixed_n, halves, curve_u, total_u, total_l, *parts = refs[5:]
    upper = bit_of("leaf", bit) == 1
    own_k, own_t = own[0], own[1]
    other_k, other_t = k_of(other), joined(*came_blocks([mine], [pairs], 4))
    low_s = split(jnp.where(upper, other_t, own_t))
    up_s = split(jnp.where(upper, own_t, other_t))
    k_low = jnp.where(upper, other_k, own_k)
    k_up_s = split(jnp.where(upper, own_k, other_k))
    for ref, value in ((total_u, up_s), (total_l, low_s), (curve_u, k_up_s)):
        ref[0], ref[1] = value
    x = dot3(k_up_s, low_s, NN)
    x_s = split(x)
    a, e = mixed[0], mixed[1]
    keep_split(halves, jnp.where(upper, a.T, e))
    a_s, e_s = split(a), split(e)
    a_n = jnp.where(upper, dot3(a_s, low_s, NN), a + dot3(e_s, x_s, TN))
    e_n = jnp.where(upper, e, dot3(up_s, e_s, NN))
    k = k_low + dot3(low_s, x_s, TN)
    t = dot3(up_s, low_s, NN)
    kept[0], kept[1] = k, t
    send_maps(parts, k, t)
    mixed_n[0], mixed_n[1] = a_n, e_n


def boundary_kernel(bit, own, other, mixed, two, one, halves, curve, total):
    k, t, k_up = own[0], split(own[1]), split(k_of(other))
    total[0], total[1] = t
    curve[0], curve[1] = k_up
    keep_split(halves, jnp.where(bit_of("leaf", bit) == 1, mixed[0].T, mixed[1]))
    x = dot3(k_up, t, NN)
    two[0], two[1], one[0] = k_blocks(k + dot3(t, split(x), TN))


def last_merge_kernel(bit, mixed, mine, pairs, curve, total, added):
    upper = bit_of("leaf", bit) == 1
    came = split(joined(*came_blocks([mine], [pairs], 4)))
    a, e = mixed[0], mixed[1]
    a_s, e_s = split(a), split(e)
    x = split(dot3(pair(curve), pair(total), NN))
    a_n = jnp.where(upper, dot3(a_s, came, NN), a + dot3(e_s, x, TN))
    e_n = jnp.where(upper, e, dot3(came, e_s, NN))
    keep_split(added, jnp.where(bit_of("leaf", bit + 1) == 1, a_n.T, e_n))


def maps(size):
    both, whole = ((2, size, size), BF16), ((2, size, size), F32)
    half = size // 2
    sends = [((i, half, half), F32) for i in (3, 2)]
    return [whole, whole, both, both, both, both] + sends


def fold_kernel(bit, own, other, send, keep):
    total = send.shape[0]
    chunk = total
    value = own[...] + other[...]
    first, second = value[:chunk], value[chunk:]
    high = bit_of("front", bit) == 1
    send[...] = jnp.where(high, first, second)
    keep[...] = jnp.where(high, second, first)


def enter_kernel(own, other, inverse, own_map, sol, message):
    drive = own[...] + other[...]
    value = dot3(split(drive), pair(inverse), NT)
    sol[...] = value
    rows = value.shape[0]
    message[:rows] = value
    message[rows:] = dot3(split(value), split(own_map[...]), NN)


def step_kernel(bit, rounds, held, *refs):
    sol, own, other, halves, curve_u, total_u, total_l = refs[:7]
    sol_n, message = refs[7 + held], refs[8 + held :]
    last = bit == rounds - 2
    upper = bit_of("leaf", bit) == 1
    rows = sol.shape[0]
    z_own, p_own = own[:rows], own[rows:]
    if last:
        z_other = p_other = other[...]
    else:
        z_other, p_other = other[:rows], other[rows:]
    z_low = jnp.where(upper, z_other, z_own)
    p_up = jnp.where(upper, p_own, p_other)
    z_low_s = split(z_low)
    middle = p_up + dot3(z_low_s, pair(curve_u), NN)
    middle_s = split(middle)
    given = split(jnp.where(upper, z_low, middle))
    sol_n[...] = sol[...] + dot3(given, pair(halves), NN)
    z_up = z_own if last else jnp.where(upper, z_own, z_other)
    p_low = p_own if last else jnp.where(upper, p_other, p_own)
    z_new = z_up + dot3(z_low_s, pair(total_u), NT)
    p_new = p_low + dot3(middle_s, pair(total_l), NN)
    if last:
        message[0][...] = jnp.where(bit_of("leaf", bit + 1) == 1, p_new, z_new)
        message[1][...] = z_new
        return
    message[0][:rows], message[0][rows:] = z_new, p_new
    if bit == rounds - 3:
        message[1][...] = jnp.where(bit_of("leaf", bit + 1) == 1, p_new, z_new)


def turn_kernel(bit, own_z, came, two, one, given):
    value = came[...]
    middle = value + dot3(split(own_z[...]), split(k_of([two[0], two[1], one[0]])), NN)
    given[...] = jnp.where(bit_of("leaf", bit) == 1, value, middle)


def passed_on(bit, last, given, received):
    away = bit_of("leaf", bit) == bit_of("leaf", last)
    return jnp.where(away, received, given)


def leave_kernel(last, sol, given, received, halves, inverse, top):
    came = passed_on(1, last, given[...], received[...])
    value = sol[...] + dot3(split(came), pair(halves), NN)
    top[...] = dot3(split(value), pair(inverse), NN)


def gather_front(x, bits):
    pieces = {0: x}
    for bit in reversed(range(bits)):
        for i in list(pieces):
            pieces[i | (1 << bit)] = exchange(pieces[i], "front", bit)
    return [pieces[i] for i in range(1 << bits)]


def local(rhs_local, dinv_local, update_local, parent, row_blocks, sep_rhs, sep_dinv, sep_coupling):
    fronts, leaves = lax.axis_size("front"), lax.axis_size("leaf")
    front_bits, rounds = fronts.bit_length() - 1, leaves.bit_length() - 1
    size = sep_dinv.shape[1]
    cols = sep_rhs.shape[1]
    chunk = cols // fronts

    (stacked,) = call(
        stack_kernel,
        "stack",
        [(HBM, sep_dinv), (HBM, sep_coupling)],
        [((2, *sep_dinv.shape), F32)],
        [pltpu.SemaphoreType.DMA((2,))],
    )
    came = {0: stacked}
    for bit in reversed(range(1, front_bits)):
        for i in list(came):
            came[i | (1 << bit)] = exchange(came[i], "front", bit)
    came[1] = exchange(stacked, "front", 0)
    acc_a, *first_halves = prepare_first(
        rhs_local, dinv_local, update_local, row_blocks, sep_rhs, stacked
    )
    first_halves, (top, row_columns, *raw) = first_halves[:4], first_halves[4:]
    for i in range(2, fronts, 2):
        held, _ = lax.optimization_barrier((came[i], acc_a))
        came[i + 1] = exchange(held, "front", 0)
    acc_b, *second_halves = prepare_second(row_columns, *raw, acc_a)
    own_map, part, inverse = block_map([came[i] for i in range(fronts)], acc_b)
    mine = exchange(part, "leaf", 0)
    solved, send, keep = local_forward(
        parent, acc_a, acc_b, top, first_halves, second_halves, own_map, fronts
    )
    mine, send = lax.optimization_barrier((mine, send))
    pairs = exchange(mine, "front", 0)
    for bit in range(front_bits):
        received = exchange(send, "front", bit)
        if bit + 1 < front_bits:
            half = ((keep.shape[0] // 2, size), F32)
            send, keep = call(
                lambda *refs, bit=bit: fold_kernel(bit + 1, *refs),
                "fold",
                [(V, keep), (V, received)],
                [half, half],
            )
    kept, mixed, *tools = call(
        first_merge_kernel,
        "merge_0",
        [(V, own_map), (V, mine), (V, pairs), (pl.ANY, send)],
        maps(size),
    )
    tools, parts = tools[:4], tools[4:]
    sol, message = call(
        enter_kernel,
        "enter",
        [(V, keep), (V, received), (V, inverse), (V, own_map)],
        [((chunk, size), F32), ((2 * chunk, size), F32)],
    )
    share = ((chunk, size), F32)
    middle = leaves // 2
    boundary = [(middle - 2 + i, middle + i) for i in range(2)]
    boundary += [(j, i) for i, j in boundary]
    paired = {i for i, _ in boundary}
    boundary += [(i, i ^ 1) for i in range(leaves) if i not in paired]
    for bit in range(rounds - 1):
        last = bit == rounds - 2
        received = exchange(short[0] if last else message, "leaf", bit)
        ahead = []
        if not last:
            other, mine = [exchange(part, "leaf", bit + 1) for part in parts]
            ahead = [other]
        if bit == rounds - 3:
            half = size // 2
            *ahead, halves, curve, own_t = call(
                lambda *refs: boundary_kernel(rounds - 2, *refs),
                "boundary",
                [(V, kept), (V, other), (V, mixed)],
                [((2, half, half), F32), ((1, half, half), F32)] + [((2, size, size), BF16)] * 3,
            )
            blocks = [lax.ppermute(b, "leaf", boundary) for b in ahead]
        sol, *message = call(
            lambda *refs, bit=bit: step_kernel(bit, rounds, len(ahead), *refs),
            f"step_{bit}",
            [(V, a) for a in (sol, message, received, *tools)] + [(pl.ANY, a) for a in ahead],
            [share] + ([share] if last else [((2 * chunk, size), F32)]) + [share] * (bit >= rounds - 3),
        )
        if not last:
            message, *short = message
        if bit == rounds - 3:
            tools = [halves, curve, own_t, own_t]
        elif not last:
            mine, _ = lax.optimization_barrier((mine, sol))
            pairs = exchange(mine, "front", 0)
            kept, mixed, *tools = call(
                lambda *refs, bit=bit: merge_kernel(bit + 1, *refs),
                f"merge_{bit + 1}",
                [(V, a) for a in (kept, other, mine, pairs, mixed)],
                maps(size),
            )
            tools, parts = tools[:4], tools[4:]
    mine, _ = lax.optimization_barrier((mine, sol))
    pairs = exchange(mine, "front", 0)
    (added,) = call(
        lambda *refs: last_merge_kernel(rounds - 2, *refs),
        "last_merge",
        [(V, a) for a in (mixed, mine, pairs, curve, own_t)],
        [((2, size, size), BF16)],
    )
    came = lax.ppermute(message[0], "leaf", boundary)
    (given,) = call(
        lambda *refs: turn_kernel(rounds - 1, *refs),
        "turn",
        [(V, a) for a in (message[1], came, *blocks)],
        [share],
    )
    for bit in reversed(range(2, rounds - 1)):
        given = passed_on(bit, rounds - 1, given, exchange(given, "leaf", bit))
    received = exchange(given, "leaf", 1)
    (top,) = call(
        lambda *refs: leave_kernel(rounds - 1, *refs),
        "leave",
        [(V, a) for a in (sol, given, received, added, inverse)],
        [share],
    )
    pieces = gather_front(top, front_bits)
    sol_local, sep_solution = local_backward(
        parent, solved, first_halves, second_halves, pieces
    )
    return (sol_local, sep_solution)


def solution(mesh):
    spread3 = P(("leaf", "front"), None, None)
    spread2 = P(("leaf", "front"), None)
    spread1 = P(("leaf", "front"))
    return jax.shard_map(
        local,
        mesh=mesh,
        in_specs=(spread3, spread3, spread3, spread1, spread2, spread2, spread2, spread2),
        out_specs=(spread3, spread2),
        check_vma=False,
    )
```

```python
import jax
import jax.numpy as jnp
from jax import lax
from jax.experimental import pallas as pl
from jax.experimental.pallas import tpu as pltpu
from jax.sharding import PartitionSpec as P

F32 = jnp.float32
BF16 = jnp.bfloat16
NN = (((1,), (0,)), ((), ()))
NT = (((1,), (1,)), ((), ()))
TN = (((0,), (0,)), ((), ()))
VMEM_BYTES = 24 << 20
HALVES = 2


def split(x):
    high = x.astype(BF16)
    return high, (x - high.astype(F32)).astype(BF16)


def dot1(a, b, dims):
    return lax.dot_general(a, b, dims, preferred_element_type=F32)


def dot3(a, b, dims):
    axis = 1 - dims[0][0][0]
    rows = a[0].shape[axis]
    both = dot1(jnp.concatenate(a, axis=axis), b[0], dims)
    return both[:rows] + (both[rows:] + dot1(a[0], b[1], dims))


def keep_split(ref, value):
    ref[0], ref[1] = split(value)


def pair(ref):
    return ref[0], ref[1]


def bit_of(axis, bit):
    return (lax.axis_index(axis) // (1 << bit)) % 2


def call(kernel, name, ins, outs, scratch=()):
    specs = [pl.BlockSpec(memory_space=space) for space, _ in ins]
    ins = [
        (space, pltpu.with_memory_space_constraint(a, HBM) if space == HBM else a)
        for space, a in ins
    ]
    return pl.pallas_call(
        kernel,
        name=name,
        in_specs=specs,
        out_specs=tuple(pl.BlockSpec(memory_space=pltpu.VMEM) for _ in outs),
        out_shape=tuple(jax.ShapeDtypeStruct(*o) for o in outs),
        scratch_shapes=list(scratch),
        compiler_params=pltpu.CompilerParams(vmem_limit_bytes=VMEM_BYTES),
    )(*[a for _, a in ins])


V = pltpu.VMEM
HBM = pltpu.HBM


def swap(x, axis, mask):
    n = lax.axis_size(axis)
    return lax.ppermute(x, axis, [(i, i ^ mask) for i in range(n)])


def exchange(x, axis, bit):
    return swap(x, axis, 1 << bit)


def prepare_nodes(count, rows_at, row_columns, dinv, upd, rhs, outs, waits):
    acc, inv_hi, inv_lo, upd_hi, upd_lo = outs
    size = dinv.shape[1]
    width = acc.shape[2]
    lane = lax.broadcasted_iota(jnp.int32, (size, size), 1).astype(F32)
    for k in range(count):
        for c in waits[k]:
            c.wait()
        inv_hi[k], inv_lo[k] = split(dinv[k])
        high, low = split(upd[k])
        chosen = (lane == row_columns[:, rows_at + k : rows_at + k + 1]).astype(BF16)
        upd_hi[k] = dot1(chosen, high, NN).astype(BF16)
        upd_lo[k] = dot1(chosen, low, NN).astype(BF16)
        turned = rhs[k].T
        for h in range(HALVES):
            acc[h, k] = turned[h * width : (h + 1) * width]


def prepare_first_kernel(nodes, *refs):
    (rows_h, sep_h, rhs_h, dinv_h, upd_h, _), refs = refs[:6], refs[6:]
    outs, (top, row_columns, rhs_n, dinv_n, upd_n), refs = refs[:5], refs[5:10], refs[10:]
    rhs_v, dinv_v, upd_v, square, rows, sep, sems, small = refs
    cols = rhs_v.shape[2]
    width = cols // HALVES
    first = nodes // 2
    few = [
        pltpu.make_async_copy(src, dst, small.at[i])
        for i, (src, dst) in enumerate(((rows_h, rows), (sep_h, sep)))
    ]
    for c in few:
        c.start()
    copies = []
    for k in range(nodes):
        ins = (upd_v, dinv_v, rhs_v) if k < first else (upd_n, dinv_n, rhs_n)
        group = [
            pltpu.make_async_copy(src.at[k], dst.at[k % first], sems.at[i, k])
            for i, (src, dst) in enumerate(zip((upd_h, dinv_h, rhs_h), ins))
        ]
        for c in group:
            c.start()
        copies.append(group)
    front = lax.axis_index("front")
    square[...] = jnp.zeros_like(square)
    for c in few:
        c.wait()
    share = sep.shape[0]
    square[pl.ds(pl.multiple_of(front * share, 8), share), :] = sep[...]
    turned = square[...].T
    for h in range(HALVES):
        top[h] = turned[h * width : (h + 1) * width]
    row_columns[...] = rows[...].astype(F32).T
    prepare_nodes(first, 0, row_columns, dinv_v, upd_v, rhs_v, outs, copies[:first])
    for group in copies[first:]:
        for c in group:
            c.wait()


def prepare_second_kernel(first, row_columns, rhs, dinv, upd, _, *outs):
    count = rhs.shape[0]
    waits = [()] * count
    prepare_nodes(count, first, row_columns, dinv, upd, rhs, outs, waits)


def prepared(count, size, cols):
    half = ((count, size, size), BF16)
    return [((HALVES, count, cols // HALVES, size), F32), half, half, half, half]


def prepare_first(rhs, dinv, update, rows, sep, after):
    nodes, size, cols = rhs.shape
    first = nodes // 2
    some = (first, size, cols)
    big = pltpu.VMEM(some, F32)
    return call(
        lambda *refs: prepare_first_kernel(nodes, *refs),
        "prepare_first",
        [(HBM, a) for a in (rows, sep, rhs, dinv, update)] + [(pl.ANY, after)],
        prepared(first, size, cols)
        + [((HALVES, cols // HALVES, size), F32), ((size, nodes), F32)]
        + [((nodes - first, *some[1:]), F32)] * 3,
        [big, big, big, pltpu.VMEM((size, cols), F32)]
        + [pltpu.VMEM(rows.shape, jnp.int32), pltpu.VMEM(sep.shape, F32)]
        + [pltpu.SemaphoreType.DMA((3, nodes)), pltpu.SemaphoreType.DMA((2,))],
    )


def prepare_second(row_columns, rhs, dinv, update, after):
    count, size, cols = rhs.shape
    first = row_columns.shape[1] - count
    return call(
        lambda *refs: prepare_second_kernel(first, *refs),
        "prepare_second",
        [(V, a) for a in (row_columns, rhs, dinv, update)] + [(pl.ANY, after)],
        prepared(count, size, cols),
    )


def forward_kernel(nodes, fronts, *refs):
    (parent_h, acc_a, acc_b, top), parts, refs = refs[:4], (refs[4:8], refs[8:12]), refs[13:]
    solved, send, keep, square, parent, sem = refs[:6]
    accs = refs[6:]
    copy = pltpu.make_async_copy(parent_h, parent, sem)
    copy.start()
    first, width = acc_a.shape[1:3]
    for h in range(HALVES):
        for k in range(nodes):
            accs[h][k] = acc_a[h, k] if k < first else acc_b[h, k - first]
        accs[h][nodes] = top[h]
    for k in range(nodes):
        inv_hi, inv_lo, upd_hi, upd_lo = parts[k // first]
        i = k % first
        inverse = (inv_hi[i], inv_lo[i])
        update = (upd_hi[i], upd_lo[i])
        for h in range(HALVES):
            value = dot3(split(accs[h][k]), inverse, NT)
            solved[k, h * width : (h + 1) * width] = value
            moved = dot3(split(value), update, NT)
            if k + h == 0:
                copy.wait()
            above = nodes if k == nodes - 1 else parent[k]
            accs[h][above] = accs[h][above] - moved
    front = lax.axis_index("front")
    chunk = width * HALVES // fronts
    for h in range(HALVES):
        square[h * width : (h + 1) * width] = accs[h][nodes]
    low_bit = front % 2
    for i in range(fronts // 2):
        for ref, own in ((keep, low_bit), (send, 1 - low_bit)):
            start = pl.multiple_of((2 * i + own) * chunk, 8)
            ref[i * chunk : (i + 1) * chunk] = square[pl.ds(start, chunk), :]


def local_forward(parent, acc_a, acc_b, top, first_halves, second_halves, after, fronts):
    first, (width, size) = acc_a.shape[1], acc_a.shape[2:]
    nodes = first + acc_b.shape[1]
    cols = width * HALVES
    part = ((cols // 2, size), F32)
    return call(
        lambda *refs: forward_kernel(nodes, fronts, *refs),
        "local_forward",
        [(HBM, parent)]
        + [(V, a) for a in (acc_a, acc_b, top, *first_halves, *second_halves)]
        + [(pl.ANY, after)],
        [((nodes, cols, size), F32), part, part],
        [pltpu.VMEM((cols, size), F32), pltpu.SMEM((nodes,), jnp.int32), pltpu.SemaphoreType.DMA]
        + [pltpu.VMEM((nodes + 1, width, size), F32)] * HALVES,
    )


def backward_kernel(nodes, fronts, *refs):
    (parent_h, solved), parts, refs = refs[:2], (refs[2:6], refs[6:10]), refs[10:]
    pieces = refs[:fronts]
    sol, sep_out = refs[fronts : 2 + fronts]
    square, parent, staged, sep_v, sem, sems = refs[2 + fronts : 8 + fronts]
    known = refs[8 + fronts :]
    first = parts[0][0].shape[0]
    copy = pltpu.make_async_copy(parent_h, parent, sem)
    copy.start()
    chunk = pieces[0].shape[0]
    width = known[0].shape[1]
    order = [p[...] for p in pieces]
    for bit in range(fronts.bit_length() - 1):
        flip = bit_of("front", bit) == 1
        order = [jnp.where(flip, order[i ^ (1 << bit)], order[i]) for i in range(fronts)]
    for i, value in enumerate(order):
        at = i * chunk
        known[at // width][nodes, at % width : at % width + chunk] = value
    outs = []
    for k in reversed(range(nodes)):
        i = k % first
        inv_hi, inv_lo, upd_hi, upd_lo = parts[k // first]
        inverse = (inv_hi[i], inv_lo[i])
        update = (upd_hi[i], upd_lo[i])
        if k == nodes - 2:
            copy.wait()
        above = nodes if k == nodes - 1 else parent[k]
        for h in range(HALVES):
            rows = slice(h * width, (h + 1) * width)
            part = solved[k, rows] - dot3(split(known[h][above]), update, NN)
            value = dot3(split(part), inverse, NN)
            known[h][k] = value
            staged[k, :, rows] = value.T
        out = pltpu.make_async_copy(staged.at[k], sol.at[k], sems.at[k])
        out.start()
        outs.append(out)
        if k == nodes - 1:
            for h in range(HALVES):
                square[:, h * width : (h + 1) * width] = known[h][nodes].T
            share = sep_v.shape[0]
            start = pl.multiple_of(lax.axis_index("front") * share, 8)
            sep_v[...] = square[pl.ds(start, share), :]
            out = pltpu.make_async_copy(sep_v, sep_out, sems.at[nodes])
            out.start()
            outs.append(out)
    for out in outs:
        out.wait()


def local_backward(parent, solved, first_halves, second_halves, pieces):
    nodes, cols, size = solved.shape
    fronts = len(pieces)
    sol, sep = jax.ShapeDtypeStruct((nodes, size, cols), F32), ((size // fronts, cols), F32)
    ins = (solved, *first_halves, *second_halves, *pieces)
    return pl.pallas_call(
        lambda *refs: backward_kernel(nodes, fronts, *refs),
        name="local_backward",
        in_specs=[pl.BlockSpec(memory_space=HBM)] + [pl.BlockSpec(memory_space=V)] * len(ins),
        out_specs=(pl.BlockSpec(memory_space=HBM),) * 2,
        out_shape=(sol, jax.ShapeDtypeStruct(*sep)),
        scratch_shapes=[pltpu.VMEM((size, cols), F32), pltpu.SMEM((nodes,), jnp.int32)]
        + [pltpu.VMEM((nodes, size, cols), F32), pltpu.VMEM(*sep), pltpu.SemaphoreType.DMA]
        + [pltpu.SemaphoreType.DMA((nodes + 1,))]
        + [pltpu.VMEM((nodes + 1, cols // HALVES, size), F32)] * HALVES,
        compiler_params=pltpu.CompilerParams(vmem_limit_bytes=VMEM_BYTES),
    )(pltpu.with_memory_space_constraint(parent, HBM), *ins)


def stack_kernel(first, second, out, sems):
    copies = [pltpu.make_async_copy(a, out.at[i], sems.at[i]) for i, a in enumerate((first, second))]
    for c in copies:
        c.start()
    for c in copies:
        c.wait()


def block_map_kernel(fronts, *refs):
    parts = refs[:fronts]
    _, total, part, inverse_halves, square = refs[fronts:]
    front = lax.axis_index("front")
    share = parts[0].shape[1]
    for i in range(fronts):
        start = pl.multiple_of((front ^ i) * share, 8)
        square[:, pl.ds(start, share), :] = parts[i][...]
    inverse = split(square[0])
    inverse_halves[0], inverse_halves[1] = inverse
    value = -dot3(inverse, split(square[1]), NN)
    total[...] = value
    half = part.shape[1]
    send_blocks([part], [value[:half], value[half:]])


def block_map(parts, after):
    fronts = len(parts)
    size = parts[0].shape[2]
    return call(
        lambda *refs: block_map_kernel(fronts, *refs),
        "block_map",
        [(V, a) for a in parts] + [(pl.ANY, after)],
        [((size, size), F32), ((1, size // 2, size), F32), ((2, size, size), BF16)],
        [pltpu.VMEM((2, size, size), F32)],
    )


def quarters(x):
    half = x.shape[0] // 2
    return [x[i : i + half, j : j + half] for i in (0, half) for j in (0, half)]


def joined(a, b, c, d):
    first, second = jnp.concatenate([a, b], axis=1), jnp.concatenate([c, d], axis=1)
    return jnp.concatenate([first, second], axis=0)


def low_core():
    return bit_of("front", 0) == 0


def send_blocks(parts, blocks):
    count = sum(part.shape[0] for part in parts)
    low = low_core()
    i = 0
    for part in parts:
        for j in range(part.shape[0]):
            part[j] = jnp.where(low, blocks[i], blocks[len(blocks) - count + i])
            i += 1


def came_blocks(mine, pairs, total):
    low = low_core()
    mine = [m[j] for m in mine for j in range(m.shape[0])]
    pairs = [p[j] for p in pairs for j in range(p.shape[0])]
    count = len(mine)
    blocks = [jnp.where(low, mine[i], pairs[i]) for i in range(count)]
    for i in range(count, total):
        j = i - total + count
        blocks.append(jnp.where(low, pairs[j], mine[j]))
    return blocks


def k_blocks(k):
    a, b, _, d = quarters(k)
    return [a, b, d]


def k_of(blocks):
    return joined(blocks[0], blocks[1], blocks[1].T, blocks[2])


def send_maps(parts, k, t):
    for i, block in enumerate(k_blocks(k)):
        parts[0][i] = block
    send_blocks(parts[1:], quarters(t))


def first_merge_kernel(*refs):
    own, mine, pairs, _, kept, mixed, halves, curve_u, total_u, total_l, *parts = refs
    upper = bit_of("leaf", 0) == 1
    came = jnp.concatenate(came_blocks([mine], [pairs], 2), axis=0)
    mine = own[...]
    low = jnp.where(upper, came, mine)
    up = jnp.where(upper, mine, came)
    low_s, up_s = split(low), split(up)
    for ref, value in ((total_u, up_s), (total_l, low_s)):
        ref[0], ref[1] = value
    k_up = dot3(up_s, up_s, TN)
    k_up_s = split(k_up)
    curve_u[0], curve_u[1] = k_up_s
    x = dot3(k_up_s, low_s, NN)
    t = dot3(up_s, low_s, NN)
    k = dot3(low_s, low_s, TN) + dot3(low_s, split(x), TN)
    kept[0], kept[1] = k, t
    send_maps(parts, k, t)
    size = low.shape[0]
    row = lax.broadcasted_iota(jnp.int32, (size, size), 0)
    col = lax.broadcasted_iota(jnp.int32, (size, size), 1)
    unit = (row == col).astype(F32)
    keep_split(halves, jnp.where(upper, up.T, unit))
    mixed[0] = jnp.where(upper, t, low + x)
    mixed[1] = jnp.where(upper, unit, up)


def merge_kernel(bit, *refs):
    own, other, mine, pairs, mixed = refs[:5]
    kept, mixed_n, halves, curve_u, total_u, total_l, *parts = refs[5:]
    upper = bit_of("leaf", bit) == 1
    own_k, own_t = own[0], own[1]
    other_k, other_t = k_of(other), joined(*came_blocks([mine], [pairs], 4))
    low_s = split(jnp.where(upper, other_t, own_t))
    up_s = split(jnp.where(upper, own_t, other_t))
    k_low = jnp.where(upper, other_k, own_k)
    k_up_s = split(jnp.where(upper, own_k, other_k))
    for ref, value in ((total_u, up_s), (total_l, low_s), (curve_u, k_up_s)):
        ref[0], ref[1] = value
    x = dot3(k_up_s, low_s, NN)
    x_s = split(x)
    a, e = mixed[0], mixed[1]
    keep_split(halves, jnp.where(upper, a.T, e))
    a_s, e_s = split(a), split(e)
    a_n = jnp.where(upper, dot3(a_s, low_s, NN), a + dot3(e_s, x_s, TN))
    e_n = jnp.where(upper, e, dot3(up_s, e_s, NN))
    k = k_low + dot3(low_s, x_s, TN)
    t = dot3(up_s, low_s, NN)
    kept[0], kept[1] = k, t
    send_maps(parts, k, t)
    mixed_n[0], mixed_n[1] = a_n, e_n


def boundary_kernel(bit, own, other, mixed, two, one, halves, curve, total):
    k, t, k_up = own[0], split(own[1]), split(k_of(other))
    total[0], total[1] = t
    curve[0], curve[1] = k_up
    keep_split(halves, jnp.where(bit_of("leaf", bit) == 1, mixed[0].T, mixed[1]))
    x = dot3(k_up, t, NN)
    two[0], two[1], one[0] = k_blocks(k + dot3(t, split(x), TN))


def last_merge_kernel(bit, mixed, mine, pairs, curve, total, added):
    upper = bit_of("leaf", bit) == 1
    came = split(joined(*came_blocks([mine], [pairs], 4)))
    a, e = mixed[0], mixed[1]
    a_s, e_s = split(a), split(e)
    x = split(dot3(pair(curve), pair(total), NN))
    a_n = jnp.where(upper, dot3(a_s, came, NN), a + dot3(e_s, x, TN))
    e_n = jnp.where(upper, e, dot3(came, e_s, NN))
    keep_split(added, jnp.where(bit_of("leaf", bit + 1) == 1, a_n.T, e_n))


def maps(size):
    both, whole = ((2, size, size), BF16), ((2, size, size), F32)
    half = size // 2
    sends = [((i, half, half), F32) for i in (3, 2)]
    return [whole, whole, both, both, both, both] + sends


def fold_kernel(bit, own, other, send, keep):
    total = send.shape[0]
    chunk = total
    value = own[...] + other[...]
    first, second = value[:chunk], value[chunk:]
    high = bit_of("front", bit) == 1
    send[...] = jnp.where(high, first, second)
    keep[...] = jnp.where(high, second, first)


def enter_kernel(own, other, inverse, own_map, sol, message):
    drive = own[...] + other[...]
    value = dot3(split(drive), pair(inverse), NT)
    sol[...] = value
    rows = value.shape[0]
    message[:rows] = value
    message[rows:] = dot3(split(value), split(own_map[...]), NN)


def step_kernel(bit, rounds, held, *refs):
    sol, own, other, halves, curve_u, total_u, total_l = refs[:7]
    sol_n, message = refs[7 + held], refs[8 + held :]
    last = bit == rounds - 2
    upper = bit_of("leaf", bit) == 1
    rows = sol.shape[0]
    z_own, p_own = own[:rows], own[rows:]
    if last:
        z_other = p_other = other[...]
    else:
        z_other, p_other = other[:rows], other[rows:]
    z_low = jnp.where(upper, z_other, z_own)
    p_up = jnp.where(upper, p_own, p_other)
    z_low_s = split(z_low)
    middle = p_up + dot3(z_low_s, pair(curve_u), NN)
    middle_s = split(middle)
    given = split(jnp.where(upper, z_low, middle))
    sol_n[...] = sol[...] + dot3(given, pair(halves), NN)
    z_up = z_own if last else jnp.where(upper, z_own, z_other)
    p_low = p_own if last else jnp.where(upper, p_other, p_own)
    z_new = z_up + dot3(z_low_s, pair(total_u), NT)
    p_new = p_low + dot3(middle_s, pair(total_l), NN)
    if last:
        message[0][...] = jnp.where(bit_of("leaf", bit + 1) == 1, p_new, z_new)
        message[1][...] = z_new
        return
    message[0][:rows], message[0][rows:] = z_new, p_new
    if bit == rounds - 3:
        message[1][...] = jnp.where(bit_of("leaf", bit + 1) == 1, p_new, z_new)


def turn_kernel(bit, own_z, came, two, one, given):
    value = came[...]
    middle = value + dot3(split(own_z[...]), split(k_of([two[0], two[1], one[0]])), NN)
    given[...] = jnp.where(bit_of("leaf", bit) == 1, value, middle)


def passed_on(bit, last, given, received):
    away = bit_of("leaf", bit) == bit_of("leaf", last)
    return jnp.where(away, received, given)


def leave_kernel(last, sol, given, received, halves, inverse, top):
    came = passed_on(1, last, given[...], received[...])
    value = sol[...] + dot3(split(came), pair(halves), NN)
    top[...] = dot3(split(value), pair(inverse), NN)


def gather_front(x, bits):
    pieces = {0: x}
    for bit in reversed(range(bits)):
        for i in list(pieces):
            pieces[i | (1 << bit)] = exchange(pieces[i], "front", bit)
    return [pieces[i] for i in range(1 << bits)]


def local(rhs_local, dinv_local, update_local, parent, row_blocks, sep_rhs, sep_dinv, sep_coupling):
    fronts, leaves = lax.axis_size("front"), lax.axis_size("leaf")
    front_bits, rounds = fronts.bit_length() - 1, leaves.bit_length() - 1
    size = sep_dinv.shape[1]
    cols = sep_rhs.shape[1]
    chunk = cols // fronts

    (stacked,) = call(
        stack_kernel,
        "stack",
        [(HBM, sep_dinv), (HBM, sep_coupling)],
        [((2, *sep_dinv.shape), F32)],
        [pltpu.SemaphoreType.DMA((2,))],
    )
    came = {0: stacked}
    for bit in reversed(range(1, front_bits)):
        for i in list(came):
            came[i | (1 << bit)] = exchange(came[i], "front", bit)
    came[1] = exchange(stacked, "front", 0)
    acc_a, *first_halves = prepare_first(
        rhs_local, dinv_local, update_local, row_blocks, sep_rhs, stacked
    )
    first_halves, (top, row_columns, *raw) = first_halves[:4], first_halves[4:]
    for i in range(2, fronts, 2):
        held, _ = lax.optimization_barrier((came[i], acc_a))
        came[i + 1] = exchange(held, "front", 0)
    acc_b, *second_halves = prepare_second(row_columns, *raw, acc_a)
    own_map, part, inverse = block_map([came[i] for i in range(fronts)], acc_b)
    mine = exchange(part, "leaf", 0)
    solved, send, keep = local_forward(
        parent, acc_a, acc_b, top, first_halves, second_halves, own_map, fronts
    )
    mine, send = lax.optimization_barrier((mine, send))
    pairs = exchange(mine, "front", 0)
    for bit in range(front_bits):
        received = exchange(send, "front", bit)
        if bit + 1 < front_bits:
            half = ((keep.shape[0] // 2, size), F32)
            send, keep = call(
                lambda *refs, bit=bit: fold_kernel(bit + 1, *refs),
                "fold",
                [(V, keep), (V, received)],
                [half, half],
            )
    kept, mixed, *tools = call(
        first_merge_kernel,
        "merge_0",
        [(V, own_map), (V, mine), (V, pairs), (pl.ANY, send)],
        maps(size),
    )
    tools, parts = tools[:4], tools[4:]
    sol, message = call(
        enter_kernel,
        "enter",
        [(V, keep), (V, received), (V, inverse), (V, own_map)],
        [((chunk, size), F32), ((2 * chunk, size), F32)],
    )
    share = ((chunk, size), F32)
    middle = leaves // 2
    boundary = [(middle - 2 + i, middle + i) for i in range(2)]
    boundary += [(j, i) for i, j in boundary]
    paired = {i for i, _ in boundary}
    boundary += [(i, i ^ 1) for i in range(leaves) if i not in paired]
    for bit in range(rounds - 1):
        last = bit == rounds - 2
        received = exchange(short[0] if last else message, "leaf", bit)
        ahead, held = [], []
        if not last:
            other, mine = [exchange(part, "leaf", bit + 1) for part in parts]
            ahead = [other]
        if bit == rounds - 3:
            half = size // 2
            *ahead, halves, curve, own_t = call(
                lambda *refs: boundary_kernel(rounds - 2, *refs),
                "boundary",
                [(V, kept), (V, other), (V, mixed)],
                [((2, half, half), F32), ((1, half, half), F32)] + [((2, size, size), BF16)] * 3,
            )
            blocks = [lax.ppermute(b, "leaf", boundary) for b in ahead]
            held = [other]
        sol, *message = call(
            lambda *refs, bit=bit: step_kernel(bit, rounds, len(held), *refs),
            f"step_{bit}",
            [(V, a) for a in (sol, message, received, *tools)] + [(pl.ANY, a) for a in held],
            [share] + ([share] if last else [((2 * chunk, size), F32)]) + [share] * (bit >= rounds - 3),
        )
        if not last:
            message, *short = message
        if bit == rounds - 3:
            tools = [halves, curve, own_t, own_t]
        elif not last:
            mine, _ = lax.optimization_barrier((mine, sol))
            pairs = exchange(mine, "front", 0)
            kept, mixed, *tools = call(
                lambda *refs, bit=bit: merge_kernel(bit + 1, *refs),
                f"merge_{bit + 1}",
                [(V, a) for a in (kept, other, mine, pairs, mixed)],
                maps(size),
            )
            tools, parts = tools[:4], tools[4:]
    mine, _ = lax.optimization_barrier((mine, sol))
    pairs = exchange(mine, "front", 0)
    (added,) = call(
        lambda *refs: last_merge_kernel(rounds - 2, *refs),
        "last_merge",
        [(V, a) for a in (mixed, mine, pairs, curve, own_t)],
        [((2, size, size), BF16)],
    )
    came = lax.ppermute(message[0], "leaf", boundary)
    (given,) = call(
        lambda *refs: turn_kernel(rounds - 1, *refs),
        "turn",
        [(V, a) for a in (message[1], came, *blocks)],
        [share],
    )
    for bit in reversed(range(2, rounds - 1)):
        given = passed_on(bit, rounds - 1, given, exchange(given, "leaf", bit))
    received = exchange(given, "leaf", 1)
    (top,) = call(
        lambda *refs: leave_kernel(rounds - 1, *refs),
        "leave",
        [(V, a) for a in (sol, given, received, added, inverse)],
        [share],
    )
    pieces = gather_front(top, front_bits)
    sol_local, sep_solution = local_backward(
        parent, solved, first_halves, second_halves, pieces
    )
    return (sol_local, sep_solution)


def solution(mesh):
    spread3 = P(("leaf", "front"), None, None)
    spread2 = P(("leaf", "front"), None)
    spread1 = P(("leaf", "front"))
    return jax.shard_map(
        local,
        mesh=mesh,
        in_specs=(spread3, spread3, spread3, spread1, spread2, spread2, spread2, spread2),
        out_specs=(spread3, spread2),
        check_vma=False,
    )
```

```python
import jax
import jax.numpy as jnp
from jax import lax
from jax.experimental import pallas as pl
from jax.experimental.pallas import tpu as pltpu
from jax.sharding import PartitionSpec as P

F32 = jnp.float32
BF16 = jnp.bfloat16
NN = (((1,), (0,)), ((), ()))
NT = (((1,), (1,)), ((), ()))
TN = (((0,), (0,)), ((), ()))
VMEM_BYTES = 24 << 20
HALVES = 2


def split(x):
    high = x.astype(BF16)
    return high, (x - high.astype(F32)).astype(BF16)


def dot1(a, b, dims):
    return lax.dot_general(a, b, dims, preferred_element_type=F32)


def dot3(a, b, dims):
    axis = 1 - dims[0][0][0]
    rows = a[0].shape[axis]
    both = dot1(jnp.concatenate(a, axis=axis), b[0], dims)
    return both[:rows] + (both[rows:] + dot1(a[0], b[1], dims))


def keep_split(ref, value):
    ref[0], ref[1] = split(value)


def pair(ref):
    return ref[0], ref[1]


def bit_of(axis, bit):
    return (lax.axis_index(axis) // (1 << bit)) % 2


def call(kernel, name, ins, outs, scratch=()):
    specs = [pl.BlockSpec(memory_space=space) for space, _ in ins]
    ins = [
        (space, pltpu.with_memory_space_constraint(a, HBM) if space == HBM else a)
        for space, a in ins
    ]
    return pl.pallas_call(
        kernel,
        name=name,
        in_specs=specs,
        out_specs=tuple(pl.BlockSpec(memory_space=pltpu.VMEM) for _ in outs),
        out_shape=tuple(jax.ShapeDtypeStruct(*o) for o in outs),
        scratch_shapes=list(scratch),
        compiler_params=pltpu.CompilerParams(vmem_limit_bytes=VMEM_BYTES),
    )(*[a for _, a in ins])


V = pltpu.VMEM
HBM = pltpu.HBM


def swap(x, axis, mask):
    n = lax.axis_size(axis)
    return lax.ppermute(x, axis, [(i, i ^ mask) for i in range(n)])


def exchange(x, axis, bit):
    return swap(x, axis, 1 << bit)


def prepare_nodes(count, rows_at, row_columns, dinv, upd, rhs, outs, waits):
    acc, inv_hi, inv_lo, upd_hi, upd_lo = outs
    size = dinv.shape[1]
    width = acc.shape[2]
    lane = lax.broadcasted_iota(jnp.int32, (size, size), 1).astype(F32)
    for k in range(count):
        for c in waits[k]:
            c.wait()
        inv_hi[k], inv_lo[k] = split(dinv[k])
        high, low = split(upd[k])
        chosen = (lane == row_columns[:, rows_at + k : rows_at + k + 1]).astype(BF16)
        upd_hi[k] = dot1(chosen, high, NN).astype(BF16)
        upd_lo[k] = dot1(chosen, low, NN).astype(BF16)
        turned = rhs[k].T
        for h in range(HALVES):
            acc[h, k] = turned[h * width : (h + 1) * width]


def prepare_first_kernel(nodes, *refs):
    (rows_h, sep_h, rhs_h, dinv_h, upd_h, _), refs = refs[:6], refs[6:]
    outs, (top, row_columns, rhs_n, dinv_n, upd_n), refs = refs[:5], refs[5:10], refs[10:]
    rhs_v, dinv_v, upd_v, square, rows, sep, sems, small = refs
    cols = rhs_v.shape[2]
    width = cols // HALVES
    first = nodes // 2
    few = [
        pltpu.make_async_copy(src, dst, small.at[i])
        for i, (src, dst) in enumerate(((rows_h, rows), (sep_h, sep)))
    ]
    for c in few:
        c.start()
    copies = []
    for k in range(nodes):
        ins = (upd_v, dinv_v, rhs_v) if k < first else (upd_n, dinv_n, rhs_n)
        group = [
            pltpu.make_async_copy(src.at[k], dst.at[k % first], sems.at[i, k])
            for i, (src, dst) in enumerate(zip((upd_h, dinv_h, rhs_h), ins))
        ]
        for c in group:
            c.start()
        copies.append(group)
    front = lax.axis_index("front")
    square[...] = jnp.zeros_like(square)
    for c in few:
        c.wait()
    share = sep.shape[0]
    square[pl.ds(pl.multiple_of(front * share, 8), share), :] = sep[...]
    turned = square[...].T
    for h in range(HALVES):
        top[h] = turned[h * width : (h + 1) * width]
    row_columns[...] = rows[...].astype(F32).T
    prepare_nodes(first, 0, row_columns, dinv_v, upd_v, rhs_v, outs, copies[:first])
    for group in copies[first:]:
        for c in group:
            c.wait()


def prepare_second_kernel(first, row_columns, rhs, dinv, upd, _, *outs):
    count = rhs.shape[0]
    waits = [()] * count
    prepare_nodes(count, first, row_columns, dinv, upd, rhs, outs, waits)


def prepared(count, size, cols):
    half = ((count, size, size), BF16)
    return [((HALVES, count, cols // HALVES, size), F32), half, half, half, half]


def prepare_first(rhs, dinv, update, rows, sep, after):
    nodes, size, cols = rhs.shape
    first = nodes // 2
    some = (first, size, cols)
    big = pltpu.VMEM(some, F32)
    return call(
        lambda *refs: prepare_first_kernel(nodes, *refs),
        "prepare_first",
        [(HBM, a) for a in (rows, sep, rhs, dinv, update)] + [(pl.ANY, after)],
        prepared(first, size, cols)
        + [((HALVES, cols // HALVES, size), F32), ((size, nodes), F32)]
        + [((nodes - first, *some[1:]), F32)] * 3,
        [big, big, big, pltpu.VMEM((size, cols), F32)]
        + [pltpu.VMEM(rows.shape, jnp.int32), pltpu.VMEM(sep.shape, F32)]
        + [pltpu.SemaphoreType.DMA((3, nodes)), pltpu.SemaphoreType.DMA((2,))],
    )


def prepare_second(row_columns, rhs, dinv, update, after):
    count, size, cols = rhs.shape
    first = row_columns.shape[1] - count
    return call(
        lambda *refs: prepare_second_kernel(first, *refs),
        "prepare_second",
        [(V, a) for a in (row_columns, rhs, dinv, update)] + [(pl.ANY, after)],
        prepared(count, size, cols),
    )


def forward_kernel(nodes, fronts, *refs):
    (parent_h, acc_a, acc_b, top), parts, refs = refs[:4], (refs[4:8], refs[8:12]), refs[13:]
    solved, send, keep, square, parent, sem = refs[:6]
    accs = refs[6:]
    copy = pltpu.make_async_copy(parent_h, parent, sem)
    copy.start()
    first, width = acc_a.shape[1:3]
    for h in range(HALVES):
        for k in range(nodes):
            accs[h][k] = acc_a[h, k] if k < first else acc_b[h, k - first]
        accs[h][nodes] = top[h]
    for k in range(nodes):
        inv_hi, inv_lo, upd_hi, upd_lo = parts[k // first]
        i = k % first
        inverse = (inv_hi[i], inv_lo[i])
        update = (upd_hi[i], upd_lo[i])
        for h in range(HALVES):
            value = dot3(split(accs[h][k]), inverse, NT)
            solved[k, h * width : (h + 1) * width] = value
            moved = dot3(split(value), update, NT)
            if k + h == 0:
                copy.wait()
            above = nodes if k == nodes - 1 else parent[k]
            accs[h][above] = accs[h][above] - moved
    front = lax.axis_index("front")
    chunk = width * HALVES // fronts
    for h in range(HALVES):
        square[h * width : (h + 1) * width] = accs[h][nodes]
    low_bit = front % 2
    for i in range(fronts // 2):
        for ref, own in ((keep, low_bit), (send, 1 - low_bit)):
            start = pl.multiple_of((2 * i + own) * chunk, 8)
            ref[i * chunk : (i + 1) * chunk] = square[pl.ds(start, chunk), :]


def local_forward(parent, acc_a, acc_b, top, first_halves, second_halves, after, fronts):
    first, (width, size) = acc_a.shape[1], acc_a.shape[2:]
    nodes = first + acc_b.shape[1]
    cols = width * HALVES
    part = ((cols // 2, size), F32)
    return call(
        lambda *refs: forward_kernel(nodes, fronts, *refs),
        "local_forward",
        [(HBM, parent)]
        + [(V, a) for a in (acc_a, acc_b, top, *first_halves, *second_halves)]
        + [(pl.ANY, after)],
        [((nodes, cols, size), F32), part, part],
        [pltpu.VMEM((cols, size), F32), pltpu.SMEM((nodes,), jnp.int32), pltpu.SemaphoreType.DMA]
        + [pltpu.VMEM((nodes + 1, width, size), F32)] * HALVES,
    )


def backward_kernel(nodes, fronts, *refs):
    (parent_h, solved), parts, refs = refs[:2], (refs[2:6], refs[6:10]), refs[10:]
    pieces = refs[:fronts]
    sol, sep_out = refs[fronts : 2 + fronts]
    square, parent, staged, sep_v, sem, sems = refs[2 + fronts : 8 + fronts]
    known = refs[8 + fronts :]
    first = parts[0][0].shape[0]
    copy = pltpu.make_async_copy(parent_h, parent, sem)
    copy.start()
    chunk = pieces[0].shape[0]
    width = known[0].shape[1]
    order = [p[...] for p in pieces]
    for bit in range(fronts.bit_length() - 1):
        flip = bit_of("front", bit) == 1
        order = [jnp.where(flip, order[i ^ (1 << bit)], order[i]) for i in range(fronts)]
    for i, value in enumerate(order):
        at = i * chunk
        known[at // width][nodes, at % width : at % width + chunk] = value
    outs = []
    for k in reversed(range(nodes)):
        i = k % first
        inv_hi, inv_lo, upd_hi, upd_lo = parts[k // first]
        inverse = (inv_hi[i], inv_lo[i])
        update = (upd_hi[i], upd_lo[i])
        if k == nodes - 2:
            copy.wait()
        above = nodes if k == nodes - 1 else parent[k]
        for h in range(HALVES):
            rows = slice(h * width, (h + 1) * width)
            part = solved[k, rows] - dot3(split(known[h][above]), update, NN)
            value = dot3(split(part), inverse, NN)
            known[h][k] = value
            staged[k, :, rows] = value.T
        out = pltpu.make_async_copy(staged.at[k], sol.at[k], sems.at[k])
        out.start()
        outs.append(out)
        if k == 0:
            for h in range(HALVES):
                square[:, h * width : (h + 1) * width] = known[h][nodes].T
            share = sep_v.shape[0]
            start = pl.multiple_of(lax.axis_index("front") * share, 8)
            sep_v[...] = square[pl.ds(start, share), :]
            out = pltpu.make_async_copy(sep_v, sep_out, sems.at[nodes])
            out.start()
            outs.append(out)
    for out in outs:
        out.wait()


def local_backward(parent, solved, first_halves, second_halves, pieces):
    nodes, cols, size = solved.shape
    fronts = len(pieces)
    sol, sep = jax.ShapeDtypeStruct((nodes, size, cols), F32), ((size // fronts, cols), F32)
    ins = (solved, *first_halves, *second_halves, *pieces)
    return pl.pallas_call(
        lambda *refs: backward_kernel(nodes, fronts, *refs),
        name="local_backward",
        in_specs=[pl.BlockSpec(memory_space=HBM)] + [pl.BlockSpec(memory_space=V)] * len(ins),
        out_specs=(pl.BlockSpec(memory_space=HBM),) * 2,
        out_shape=(sol, jax.ShapeDtypeStruct(*sep)),
        scratch_shapes=[pltpu.VMEM((size, cols), F32), pltpu.SMEM((nodes,), jnp.int32)]
        + [pltpu.VMEM((nodes, size, cols), F32), pltpu.VMEM(*sep), pltpu.SemaphoreType.DMA]
        + [pltpu.SemaphoreType.DMA((nodes + 1,))]
        + [pltpu.VMEM((nodes + 1, cols // HALVES, size), F32)] * HALVES,
        compiler_params=pltpu.CompilerParams(vmem_limit_bytes=VMEM_BYTES),
    )(pltpu.with_memory_space_constraint(parent, HBM), *ins)


def stack_kernel(first, second, out, sems):
    copies = [pltpu.make_async_copy(a, out.at[i], sems.at[i]) for i, a in enumerate((first, second))]
    for c in copies:
        c.start()
    for c in copies:
        c.wait()


def block_map_kernel(fronts, *refs):
    parts = refs[:fronts]
    _, total, part, inverse_halves, square = refs[fronts:]
    front = lax.axis_index("front")
    share = parts[0].shape[1]
    for i in range(fronts):
        start = pl.multiple_of((front ^ i) * share, 8)
        square[:, pl.ds(start, share), :] = parts[i][...]
    inverse = split(square[0])
    inverse_halves[0], inverse_halves[1] = inverse
    value = -dot3(inverse, split(square[1]), NN)
    total[...] = value
    half = part.shape[1]
    send_blocks([part], [value[:half], value[half:]])


def block_map(parts, after):
    fronts = len(parts)
    size = parts[0].shape[2]
    return call(
        lambda *refs: block_map_kernel(fronts, *refs),
        "block_map",
        [(V, a) for a in parts] + [(pl.ANY, after)],
        [((size, size), F32), ((1, size // 2, size), F32), ((2, size, size), BF16)],
        [pltpu.VMEM((2, size, size), F32)],
    )


def quarters(x):
    half = x.shape[0] // 2
    return [x[i : i + half, j : j + half] for i in (0, half) for j in (0, half)]


def joined(a, b, c, d):
    first, second = jnp.concatenate([a, b], axis=1), jnp.concatenate([c, d], axis=1)
    return jnp.concatenate([first, second], axis=0)


def low_core():
    return bit_of("front", 0) == 0


def send_blocks(parts, blocks):
    count = sum(part.shape[0] for part in parts)
    low = low_core()
    i = 0
    for part in parts:
        for j in range(part.shape[0]):
            part[j] = jnp.where(low, blocks[i], blocks[len(blocks) - count + i])
            i += 1


def came_blocks(mine, pairs, total):
    low = low_core()
    mine = [m[j] for m in mine for j in range(m.shape[0])]
    pairs = [p[j] for p in pairs for j in range(p.shape[0])]
    count = len(mine)
    blocks = [jnp.where(low, mine[i], pairs[i]) for i in range(count)]
    for i in range(count, total):
        j = i - total + count
        blocks.append(jnp.where(low, pairs[j], mine[j]))
    return blocks


def k_blocks(k):
    a, b, _, d = quarters(k)
    return [a, b, d]


def k_of(blocks):
    return joined(blocks[0], blocks[1], blocks[1].T, blocks[2])


def send_maps(parts, k, t):
    for i, block in enumerate(k_blocks(k)):
        parts[0][i] = block
    send_blocks(parts[1:], quarters(t))


def first_merge_kernel(*refs):
    own, mine, pairs, _, kept, mixed, halves, curve_u, total_u, total_l, *parts = refs
    upper = bit_of("leaf", 0) == 1
    came = jnp.concatenate(came_blocks([mine], [pairs], 2), axis=0)
    mine = own[...]
    low = jnp.where(upper, came, mine)
    up = jnp.where(upper, mine, came)
    low_s, up_s = split(low), split(up)
    for ref, value in ((total_u, up_s), (total_l, low_s)):
        ref[0], ref[1] = value
    k_up = dot3(up_s, up_s, TN)
    k_up_s = split(k_up)
    curve_u[0], curve_u[1] = k_up_s
    x = dot3(k_up_s, low_s, NN)
    t = dot3(up_s, low_s, NN)
    k = dot3(low_s, low_s, TN) + dot3(low_s, split(x), TN)
    kept[0], kept[1] = k, t
    send_maps(parts, k, t)
    size = low.shape[0]
    row = lax.broadcasted_iota(jnp.int32, (size, size), 0)
    col = lax.broadcasted_iota(jnp.int32, (size, size), 1)
    unit = (row == col).astype(F32)
    keep_split(halves, jnp.where(upper, up.T, unit))
    mixed[0] = jnp.where(upper, t, low + x)
    mixed[1] = jnp.where(upper, unit, up)


def merge_kernel(bit, *refs):
    own, other, mine, pairs, mixed = refs[:5]
    kept, mixed_n, halves, curve_u, total_u, total_l, *parts = refs[5:]
    upper = bit_of("leaf", bit) == 1
    own_k, own_t = own[0], own[1]
    other_k, other_t = k_of(other), joined(*came_blocks([mine], [pairs], 4))
    low_s = split(jnp.where(upper, other_t, own_t))
    up_s = split(jnp.where(upper, own_t, other_t))
    k_low = jnp.where(upper, other_k, own_k)
    k_up_s = split(jnp.where(upper, own_k, other_k))
    for ref, value in ((total_u, up_s), (total_l, low_s), (curve_u, k_up_s)):
        ref[0], ref[1] = value
    x = dot3(k_up_s, low_s, NN)
    x_s = split(x)
    a, e = mixed[0], mixed[1]
    keep_split(halves, jnp.where(upper, a.T, e))
    a_s, e_s = split(a), split(e)
    a_n = jnp.where(upper, dot3(a_s, low_s, NN), a + dot3(e_s, x_s, TN))
    e_n = jnp.where(upper, e, dot3(up_s, e_s, NN))
    k = k_low + dot3(low_s, x_s, TN)
    t = dot3(up_s, low_s, NN)
    kept[0], kept[1] = k, t
    send_maps(parts, k, t)
    mixed_n[0], mixed_n[1] = a_n, e_n


def boundary_kernel(bit, own, other, mixed, two, one, halves, curve, total):
    k, t, k_up = own[0], split(own[1]), split(k_of(other))
    total[0], total[1] = t
    curve[0], curve[1] = k_up
    keep_split(halves, jnp.where(bit_of("leaf", bit) == 1, mixed[0].T, mixed[1]))
    x = dot3(k_up, t, NN)
    two[0], two[1], one[0] = k_blocks(k + dot3(t, split(x), TN))


def last_merge_kernel(bit, mixed, mine, pairs, curve, total, added):
    upper = bit_of("leaf", bit) == 1
    came = split(joined(*came_blocks([mine], [pairs], 4)))
    a, e = mixed[0], mixed[1]
    a_s, e_s = split(a), split(e)
    x = split(dot3(pair(curve), pair(total), NN))
    a_n = jnp.where(upper, dot3(a_s, came, NN), a + dot3(e_s, x, TN))
    e_n = jnp.where(upper, e, dot3(came, e_s, NN))
    keep_split(added, jnp.where(bit_of("leaf", bit + 1) == 1, a_n.T, e_n))


def maps(size):
    both, whole = ((2, size, size), BF16), ((2, size, size), F32)
    half = size // 2
    sends = [((i, half, half), F32) for i in (3, 2)]
    return [whole, whole, both, both, both, both] + sends


def fold_kernel(bit, own, other, send, keep):
    total = send.shape[0]
    chunk = total
    value = own[...] + other[...]
    first, second = value[:chunk], value[chunk:]
    high = bit_of("front", bit) == 1
    send[...] = jnp.where(high, first, second)
    keep[...] = jnp.where(high, second, first)


def enter_kernel(own, other, inverse, own_map, sol, message):
    drive = own[...] + other[...]
    value = dot3(split(drive), pair(inverse), NT)
    sol[...] = value
    rows = value.shape[0]
    message[:rows] = value
    message[rows:] = dot3(split(value), split(own_map[...]), NN)


def step_kernel(bit, rounds, held, *refs):
    sol, own, other, halves, curve_u, total_u, total_l = refs[:7]
    sol_n, message = refs[7 + held], refs[8 + held :]
    last = bit == rounds - 2
    upper = bit_of("leaf", bit) == 1
    rows = sol.shape[0]
    z_own, p_own = own[:rows], own[rows:]
    if last:
        z_other = p_other = other[...]
    else:
        z_other, p_other = other[:rows], other[rows:]
    z_low = jnp.where(upper, z_other, z_own)
    p_up = jnp.where(upper, p_own, p_other)
    z_low_s = split(z_low)
    middle = p_up + dot3(z_low_s, pair(curve_u), NN)
    middle_s = split(middle)
    given = split(jnp.where(upper, z_low, middle))
    sol_n[...] = sol[...] + dot3(given, pair(halves), NN)
    z_up = z_own if last else jnp.where(upper, z_own, z_other)
    p_low = p_own if last else jnp.where(upper, p_other, p_own)
    z_new = z_up + dot3(z_low_s, pair(total_u), NT)
    p_new = p_low + dot3(middle_s, pair(total_l), NN)
    if last:
        message[0][...] = jnp.where(bit_of("leaf", bit + 1) == 1, p_new, z_new)
        message[1][...] = z_new
        return
    message[0][:rows], message[0][rows:] = z_new, p_new
    if bit == rounds - 3:
        message[1][...] = jnp.where(bit_of("leaf", bit + 1) == 1, p_new, z_new)


def turn_kernel(bit, own_z, came, two, one, given):
    value = came[...]
    middle = value + dot3(split(own_z[...]), split(k_of([two[0], two[1], one[0]])), NN)
    given[...] = jnp.where(bit_of("leaf", bit) == 1, value, middle)


def passed_on(bit, last, given, received):
    away = bit_of("leaf", bit) == bit_of("leaf", last)
    return jnp.where(away, received, given)


def leave_kernel(last, sol, given, received, halves, inverse, top):
    came = passed_on(1, last, given[...], received[...])
    value = sol[...] + dot3(split(came), pair(halves), NN)
    top[...] = dot3(split(value), pair(inverse), NN)


def gather_front(x, bits):
    pieces = {0: x}
    for bit in reversed(range(bits)):
        for i in list(pieces):
            pieces[i | (1 << bit)] = exchange(pieces[i], "front", bit)
    return [pieces[i] for i in range(1 << bits)]


def local(rhs_local, dinv_local, update_local, parent, row_blocks, sep_rhs, sep_dinv, sep_coupling):
    fronts, leaves = lax.axis_size("front"), lax.axis_size("leaf")
    front_bits, rounds = fronts.bit_length() - 1, leaves.bit_length() - 1
    size = sep_dinv.shape[1]
    cols = sep_rhs.shape[1]
    chunk = cols // fronts

    (stacked,) = call(
        stack_kernel,
        "stack",
        [(HBM, sep_dinv), (HBM, sep_coupling)],
        [((2, *sep_dinv.shape), F32)],
        [pltpu.SemaphoreType.DMA((2,))],
    )
    came = {0: stacked}
    for bit in reversed(range(1, front_bits)):
        for i in list(came):
            came[i | (1 << bit)] = exchange(came[i], "front", bit)
    came[1] = exchange(stacked, "front", 0)
    acc_a, *first_halves = prepare_first(
        rhs_local, dinv_local, update_local, row_blocks, sep_rhs, stacked
    )
    first_halves, (top, row_columns, *raw) = first_halves[:4], first_halves[4:]
    for i in range(2, fronts, 2):
        held, _ = lax.optimization_barrier((came[i], acc_a))
        came[i + 1] = exchange(held, "front", 0)
    acc_b, *second_halves = prepare_second(row_columns, *raw, acc_a)
    own_map, part, inverse = block_map([came[i] for i in range(fronts)], acc_b)
    mine = exchange(part, "leaf", 0)
    solved, send, keep = local_forward(
        parent, acc_a, acc_b, top, first_halves, second_halves, own_map, fronts
    )
    mine, send = lax.optimization_barrier((mine, send))
    pairs = exchange(mine, "front", 0)
    for bit in range(front_bits):
        received = exchange(send, "front", bit)
        if bit + 1 < front_bits:
            half = ((keep.shape[0] // 2, size), F32)
            send, keep = call(
                lambda *refs, bit=bit: fold_kernel(bit + 1, *refs),
                "fold",
                [(V, keep), (V, received)],
                [half, half],
            )
    kept, mixed, *tools = call(
        first_merge_kernel,
        "merge_0",
        [(V, own_map), (V, mine), (V, pairs), (pl.ANY, send)],
        maps(size),
    )
    tools, parts = tools[:4], tools[4:]
    sol, message = call(
        enter_kernel,
        "enter",
        [(V, keep), (V, received), (V, inverse), (V, own_map)],
        [((chunk, size), F32), ((2 * chunk, size), F32)],
    )
    share = ((chunk, size), F32)
    middle = leaves // 2
    boundary = [(middle - 2 + i, middle + i) for i in range(2)]
    boundary += [(j, i) for i, j in boundary]
    paired = {i for i, _ in boundary}
    boundary += [(i, i ^ 1) for i in range(leaves) if i not in paired]
    for bit in range(rounds - 1):
        last = bit == rounds - 2
        received = exchange(short[0] if last else message, "leaf", bit)
        ahead, held = [], []
        if not last:
            other, mine = [exchange(part, "leaf", bit + 1) for part in parts]
            ahead = [other]
        if bit == rounds - 3:
            half = size // 2
            *ahead, halves, curve, own_t = call(
                lambda *refs: boundary_kernel(rounds - 2, *refs),
                "boundary",
                [(V, kept), (V, other), (V, mixed)],
                [((2, half, half), F32), ((1, half, half), F32)] + [((2, size, size), BF16)] * 3,
            )
            blocks = [lax.ppermute(b, "leaf", boundary) for b in ahead]
            held = [other]
        sol, *message = call(
            lambda *refs, bit=bit: step_kernel(bit, rounds, len(held), *refs),
            f"step_{bit}",
            [(V, a) for a in (sol, message, received, *tools)] + [(pl.ANY, a) for a in held],
            [share] + ([share] if last else [((2 * chunk, size), F32)]) + [share] * (bit >= rounds - 3),
        )
        if not last:
            message, *short = message
        if bit == rounds - 3:
            tools = [halves, curve, own_t, own_t]
        elif not last:
            mine, _ = lax.optimization_barrier((mine, sol))
            pairs = exchange(mine, "front", 0)
            kept, mixed, *tools = call(
                lambda *refs, bit=bit: merge_kernel(bit + 1, *refs),
                f"merge_{bit + 1}",
                [(V, a) for a in (kept, other, mine, pairs, mixed)],
                maps(size),
            )
            tools, parts = tools[:4], tools[4:]
    mine, _ = lax.optimization_barrier((mine, sol))
    pairs = exchange(mine, "front", 0)
    (added,) = call(
        lambda *refs: last_merge_kernel(rounds - 2, *refs),
        "last_merge",
        [(V, a) for a in (mixed, mine, pairs, curve, own_t)],
        [((2, size, size), BF16)],
    )
    came = lax.ppermute(message[0], "leaf", boundary)
    (given,) = call(
        lambda *refs: turn_kernel(rounds - 1, *refs),
        "turn",
        [(V, a) for a in (message[1], came, *blocks)],
        [share],
    )
    for bit in reversed(range(2, rounds - 1)):
        given = passed_on(bit, rounds - 1, given, exchange(given, "leaf", bit))
    received = exchange(given, "leaf", 1)
    (top,) = call(
        lambda *refs: leave_kernel(rounds - 1, *refs),
        "leave",
        [(V, a) for a in (sol, given, received, added, inverse)],
        [share],
    )
    pieces = gather_front(top, front_bits)
    sol_local, sep_solution = local_backward(
        parent, solved, first_halves, second_halves, pieces
    )
    return (sol_local, sep_solution)


def solution(mesh):
    spread3 = P(("leaf", "front"), None, None)
    spread2 = P(("leaf", "front"), None)
    spread1 = P(("leaf", "front"))
    return jax.shard_map(
        local,
        mesh=mesh,
        in_specs=(spread3, spread3, spread3, spread1, spread2, spread2, spread2, spread2),
        out_specs=(spread3, spread2),
        check_vma=False,
    )
```

```python
import jax
import jax.numpy as jnp
from jax import lax
from jax.experimental import pallas as pl
from jax.experimental.pallas import tpu as pltpu
from jax.sharding import PartitionSpec as P

F32 = jnp.float32
BF16 = jnp.bfloat16
NN = (((1,), (0,)), ((), ()))
NT = (((1,), (1,)), ((), ()))
TN = (((0,), (0,)), ((), ()))
VMEM_BYTES = 24 << 20
HALVES = 2


def split(x):
    high = x.astype(BF16)
    return high, (x - high.astype(F32)).astype(BF16)


def dot1(a, b, dims):
    return lax.dot_general(a, b, dims, preferred_element_type=F32)


def dot3(a, b, dims):
    axis = 1 - dims[0][0][0]
    rows = a[0].shape[axis]
    both = dot1(jnp.concatenate(a, axis=axis), b[0], dims)
    return both[:rows] + (both[rows:] + dot1(a[0], b[1], dims))


def keep_split(ref, value):
    ref[0], ref[1] = split(value)


def pair(ref):
    return ref[0], ref[1]


def bit_of(axis, bit):
    return (lax.axis_index(axis) // (1 << bit)) % 2


def call(kernel, name, ins, outs, scratch=()):
    specs = [pl.BlockSpec(memory_space=space) for space, _ in ins]
    ins = [
        (space, pltpu.with_memory_space_constraint(a, HBM) if space == HBM else a)
        for space, a in ins
    ]
    return pl.pallas_call(
        kernel,
        name=name,
        in_specs=specs,
        out_specs=tuple(pl.BlockSpec(memory_space=pltpu.VMEM) for _ in outs),
        out_shape=tuple(jax.ShapeDtypeStruct(*o) for o in outs),
        scratch_shapes=list(scratch),
        compiler_params=pltpu.CompilerParams(vmem_limit_bytes=VMEM_BYTES),
    )(*[a for _, a in ins])


V = pltpu.VMEM
HBM = pltpu.HBM


def swap(x, axis, mask):
    n = lax.axis_size(axis)
    return lax.ppermute(x, axis, [(i, i ^ mask) for i in range(n)])


def exchange(x, axis, bit):
    return swap(x, axis, 1 << bit)


def prepare_nodes(count, rows_at, row_columns, dinv, upd, rhs, outs, waits):
    acc, inv_hi, inv_lo, upd_hi, upd_lo = outs
    size = dinv.shape[1]
    width = acc.shape[2]
    lane = lax.broadcasted_iota(jnp.int32, (size, size), 1).astype(F32)
    for k in range(count):
        for c in waits[k]:
            c.wait()
        inv_hi[k], inv_lo[k] = split(dinv[k])
        high, low = split(upd[k])
        chosen = (lane == row_columns[:, rows_at + k : rows_at + k + 1]).astype(BF16)
        upd_hi[k] = dot1(chosen, high, NN).astype(BF16)
        upd_lo[k] = dot1(chosen, low, NN).astype(BF16)
        turned = rhs[k].T
        for h in range(HALVES):
            acc[h, k] = turned[h * width : (h + 1) * width]


def prepare_first_kernel(nodes, *refs):
    (rows_h, sep_h, rhs_h, dinv_h, upd_h, _), refs = refs[:6], refs[6:]
    outs, (top, row_columns, rhs_n, dinv_n, upd_n), refs = refs[:5], refs[5:10], refs[10:]
    rhs_v, dinv_v, upd_v, square, rows, sep, sems, small = refs
    cols = rhs_v.shape[2]
    width = cols // HALVES
    first = nodes // 2
    few = [
        pltpu.make_async_copy(src, dst, small.at[i])
        for i, (src, dst) in enumerate(((rows_h, rows), (sep_h, sep)))
    ]
    for c in few:
        c.start()
    copies = []
    for k in range(nodes):
        ins = (upd_v, dinv_v, rhs_v) if k < first else (upd_n, dinv_n, rhs_n)
        group = [
            pltpu.make_async_copy(src.at[k], dst.at[k % first], sems.at[i, k])
            for i, (src, dst) in enumerate(zip((upd_h, rhs_h, dinv_h), (ins[0], ins[2], ins[1])))
        ]
        for c in group:
            c.start()
        copies.append(group)
    front = lax.axis_index("front")
    square[...] = jnp.zeros_like(square)
    for c in few:
        c.wait()
    share = sep.shape[0]
    square[pl.ds(pl.multiple_of(front * share, 8), share), :] = sep[...]
    turned = square[...].T
    for h in range(HALVES):
        top[h] = turned[h * width : (h + 1) * width]
    row_columns[...] = rows[...].astype(F32).T
    prepare_nodes(first, 0, row_columns, dinv_v, upd_v, rhs_v, outs, copies[:first])
    for group in copies[first:]:
        for c in group:
            c.wait()


def prepare_second_kernel(first, row_columns, rhs, dinv, upd, _, *outs):
    count = rhs.shape[0]
    waits = [()] * count
    prepare_nodes(count, first, row_columns, dinv, upd, rhs, outs, waits)


def prepared(count, size, cols):
    half = ((count, size, size), BF16)
    return [((HALVES, count, cols // HALVES, size), F32), half, half, half, half]


def prepare_first(rhs, dinv, update, rows, sep, after):
    nodes, size, cols = rhs.shape
    first = nodes // 2
    some = (first, size, cols)
    big = pltpu.VMEM(some, F32)
    return call(
        lambda *refs: prepare_first_kernel(nodes, *refs),
        "prepare_first",
        [(HBM, a) for a in (rows, sep, rhs, dinv, update)] + [(pl.ANY, after)],
        prepared(first, size, cols)
        + [((HALVES, cols // HALVES, size), F32), ((size, nodes), F32)]
        + [((nodes - first, *some[1:]), F32)] * 3,
        [big, big, big, pltpu.VMEM((size, cols), F32)]
        + [pltpu.VMEM(rows.shape, jnp.int32), pltpu.VMEM(sep.shape, F32)]
        + [pltpu.SemaphoreType.DMA((3, nodes)), pltpu.SemaphoreType.DMA((2,))],
    )


def prepare_second(row_columns, rhs, dinv, update, after):
    count, size, cols = rhs.shape
    first = row_columns.shape[1] - count
    return call(
        lambda *refs: prepare_second_kernel(first, *refs),
        "prepare_second",
        [(V, a) for a in (row_columns, rhs, dinv, update)] + [(pl.ANY, after)],
        prepared(count, size, cols),
    )


def forward_kernel(nodes, fronts, *refs):
    (parent_h, acc_a, acc_b, top), parts, refs = refs[:4], (refs[4:8], refs[8:12]), refs[13:]
    solved, send, keep, square, parent, sem = refs[:6]
    accs = refs[6:]
    copy = pltpu.make_async_copy(parent_h, parent, sem)
    copy.start()
    first, width = acc_a.shape[1:3]
    for h in range(HALVES):
        for k in range(nodes):
            accs[h][k] = acc_a[h, k] if k < first else acc_b[h, k - first]
        accs[h][nodes] = top[h]
    for k in range(nodes):
        inv_hi, inv_lo, upd_hi, upd_lo = parts[k // first]
        i = k % first
        inverse = (inv_hi[i], inv_lo[i])
        update = (upd_hi[i], upd_lo[i])
        for h in range(HALVES):
            value = dot3(split(accs[h][k]), inverse, NT)
            solved[k, h * width : (h + 1) * width] = value
            moved = dot3(split(value), update, NT)
            if k + h == 0:
                copy.wait()
            above = nodes if k == nodes - 1 else parent[k]
            accs[h][above] = accs[h][above] - moved
    front = lax.axis_index("front")
    chunk = width * HALVES // fronts
    for h in range(HALVES):
        square[h * width : (h + 1) * width] = accs[h][nodes]
    low_bit = front % 2
    for i in range(fronts // 2):
        for ref, own in ((keep, low_bit), (send, 1 - low_bit)):
            start = pl.multiple_of((2 * i + own) * chunk, 8)
            ref[i * chunk : (i + 1) * chunk] = square[pl.ds(start, chunk), :]


def local_forward(parent, acc_a, acc_b, top, first_halves, second_halves, after, fronts):
    first, (width, size) = acc_a.shape[1], acc_a.shape[2:]
    nodes = first + acc_b.shape[1]
    cols = width * HALVES
    part = ((cols // 2, size), F32)
    return call(
        lambda *refs: forward_kernel(nodes, fronts, *refs),
        "local_forward",
        [(HBM, parent)]
        + [(V, a) for a in (acc_a, acc_b, top, *first_halves, *second_halves)]
        + [(pl.ANY, after)],
        [((nodes, cols, size), F32), part, part],
        [pltpu.VMEM((cols, size), F32), pltpu.SMEM((nodes,), jnp.int32), pltpu.SemaphoreType.DMA]
        + [pltpu.VMEM((nodes + 1, width, size), F32)] * HALVES,
    )


def backward_kernel(nodes, fronts, *refs):
    (parent_h, solved), parts, refs = refs[:2], (refs[2:6], refs[6:10]), refs[10:]
    pieces = refs[:fronts]
    sol, sep_out = refs[fronts : 2 + fronts]
    square, parent, staged, sep_v, sem, sems = refs[2 + fronts : 8 + fronts]
    known = refs[8 + fronts :]
    first = parts[0][0].shape[0]
    copy = pltpu.make_async_copy(parent_h, parent, sem)
    copy.start()
    chunk = pieces[0].shape[0]
    width = known[0].shape[1]
    order = [p[...] for p in pieces]
    for bit in range(fronts.bit_length() - 1):
        flip = bit_of("front", bit) == 1
        order = [jnp.where(flip, order[i ^ (1 << bit)], order[i]) for i in range(fronts)]
    for i, value in enumerate(order):
        at = i * chunk
        known[at // width][nodes, at % width : at % width + chunk] = value
    outs = []
    for k in reversed(range(nodes)):
        i = k % first
        inv_hi, inv_lo, upd_hi, upd_lo = parts[k // first]
        inverse = (inv_hi[i], inv_lo[i])
        update = (upd_hi[i], upd_lo[i])
        if k == nodes - 2:
            copy.wait()
        above = nodes if k == nodes - 1 else parent[k]
        for h in range(HALVES):
            rows = slice(h * width, (h + 1) * width)
            part = solved[k, rows] - dot3(split(known[h][above]), update, NN)
            value = dot3(split(part), inverse, NN)
            known[h][k] = value
            staged[k, :, rows] = value.T
        out = pltpu.make_async_copy(staged.at[k], sol.at[k], sems.at[k])
        out.start()
        outs.append(out)
        if k == nodes - 1:
            for h in range(HALVES):
                square[:, h * width : (h + 1) * width] = known[h][nodes].T
            share = sep_v.shape[0]
            start = pl.multiple_of(lax.axis_index("front") * share, 8)
            sep_v[...] = square[pl.ds(start, share), :]
            out = pltpu.make_async_copy(sep_v, sep_out, sems.at[nodes])
            out.start()
            outs.append(out)
    for out in outs:
        out.wait()


def local_backward(parent, solved, first_halves, second_halves, pieces):
    nodes, cols, size = solved.shape
    fronts = len(pieces)
    sol, sep = jax.ShapeDtypeStruct((nodes, size, cols), F32), ((size // fronts, cols), F32)
    ins = (solved, *first_halves, *second_halves, *pieces)
    return pl.pallas_call(
        lambda *refs: backward_kernel(nodes, fronts, *refs),
        name="local_backward",
        in_specs=[pl.BlockSpec(memory_space=HBM)] + [pl.BlockSpec(memory_space=V)] * len(ins),
        out_specs=(pl.BlockSpec(memory_space=HBM),) * 2,
        out_shape=(sol, jax.ShapeDtypeStruct(*sep)),
        scratch_shapes=[pltpu.VMEM((size, cols), F32), pltpu.SMEM((nodes,), jnp.int32)]
        + [pltpu.VMEM((nodes, size, cols), F32), pltpu.VMEM(*sep), pltpu.SemaphoreType.DMA]
        + [pltpu.SemaphoreType.DMA((nodes + 1,))]
        + [pltpu.VMEM((nodes + 1, cols // HALVES, size), F32)] * HALVES,
        compiler_params=pltpu.CompilerParams(vmem_limit_bytes=VMEM_BYTES),
    )(pltpu.with_memory_space_constraint(parent, HBM), *ins)


def stack_kernel(first, second, out, sems):
    copies = [pltpu.make_async_copy(a, out.at[i], sems.at[i]) for i, a in enumerate((first, second))]
    for c in copies:
        c.start()
    for c in copies:
        c.wait()


def block_map_kernel(fronts, *refs):
    parts = refs[:fronts]
    _, total, part, inverse_halves, square = refs[fronts:]
    front = lax.axis_index("front")
    share = parts[0].shape[1]
    for i in range(fronts):
        start = pl.multiple_of((front ^ i) * share, 8)
        square[:, pl.ds(start, share), :] = parts[i][...]
    inverse = split(square[0])
    inverse_halves[0], inverse_halves[1] = inverse
    value = -dot3(inverse, split(square[1]), NN)
    total[...] = value
    half = part.shape[1]
    send_blocks([part], [value[:half], value[half:]])


def block_map(parts, after):
    fronts = len(parts)
    size = parts[0].shape[2]
    return call(
        lambda *refs: block_map_kernel(fronts, *refs),
        "block_map",
        [(V, a) for a in parts] + [(pl.ANY, after)],
        [((size, size), F32), ((1, size // 2, size), F32), ((2, size, size), BF16)],
        [pltpu.VMEM((2, size, size), F32)],
    )


def quarters(x):
    half = x.shape[0] // 2
    return [x[i : i + half, j : j + half] for i in (0, half) for j in (0, half)]


def joined(a, b, c, d):
    first, second = jnp.concatenate([a, b], axis=1), jnp.concatenate([c, d], axis=1)
    return jnp.concatenate([first, second], axis=0)


def low_core():
    return bit_of("front", 0) == 0


def send_blocks(parts, blocks):
    count = sum(part.shape[0] for part in parts)
    low = low_core()
    i = 0
    for part in parts:
        for j in range(part.shape[0]):
            part[j] = jnp.where(low, blocks[i], blocks[len(blocks) - count + i])
            i += 1


def came_blocks(mine, pairs, total):
    low = low_core()
    mine = [m[j] for m in mine for j in range(m.shape[0])]
    pairs = [p[j] for p in pairs for j in range(p.shape[0])]
    count = len(mine)
    blocks = [jnp.where(low, mine[i], pairs[i]) for i in range(count)]
    for i in range(count, total):
        j = i - total + count
        blocks.append(jnp.where(low, pairs[j], mine[j]))
    return blocks


def k_blocks(k):
    a, b, _, d = quarters(k)
    return [a, b, d]


def k_of(blocks):
    return joined(blocks[0], blocks[1], blocks[1].T, blocks[2])


def send_maps(parts, k, t):
    for i, block in enumerate(k_blocks(k)):
        parts[0][i] = block
    send_blocks(parts[1:], quarters(t))


def first_merge_kernel(*refs):
    own, mine, pairs, _, kept, mixed, halves, curve_u, total_u, total_l, *parts = refs
    upper = bit_of("leaf", 0) == 1
    came = jnp.concatenate(came_blocks([mine], [pairs], 2), axis=0)
    mine = own[...]
    low = jnp.where(upper, came, mine)
    up = jnp.where(upper, mine, came)
    low_s, up_s = split(low), split(up)
    for ref, value in ((total_u, up_s), (total_l, low_s)):
        ref[0], ref[1] = value
    k_up = dot3(up_s, up_s, TN)
    k_up_s = split(k_up)
    curve_u[0], curve_u[1] = k_up_s
    x = dot3(k_up_s, low_s, NN)
    t = dot3(up_s, low_s, NN)
    k = dot3(low_s, low_s, TN) + dot3(low_s, split(x), TN)
    kept[0], kept[1] = k, t
    send_maps(parts, k, t)
    size = low.shape[0]
    row = lax.broadcasted_iota(jnp.int32, (size, size), 0)
    col = lax.broadcasted_iota(jnp.int32, (size, size), 1)
    unit = (row == col).astype(F32)
    keep_split(halves, jnp.where(upper, up.T, unit))
    mixed[0] = jnp.where(upper, t, low + x)
    mixed[1] = jnp.where(upper, unit, up)


def merge_kernel(bit, *refs):
    own, other, mine, pairs, mixed = refs[:5]
    kept, mixed_n, halves, curve_u, total_u, total_l, *parts = refs[5:]
    upper = bit_of("leaf", bit) == 1
    own_k, own_t = own[0], own[1]
    other_k, other_t = k_of(other), joined(*came_blocks([mine], [pairs], 4))
    low_s = split(jnp.where(upper, other_t, own_t))
    up_s = split(jnp.where(upper, own_t, other_t))
    k_low = jnp.where(upper, other_k, own_k)
    k_up_s = split(jnp.where(upper, own_k, other_k))
    for ref, value in ((total_u, up_s), (total_l, low_s), (curve_u, k_up_s)):
        ref[0], ref[1] = value
    x = dot3(k_up_s, low_s, NN)
    x_s = split(x)
    a, e = mixed[0], mixed[1]
    keep_split(halves, jnp.where(upper, a.T, e))
    a_s, e_s = split(a), split(e)
    a_n = jnp.where(upper, dot3(a_s, low_s, NN), a + dot3(e_s, x_s, TN))
    e_n = jnp.where(upper, e, dot3(up_s, e_s, NN))
    k = k_low + dot3(low_s, x_s, TN)
    t = dot3(up_s, low_s, NN)
    kept[0], kept[1] = k, t
    send_maps(parts, k, t)
    mixed_n[0], mixed_n[1] = a_n, e_n


def boundary_kernel(bit, own, other, mixed, two, one, halves, curve, total):
    k, t, k_up = own[0], split(own[1]), split(k_of(other))
    total[0], total[1] = t
    curve[0], curve[1] = k_up
    keep_split(halves, jnp.where(bit_of("leaf", bit) == 1, mixed[0].T, mixed[1]))
    x = dot3(k_up, t, NN)
    two[0], two[1], one[0] = k_blocks(k + dot3(t, split(x), TN))


def last_merge_kernel(bit, mixed, mine, pairs, curve, total, added):
    upper = bit_of("leaf", bit) == 1
    came = split(joined(*came_blocks([mine], [pairs], 4)))
    a, e = mixed[0], mixed[1]
    a_s, e_s = split(a), split(e)
    x = split(dot3(pair(curve), pair(total), NN))
    a_n = jnp.where(upper, dot3(a_s, came, NN), a + dot3(e_s, x, TN))
    e_n = jnp.where(upper, e, dot3(came, e_s, NN))
    keep_split(added, jnp.where(bit_of("leaf", bit + 1) == 1, a_n.T, e_n))


def maps(size):
    both, whole = ((2, size, size), BF16), ((2, size, size), F32)
    half = size // 2
    sends = [((i, half, half), F32) for i in (3, 2)]
    return [whole, whole, both, both, both, both] + sends


def fold_kernel(bit, own, other, send, keep):
    total = send.shape[0]
    chunk = total
    value = own[...] + other[...]
    first, second = value[:chunk], value[chunk:]
    high = bit_of("front", bit) == 1
    send[...] = jnp.where(high, first, second)
    keep[...] = jnp.where(high, second, first)


def enter_kernel(own, other, inverse, own_map, sol, message):
    drive = own[...] + other[...]
    value = dot3(split(drive), pair(inverse), NT)
    sol[...] = value
    rows = value.shape[0]
    message[:rows] = value
    message[rows:] = dot3(split(value), split(own_map[...]), NN)


def step_kernel(bit, rounds, held, *refs):
    sol, own, other, halves, curve_u, total_u, total_l = refs[:7]
    sol_n, message = refs[7 + held], refs[8 + held :]
    last = bit == rounds - 2
    upper = bit_of("leaf", bit) == 1
    rows = sol.shape[0]
    z_own, p_own = own[:rows], own[rows:]
    if last:
        z_other = p_other = other[...]
    else:
        z_other, p_other = other[:rows], other[rows:]
    z_low = jnp.where(upper, z_other, z_own)
    p_up = jnp.where(upper, p_own, p_other)
    z_low_s = split(z_low)
    middle = p_up + dot3(z_low_s, pair(curve_u), NN)
    middle_s = split(middle)
    given = split(jnp.where(upper, z_low, middle))
    sol_n[...] = sol[...] + dot3(given, pair(halves), NN)
    z_up = z_own if last else jnp.where(upper, z_own, z_other)
    p_low = p_own if last else jnp.where(upper, p_other, p_own)
    z_new = z_up + dot3(z_low_s, pair(total_u), NT)
    p_new = p_low + dot3(middle_s, pair(total_l), NN)
    if last:
        message[0][...] = jnp.where(bit_of("leaf", bit + 1) == 1, p_new, z_new)
        message[1][...] = z_new
        return
    message[0][:rows], message[0][rows:] = z_new, p_new
    if bit == rounds - 3:
        message[1][...] = jnp.where(bit_of("leaf", bit + 1) == 1, p_new, z_new)


def turn_kernel(bit, own_z, came, two, one, given):
    value = came[...]
    middle = value + dot3(split(own_z[...]), split(k_of([two[0], two[1], one[0]])), NN)
    given[...] = jnp.where(bit_of("leaf", bit) == 1, value, middle)


def passed_on(bit, last, given, received):
    away = bit_of("leaf", bit) == bit_of("leaf", last)
    return jnp.where(away, received, given)


def leave_kernel(last, sol, given, received, halves, inverse, top):
    came = passed_on(1, last, given[...], received[...])
    value = sol[...] + dot3(split(came), pair(halves), NN)
    top[...] = dot3(split(value), pair(inverse), NN)


def gather_front(x, bits):
    pieces = {0: x}
    for bit in reversed(range(bits)):
        for i in list(pieces):
            pieces[i | (1 << bit)] = exchange(pieces[i], "front", bit)
    return [pieces[i] for i in range(1 << bits)]


def local(rhs_local, dinv_local, update_local, parent, row_blocks, sep_rhs, sep_dinv, sep_coupling):
    fronts, leaves = lax.axis_size("front"), lax.axis_size("leaf")
    front_bits, rounds = fronts.bit_length() - 1, leaves.bit_length() - 1
    size = sep_dinv.shape[1]
    cols = sep_rhs.shape[1]
    chunk = cols // fronts

    (stacked,) = call(
        stack_kernel,
        "stack",
        [(HBM, sep_dinv), (HBM, sep_coupling)],
        [((2, *sep_dinv.shape), F32)],
        [pltpu.SemaphoreType.DMA((2,))],
    )
    came = {0: stacked}
    for bit in reversed(range(1, front_bits)):
        for i in list(came):
            came[i | (1 << bit)] = exchange(came[i], "front", bit)
    came[1] = exchange(stacked, "front", 0)
    acc_a, *first_halves = prepare_first(
        rhs_local, dinv_local, update_local, row_blocks, sep_rhs, stacked
    )
    first_halves, (top, row_columns, *raw) = first_halves[:4], first_halves[4:]
    for i in range(2, fronts, 2):
        held, _ = lax.optimization_barrier((came[i], acc_a))
        came[i + 1] = exchange(held, "front", 0)
    acc_b, *second_halves = prepare_second(row_columns, *raw, acc_a)
    own_map, part, inverse = block_map([came[i] for i in range(fronts)], acc_b)
    mine = exchange(part, "leaf", 0)
    solved, send, keep = local_forward(
        parent, acc_a, acc_b, top, first_halves, second_halves, own_map, fronts
    )
    mine, send = lax.optimization_barrier((mine, send))
    pairs = exchange(mine, "front", 0)
    for bit in range(front_bits):
        received = exchange(send, "front", bit)
        if bit + 1 < front_bits:
            half = ((keep.shape[0] // 2, size), F32)
            send, keep = call(
                lambda *refs, bit=bit: fold_kernel(bit + 1, *refs),
                "fold",
                [(V, keep), (V, received)],
                [half, half],
            )
    kept, mixed, *tools = call(
        first_merge_kernel,
        "merge_0",
        [(V, own_map), (V, mine), (V, pairs), (pl.ANY, send)],
        maps(size),
    )
    tools, parts = tools[:4], tools[4:]
    sol, message = call(
        enter_kernel,
        "enter",
        [(V, keep), (V, received), (V, inverse), (V, own_map)],
        [((chunk, size), F32), ((2 * chunk, size), F32)],
    )
    share = ((chunk, size), F32)
    middle = leaves // 2
    boundary = [(middle - 2 + i, middle + i) for i in range(2)]
    boundary += [(j, i) for i, j in boundary]
    paired = {i for i, _ in boundary}
    boundary += [(i, i ^ 1) for i in range(leaves) if i not in paired]
    for bit in range(rounds - 1):
        last = bit == rounds - 2
        received = exchange(short[0] if last else message, "leaf", bit)
        ahead, held = [], []
        if not last:
            other, mine = [exchange(part, "leaf", bit + 1) for part in parts]
            ahead = [other]
        if bit == rounds - 3:
            half = size // 2
            *ahead, halves, curve, own_t = call(
                lambda *refs: boundary_kernel(rounds - 2, *refs),
                "boundary",
                [(V, kept), (V, other), (V, mixed)],
                [((2, half, half), F32), ((1, half, half), F32)] + [((2, size, size), BF16)] * 3,
            )
            blocks = [lax.ppermute(b, "leaf", boundary) for b in ahead]
            held = [other]
        sol, *message = call(
            lambda *refs, bit=bit: step_kernel(bit, rounds, len(held), *refs),
            f"step_{bit}",
            [(V, a) for a in (sol, message, received, *tools)] + [(pl.ANY, a) for a in held],
            [share] + ([share] if last else [((2 * chunk, size), F32)]) + [share] * (bit >= rounds - 3),
        )
        if not last:
            message, *short = message
        if bit == rounds - 3:
            tools = [halves, curve, own_t, own_t]
        elif not last:
            mine, _ = lax.optimization_barrier((mine, sol))
            pairs = exchange(mine, "front", 0)
            kept, mixed, *tools = call(
                lambda *refs, bit=bit: merge_kernel(bit + 1, *refs),
                f"merge_{bit + 1}",
                [(V, a) for a in (kept, other, mine, pairs, mixed)],
                maps(size),
            )
            tools, parts = tools[:4], tools[4:]
    mine, _ = lax.optimization_barrier((mine, sol))
    pairs = exchange(mine, "front", 0)
    (added,) = call(
        lambda *refs: last_merge_kernel(rounds - 2, *refs),
        "last_merge",
        [(V, a) for a in (mixed, mine, pairs, curve, own_t)],
        [((2, size, size), BF16)],
    )
    came = lax.ppermute(message[0], "leaf", boundary)
    (given,) = call(
        lambda *refs: turn_kernel(rounds - 1, *refs),
        "turn",
        [(V, a) for a in (message[1], came, *blocks)],
        [share],
    )
    for bit in reversed(range(2, rounds - 1)):
        given = passed_on(bit, rounds - 1, given, exchange(given, "leaf", bit))
    received = exchange(given, "leaf", 1)
    (top,) = call(
        lambda *refs: leave_kernel(rounds - 1, *refs),
        "leave",
        [(V, a) for a in (sol, given, received, added, inverse)],
        [share],
    )
    pieces = gather_front(top, front_bits)
    sol_local, sep_solution = local_backward(
        parent, solved, first_halves, second_halves, pieces
    )
    return (sol_local, sep_solution)


def solution(mesh):
    spread3 = P(("leaf", "front"), None, None)
    spread2 = P(("leaf", "front"), None)
    spread1 = P(("leaf", "front"))
    return jax.shard_map(
        local,
        mesh=mesh,
        in_specs=(spread3, spread3, spread3, spread1, spread2, spread2, spread2, spread2),
        out_specs=(spread3, spread2),
        check_vma=False,
    )
```
